32 devices in a mesh: dp: 16 (over z, x, core), tensor: 2 (over y).
Axes of the slice: x: 2, y: 2, z: 4, core: 2. Of those that a mesh axis runs over, the one named last changes fastest.
Arguments:
- block_input: float32 [1024, 16, 1024], P('tensor', 'dp'), may hold values from -6 to 6, as said below
- segment_ids: int32 [16, 1024], P('dp'), may hold values from 0 to 2, never falling along the last dimension, each value on 1 to 512 neighbouring positions
- random_blocks: int32 [16, 16, 16, 3], P('dp', 'tensor'), may hold values from 0 to 15
- w_qkv: float32 [2, 3, 1024, 1024], P(None, None, None, 'tensor'), may hold values from -0.125 to 0.125, as said below
- b_qv: float32 [2, 2, 1024], P(None, None, 'tensor'), may hold values from -3 to 3
- w_out: float32 [2, 1024, 1024], P(None, 'tensor'), may hold values from -3 to 3
- b_out: float32 [2, 1024], replicated, may hold values from -3 to 3
- w_in: float32 [2, 1024, 4096], P(None, None, 'tensor'), may hold values from -0.1875 to 0.1875
- b_in: float32 [2, 4096], P(None, 'tensor'), may hold values from -3 to 3
- w_down: float32 [2, 4096, 1024], P(None, 'tensor'), may hold values from -0.09375 to 0.09375
- b_down: float32 [2, 1024], replicated, may hold values from -3 to 3
- ln_gain: float32 [2, 2, 1024], replicated, may hold values from 0.5 to 1.5
- ln_bias: float32 [2, 2, 1024], replicated, may hold values from -2 to 2
- cotangent: float32 [1024, 16, 1024], P('tensor', 'dp'), may hold values from -6 to 6
Outputs:
- block_output: float32 [1024, 16, 1024], P('tensor', 'dp')
- input_grad: float32 [1024, 16, 1024], P('tensor', 'dp')
- grad_w_qkv: float32 [2, 3, 1024, 1024], P(None, None, None, 'tensor')
- grad_b_qv: float32 [2, 2, 1024], P(None, None, 'tensor')
- grad_w_out: float32 [2, 1024, 1024], P(None, 'tensor')
- grad_b_out: float32 [2, 1024], replicated
- grad_w_in: float32 [2, 1024, 4096], P(None, None, 'tensor')
- grad_b_in: float32 [2, 4096], P(None, 'tensor')
- grad_w_down: float32 [2, 4096, 1024], P(None, 'tensor')
- grad_b_down: float32 [2, 1024], replicated
- grad_ln_gain: float32 [2, 2, 1024], replicated
- grad_ln_bias: float32 [2, 2, 1024], replicated
The draws below stay inside these ranges and needn't reach their ends.
Inputs may be any that keep to these rules, and one draw needn't show every extreme that they name: `segment_ids`: along each sequence the numbers never fall; each of 0 to 2 appears, on at most 512 positions. `block_input`: independent entries of mean 0 and deviation about 1. `w_qkv`: independent entries of mean 0 and deviation about 1 / sqrt(1024).
All inputs are finite; a program needn't handle non-finite values.
Results may differ from the reference program's by a relative error of at most 0.02.
Values may be sent and summed in bfloat16 or wider, within the bound.
A program may use at most 448 MiB of HBM per device.

```python
import math
import jax
import jax.numpy as jnp
import numpy as np
from jax import lax

D = 1024
HEADS = 16
HEAD_DIM = 64
FF = 4096
BLOCK = 64
RANDOM = 3
LAYERS = 2
LEN = 1024
DOCS = 3
SEQS = 16
NBLK = 16


def draw_block_input(key, part):
    values = jax.random.truncated_normal(jax.random.fold_in(key, 11), -6.0, 6.0, (LEN, SEQS, D), jnp.float32)
    return values


def draw_w_qkv(key, part):
    values = jax.random.truncated_normal(jax.random.fold_in(key, 23), -4.0, 4.0, (LAYERS, 3, D, D), jnp.float32)
    return values * D ** (-0.5)


def plant(values, key, least, largest):
    longest = values.shape.index(max(values.shape))
    spots = []
    for shift in (0, 1):
        where = [jax.random.randint(jax.random.fold_in(key, axis), (), 0, length) for axis, length in enumerate(values.shape)]
        where[longest] = (where[longest] + shift) % values.shape[longest]
        spots.append(tuple(where))
    return values.at[spots[0]].set(least).at[spots[1]].set(largest)


def shard_levels(stream_key, extent, cuts, smallest, top_value):
    def one(dim, blocks):
        draws = jax.random.uniform(jax.random.fold_in(jax.random.fold_in(stream_key, 6), dim), (blocks,), jnp.float32, smallest / len(cuts), top_value / len(cuts))
        return jnp.repeat(jnp.exp(draws), extent[dim] // blocks).reshape((-1,) + (1,) * (len(extent) - dim - 1))

    gain = one(*cuts[0])
    for cut in cuts[1:]:
        gain = gain * one(*cut)
    return gain


def length_profile(count, total, reach, lean):
    loads = [(1 << 20) // math.isqrt(standing ** lean) + 1 for standing in range(2, count + 1)]
    surplus, holding = total - reach - (count - 1), [1] * (count - 1)
    while surplus > 0:
        movable = [i for i in range(count - 1) if holding[i] < reach]
        mass, budget = sum([loads[i] for i in movable]), surplus
        for i in movable:
            extra = min(reach - holding[i], max(1, budget * loads[i] // mass), surplus)
            holding[i] = holding[i] + extra
            surplus = surplus - extra
    return np.array([reach] + holding)


def ragged(own_key, number_of, total, bound, skew):
    if number_of == 2:
        one = jax.random.randint(own_key, (), max(1, total - bound), min(bound, total - 1) + 1)
        return jnp.stack([one, total - one])
    lengths = jnp.asarray(length_profile(number_of, total, bound, skew), jnp.int32)
    couples = (number_of - 1) // 2
    source_of, sink = lengths[1:1 + 2 * couples:2], lengths[2:2 + 2 * couples:2]
    margin = jnp.minimum(source_of - 1, bound - sink)
    moved = jax.random.randint(jax.random.fold_in(own_key, 1), (couples,), 0, 1 << 20) % (margin + 1)
    lengths = lengths.at[1:1 + 2 * couples:2].set(source_of - moved).at[2:2 + 2 * couples:2].set(sink + moved)
    return lengths[jax.random.permutation(jax.random.fold_in(own_key, 2), number_of)]


def gaussian(rng, extent, scale, limit, pieces=(), dtype=jnp.bfloat16):
    values = scale * jax.random.normal(rng, extent, jnp.float32)
    if pieces:
        values = values * shard_levels(rng, extent, pieces, -0.22, 0.18)
    return jnp.clip(values, -limit, limit).astype(dtype)


def setup_inputs(seed: int = 0) -> dict:
    streams_of = jax.random.split(jax.random.key(seed), 15)
    block_input = draw_block_input(jax.random.fold_in(streams_of[14], 71), 0)
    segment_ids = jax.vmap(lambda own: jnp.searchsorted(jnp.cumsum(ragged(own, DOCS, LEN, LEN // 2, 2)), jnp.arange(LEN), side="right"))(jax.random.split(streams_of[1], SEQS)).reshape((SEQS, LEN)).astype(jnp.int32)
    random_blocks = plant(jax.random.randint(streams_of[2], (SEQS, HEADS, NBLK, RANDOM), 0, NBLK), jax.random.fold_in(streams_of[2], 1), 0, NBLK - 1).astype(jnp.int32)
    w_qkv = draw_w_qkv(jax.random.fold_in(streams_of[14], 71), 0)
    b_qv = gaussian(streams_of[4], (LAYERS, 2, D), 0.5, 3.0, ((2, 2),), jnp.float32)
    w_out = gaussian(streams_of[5], (LAYERS, D, D), (max(D // 256, 1)) ** -0.5, 3.0, ((1, 2),), jnp.float32)
    b_out = gaussian(streams_of[6], (LAYERS, D), 0.5, 3.0, (), jnp.float32)
    w_in = gaussian(streams_of[7], (LAYERS, D, FF), D ** -0.5, 0.1875, ((2, 2),), jnp.float32)
    b_in = gaussian(streams_of[8], (LAYERS, FF), 0.5, 3.0, ((1, 2),), jnp.float32)
    w_down = gaussian(streams_of[9], (LAYERS, FF, D), FF ** -0.5, 0.09375, ((1, 2),), jnp.float32)
    b_down = gaussian(streams_of[10], (LAYERS, D), 0.5, 3.0, (), jnp.float32)
    ln_gain = jnp.clip(1.0 + 0.1 * jax.random.normal(streams_of[11], (LAYERS, 2, D), jnp.float32), 0.5, 1.5)
    ln_bias = gaussian(streams_of[12], (LAYERS, 2, D), 0.3, 2.0, (), jnp.float32)
    cotangent = gaussian(streams_of[13], (LEN, SEQS, D), 1.0, 6.0, ((0, 2), (1, 16)), jnp.float32)
    return {"block_input": block_input, "segment_ids": segment_ids, "random_blocks": random_blocks, "w_qkv": w_qkv, "b_qv": b_qv, "w_out": w_out, "b_out": b_out, "w_in": w_in, "b_in": b_in, "w_down": w_down, "b_down": b_down, "ln_gain": ln_gain, "ln_bias": ln_bias, "cotangent": cotangent}


@jax.custom_vjp
def low(v):
    return lax.optimization_barrier(v.astype(jnp.bfloat16)).astype(jnp.float32)

@jax.custom_vjp
def low_back(v):
    return v

def low_keep(v):
    return (low(v), None)

def low_pass(kept, grad):
    return (grad,)

def back_keep(v):
    return (v, None)

def back_low(kept, grad):
    return (low(grad),)
low.defvjp(low_keep, low_pass)
low_back.defvjp(back_keep, back_low)

def norm_rows(values, gain_row, shift_row):
    row_mean = lax.optimization_barrier(jnp.mean(values, axis=-1, keepdims=True))
    centred = values - row_mean
    variance = lax.optimization_barrier(jnp.mean(centred * centred, axis=-1, keepdims=True))
    return centred * lax.rsqrt(variance + 1e-06) * gain_row + shift_row

def block_mask(chosen_blocks, segment_rows):
    nblocks = chosen_blocks.shape[2]
    block_index = jnp.arange(nblocks)
    near_blocks = jnp.abs(block_index[:, None] - block_index[None, :]) <= 1
    edge_blocks = (block_index[None, :] == 0) | (block_index[None, :] == nblocks - 1) | (block_index[:, None] == 0) | (block_index[:, None] == nblocks - 1)
    picked_blocks = jnp.any(chosen_blocks[..., None] == block_index, axis=3)
    allowed = near_blocks | edge_blocks | picked_blocks
    block_rows = segment_rows.shape[1] // nblocks
    allowed = jnp.repeat(jnp.repeat(allowed, block_rows, axis=2), block_rows, axis=3)
    same_doc = segment_rows[:, :, None] == segment_rows[:, None, :]
    return allowed & same_doc[:, None]

def one_layer(rows_in, allowed, wq, bq, wo, bo, inner_projection_weight, inner_bias, down_projection_weight, bd, gains, shifts):
    highest_precision = lax.Precision.HIGHEST
    score_scale = HEAD_DIM ** (-0.5)
    length, group_size, model_width = rows_in.shape
    rows_low = low(rows_in)
    projected = jnp.einsum('lsd,tdc->tlsc', rows_low, low(wq), precision=highest_precision)
    qkv_bias = jnp.stack([bq[0], jnp.zeros_like(bq[0]), bq[1]])
    projected = low(low_back(projected + qkv_bias[:, None, None, :]))
    head_view = projected.reshape(3, length, group_size, HEADS, HEAD_DIM)
    queries, key_rows, value_rows = (head_view[0], head_view[1], head_view[2])
    scores = low_back(jnp.einsum('qshd,kshd->shqk', queries, key_rows, precision=highest_precision) * score_scale)
    scores = jnp.where(allowed, scores, -1e+30)
    row_top = lax.optimization_barrier(jnp.max(scores, axis=-1, keepdims=True))
    exp_scores = jnp.exp(scores - row_top)
    attn_probs = exp_scores / lax.optimization_barrier(jnp.sum(exp_scores, axis=-1, keepdims=True))
    context = jnp.einsum('shqk,kshd->qshd', low(attn_probs), value_rows, precision=highest_precision)
    context = low(low_back(context.reshape(length, group_size, model_width)))
    attn_out = low_back(jnp.einsum('lsc,cd->lsd', context, low(wo), precision=highest_precision))
    hidden_rows = norm_rows(rows_in + attn_out + bo, gains[0], shifts[0])
    preactivation = low_back(jnp.einsum('twn,nj->twj', low(hidden_rows), low(inner_projection_weight), precision=highest_precision) + inner_bias)
    activation_output = low(jax.nn.gelu(preactivation, approximate=False))
    feedforward_output = low_back(jnp.einsum('unj,jp->unp', activation_output, low(down_projection_weight), precision=highest_precision))
    return norm_rows(hidden_rows + feedforward_output + bd, gains[1], shifts[1])

def forward(block_input, w_qkv, b_qv, w_out, b_out, w_in, b_in, w_down, b_down, ln_gain, ln_bias, segment_ids, random_blocks):
    group_size = math.gcd(SEQS, 2)
    group_count = SEQS // group_size
    inputs = block_input.reshape(LEN, group_count, group_size, D).transpose(1, 0, 2, 3)
    segment_groups = segment_ids.reshape(group_count, group_size, LEN)
    random_groups = random_blocks.reshape(group_count, group_size, HEADS, LEN // BLOCK, RANDOM)

    def group_step(carry_value, group_items):
        rows_now, segment_rows, chosen_blocks = group_items
        allowed = block_mask(chosen_blocks, segment_rows)
        for layer_index in range(LAYERS):
            rows_now = one_layer(rows_now, allowed, w_qkv[layer_index], b_qv[layer_index], w_out[layer_index], b_out[layer_index], w_in[layer_index], b_in[layer_index], w_down[layer_index], b_down[layer_index], ln_gain[layer_index], ln_bias[layer_index])
        return (carry_value, rows_now)
    _, outputs = lax.scan(jax.checkpoint(group_step), jnp.zeros((), jnp.float32), (inputs, segment_groups, random_groups))
    return outputs.transpose(1, 0, 2, 3).reshape(LEN, SEQS, D)

def reference(block_input, segment_ids, random_blocks, w_qkv, b_qv, w_out, b_out, w_in, b_in, w_down, b_down, ln_gain, ln_bias, cotangent):

    def run_all(rows_in, wq, bq, wo, bo, inner_projection_weight, inner_bias, down_projection_weight, bd, gains, shifts):
        return forward(rows_in, wq, bq, wo, bo, inner_projection_weight, inner_bias, down_projection_weight, bd, gains, shifts, segment_ids, random_blocks)
    result, pull_back = jax.vjp(run_all, block_input, w_qkv, b_qv, w_out, b_out, w_in, b_in, w_down, b_down, ln_gain, ln_bias)
    grads = pull_back(cotangent)
    return (result, grads[0], grads[1], grads[2], grads[3], grads[4], grads[5], grads[6], grads[7], grads[8], grads[9], grads[10])
```

```python
import functools

import jax
import jax.numpy as jnp
from jax import lax
from jax.experimental import pallas as pl
from jax.experimental.pallas import tpu as pltpu
from jax.sharding import PartitionSpec as P

HEAD_DIM = 64
BIG = -1e30
BF16 = jnp.bfloat16
F32 = jnp.float32
MESH = pl.DeviceIdType.MESH
VMEM_LIMIT = 56 << 20

FLIP_Y, FLIP_C, FLIP_X, FLIP_Z0, FLIP_Z1 = 1, 2, 4, 8, 16
DEVICES = 32

GROUPS = 12
OUT_GROUP = 3
FF_GROUPS = 4


def in_group(s):
    return 4 + 2 * s


def down_group(s):
    return 5 + 2 * s


def flip(values, bit):
    pairs = [(i, i ^ bit) for i in range(DEVICES)]
    return jax.tree.map(lambda v: lax.ppermute(v, ("dp", "tensor"), pairs), values)


def swap_core_and_y(values):
    pairs = [(i, i ^ 3 if (i & 1) != ((i >> 1) & 1) else i) for i in range(DEVICES)]
    return jax.tree.map(lambda v: lax.ppermute(v, ("dp", "tensor"), pairs), values)


def nt(a, b):
    return lax.dot_general(a, b, (((1,), (1,)), ((), ())), preferred_element_type=F32)


def nn(a, b):
    return lax.dot_general(a, b, (((1,), (0,)), ((), ())), preferred_element_type=F32)


def tn(a, b):
    return lax.dot_general(a, b, (((0,), (0,)), ((), ())), preferred_element_type=F32)


def block_of(ref):
    width = ref.shape[-1]
    return ref[...].reshape(-1, width)


def convert_kernel(transposed, code_ref, w_ref, *refs):
    o_ref, t_ref = refs[-2:]
    code = code_ref[0]
    half = w_ref[...].reshape(w_ref.shape[-2:])
    t_ref[...] = half.T if transposed else half
    for j in range(16):
        start = pl.multiple_of((j ^ code) * 32, 32)
        o_ref[j // 8, 0, 0, (j % 8) * 32 : (j % 8 + 1) * 32, :] = t_ref[pl.ds(start, 32), :].astype(BF16)


def convert(w, block, index, transposed, count, group, into, total, code):
    width = 1024
    more = [] if into is None else [into]
    return pl.pallas_call(
        functools.partial(convert_kernel, transposed),
        out_shape=jax.ShapeDtypeStruct((2, total, 2, 256, width), BF16),
        grid_spec=pltpu.PrefetchScalarGridSpec(
            num_scalar_prefetch=1,
            grid=(count,),
            in_specs=[pl.BlockSpec(block, lambda i, code: index(i))]
            + [pl.BlockSpec(memory_space=pl.ANY) for _ in more],
            out_specs=pl.BlockSpec((2, 1, 1, 256, width), lambda i, code: (0, group(i), 0, 0, 0)),
            scratch_shapes=[pltpu.VMEM((512, width), F32)],
        ),
        input_output_aliases={2: 0} if more else {},
        compiler_params=pltpu.CompilerParams(vmem_limit_bytes=VMEM_LIMIT),
        cost_estimate=pl.CostEstimate(flops=0, bytes_accessed=count * 512 * width * 6, transcendentals=0),
        name="convert",
    )(code, w, *more)


def place_kernel(transposed, code_ref, g_ref, *refs):
    o_ref, t_ref = refs[-2:]
    code = code_ref[0]
    for j in range(16):
        start = pl.multiple_of((j ^ code) * 32, 32)
        t_ref[j * 32 : (j + 1) * 32, :] = g_ref[0, pl.ds(start, 32), :].astype(F32)
    placed = t_ref[...].T if transposed else t_ref[...]
    o_ref[...] = placed.reshape(o_ref.shape)


def place(grads, shape, block, index, transposed, count, group, into, code):
    width = grads.shape[-1]
    more = [] if into is None else [into]
    return pl.pallas_call(
        functools.partial(place_kernel, transposed),
        out_shape=jax.ShapeDtypeStruct(shape, F32),
        grid_spec=pltpu.PrefetchScalarGridSpec(
            num_scalar_prefetch=1,
            grid=(count,),
            in_specs=[pl.BlockSpec((1, 512, width), lambda i, code: (group(i), 0, 0))]
            + [pl.BlockSpec(memory_space=pl.ANY) for _ in more],
            out_specs=pl.BlockSpec(block, lambda i, code: index(i)),
            scratch_shapes=[pltpu.VMEM((512, width), F32)],
        ),
        input_output_aliases={2: 0} if more else {},
        compiler_params=pltpu.CompilerParams(vmem_limit_bytes=VMEM_LIMIT),
        cost_estimate=pl.CostEstimate(flops=0, bytes_accessed=count * 512 * width * 6, transcendentals=0),
        name="place",
    )(code, grads, *more)


def partner(bit):
    dp, y = lax.axis_index("dp"), lax.axis_index("tensor")
    if bit == FLIP_Y:
        return (dp, 1 - y)
    step = bit // 2
    up = (dp // step) % 2
    return (dp + step * (1 - 2 * up), y)


def greet(bits):
    barrier = pltpu.get_barrier_semaphore()
    for bit in bits:
        pl.semaphore_signal(barrier, inc=1, device_id=partner(bit), device_id_type=MESH)
    pl.semaphore_wait(barrier, len(bits))


class Link:
    def __init__(self, send_sem, recv_sem):
        self.send_sem, self.recv_sem, self.used, self.open = send_sem, recv_sem, 0, []

    def start(self, source, target, bit):
        copy = pltpu.make_async_remote_copy(
            src_ref=source,
            dst_ref=target,
            send_sem=self.send_sem.at[self.used],
            recv_sem=self.recv_sem.at[self.used],
            device_id=partner(bit),
            device_id_type=MESH,
        )
        copy.start()
        self.used += 1
        self.open.append(copy)
        return copy

    def finish(self):
        for copy in self.open:
            copy.wait_send()


def timetable(chains, window):
    events, clock = [], 0.0
    queue = {}
    ready = [(i, 0) for i in range(len(chains))]
    flying = []
    free = {}
    while ready or flying:
        moved = True
        while moved:
            moved = False
            for item in sorted(ready, key=lambda it: (it[0], it[1])):
                link, time = chains[item[0]][item[1]]
                if sum(1 for f in flying if f[2] == link) < window:
                    begin = max(clock, free.get(link, 0.0))
                    free[link] = begin + time
                    flying.append((begin + time + 2.0, item, link))
                    events.append(("start",) + item)
                    ready.remove(item)
                    moved = True
                    break
        flying.sort()
        clock, item, _ = flying.pop(0)
        events.append(("land",) + item)
        if item[1] + 1 < len(chains[item[0]]):
            ready.append((item[0], item[1] + 1))
    return events


def spread_kernel(chunks, w_in_ref, w_ref, send_sem, recv_sem):
    del w_in_ref
    greet((FLIP_Y, FLIP_X, FLIP_Z0, FLIP_C))
    chains, copies = [], []
    for k in chunks:
        if k % GROUPS < 4:
            steps = [
                (FLIP_Y, 5.7, w_ref.at[0, k, 0, pl.ds(0, 128)], w_ref.at[0, k, 1, pl.ds(0, 128)]),
                (FLIP_X, 5.7, w_ref.at[0, k, 1, pl.ds(0, 128)], w_ref.at[0, k, 1, pl.ds(128, 128)]),
            ]
        else:
            steps = [
                (FLIP_Y, 2.9, w_ref.at[0, k, 0, pl.ds(0, 64)], w_ref.at[0, k, 1, pl.ds(0, 64)]),
                (FLIP_Z0, 2.9, w_ref.at[0, k, 1, pl.ds(0, 64)], w_ref.at[0, k, 1, pl.ds(64, 64)]),
                (FLIP_X, 5.7, w_ref.at[0, k, 1, pl.ds(0, 128)], w_ref.at[0, k, 1, pl.ds(128, 128)]),
            ]
            if (k // 2) % 2 == 0:
                steps = [
                    (FLIP_Y, 2.9, w_ref.at[0, k, 0, pl.ds(0, 64)], w_ref.at[0, k, 1, pl.ds(0, 64)]),
                    (FLIP_X, 2.9, w_ref.at[0, k, 1, pl.ds(0, 64)], w_ref.at[0, k, 1, pl.ds(128, 64)]),
                    (FLIP_Z0, 2.9, w_ref.at[0, k, 1, pl.ds(0, 64)], w_ref.at[0, k, 1, pl.ds(64, 64)]),
                    (FLIP_Z0, 2.9, w_ref.at[0, k, 1, pl.ds(128, 64)], w_ref.at[0, k, 1, pl.ds(192, 64)]),
                ]
        steps.append((FLIP_C, 0.9, w_ref.at[0, k, 1], w_ref.at[1, k, 1]))
        chains.append(steps)
        copies.append([None] * len(steps))
    link = Link(send_sem, recv_sem)
    for event, i, step in timetable([[(s[0], s[1]) for s in chain] for chain in chains], 2):
        bit, _, source, target = chains[i][step]
        if event == "start":
            copies[i][step] = link.start(source, target, bit)
        else:
            copies[i][step].wait_recv()
    link.finish()


def spread_weights(weights, chunks):
    count = sum(3 if k % GROUPS < 4 else (5 if (k // 2) % 2 == 0 else 4) for k in chunks)
    return pl.pallas_call(
        functools.partial(spread_kernel, chunks),
        out_shape=jax.ShapeDtypeStruct(weights.shape, weights.dtype),
        in_specs=[pl.BlockSpec(memory_space=pl.ANY)],
        out_specs=pl.BlockSpec(memory_space=pl.ANY),
        scratch_shapes=[pltpu.SemaphoreType.DMA((count,)), pltpu.SemaphoreType.DMA((count,))],
        input_output_aliases={0: 0},
        compiler_params=pltpu.CompilerParams(collective_id=0, has_side_effects=True),
        cost_estimate=pl.CostEstimate(flops=0, bytes_accessed=50 << 20, transcendentals=0),
        name="spread_weights",
    )(weights)


def add_rows(into, other, rows):
    def step(i, _):
        at = pl.ds(pl.multiple_of(i * 32, 32), 32)
        into[at, :] = (into[at, :].astype(F32) + other[at, :].astype(F32)).astype(BF16)
        return 0

    lax.fori_loop(0, rows // 32, step, 0)


def reduce_kernel(chunks, g_ref, o_ref, y_buf, x_buf, z0_buf, z1_buf, all_buf, keep_buf, send_sem, recv_sem, keep_sem, out_sem):
    greet((FLIP_Y, FLIP_X, FLIP_Z0, FLIP_Z1, FLIP_C))
    chains, copies = [], []
    for i, k in enumerate(chunks):
        ys, al = y_buf.at[i], all_buf.at[i]
        chains.append(
            [
                (FLIP_Y, 11.4, g_ref.at[k, pl.ds(256, 256)], ys),
                (FLIP_X, 5.7, ys.at[pl.ds(128, 128)], x_buf.at[i]),
                (FLIP_Z0, 2.9, ys.at[pl.ds(64, 64)], z0_buf.at[i]),
                (FLIP_Z1, 2.9, ys.at[pl.ds(32, 32)], z1_buf.at[i]),
                (FLIP_Z1, 2.9, al.at[pl.ds(0, 32)], al.at[pl.ds(32, 32)]),
                (FLIP_Z0, 2.9, al.at[pl.ds(0, 64)], al.at[pl.ds(64, 64)]),
                (FLIP_X, 5.7, al.at[pl.ds(0, 128)], al.at[pl.ds(128, 128)]),
                (FLIP_C, 0.9, al, o_ref.at[k, pl.ds(256, 256)]),
            ]
        )
        copies.append([None] * 8)
    link = Link(send_sem, recv_sem)
    keeps, outs = {}, {}

    def fetch(i):
        if i < len(chunks):
            keeps[i] = pltpu.make_async_copy(
                g_ref.at[chunks[i], pl.ds(0, 256)], keep_buf.at[i % 2], keep_sem.at[i % 2]
            )
            keeps[i].start()

    fetch(0)
    fetch(1)
    for event, i, step in timetable([[(s[0], s[1]) for s in chain] for chain in chains], 2):
        bit, _, source, target = chains[i][step]
        if event == "start":
            if step == 7:
                outs[i] = pltpu.make_async_copy(source, o_ref.at[chunks[i], pl.ds(0, 256)], out_sem.at[i])
                outs[i].start()
            copies[i][step] = link.start(source, target, bit)
            continue
        copies[i][step].wait_recv()
        if step == 0:
            keeps[i].wait()
            add_rows(y_buf.at[i], keep_buf.at[i % 2], 256)
            fetch(i + 2)
        elif step == 1:
            add_rows(y_buf.at[i], x_buf.at[i], 128)
        elif step == 2:
            add_rows(y_buf.at[i], z0_buf.at[i], 64)
        elif step == 3:
            add_rows(y_buf.at[i], z1_buf.at[i], 32)
            all_buf[i, 0:32, :] = y_buf[i, 0:32, :]
    link.finish()
    for copy in outs.values():
        copy.wait()


def reduce_gradients(grads, chunks):
    n = len(chunks)
    width = grads.shape[-1]
    return pl.pallas_call(
        functools.partial(reduce_kernel, chunks),
        out_shape=jax.ShapeDtypeStruct(grads.shape, grads.dtype),
        in_specs=[pl.BlockSpec(memory_space=pl.ANY)],
        out_specs=pl.BlockSpec(memory_space=pl.ANY),
        scratch_shapes=[
            pltpu.VMEM((n, 256, width), BF16),
            pltpu.VMEM((n, 128, width), BF16),
            pltpu.VMEM((n, 64, width), BF16),
            pltpu.VMEM((n, 32, width), BF16),
            pltpu.VMEM((n, 256, width), BF16),
            pltpu.VMEM((2, 256, width), BF16),
            pltpu.SemaphoreType.DMA((8 * n,)),
            pltpu.SemaphoreType.DMA((8 * n,)),
            pltpu.SemaphoreType.DMA((2,)),
            pltpu.SemaphoreType.DMA((n,)),
        ],
        compiler_params=pltpu.CompilerParams(
            collective_id=1, has_side_effects=True, vmem_limit_bytes=VMEM_LIMIT
        ),
        cost_estimate=pl.CostEstimate(flops=0, bytes_accessed=100 << 20, transcendentals=0),
        name="reduce_gradients",
    )(grads)


def qkv_kernel(x_ref, w_ref, bias_ref, o_ref):
    o_ref[0] = (nt(x_ref[...], block_of(w_ref)) + bias_ref[0, 0]).astype(BF16)


def project_qkv(x_low, weights, bias, first):
    rows, width = x_low.shape
    return pl.pallas_call(
        qkv_kernel,
        out_shape=jax.ShapeDtypeStruct((3, rows, width), BF16),
        grid=(2, 3),
        in_specs=[
            pl.BlockSpec((rows, width), lambda a, t: (0, 0)),
            pl.BlockSpec((1, 1, 2, 256, width), lambda a, t: (a, first + t, 0, 0, 0)),
            pl.BlockSpec((1, 1, 1, 512), lambda a, t: (t, a, 0, 0)),
        ],
        out_specs=pl.BlockSpec((1, rows, 512), lambda a, t: (t, 0, a)),
        compiler_params=pltpu.CompilerParams(vmem_limit_bytes=VMEM_LIMIT),
        cost_estimate=pl.CostEstimate(flops=6 * rows * width * width, bytes_accessed=10 << 20, transcendentals=0),
        name="project_qkv",
    )(x_low, weights, bias)


def norm(r, gain, shift):
    centred = r - jnp.mean(r, axis=-1, keepdims=True)
    rstd = lax.rsqrt(jnp.mean(centred * centred, axis=-1, keepdims=True) + 1e-06)
    return centred * rstd * gain + shift


def norm_back(dy, r, gain):
    centred = r - jnp.mean(r, axis=-1, keepdims=True)
    rstd = lax.rsqrt(jnp.mean(centred * centred, axis=-1, keepdims=True) + 1e-06)
    unit = centred * rstd
    dunit = dy * gain
    dr = rstd * (
        dunit
        - jnp.mean(dunit, axis=-1, keepdims=True)
        - unit * jnp.mean(dunit * unit, axis=-1, keepdims=True)
    )
    return dr, dy * unit


def gelu_and_slope(u):
    cdf = 0.5 * (1.0 + lax.erf(u * (0.5**0.5)))
    pdf = jnp.exp(-0.5 * u * u) * 0.3989422804014327
    return u * cdf, cdf + u * pdf


TILE = 64


def row_tiles(rows, body):
    def step(i, _):
        body(pl.ds(pl.multiple_of(i * TILE, TILE), TILE))
        return 0

    lax.fori_loop(0, rows // TILE, step, 0)


def forward_kernel(
    ctx_ref, x_ref, wo_ref, wi_ref, wd_ref, bi_ref, vec_ref,
    r1_ref, hl_ref, g_ref, slope_ref, r2_ref, x2_ref, xl_ref, acc_ref,
):
    step = pl.program_id(0) * pl.num_programs(1) + pl.program_id(1)
    rows = x_ref.shape[0]

    @pl.when(step == 0)
    def _():
        acc_ref[...] = nn(ctx_ref[:, :512], block_of(wo_ref.at[0])) + nn(ctx_ref[:, 512:], block_of(wo_ref.at[1]))

        def body(at):
            r1 = x_ref[at, :] + acc_ref[at, :] + vec_ref[0:1, :]
            r1_ref[at, :] = r1
            h = norm(r1, vec_ref[1:2, :], vec_ref[2:3, :])
            hl_ref[at, :] = h.astype(BF16)
            acc_ref[at, :] = h + vec_ref[3:4, :]

        row_tiles(rows, body)

    u = nt(hl_ref[...], block_of(wi_ref)) + bi_ref[0, 0]
    g, slope = gelu_and_slope(u)
    g = g.astype(BF16)
    g_ref[...] = g
    slope_ref[...] = slope.astype(BF16)
    acc_ref[...] += nn(g, block_of(wd_ref))

    @pl.when(step == 2 * FF_GROUPS - 1)
    def _():
        def body(at):
            r2 = acc_ref[at, :]
            r2_ref[at, :] = r2
            x2 = norm(r2, vec_ref[4:5, :], vec_ref[5:6, :])
            x2_ref[at, :] = x2
            xl_ref[at, :] = x2.astype(BF16)

        row_tiles(rows, body)


def weight_spec(group, width):
    return pl.BlockSpec((1, 1, 2, 256, width), lambda a, s: (a, group(s), 0, 0, 0))


def forward_tail(ctx, x, weights, bias_in, vectors, first):
    rows, width = x.shape
    whole = pl.BlockSpec((rows, width), lambda a, s: (0, 0))
    hidden = pl.BlockSpec((rows, 512), lambda a, s: (0, a * FF_GROUPS + s))
    sums = jax.ShapeDtypeStruct((rows, width), F32)
    low = jax.ShapeDtypeStruct((rows, width), BF16)
    wide = jax.ShapeDtypeStruct((rows, 4 * width), BF16)
    return pl.pallas_call(
        forward_kernel,
        out_shape=(sums, low, wide, wide, sums, sums, low),
        grid=(2, FF_GROUPS),
        in_specs=[
            whole,
            whole,
            pl.BlockSpec((2, 1, 2, 256, width), lambda a, s: (0, first + OUT_GROUP, 0, 0, 0)),
            weight_spec(lambda s: first + in_group(s), width),
            weight_spec(lambda s: first + down_group(s), width),
            pl.BlockSpec((1, 1, 1, 512), lambda a, s: (a, s, 0, 0)),
            pl.BlockSpec((8, width), lambda a, s: (0, 0)),
        ],
        out_specs=(whole, whole, hidden, hidden, whole, whole, whole),
        scratch_shapes=[pltpu.VMEM((rows, width), F32)],
        compiler_params=pltpu.CompilerParams(vmem_limit_bytes=VMEM_LIMIT),
        cost_estimate=pl.CostEstimate(
            flops=18 * rows * width * width, bytes_accessed=40 << 20, transcendentals=8 * rows * width
        ),
        name="forward_tail",
    )(ctx, x, weights, weights, weights, bias_in, vectors)


def backward_kernel(
    dx_ref, r2_ref, r1_ref, slope_ref, wo_ref, wi_ref, wd_ref, vec_ref,
    dm_ref, du_ref, dr1_ref, da_ref, dctx_ref, dbi_ref, small_ref, acc_ref,
):
    step = pl.program_id(0) * pl.num_programs(1) + pl.program_id(1)
    rows = dx_ref.shape[0]

    def column_sums(parts):
        return [jnp.sum(p, axis=0, keepdims=True) for p in parts]

    @pl.when(step == 0)
    def _():
        small_ref[...] = jnp.zeros_like(small_ref)

        def body(at):
            dy = dx_ref[at, :]
            dr, gain_part = norm_back(dy, r2_ref[at, :], vec_ref[4:5, :])
            acc_ref[at, :] = dr
            dm_ref[at, :] = dr.astype(BF16)
            for i, p in enumerate(column_sums((gain_part, dy, dr))):
                small_ref[i : i + 1, :] += p

        row_tiles(rows, body)

    dg = nt(dm_ref[...], block_of(wd_ref))
    du = (dg * slope_ref[...].astype(F32)).astype(BF16)
    du_ref[...] = du
    dbi_ref[0, 0] = jnp.sum(du.astype(F32), axis=0, keepdims=True)
    acc_ref[...] += nn(du, block_of(wi_ref))

    @pl.when(step == 2 * FF_GROUPS - 1)
    def _():
        def body(at):
            dy = acc_ref[at, :]
            dr, gain_part = norm_back(dy, r1_ref[at, :], vec_ref[1:2, :])
            dr1_ref[at, :] = dr
            da_ref[at, :] = dr.astype(BF16)
            for i, p in enumerate(column_sums((gain_part, dy, dr))):
                small_ref[3 + i : 4 + i, :] += p

        row_tiles(rows, body)
        for a in range(2):
            dctx_ref[:, a * 512 : (a + 1) * 512] = nt(da_ref[...], block_of(wo_ref.at[a])).astype(BF16)


def backward_head(dx, r2, r1, slope, weights, vectors, first):
    rows, width = dx.shape
    whole = pl.BlockSpec((rows, width), lambda a, s: (0, 0))
    hidden = pl.BlockSpec((rows, 512), lambda a, s: (0, a * FF_GROUPS + s))
    sums = jax.ShapeDtypeStruct((rows, width), F32)
    low = jax.ShapeDtypeStruct((rows, width), BF16)
    return pl.pallas_call(
        backward_kernel,
        out_shape=(
            low,
            jax.ShapeDtypeStruct((rows, 4 * width), BF16),
            sums,
            low,
            low,
            jax.ShapeDtypeStruct((2, FF_GROUPS, 1, 512), F32),
            jax.ShapeDtypeStruct((8, width), F32),
        ),
        grid=(2, FF_GROUPS),
        in_specs=[
            whole,
            whole,
            whole,
            hidden,
            pl.BlockSpec((2, 1, 2, 256, width), lambda a, s: (0, first + OUT_GROUP, 0, 0, 0)),
            weight_spec(lambda s: first + in_group(s), width),
            weight_spec(lambda s: first + down_group(s), width),
            pl.BlockSpec((8, width), lambda a, s: (0, 0)),
        ],
        out_specs=(
            whole,
            hidden,
            whole,
            whole,
            whole,
            pl.BlockSpec((1, 1, 1, 512), lambda a, s: (a, s, 0, 0)),
            pl.BlockSpec((8, width), lambda a, s: (0, 0)),
        ),
        scratch_shapes=[pltpu.VMEM((rows, width), F32)],
        compiler_params=pltpu.CompilerParams(vmem_limit_bytes=VMEM_LIMIT),
        cost_estimate=pl.CostEstimate(flops=18 * rows * width * width, bytes_accessed=40 << 20, transcendentals=0),
        name="backward_head",
    )(dx, r2, r1, slope, weights, weights, weights, vectors)


def input_kernel(d_ref, dr1_ref, w_ref, dx_ref, sums_ref):
    @pl.when((pl.program_id(0) == 0) & (pl.program_id(1) == 0))
    def _():
        dx_ref[...] = dr1_ref[...]

    d = d_ref[0]
    sums_ref[0, 0] = jnp.sum(d.astype(F32), axis=0, keepdims=True)
    dx_ref[...] += nn(d, block_of(w_ref))


def input_gradient(d_qkv, dr1, weights, first):
    rows, width = dr1.shape
    whole = pl.BlockSpec((rows, width), lambda a, t: (0, 0))
    return pl.pallas_call(
        input_kernel,
        out_shape=(jax.ShapeDtypeStruct((rows, width), F32), jax.ShapeDtypeStruct((3, 2, 1, 512), F32)),
        grid=(2, 3),
        in_specs=[
            pl.BlockSpec((1, rows, 512), lambda a, t: (t, 0, a)),
            whole,
            weight_spec(lambda t: first + t, width),
        ],
        out_specs=(whole, pl.BlockSpec((1, 1, 1, 512), lambda a, t: (t, a, 0, 0))),
        compiler_params=pltpu.CompilerParams(vmem_limit_bytes=VMEM_LIMIT),
        cost_estimate=pl.CostEstimate(flops=6 * rows * width * width, bytes_accessed=12 << 20, transcendentals=0),
        name="input_gradient",
    )(d_qkv, dr1, weights)


def unit_kernel(left_ref, left_sib_ref, right_ref, right_sib_ref, *refs):
    o_ref = refs[-1]
    left = left_ref[...].reshape(left_ref.shape[-2:])
    left_sib = left_sib_ref[...].reshape(left_sib_ref.shape[-2:])
    o_ref[0] = (tn(left, right_ref[...]) + tn(left_sib, right_sib_ref[...])).astype(BF16)


def unit_gradient(left, left_sib, right, right_sib, into, total, count, group):
    rows, width = right.shape
    more = [] if into is None else [into]
    side = (
        pl.BlockSpec((1, rows, 512), lambda i: (i, 0, 0))
        if left.ndim == 3
        else pl.BlockSpec((rows, 512), lambda i: (0, i))
    )
    whole = pl.BlockSpec((rows, width), lambda i: (0, 0))
    return pl.pallas_call(
        unit_kernel,
        out_shape=jax.ShapeDtypeStruct((total, 512, width), BF16),
        grid=(count,),
        in_specs=[side, side, whole, whole] + [pl.BlockSpec(memory_space=pl.ANY) for _ in more],
        out_specs=pl.BlockSpec((1, 512, width), lambda i: (group(i), 0, 0)),
        input_output_aliases={4: 0} if more else {},
        compiler_params=pltpu.CompilerParams(vmem_limit_bytes=VMEM_LIMIT),
        cost_estimate=pl.CostEstimate(
            flops=4 * rows * width * 512 * count, bytes_accessed=(count * 2 + 2) << 20, transcendentals=0
        ),
        name="unit_gradient",
    )(left, left_sib, right, right_sib, *more)


def pair_lanes(values, e):
    lane = lax.broadcasted_iota(jnp.int32, values.shape, 1)
    return jnp.where(lane // HEAD_DIM == e, values, jnp.zeros_like(values))


def attend_kernel(q_ref, ko_ref, vo_ref, ks_ref, vs_ref, hot_ref, mask_ref, ctx_ref, lse_ref):
    scale = HEAD_DIM**-0.5
    keys = jnp.concatenate([ko_ref[...], ks_ref[...]], axis=0)
    values_t = jnp.concatenate([vo_ref[...], vs_ref[...]], axis=0).T
    query = q_ref[...] * jnp.asarray(scale, BF16)
    heads = []
    for e in range(2):
        right = jnp.concatenate([pair_lanes(query, e), hot_ref[...]], axis=1)
        left = jnp.concatenate([keys, mask_ref[e]], axis=1)
        s = nt(left, right)
        top = jnp.max(s, axis=0, keepdims=True)
        p = jnp.exp(s - top)
        total = jnp.sum(p, axis=0, keepdims=True)
        c = nn(values_t[e * HEAD_DIM : (e + 1) * HEAD_DIM, :], p.astype(BF16))
        heads.append(c * (1.0 / total))
        lse_ref[0, e : e + 1, :] = top + jnp.log(total)
    ctx_ref[...] = jnp.concatenate(heads, axis=0).T.astype(BF16)


def attend(q, k, v, k_sib, v_sib, hot, mask):
    rows, width = q.shape
    pairs = width // 128
    own = pl.BlockSpec((rows, 128), lambda p: (0, p))
    sib = pl.BlockSpec((rows, 128), lambda p: (0, p ^ (pairs // 2)))
    return pl.pallas_call(
        attend_kernel,
        out_shape=(
            jax.ShapeDtypeStruct((rows, width), BF16),
            jax.ShapeDtypeStruct((pairs, 2, rows), F32),
        ),
        grid=(pairs,),
        in_specs=[
            own,
            own,
            own,
            sib,
            sib,
            pl.BlockSpec((rows, 128), lambda p: (0, 0)),
            pl.BlockSpec((2, 2 * rows, 128), lambda p: (p, 0, 0)),
        ],
        out_specs=(own, pl.BlockSpec((1, 2, rows), lambda p: (p, 0, 0))),
        compiler_params=pltpu.CompilerParams(vmem_limit_bytes=VMEM_LIMIT),
        cost_estimate=pl.CostEstimate(
            flops=8 * rows * rows * 128 * pairs * 2, bytes_accessed=16 << 20, transcendentals=4 * rows * rows * pairs
        ),
        name="attend",
    )(q, k, v, k_sib, v_sib, hot, mask)


def attend_back_kernel(
    q_ref, ko_ref, vo_ref, ks_ref, vs_ref, hot_ref, mask_ref, ctx_ref, lse_ref, dctx_ref,
    dq_ref, dko_ref, dvo_ref, dks_ref, dvs_ref,
):
    scale = HEAD_DIM**-0.5
    rows = q_ref.shape[0]
    keys = jnp.concatenate([ko_ref[...], ks_ref[...]], axis=0)
    keys_t = keys.T
    values = jnp.concatenate([vo_ref[...], vs_ref[...]], axis=0)
    query = q_ref[...] * jnp.asarray(scale, BF16)
    dctx = dctx_ref[...]
    delta_t = (dctx.astype(F32) * ctx_ref[...].astype(F32)).T
    dq_heads, dk, dv = [], 0.0, 0.0
    for e in range(2):
        query_e = pair_lanes(query, e)
        dctx_e = pair_lanes(dctx, e)
        right = jnp.concatenate([query_e, hot_ref[...]], axis=1)
        left = jnp.concatenate([keys, mask_ref[e]], axis=1)
        p = jnp.exp(nt(left, right) - lse_ref[0, e : e + 1, :])
        dp = nt(values, dctx_e)
        delta = jnp.sum(delta_t[e * HEAD_DIM : (e + 1) * HEAD_DIM, :], axis=0, keepdims=True)
        ds = (p * (dp - delta)).astype(BF16)
        dk = dk + nn(ds, query_e)
        dv = dv + nn(p.astype(BF16), dctx_e)
        dq_heads.append(nn(keys_t[e * HEAD_DIM : (e + 1) * HEAD_DIM, :], ds) * scale)
    dq_ref[...] = jnp.concatenate(dq_heads, axis=0).T.astype(BF16)
    dko_ref[...] = dk[:rows]
    dvo_ref[...] = dv[:rows]
    dks_ref[...] = dk[rows:].astype(BF16)
    dvs_ref[...] = dv[rows:].astype(BF16)


def attend_back(q, k, v, k_sib, v_sib, hot, mask, ctx, lse, dctx):
    rows, width = q.shape
    pairs = width // 128
    own = pl.BlockSpec((rows, 128), lambda p: (0, p))
    sib = pl.BlockSpec((rows, 128), lambda p: (0, p ^ (pairs // 2)))
    return pl.pallas_call(
        attend_back_kernel,
        out_shape=(
            jax.ShapeDtypeStruct((rows, width), BF16),
            jax.ShapeDtypeStruct((rows, width), F32),
            jax.ShapeDtypeStruct((rows, width), F32),
            jax.ShapeDtypeStruct((rows, width), BF16),
            jax.ShapeDtypeStruct((rows, width), BF16),
        ),
        grid=(pairs,),
        in_specs=[
            own,
            own,
            own,
            sib,
            sib,
            pl.BlockSpec((rows, 128), lambda p: (0, 0)),
            pl.BlockSpec((2, 2 * rows, 128), lambda p: (p, 0, 0)),
            own,
            pl.BlockSpec((1, 2, rows), lambda p: (p, 0, 0)),
            own,
        ],
        out_specs=(own, own, own, sib, sib),
        compiler_params=pltpu.CompilerParams(vmem_limit_bytes=VMEM_LIMIT),
        cost_estimate=pl.CostEstimate(
            flops=20 * rows * rows * 128 * pairs * 2, bytes_accessed=24 << 20, transcendentals=4 * rows * rows * pairs
        ),
        name="attend_back",
    )(q, k, v, k_sib, v_sib, hot, mask, ctx, lse, dctx)


def flip_order(values, axis, bits):
    for i, bit in enumerate(bits):
        values = jnp.where(bit == 0, values, jnp.flip(values, axis + i))
    return values


def sum_everywhere(values):
    for bit in (FLIP_C, FLIP_Y, FLIP_X, FLIP_Z0, FLIP_Z1):
        values = values + flip(values, bit)
    return values


def sequence_shards(
    block_input, segment_ids, random_blocks, w_qkv, b_qv, w_out, b_out, w_in, b_in, w_down, b_down,
    ln_gain, ln_bias, cotangent,
):
    y = lax.axis_index("tensor")
    dp = lax.axis_index("dp")
    core, x_bit, z0, z1 = dp % 2, (dp // 2) % 2, (dp // 4) % 2, dp // 8
    code = core * 8 + x_bit * 4 + z0 * 2 + z1
    code_arg = code.reshape(1).astype(jnp.int32)
    device_bits = (core, x_bit, z0, z1)

    rows, _, width = block_input.shape
    layers = w_qkv.shape[0]
    blocks = random_blocks.shape[2]
    own_blocks = blocks // 2
    heads = random_blocks.shape[1] * 2

    stream_low = swap_core_and_y(block_input[:, 0].astype(BF16))
    upstream_low = swap_core_and_y(cotangent[:, 0].astype(BF16))

    chosen = random_blocks[0]
    packed = jnp.concatenate(
        [chosen.reshape(-1), flip(chosen, FLIP_Y).reshape(-1), segment_ids[0]]
    )
    packed = jnp.where(core == y, packed, flip(packed, FLIP_C))
    chosen = packed[: 2 * chosen.size].reshape(2, heads // 2, blocks, -1)
    segments = packed[2 * random_blocks.size :]
    chosen = flip_order(chosen.reshape(2, 2, 2, 2, blocks, -1), 1, device_bits[:3])
    chosen = chosen.transpose(1, 0, 2, 3, 4, 5).reshape(heads, blocks, -1)
    segments = segments.reshape(2, rows)
    segments = jnp.where(core == 0, segments, segments[::-1]).reshape(-1)
    query_block = core * own_blocks + jnp.arange(own_blocks)
    key_block = jnp.arange(blocks) ^ (core * own_blocks)
    allowed = (
        (jnp.abs(query_block[:, None] - key_block[None, :]) <= 1)
        | (key_block[None, :] == 0)
        | (key_block[None, :] == blocks - 1)
        | (query_block[:, None] == 0)
        | (query_block[:, None] == blocks - 1)
    )
    chosen = lax.dynamic_slice_in_dim(chosen, core * own_blocks, own_blocks, axis=1)
    allowed = allowed[None] | jnp.any(chosen[:, :, None, :] == key_block[None, None, :, None], axis=3)
    block_rows = rows // own_blocks
    block_part = jnp.where(allowed, 0.0, BIG).astype(BF16).transpose(0, 2, 1)
    block_part = jnp.repeat(block_part, block_rows, axis=1)
    documents = jnp.arange(128 - own_blocks)
    document_part = jnp.where(
        (segments[:, None] == documents[None, :]) | (documents[None, :] > 7), 0.0, BIG
    ).astype(BF16)
    mask = jnp.concatenate(
        [block_part, jnp.broadcast_to(document_part[None], (heads,) + document_part.shape)], axis=2
    )
    hot = jnp.concatenate(
        [
            jnp.repeat(jnp.eye(own_blocks, dtype=BF16), block_rows, axis=0),
            (segments[:rows, None] == documents[None, :]).astype(BF16),
        ],
        axis=1,
    )

    bias_pack = jnp.concatenate(
        [
            flip_order(b_qv.reshape(layers * 2, 2, 2, 2, 2, -1), 1, device_bits).reshape(-1),
            flip_order(b_in.reshape(layers * FF_GROUPS, 2, 2, 2, 2, -1), 1, device_bits).reshape(-1),
        ]
    )
    bias_far = flip(bias_pack, FLIP_Y)
    n_qv = b_qv.size

    def local_bias(near, far, count):
        near, far = near.reshape(count, 2, 1, 256), far.reshape(count, 2, 1, 256)
        return jnp.concatenate([near, far], axis=2).reshape(count, 2, 512)

    bias_qv = local_bias(bias_pack[:n_qv], bias_far[:n_qv], layers * 2).reshape(layers, 2, 2, 1, 512)
    bias_qkv = jnp.stack([bias_qv[:, 0], jnp.zeros_like(bias_qv[:, 0]), bias_qv[:, 1]], axis=1)
    bias_in = local_bias(bias_pack[n_qv:], bias_far[n_qv:], layers * FF_GROUPS)
    bias_in = bias_in.reshape(layers, FF_GROUPS, 2, 1, 512).swapaxes(1, 2)

    total = layers * GROUPS
    weights = None
    for layer in range(layers):
        first = layer * GROUPS
        put = functools.partial(convert, total=total, code=code_arg)
        weights = put(
            w_qkv, (1, 1, width, 512), lambda i, l=layer: (l, i, 0, 0), True, 3, lambda i, f=first: f + i, weights
        )
        weights = put(
            w_out, (1, 512, width), lambda i, l=layer: (l, 0, 0), False, 1, lambda i, f=first: f + OUT_GROUP, weights
        )
        weights = put(
            w_in, (1, width, 512), lambda i, l=layer: (l, 0, i), True, FF_GROUPS,
            lambda i, f=first: f + in_group(i), weights,
        )
        weights = put(
            w_down, (1, 512, width), lambda i, l=layer: (l, i, 0), False, FF_GROUPS,
            lambda i, f=first: f + down_group(i), weights,
        )
    weights = spread_weights(weights, tuple(range(total)))

    vectors = [
        jnp.stack(
            [
                b_out[l], ln_gain[l, 0], ln_bias[l, 0], b_down[l], ln_gain[l, 1], ln_bias[l, 1],
                b_out[l], b_out[l],
            ]
        )
        for l in range(layers)
    ]
    stream, stream_now = stream_low.astype(F32), stream_low
    saved = []
    half = width // 2
    for layer in range(layers):
        first = layer * GROUPS
        xb = stream_now
        qkv = project_qkv(xb, weights, bias_qkv[layer], first)
        q, k, v = qkv[0], qkv[1], qkv[2]
        k_sib, v_sib = flip((k, v), FLIP_C)
        ctx, lse = attend(q, k, v, k_sib, v_sib, hot, mask)
        r1, hidden, g, slope, r2, stream, stream_now = forward_tail(
            ctx, stream, weights, bias_in[layer], vectors[layer], first
        )
        xb_sib, hidden_sib = flip((xb, hidden), FLIP_C)
        ctx_sib = flip(ctx[:, half:], FLIP_C)
        g_sib = flip(g[:, 4 * half :], FLIP_C)
        saved.append((xb, xb_sib, q, k, v, k_sib, v_sib, ctx, ctx_sib, lse, r1, hidden, hidden_sib, g, g_sib, slope, r2))
    block_output = swap_core_and_y(stream_now).astype(F32)[:, None]

    upstream = upstream_low.astype(F32)
    grads = None
    small = [None] * layers
    for layer in reversed(range(layers)):
        first = layer * GROUPS
        xb, xb_sib, q, k, v, k_sib, v_sib, ctx, ctx_sib, lse, r1, hidden, hidden_sib, g, g_sib, slope, r2 = saved[layer]
        dm, du, dr1, da, dctx, d_b_in, rows_small = backward_head(
            upstream, r2, r1, slope, weights, vectors[layer], first
        )
        dm_sib, da_sib = flip((dm, da), FLIP_C)
        du_sib = flip(du[:, 4 * half :], FLIP_C)
        unit = functools.partial(unit_gradient, total=total)
        grads = unit(g, g_sib, dm, dm_sib, grads, count=FF_GROUPS, group=lambda i, f=first: f + down_group(i))
        grads = unit(du, du_sib, hidden, hidden_sib, grads, count=FF_GROUPS, group=lambda i, f=first: f + in_group(i))
        grads = unit(ctx, ctx_sib, da, da_sib, grads, count=1, group=lambda i, f=first: f + OUT_GROUP)
        dq, dk, dv, dk_sib, dv_sib = attend_back(q, k, v, k_sib, v_sib, hot, mask, ctx, lse, dctx)
        dk_far, dv_far = flip((dk_sib, dv_sib), FLIP_C)
        d_qkv = jnp.stack(
            [dq, (dk + dk_far.astype(F32)).astype(BF16), (dv + dv_far.astype(F32)).astype(BF16)]
        )
        d_qkv_sib = flip(d_qkv[:, :, half:], FLIP_C)
        grads = unit(d_qkv, d_qkv_sib, xb, xb_sib, grads, count=3, group=lambda i, f=first: f + i)
        upstream, qkv_sums = input_gradient(d_qkv, dr1, weights, first)
        small[layer] = (
            jnp.stack([qkv_sums[0], qkv_sums[2]]),
            rows_small[5],
            d_b_in,
            rows_small[2],
            jnp.stack([rows_small[3], rows_small[0]]),
            jnp.stack([rows_small[4], rows_small[1]]),
        )
    input_grad = swap_core_and_y(upstream.astype(BF16)).astype(F32)[:, None]
    grads = reduce_gradients(grads, tuple(range(total)))

    placed = [None] * 4
    for layer in range(layers):
        first = layer * GROUPS
        put = functools.partial(place, grads, code=code_arg)
        placed[0] = put(
            w_qkv.shape, (1, 1, width, 512), lambda i, l=layer: (l, i, 0, 0), True, 3, lambda i, f=first: f + i, placed[0]
        )
        placed[1] = put(
            w_out.shape, (1, 512, width), lambda i, l=layer: (l, 0, 0), False, 1,
            lambda i, f=first: f + OUT_GROUP, placed[1],
        )
        placed[2] = put(
            w_in.shape, (1, width, 512), lambda i, l=layer: (l, 0, i), True, FF_GROUPS,
            lambda i, f=first: f + in_group(i), placed[2],
        )
        placed[3] = put(
            w_down.shape, (1, 512, width), lambda i, l=layer: (l, i, 0), False, FF_GROUPS,
            lambda i, f=first: f + down_group(i), placed[3],
        )
    stacks = [jnp.stack([small[layer][member] for layer in range(layers)]) for member in range(6)]
    stacks[2] = stacks[2].swapaxes(1, 2)

    def global_order(values, lead):
        values = values.reshape(lead, 2, 2, 2, 2, 2, 32).swapaxes(1, 2)
        values = flip_order(values, 1, (y,) + device_bits)
        return values.swapaxes(0, 1).reshape(2, -1)

    stacks[0] = global_order(stacks[0], layers * 2)
    stacks[2] = global_order(stacks[2], layers * FF_GROUPS)
    summed = sum_everywhere(jnp.concatenate([s.reshape(-1) for s in stacks]))
    parts, at = [], 0
    for s in stacks:
        parts.append(summed[at : at + s.size].reshape(s.shape))
        at += s.size
    g_b_qv = lax.dynamic_index_in_dim(parts[0], y, axis=0, keepdims=False).reshape(b_qv.shape)
    g_b_in = lax.dynamic_index_in_dim(parts[2], y, axis=0, keepdims=False).reshape(b_in.shape)
    return (
        block_output,
        input_grad,
        placed[0],
        g_b_qv,
        placed[1],
        parts[1],
        placed[2],
        g_b_in,
        placed[3],
        parts[3],
        parts[4],
        parts[5],
    )


def as_sent(array):

    def short(part):
        return part.astype(jnp.bfloat16) if part.dtype == jnp.float32 else part

    return jax.tree.map(short, array)


def norm_rows(values, gain_row, shift_row):
    row_mean = jnp.mean(values, axis=-1, keepdims=True)
    centred = values - row_mean
    variance = jnp.mean(centred * centred, axis=-1, keepdims=True)
    return centred * lax.rsqrt(variance + 1e-06) * gain_row + shift_row


def gelu_exact(values):
    return jax.nn.gelu(values, approximate=False)


def block_mask(chosen_blocks, segment_rows):
    nblocks = chosen_blocks.shape[2]
    block_index = jnp.arange(nblocks)
    near_blocks = jnp.abs(block_index[:, None] - block_index[None, :]) <= 1
    edge_blocks = (
        (block_index[None, :] == 0)
        | (block_index[None, :] == nblocks - 1)
        | (block_index[:, None] == 0)
        | (block_index[:, None] == nblocks - 1)
    )
    picked_blocks = jnp.any(chosen_blocks[..., None] == block_index, axis=3)
    allowed = near_blocks | edge_blocks | picked_blocks
    block_rows = segment_rows.shape[1] // nblocks
    allowed = jnp.repeat(jnp.repeat(allowed, block_rows, axis=2), block_rows, axis=3)
    same_doc = segment_rows[:, :, None] == segment_rows[:, None, :]
    return allowed & same_doc[:, None]


def masked_scores(queries, key_rows, allowed, score_scale):
    scores = (
        jnp.einsum("qshd,kshd->shqk", queries, key_rows, preferred_element_type=jnp.float32)
        * score_scale
    )
    return jnp.where(allowed, scores, -1e30)


def shards(
    block_input,
    segment_ids,
    random_blocks,
    w_qkv,
    b_qv,
    w_out,
    b_out,
    w_in,
    b_in,
    w_down,
    b_down,
    ln_gain,
    ln_bias,
    cotangent,
):
    score_scale = HEAD_DIM ** (-0.5)
    shard_rows, seq_count, model_width = block_input.shape
    layers = w_qkv.shape[0]
    local_width = w_qkv.shape[3]
    local_heads = local_width // HEAD_DIM
    allowed = block_mask(random_blocks, segment_ids)
    saved_acts = []
    stream = block_input
    for layer_index in range(layers):
        w_proj = w_qkv[layer_index].astype(jnp.bfloat16)
        w_mix = w_out[layer_index].astype(jnp.bfloat16)
        rows_low = stream.astype(jnp.bfloat16)
        full_rows = lax.all_gather(rows_low, "tensor", axis=0, tiled=True)
        length = full_rows.shape[0]
        projected = jnp.einsum(
            "lsd,tdc->tlsc", full_rows, w_proj, preferred_element_type=jnp.float32
        )
        qkv_bias = jnp.stack(
            [b_qv[layer_index, 0], jnp.zeros_like(b_qv[layer_index, 0]), b_qv[layer_index, 1]]
        )
        qkv_low = (projected + qkv_bias[:, None, None, :]).astype(jnp.bfloat16)
        head_view = qkv_low.reshape(3, length, seq_count, local_heads, HEAD_DIM)
        scores = masked_scores(head_view[0], head_view[1], allowed, score_scale)
        row_top = jnp.max(scores, axis=-1, keepdims=True)
        log_total = row_top + jnp.log(jnp.sum(jnp.exp(scores - row_top), axis=-1, keepdims=True))
        probs_low = jnp.exp(scores - log_total).astype(jnp.bfloat16)
        context = jnp.einsum(
            "shqk,kshd->qshd", probs_low, head_view[2], preferred_element_type=jnp.float32
        )
        context = context.reshape(length, seq_count, local_width).astype(jnp.bfloat16)
        mixed = lax.psum_scatter(
            jnp.einsum("lsc,cd->lsd", context, w_mix, preferred_element_type=jnp.float32).astype(
                jnp.bfloat16
            ),
            "tensor",
            scatter_dimension=0,
            tiled=True,
        ).astype(jnp.float32)
        first_sum = stream + mixed + b_out[layer_index]
        hidden_rows = norm_rows(first_sum, ln_gain[layer_index, 0], ln_bias[layer_index, 0])
        hidden_low = hidden_rows.astype(jnp.bfloat16)
        up_weight = w_in[layer_index].astype(jnp.bfloat16)
        backward_weight = w_down[layer_index].astype(jnp.bfloat16)
        hidden_full = lax.all_gather(hidden_low, "tensor", axis=0, tiled=True)
        preactivation = (
            jnp.einsum("twn,nj->twj", hidden_full, up_weight, preferred_element_type=jnp.float32)
            + b_in[layer_index]
        )
        activation_reduced = gelu_exact(preactivation).astype(jnp.bfloat16)
        grown = lax.psum_scatter(
            jnp.einsum(
                "unj,jp->unp",
                activation_reduced,
                backward_weight,
                preferred_element_type=jnp.float32,
            ).astype(jnp.bfloat16),
            "tensor",
            scatter_dimension=0,
            tiled=True,
        ).astype(jnp.float32)
        second_sum = hidden_rows + grown + b_down[layer_index]
        stream = norm_rows(second_sum, ln_gain[layer_index, 1], ln_bias[layer_index, 1])
        keep_rows, keep_hidden = (full_rows, hidden_full)
        saved_acts.append(
            (
                keep_rows,
                head_view,
                log_total,
                context,
                first_sum,
                keep_hidden,
                preactivation,
                activation_reduced,
                second_sum,
                up_weight,
                backward_weight,
            )
        )
    upstream = cotangent
    grads_by_layer = [None] * layers
    for layer_index in reversed(range(layers)):
        (
            keep_rows,
            head_view,
            log_total,
            context,
            first_sum,
            keep_hidden,
            preactivation,
            activation_reduced,
            second_sum,
            up_weight,
            backward_weight,
        ) = saved_acts[layer_index]
        full_rows, hidden_full = (keep_rows, keep_hidden)
        length = full_rows.shape[0]
        w_proj = w_qkv[layer_index].astype(jnp.bfloat16)
        w_mix = w_out[layer_index].astype(jnp.bfloat16)
        _, pull_second = jax.vjp(
            norm_rows, second_sum, ln_gain[layer_index, 1], ln_bias[layer_index, 1]
        )
        d_second, d_gain_two, d_shift_two = pull_second(upstream)
        _, pull_gelu = jax.vjp(gelu_exact, preactivation)
        widened_full = lax.all_gather(d_second.astype(jnp.bfloat16), "tensor", axis=0, tiled=True)
        down_gradient = jnp.einsum(
            "uxc,uxw->cw", activation_reduced, widened_full, preferred_element_type=jnp.float32
        )
        activation_gradient = jnp.einsum(
            "mra,xa->mrx", widened_full, backward_weight, preferred_element_type=jnp.float32
        )
        preactivation_gradient_reduced = pull_gelu(activation_gradient)[0].astype(jnp.bfloat16)
        up_gradient = jnp.einsum(
            "kmx,kmt->xt",
            hidden_full,
            preactivation_gradient_reduced,
            preferred_element_type=jnp.float32,
        )
        g_up_bias = jnp.sum(preactivation_gradient_reduced.astype(jnp.float32), axis=(0, 1))
        d_hidden = d_second + lax.psum_scatter(
            jnp.einsum(
                "hmp,tp->hmt",
                preactivation_gradient_reduced,
                up_weight,
                preferred_element_type=jnp.float32,
            ).astype(jnp.bfloat16),
            "tensor",
            scatter_dimension=0,
            tiled=True,
        ).astype(jnp.float32)
        _, pull_first = jax.vjp(
            norm_rows, first_sum, ln_gain[layer_index, 0], ln_bias[layer_index, 0]
        )
        d_first, d_gain_one, d_shift_one = pull_first(d_hidden)
        full_mixed = lax.all_gather(d_first.astype(jnp.bfloat16), "tensor", axis=0, tiled=True)
        g_out = jnp.einsum("lsc,lsd->cd", context, full_mixed, preferred_element_type=jnp.float32)
        d_context = jnp.einsum(
            "lsd,cd->lsc", full_mixed, w_mix, preferred_element_type=jnp.float32
        ).astype(jnp.bfloat16)
        d_context = d_context.reshape(length, seq_count, local_heads, HEAD_DIM)
        queries, key_rows, value_rows = (head_view[0], head_view[1], head_view[2])
        scores = masked_scores(queries, key_rows, allowed, score_scale)
        attn_probs = jnp.exp(scores - log_total)
        probs_low = attn_probs.astype(jnp.bfloat16)
        d_probs = jnp.einsum(
            "qshd,kshd->shqk", d_context, value_rows, preferred_element_type=jnp.float32
        )
        d_scores = attn_probs * (d_probs - jnp.sum(d_probs * attn_probs, axis=-1, keepdims=True))
        d_scores = d_scores.astype(jnp.bfloat16)
        d_query = (
            jnp.einsum("shqk,kshd->qshd", d_scores, key_rows, preferred_element_type=jnp.float32)
            * score_scale
        )
        d_key = (
            jnp.einsum("shqk,qshd->kshd", d_scores, queries, preferred_element_type=jnp.float32)
            * score_scale
        )
        d_value = jnp.einsum(
            "shqk,qshd->kshd", probs_low, d_context, preferred_element_type=jnp.float32
        )
        d_qkv = (
            jnp.stack([d_query, d_key, d_value])
            .reshape(3, length, seq_count, local_width)
            .astype(jnp.bfloat16)
        )
        g_proj = jnp.einsum("lsd,tlsc->tdc", full_rows, d_qkv, preferred_element_type=jnp.float32)
        qkv_sums = jnp.sum(d_qkv.astype(jnp.float32), axis=(1, 2))
        g_bias = jnp.stack([qkv_sums[0], qkv_sums[2]])
        upstream = d_first + lax.psum_scatter(
            jnp.einsum("tlsc,tdc->lsd", d_qkv, w_proj, preferred_element_type=jnp.float32).astype(
                jnp.bfloat16
            ),
            "tensor",
            scatter_dimension=0,
            tiled=True,
        ).astype(jnp.float32)
        weight_grads = (g_proj, g_bias, g_out, up_gradient, g_up_bias, down_gradient)
        small_grads = (
            jnp.sum(d_first, axis=(0, 1)),
            jnp.sum(d_second, axis=(0, 1)),
            jnp.stack([d_gain_one, d_gain_two]),
            jnp.stack([d_shift_one, d_shift_two]),
        )
        grads_by_layer[layer_index] = (weight_grads, small_grads)
    weight_stack = tuple(
        (
            jnp.stack([grads_by_layer[layer_index][0][member] for layer_index in range(layers)])
            for member in range(6)
        )
    )
    small_stack = tuple(
        (
            jnp.stack([grads_by_layer[layer_index][1][member] for layer_index in range(layers)])
            for member in range(4)
        )
    )
    weight_stack = jax.tree.map(
        lambda part: part.astype(jnp.float32), lax.psum(as_sent(weight_stack), "dp")
    )
    small_stack = lax.psum(small_stack, ("dp", "tensor"))
    return (
        stream,
        upstream,
        weight_stack[0],
        weight_stack[1],
        weight_stack[2],
        small_stack[0],
        weight_stack[3],
        weight_stack[4],
        weight_stack[5],
        small_stack[1],
        small_stack[2],
        small_stack[3],
    )


def solution(mesh):
    by_sequence = mesh.shape["tensor"] == 2 and mesh.shape["dp"] == 16
    return jax.shard_map(
        sequence_shards if by_sequence else shards,
        mesh=mesh,
        in_specs=(
            P("tensor", "dp", None),
            P("dp", None),
            P("dp", "tensor", None, None),
            P(None, None, None, "tensor"),
            P(None, None, "tensor"),
            P(None, "tensor", None),
            P(),
            P(None, None, "tensor"),
            P(None, "tensor"),
            P(None, "tensor", None),
            P(),
            P(),
            P(),
            P("tensor", "dp", None),
        ),
        out_specs=(
            P("tensor", "dp", None),
            P("tensor", "dp", None),
            P(None, None, None, "tensor"),
            P(None, None, "tensor"),
            P(None, "tensor", None),
            P(),
            P(None, None, "tensor"),
            P(None, "tensor"),
            P(None, "tensor", None),
            P(),
            P(),
            P(),
        ),
        check_vma=False,
    )
```

```python
import functools

import jax
import jax.numpy as jnp
from jax import lax
from jax.experimental import pallas as pl
from jax.experimental.pallas import tpu as pltpu
from jax.sharding import PartitionSpec as P

HEAD_DIM = 64
BIG = -1e30
BF16 = jnp.bfloat16
F32 = jnp.float32
MESH = pl.DeviceIdType.MESH
VMEM_LIMIT = 56 << 20

FLIP_Y, FLIP_C, FLIP_X, FLIP_Z0, FLIP_Z1 = 1, 2, 4, 8, 16
DEVICES = 32

GROUPS = 12
OUT_GROUP = 3
FF_GROUPS = 4


def in_group(s):
    return 4 + 2 * s


def down_group(s):
    return 5 + 2 * s


def flip(values, bit):
    pairs = [(i, i ^ bit) for i in range(DEVICES)]
    return jax.tree.map(lambda v: lax.ppermute(v, ("dp", "tensor"), pairs), values)


def swap_core_and_y(values):
    pairs = [(i, i ^ 3 if (i & 1) != ((i >> 1) & 1) else i) for i in range(DEVICES)]
    return jax.tree.map(lambda v: lax.ppermute(v, ("dp", "tensor"), pairs), values)


def nt(a, b):
    return lax.dot_general(a, b, (((1,), (1,)), ((), ())), preferred_element_type=F32)


def nn(a, b):
    return lax.dot_general(a, b, (((1,), (0,)), ((), ())), preferred_element_type=F32)


def tn(a, b):
    return lax.dot_general(a, b, (((0,), (0,)), ((), ())), preferred_element_type=F32)


def block_of(ref):
    width = ref.shape[-1]
    return ref[...].reshape(-1, width)


def convert_kernel(transposed, code_ref, w_ref, *refs):
    o_ref, t_ref = refs[-2:]
    code = code_ref[0]
    half = w_ref[...].reshape(w_ref.shape[-2:])
    t_ref[...] = half.T if transposed else half
    for j in range(16):
        start = pl.multiple_of((j ^ code) * 32, 32)
        o_ref[j // 8, 0, 0, (j % 8) * 32 : (j % 8 + 1) * 32, :] = t_ref[pl.ds(start, 32), :].astype(BF16)


def convert(w, block, index, transposed, count, group, into, total, code):
    width = 1024
    more = [] if into is None else [into]
    return pl.pallas_call(
        functools.partial(convert_kernel, transposed),
        out_shape=jax.ShapeDtypeStruct((2, total, 2, 256, width), BF16),
        grid_spec=pltpu.PrefetchScalarGridSpec(
            num_scalar_prefetch=1,
            grid=(count,),
            in_specs=[pl.BlockSpec(block, lambda i, code: index(i))]
            + [pl.BlockSpec(memory_space=pl.ANY) for _ in more],
            out_specs=pl.BlockSpec((2, 1, 1, 256, width), lambda i, code: (0, group(i), 0, 0, 0)),
            scratch_shapes=[pltpu.VMEM((512, width), F32)],
        ),
        input_output_aliases={2: 0} if more else {},
        compiler_params=pltpu.CompilerParams(vmem_limit_bytes=VMEM_LIMIT),
        cost_estimate=pl.CostEstimate(flops=0, bytes_accessed=count * 512 * width * 6, transcendentals=0),
        name="convert",
    )(code, w, *more)


def place_kernel(transposed, code_ref, g_ref, *refs):
    o_ref, t_ref = refs[-2:]
    code = code_ref[0]
    for j in range(16):
        start = pl.multiple_of((j ^ code) * 32, 32)
        t_ref[j * 32 : (j + 1) * 32, :] = g_ref[0, pl.ds(start, 32), :].astype(F32)
    placed = t_ref[...].T if transposed else t_ref[...]
    o_ref[...] = placed.reshape(o_ref.shape)


def place(grads, shape, block, index, transposed, count, group, into, code):
    width = grads.shape[-1]
    more = [] if into is None else [into]
    return pl.pallas_call(
        functools.partial(place_kernel, transposed),
        out_shape=jax.ShapeDtypeStruct(shape, F32),
        grid_spec=pltpu.PrefetchScalarGridSpec(
            num_scalar_prefetch=1,
            grid=(count,),
            in_specs=[pl.BlockSpec((1, 512, width), lambda i, code: (group(i), 0, 0))]
            + [pl.BlockSpec(memory_space=pl.ANY) for _ in more],
            out_specs=pl.BlockSpec(block, lambda i, code: index(i)),
            scratch_shapes=[pltpu.VMEM((512, width), F32)],
        ),
        input_output_aliases={2: 0} if more else {},
        compiler_params=pltpu.CompilerParams(vmem_limit_bytes=VMEM_LIMIT),
        cost_estimate=pl.CostEstimate(flops=0, bytes_accessed=count * 512 * width * 6, transcendentals=0),
        name="place",
    )(code, grads, *more)


def partner(bit):
    dp, y = lax.axis_index("dp"), lax.axis_index("tensor")
    if bit == FLIP_Y:
        return (dp, 1 - y)
    step = bit // 2
    up = (dp // step) % 2
    return (dp + step * (1 - 2 * up), y)


def greet(bits):
    barrier = pltpu.get_barrier_semaphore()
    for bit in bits:
        pl.semaphore_signal(barrier, inc=1, device_id=partner(bit), device_id_type=MESH)
    pl.semaphore_wait(barrier, len(bits))


class Link:
    def __init__(self, send_sem, recv_sem):
        self.send_sem, self.recv_sem, self.used, self.open = send_sem, recv_sem, 0, []

    def start(self, source, target, bit):
        copy = pltpu.make_async_remote_copy(
            src_ref=source,
            dst_ref=target,
            send_sem=self.send_sem.at[self.used],
            recv_sem=self.recv_sem.at[self.used],
            device_id=partner(bit),
            device_id_type=MESH,
        )
        copy.start()
        self.used += 1
        self.open.append(copy)
        return copy

    def finish(self):
        for copy in self.open:
            copy.wait_send()


def timetable(chains, window):
    events, clock = [], 0.0
    queue = {}
    ready = [(i, 0) for i in range(len(chains))]
    flying = []
    free = {}
    while ready or flying:
        moved = True
        while moved:
            moved = False
            for item in sorted(ready, key=lambda it: (it[0], it[1])):
                link, time = chains[item[0]][item[1]]
                if sum(1 for f in flying if f[2] == link) < window:
                    begin = max(clock, free.get(link, 0.0))
                    free[link] = begin + time
                    flying.append((begin + time + 2.0, item, link))
                    events.append(("start",) + item)
                    ready.remove(item)
                    moved = True
                    break
        flying.sort()
        clock, item, _ = flying.pop(0)
        events.append(("land",) + item)
        if item[1] + 1 < len(chains[item[0]]):
            ready.append((item[0], item[1] + 1))
    return events


def spread_kernel(chunks, w_in_ref, w_ref, send_sem, recv_sem):
    del w_in_ref
    greet((FLIP_Y, FLIP_X, FLIP_Z0, FLIP_C))
    chains, copies = [], []
    for k in chunks:
        if k % GROUPS < 4:
            steps = [
                (FLIP_Y, 5.7, w_ref.at[0, k, 0, pl.ds(0, 128)], w_ref.at[0, k, 1, pl.ds(0, 128)]),
                (FLIP_X, 5.7, w_ref.at[0, k, 1, pl.ds(0, 128)], w_ref.at[0, k, 1, pl.ds(128, 128)]),
            ]
        else:
            steps = [
                (FLIP_Y, 2.9, w_ref.at[0, k, 0, pl.ds(0, 64)], w_ref.at[0, k, 1, pl.ds(0, 64)]),
                (FLIP_Z0, 2.9, w_ref.at[0, k, 1, pl.ds(0, 64)], w_ref.at[0, k, 1, pl.ds(64, 64)]),
                (FLIP_X, 5.7, w_ref.at[0, k, 1, pl.ds(0, 128)], w_ref.at[0, k, 1, pl.ds(128, 128)]),
            ]
            if (k // 2) % 2 == 0:
                steps = [
                    (FLIP_Y, 2.9, w_ref.at[0, k, 0, pl.ds(0, 64)], w_ref.at[0, k, 1, pl.ds(0, 64)]),
                    (FLIP_X, 2.9, w_ref.at[0, k, 1, pl.ds(0, 64)], w_ref.at[0, k, 1, pl.ds(128, 64)]),
                    (FLIP_Z0, 2.9, w_ref.at[0, k, 1, pl.ds(0, 64)], w_ref.at[0, k, 1, pl.ds(64, 64)]),
                    (FLIP_Z0, 2.9, w_ref.at[0, k, 1, pl.ds(128, 64)], w_ref.at[0, k, 1, pl.ds(192, 64)]),
                ]
        steps.append((FLIP_C, 0.9, w_ref.at[0, k, 1], w_ref.at[1, k, 1]))
        chains.append(steps)
        copies.append([None] * len(steps))
    link = Link(send_sem, recv_sem)
    for event, i, step in timetable([[(s[0], s[1]) for s in chain] for chain in chains], 2):
        bit, _, source, target = chains[i][step]
        if event == "start":
            copies[i][step] = link.start(source, target, bit)
        else:
            copies[i][step].wait_recv()
    link.finish()


def spread_weights(weights, chunks):
    count = sum(3 if k % GROUPS < 4 else (5 if (k // 2) % 2 == 0 else 4) for k in chunks)
    return pl.pallas_call(
        functools.partial(spread_kernel, chunks),
        out_shape=jax.ShapeDtypeStruct(weights.shape, weights.dtype),
        in_specs=[pl.BlockSpec(memory_space=pl.ANY)],
        out_specs=pl.BlockSpec(memory_space=pl.ANY),
        scratch_shapes=[pltpu.SemaphoreType.DMA((count,)), pltpu.SemaphoreType.DMA((count,))],
        input_output_aliases={0: 0},
        compiler_params=pltpu.CompilerParams(collective_id=0, has_side_effects=True),
        cost_estimate=pl.CostEstimate(flops=0, bytes_accessed=50 << 20, transcendentals=0),
        name="spread_weights",
    )(weights)


def add_rows(into, other, rows):
    def step(i, _):
        at = pl.ds(pl.multiple_of(i * 32, 32), 32)
        into[at, :] = (into[at, :].astype(F32) + other[at, :].astype(F32)).astype(BF16)
        return 0

    lax.fori_loop(0, rows // 32, step, 0)


SLOTS = 8
LAST_TICK = 10


class Reduction:
    def __init__(self, grads, sums, count, bufs, sems):
        self.grads, self.sums, self.count = grads, sums, count
        self.y_buf, self.x_buf, self.z0_buf, self.z1_buf, self.all_buf, self.keep_buf = bufs
        self.send_sem, self.recv_sem, self.keep_sem, self.out_sem, self.in_free, self.out_free = sems

    def copy(self, step, i):
        slot = lax.rem(i, SLOTS)
        ys, al = self.y_buf.at[slot], self.all_buf.at[slot]
        bit, source, target = (
            (FLIP_Y, self.grads.at[i, pl.ds(256, 256)], ys),
            (FLIP_X, ys.at[pl.ds(128, 128)], self.x_buf.at[slot]),
            (FLIP_Z0, ys.at[pl.ds(64, 64)], self.z0_buf.at[slot]),
            (FLIP_Z1, ys.at[pl.ds(32, 32)], self.z1_buf.at[slot]),
            (FLIP_Z1, al.at[pl.ds(0, 32)], al.at[pl.ds(32, 32)]),
            (FLIP_Z0, al.at[pl.ds(0, 64)], al.at[pl.ds(64, 64)]),
            (FLIP_X, al.at[pl.ds(0, 128)], al.at[pl.ds(128, 128)]),
            (FLIP_C, al, self.sums.at[i, pl.ds(256, 256)]),
        )[step]
        return pltpu.make_async_remote_copy(
            src_ref=source,
            dst_ref=target,
            send_sem=self.send_sem.at[step, slot],
            recv_sem=self.recv_sem.at[step, slot],
            device_id=partner(bit),
            device_id_type=MESH,
        )

    def keep(self, i):
        slot = lax.rem(i, 2)
        return pltpu.make_async_copy(
            self.grads.at[i, pl.ds(0, 256)], self.keep_buf.at[slot], self.keep_sem.at[slot]
        )

    def out(self, i):
        slot = lax.rem(i, SLOTS)
        return pltpu.make_async_copy(
            self.all_buf.at[slot], self.sums.at[i, pl.ds(0, 256)], self.out_sem.at[slot]
        )

    def take(self, sem, i):
        @pl.when(i >= SLOTS)
        def _():
            pl.semaphore_wait(sem, 1)

    def give(self, sem, bit, i):
        @pl.when(i + SLOTS < self.count)
        def _():
            pl.semaphore_signal(sem, inc=1, device_id=partner(bit), device_id_type=MESH)

    def tick(self, t):
        def at(offset, body):
            i = t - offset
            pl.when((i >= 0) & (i < self.count))(lambda: body(i, lax.rem(i, SLOTS)))

        def set_out(i, slot):
            self.take(self.in_free.at[0], i)
            self.copy(0, i).start()
            self.keep(i).start()

        def finish(i, slot):
            self.copy(7, i).wait()
            self.out(i).wait()
            for n, bit in enumerate((FLIP_X, FLIP_Z0, FLIP_Z1)):
                self.give(self.out_free.at[n], bit, i)

        def to_core(i, slot):
            self.copy(6, i).wait()
            self.copy(7, i).start()
            self.out(i).start()

        def back_x(i, slot):
            self.copy(5, i).wait()
            self.take(self.out_free.at[0], i)
            self.copy(6, i).start()

        def back_z0(i, slot):
            self.copy(4, i).wait()
            self.take(self.out_free.at[1], i)
            self.copy(5, i).start()

        def back_z1(i, slot):
            self.copy(3, i).wait()
            add_rows(self.y_buf.at[slot], self.z1_buf.at[slot], 32)
            self.all_buf[slot, 0:32, :] = self.y_buf[slot, 0:32, :]
            for n, bit in enumerate((FLIP_Y, FLIP_X, FLIP_Z0, FLIP_Z1)):
                self.give(self.in_free.at[n], bit, i)
            self.take(self.out_free.at[2], i)
            self.copy(4, i).start()

        def on_z1(i, slot):
            self.copy(2, i).wait()
            add_rows(self.y_buf.at[slot], self.z0_buf.at[slot], 64)
            self.take(self.in_free.at[3], i)
            self.copy(3, i).start()

        def on_z0(i, slot):
            self.copy(1, i).wait()
            add_rows(self.y_buf.at[slot], self.x_buf.at[slot], 128)
            self.take(self.in_free.at[2], i)
            self.copy(2, i).start()

        def on_x(i, slot):
            self.copy(0, i).wait()
            self.keep(i).wait()
            add_rows(self.y_buf.at[slot], self.keep_buf.at[lax.rem(i, 2)], 256)
            self.take(self.in_free.at[1], i)
            self.copy(1, i).start()

        at(0, set_out)
        at(10, finish)
        at(9, to_core)
        at(7, back_x)
        at(6, back_z0)
        at(5, back_z1)
        at(4, on_z1)
        at(3, on_z0)
        at(1, on_x)


def stream(count, feeds, body):
    for copy in feeds(0, 0):
        copy.start()

    def step(i, _):
        slot = lax.rem(i, 2)

        @pl.when(i + 1 < count)
        def _():
            for copy in feeds(i + 1, 1 - slot):
                copy.start()

        for copy in feeds(i, slot):
            copy.wait()
        body(i, slot)
        return 0

    lax.fori_loop(0, count, step, 0)


def qkv_kernel(x_ref, w_ref, bias_ref, o_ref):
    o_ref[0] = (nt(x_ref[...], block_of(w_ref)) + bias_ref[0, 0]).astype(BF16)


def project_qkv(x_low, weights, bias, first):
    rows, width = x_low.shape
    return pl.pallas_call(
        qkv_kernel,
        out_shape=jax.ShapeDtypeStruct((3, rows, width), BF16),
        grid=(2, 3),
        in_specs=[
            pl.BlockSpec((rows, width), lambda a, t: (0, 0)),
            pl.BlockSpec((1, 1, 2, 256, width), lambda a, t: (a, first + t, 0, 0, 0)),
            pl.BlockSpec((1, 1, 1, 512), lambda a, t: (t, a, 0, 0)),
        ],
        out_specs=pl.BlockSpec((1, rows, 512), lambda a, t: (t, 0, a)),
        compiler_params=pltpu.CompilerParams(vmem_limit_bytes=VMEM_LIMIT),
        cost_estimate=pl.CostEstimate(flops=6 * rows * width * width, bytes_accessed=10 << 20, transcendentals=0),
        name="project_qkv",
    )(x_low, weights, bias)


def norm(r, gain, shift):
    centred = r - jnp.mean(r, axis=-1, keepdims=True)
    rstd = lax.rsqrt(jnp.mean(centred * centred, axis=-1, keepdims=True) + 1e-06)
    return centred * rstd * gain + shift


def norm_back(dy, r, gain):
    centred = r - jnp.mean(r, axis=-1, keepdims=True)
    rstd = lax.rsqrt(jnp.mean(centred * centred, axis=-1, keepdims=True) + 1e-06)
    unit = centred * rstd
    dunit = dy * gain
    dr = rstd * (
        dunit
        - jnp.mean(dunit, axis=-1, keepdims=True)
        - unit * jnp.mean(dunit * unit, axis=-1, keepdims=True)
    )
    return dr, dy * unit


def gelu_and_slope(u):
    cdf = 0.5 * (1.0 + lax.erf(u * (0.5**0.5)))
    pdf = jnp.exp(-0.5 * u * u) * 0.3989422804014327
    return u * cdf, cdf + u * pdf


TILE = 64


def row_tiles(rows, body):
    def step(i, _):
        body(pl.ds(pl.multiple_of(i * TILE, TILE), TILE))
        return 0

    lax.fori_loop(0, rows // TILE, step, 0)


def forward_kernel(
    ctx_ref, x_ref, wo_ref, wi_ref, wd_ref, bi_ref, vec_ref,
    r1_ref, hl_ref, g_ref, slope_ref, r2_ref, x2_ref, xl_ref, acc_ref,
):
    step = pl.program_id(0) * pl.num_programs(1) + pl.program_id(1)
    rows = x_ref.shape[0]

    @pl.when(step == 0)
    def _():
        acc_ref[...] = nn(ctx_ref[:, :512], block_of(wo_ref.at[0])) + nn(ctx_ref[:, 512:], block_of(wo_ref.at[1]))

        def body(at):
            r1 = x_ref[at, :] + acc_ref[at, :] + vec_ref[0:1, :]
            r1_ref[at, :] = r1
            h = norm(r1, vec_ref[1:2, :], vec_ref[2:3, :])
            hl_ref[at, :] = h.astype(BF16)
            acc_ref[at, :] = h + vec_ref[3:4, :]

        row_tiles(rows, body)

    u = nt(hl_ref[...], block_of(wi_ref)) + bi_ref[0, 0]
    g, slope = gelu_and_slope(u)
    g = g.astype(BF16)
    g_ref[...] = g
    slope_ref[...] = slope.astype(BF16)
    acc_ref[...] += nn(g, block_of(wd_ref))

    @pl.when(step == 2 * FF_GROUPS - 1)
    def _():
        def body(at):
            r2 = acc_ref[at, :]
            r2_ref[at, :] = r2
            x2 = norm(r2, vec_ref[4:5, :], vec_ref[5:6, :])
            x2_ref[at, :] = x2
            xl_ref[at, :] = x2.astype(BF16)

        row_tiles(rows, body)


def weight_spec(group, width):
    return pl.BlockSpec((1, 1, 2, 256, width), lambda a, s: (a, group(s), 0, 0, 0))


def forward_tail(ctx, x, weights, bias_in, vectors, first):
    rows, width = x.shape
    whole = pl.BlockSpec((rows, width), lambda a, s: (0, 0))
    hidden = pl.BlockSpec((rows, 512), lambda a, s: (0, a * FF_GROUPS + s))
    sums = jax.ShapeDtypeStruct((rows, width), F32)
    low = jax.ShapeDtypeStruct((rows, width), BF16)
    wide = jax.ShapeDtypeStruct((rows, 4 * width), BF16)
    return pl.pallas_call(
        forward_kernel,
        out_shape=(sums, low, wide, wide, sums, sums, low),
        grid=(2, FF_GROUPS),
        in_specs=[
            whole,
            whole,
            pl.BlockSpec((2, 1, 2, 256, width), lambda a, s: (0, first + OUT_GROUP, 0, 0, 0)),
            weight_spec(lambda s: first + in_group(s), width),
            weight_spec(lambda s: first + down_group(s), width),
            pl.BlockSpec((1, 1, 1, 512), lambda a, s: (a, s, 0, 0)),
            pl.BlockSpec((8, width), lambda a, s: (0, 0)),
        ],
        out_specs=(whole, whole, hidden, hidden, whole, whole, whole),
        scratch_shapes=[pltpu.VMEM((rows, width), F32)],
        compiler_params=pltpu.CompilerParams(vmem_limit_bytes=VMEM_LIMIT),
        cost_estimate=pl.CostEstimate(
            flops=18 * rows * width * width, bytes_accessed=40 << 20, transcendentals=8 * rows * width
        ),
        name="forward_tail",
    )(ctx, x, weights, weights, weights, bias_in, vectors)


def pair_lanes(values, e):
    lane = lax.broadcasted_iota(jnp.int32, values.shape, 1)
    return jnp.where(lane // HEAD_DIM == e, values, jnp.zeros_like(values))


def attend_kernel(q_ref, ko_ref, vo_ref, ks_ref, vs_ref, hot_ref, mask_ref, ctx_ref, lse_ref):
    scale = HEAD_DIM**-0.5
    keys = jnp.concatenate([ko_ref[...], ks_ref[...]], axis=0)
    values_t = jnp.concatenate([vo_ref[...], vs_ref[...]], axis=0).T
    query = q_ref[...] * jnp.asarray(scale, BF16)
    heads = []
    for e in range(2):
        right = jnp.concatenate([pair_lanes(query, e), hot_ref[...]], axis=1)
        left = jnp.concatenate([keys, mask_ref[e]], axis=1)
        s = nt(left, right)
        top = jnp.max(s, axis=0, keepdims=True)
        p = jnp.exp(s - top)
        total = jnp.sum(p, axis=0, keepdims=True)
        c = nn(values_t[e * HEAD_DIM : (e + 1) * HEAD_DIM, :], p.astype(BF16))
        heads.append(c * (1.0 / total))
        lse_ref[0, e : e + 1, :] = top + jnp.log(total)
    ctx_ref[...] = jnp.concatenate(heads, axis=0).T.astype(BF16)


def attend(q, k, v, k_sib, v_sib, hot, mask):
    rows, width = q.shape
    pairs = width // 128
    own = pl.BlockSpec((rows, 128), lambda p: (0, p))
    sib = pl.BlockSpec((rows, 128), lambda p: (0, p ^ (pairs // 2)))
    return pl.pallas_call(
        attend_kernel,
        out_shape=(
            jax.ShapeDtypeStruct((rows, width), BF16),
            jax.ShapeDtypeStruct((pairs, 2, rows), F32),
        ),
        grid=(pairs,),
        in_specs=[
            own,
            own,
            own,
            sib,
            sib,
            pl.BlockSpec((rows, 128), lambda p: (0, 0)),
            pl.BlockSpec((2, 2 * rows, 128), lambda p: (p, 0, 0)),
        ],
        out_specs=(own, pl.BlockSpec((1, 2, rows), lambda p: (p, 0, 0))),
        compiler_params=pltpu.CompilerParams(vmem_limit_bytes=VMEM_LIMIT),
        cost_estimate=pl.CostEstimate(
            flops=8 * rows * rows * 128 * pairs * 2, bytes_accessed=16 << 20, transcendentals=4 * rows * rows * pairs
        ),
        name="attend",
    )(q, k, v, k_sib, v_sib, hot, mask)


def attend_back_pair(query, keys, values, hot, mask, ctx, lse, dctx):
    scale = HEAD_DIM**-0.5
    rows = query.shape[0]
    query = query * jnp.asarray(scale, BF16)
    keys_t = keys.T
    delta_t = (dctx.astype(F32) * ctx.astype(F32)).T
    tile = rows // 2
    dk, dv, dq = 0.0, 0.0, []
    for part in range(2):
        at = slice(part * tile, (part + 1) * tile)
        heads = []
        for e in range(2):
            lanes = slice(e * HEAD_DIM, (e + 1) * HEAD_DIM)
            query_e = pair_lanes(query[at], e)
            dctx_e = pair_lanes(dctx[at], e)
            right = jnp.concatenate([query_e, hot[at]], axis=1)
            left = jnp.concatenate([keys, mask[e]], axis=1)
            p = jnp.exp(nt(left, right) - lse[e : e + 1, at])
            dp = nt(values, dctx_e)
            delta = jnp.sum(delta_t[lanes, at], axis=0, keepdims=True)
            ds = (p * (dp - delta)).astype(BF16)
            dk = dk + nn(ds, query_e)
            dv = dv + nn(p.astype(BF16), dctx_e)
            heads.append(nn(keys_t[lanes, :], ds) * scale)
        dq.append(jnp.concatenate(heads, axis=0).T)
    return jnp.concatenate(dq, axis=0), dk, dv


PER_LAYER = 14


def backward_kernel(layers, *refs):
    refs = list(refs)
    up_ref, w_ref, hot_ref, mask_ref, vec_ref = refs[:5]
    saved = [refs[5 + PER_LAYER * l : 5 + PER_LAYER * (l + 1)] for l in range(layers)]
    at_ref = 5 + PER_LAYER * layers
    grads, sums, dx_out, dbi_ref, qkv_sums_ref, small_ref = refs[at_ref : at_ref + 6]
    (
        acc, dr1, dm, dm_sib, da, da_sib, du, du_sib, dctx, dqkv, d_sib, kv_out, kv_far,
        wa_buf, wb_buf, r_buf, slope_buf, left_buf, left_sib_buf, right_buf, right_sib_buf,
        pair_buf, lse_buf, mask_buf, hot_buf, unit_buf,
        y_buf, x_buf, z0_buf, z1_buf, all_buf, keep_buf,
        feed_sem, load_sem, store_sem, core_send, core_recv, du_send, du_recv,
        send_sem, recv_sem, keep_sem, out_sem, in_free, out_free,
    ) = refs[at_ref + 6 :]
    rows, width = acc.shape
    total = layers * GROUPS
    reduction = Reduction(
        grads, sums, total,
        (y_buf, x_buf, z0_buf, z1_buf, all_buf, keep_buf),
        (send_sem, recv_sem, keep_sem, out_sem, in_free, out_free),
    )
    greet((FLIP_Y, FLIP_X, FLIP_Z0, FLIP_Z1, FLIP_C))

    def feed(n, slot, source, target):
        return pltpu.make_async_copy(source, target, feed_sem.at[n, slot])

    def load(n, source, target):
        return pltpu.make_async_copy(source, target, load_sem.at[n])

    def exchange(n, source, target):
        return pltpu.make_async_remote_copy(
            src_ref=source, dst_ref=target, send_sem=core_send.at[n], recv_sem=core_recv.at[n],
            device_id=partner(FLIP_C), device_id_type=MESH,
        )

    def give_du(j, n):
        return pltpu.make_async_remote_copy(
            src_ref=du.at[j], dst_ref=du_sib.at[n], send_sem=du_send.at[n], recv_sem=du_recv.at[n],
            device_id=partner(FLIP_C), device_id_type=MESH,
        )

    def weight(a, group):
        return w_ref.at[a, group]

    def columns(ref, i, size):
        return ref.at[:, pl.ds(pl.multiple_of(i * size, size), size)]

    def unit(left, left_sib, right, right_sib, index):
        unit_buf[...] = (tn(left, right) + tn(left_sib, right_sib)).astype(BF16)
        store = pltpu.make_async_copy(unit_buf, grads.at[index], store_sem.at[0])
        store.start()
        store.wait()

    def add_small(l, row, value):
        small_ref[l, row : row + 1, :] += jnp.sum(value, axis=0, keepdims=True)

    start_up = load(0, up_ref, da)
    start_up.start()
    start_hot = load(1, hot_ref, hot_buf)
    start_hot.start()
    start_up.wait()
    start_hot.wait()
    small_ref[...] = jnp.zeros_like(small_ref)

    def widen(at):
        acc[at, :] = da[at, :].astype(F32)

    row_tiles(rows, widen)
    done = 0
    for l in reversed(range(layers)):
        qkv_ref, sib_ref, ctx_ref, ctx_sib_ref, lse_ref, r1_ref, r2_ref, hl_ref, hl_sib_ref, g_ref, g_sib_ref, slope_ref, xb_ref, xb_sib_ref = saved[l]
        first = l * GROUPS
        base = (layers - 1 - l) * GROUPS
        clock = 11 * (layers - 1 - l)

        r_load = load(0, r2_ref, r_buf)
        r_load.start()
        r_load.wait()

        def second(at):
            dy = acc[at, :]
            dr, part = norm_back(dy, r_buf[at, :], vec_ref[l, 4:5, :])
            acc[at, :] = dr
            dm[at, :] = dr.astype(BF16)
            add_small(l, 0, part)
            add_small(l, 1, dy)
            add_small(l, 2, dr)

        row_tiles(rows, second)
        dm_copy = exchange(0, dm, dm_sib)
        dm_copy.start()
        r_load = load(0, r1_ref, r_buf)
        r_load.start()
        right_load = load(1, hl_ref, right_buf)
        right_load.start()
        right_sib_load = load(2, hl_sib_ref, right_sib_buf)
        right_sib_load.start()
        dm_copy.wait()

        def down_feeds(i, slot):
            return (
                feed(0, slot, columns(g_ref, i, 512), left_buf.at[slot]),
                feed(1, slot, columns(g_sib_ref, i, 512), left_sib_buf.at[slot]),
            )

        def down_body(i, slot):
            unit(left_buf[slot], left_sib_buf[slot], dm[...], dm_sib[...], base + i)
            pl.when(lax.rem(i, 3) == 0)(lambda: reduction.tick(clock + lax.div(i, 3)))

        stream(FF_GROUPS, down_feeds, down_body)

        def place_of(i):
            a = 1 - lax.div(i, FF_GROUPS)
            return a, lax.rem(i, FF_GROUPS)

        def ff_feeds(i, slot):
            a, n = place_of(i)
            j = a * FF_GROUPS + n
            return (
                feed(0, slot, weight(a, first + down_group(n)), wa_buf.at[slot]),
                feed(1, slot, weight(a, first + in_group(n)), wb_buf.at[slot]),
                feed(2, slot, columns(slope_ref, j, 512), slope_buf.at[slot]),
            )

        def ff_body(i, slot):
            a, n = place_of(i)
            j = a * FF_GROUPS + n
            dg = nt(dm[...], block_of(wa_buf.at[slot]))
            d = (dg * slope_buf[slot].astype(F32)).astype(BF16)
            du[j] = d
            pl.when(a == 1)(lambda: give_du(j, n).start())
            dbi_ref[l, a, n] = jnp.sum(d.astype(F32), axis=0, keepdims=True)
            acc[...] += nn(d, block_of(wb_buf.at[slot]))
            pl.when(lax.rem(i, 3) == 2)(lambda: reduction.tick(clock + 2 + lax.div(i, 3)))

        stream(2 * FF_GROUPS, ff_feeds, ff_body)

        r_load.wait()

        def first_norm(at):
            dy = acc[at, :]
            dr, part = norm_back(dy, r_buf[at, :], vec_ref[l, 1:2, :])
            dr1[at, :] = dr
            da[at, :] = dr.astype(BF16)
            add_small(l, 3, part)
            add_small(l, 4, dy)
            add_small(l, 5, dr)

        row_tiles(rows, first_norm)
        da_copy = exchange(1, da, da_sib)
        da_copy.start()

        def out_feeds(i, slot):
            return (feed(0, slot, weight(i, first + OUT_GROUP), wa_buf.at[slot]),)

        def out_body(i, slot):
            dctx[:, pl.ds(pl.multiple_of(i * 512, 512), 512)] = nt(da[...], block_of(wa_buf.at[slot])).astype(BF16)

        stream(2, out_feeds, out_body)

        right_load.wait()
        right_sib_load.wait()

        def in_body(n, _):
            give_du(FF_GROUPS + n, n).wait()
            unit(du[n], du_sib[n], right_buf[...], right_sib_buf[...], base + FF_GROUPS + n)
            pl.when(lax.rem(n, 3) == 0)(lambda: reduction.tick(clock + 4 + lax.div(n, 3)))
            return 0

        lax.fori_loop(0, FF_GROUPS, in_body, 0)

        right_load = load(1, xb_ref, right_buf)
        right_load.start()
        right_sib_load = load(2, xb_sib_ref, right_sib_buf)
        right_sib_load.start()
        left_load = load(3, columns(ctx_ref, 0, 512), left_buf.at[0])
        left_load.start()
        left_sib_load = load(4, ctx_sib_ref, left_sib_buf.at[0])
        left_sib_load.start()
        da_copy.wait()
        left_load.wait()
        left_sib_load.wait()
        unit(left_buf[0], left_sib_buf[0], da[...], da_sib[...], base + 2 * FF_GROUPS)

        pairs = width // 128

        def pair_feeds(p, slot):
            far = lax.rem(p + pairs // 2, pairs)
            return (
                feed(0, slot, columns(qkv_ref.at[0], p, 128), pair_buf.at[slot, 0, pl.ds(0, rows)]),
                feed(1, slot, columns(qkv_ref.at[1], p, 128), pair_buf.at[slot, 1, pl.ds(0, rows)]),
                feed(2, slot, columns(sib_ref.at[0], far, 128), pair_buf.at[slot, 1, pl.ds(rows, rows)]),
                feed(3, slot, columns(qkv_ref.at[2], p, 128), pair_buf.at[slot, 2, pl.ds(0, rows)]),
                feed(4, slot, columns(sib_ref.at[1], far, 128), pair_buf.at[slot, 2, pl.ds(rows, rows)]),
                feed(5, slot, columns(ctx_ref, p, 128), pair_buf.at[slot, 3, pl.ds(0, rows)]),
                feed(6, slot, lse_ref.at[p], lse_buf.at[slot]),
                feed(7, slot, mask_ref.at[pl.ds(2 * p, 2)], mask_buf.at[slot]),
            )

        def pair_body(p, slot):
            far = lax.rem(p + pairs // 2, pairs)
            here = pl.ds(pl.multiple_of(p * 128, 128), 128)
            dq, dk, dv = attend_back_pair(
                pair_buf[slot, 0, 0:rows], pair_buf[slot, 1], pair_buf[slot, 2], hot_buf[...], mask_buf[slot],
                pair_buf[slot, 3, 0:rows], lse_buf[slot], dctx[:, here],
            )
            dqkv[0, :, here] = dq.astype(BF16)
            dqkv[1, :, here] = dk[:rows].astype(BF16)
            dqkv[2, :, here] = dv[:rows].astype(BF16)
            there = pl.ds(pl.multiple_of(far * 128, 128), 128)
            kv_out[0, :, there] = dk[rows:].astype(BF16)
            kv_out[1, :, there] = dv[rows:].astype(BF16)
            pl.when(lax.rem(p, 3) == 1)(lambda: reduction.tick(clock + 6 + lax.div(p, 3)))

        stream(pairs, pair_feeds, pair_body)
        kv_copy = exchange(2, kv_out, kv_far)
        kv_copy.start()
        kv_copy.wait()
        for n in range(2):
            add_rows(dqkv.at[1 + n], kv_far.at[n], rows)
        d_copy = exchange(3, dqkv.at[:, :, pl.ds(512, 512)], d_sib)
        d_copy.start()
        right_load.wait()
        right_sib_load.wait()
        d_copy.wait()

        def qkv_body(n, _):
            unit(dqkv[n, :, 0:512], d_sib[n], right_buf[...], right_sib_buf[...], base + 2 * FF_GROUPS + 1 + n)
            return 0

        lax.fori_loop(0, 3, qkv_body, 0)
        reduction.tick(clock + 9)

        def start_dx(at):
            acc[at, :] = dr1[at, :]

        row_tiles(rows, start_dx)

        def dx_feeds(i, slot):
            return (feed(0, slot, weight(lax.rem(i, 2), first + lax.div(i, 2)), wa_buf.at[slot]),)

        def dx_body(i, slot):
            a, n = lax.rem(i, 2), lax.div(i, 2)
            d = dqkv[n, :, pl.ds(pl.multiple_of(a * 512, 512), 512)]
            qkv_sums_ref[l, n, a] = jnp.sum(d.astype(F32), axis=0, keepdims=True)
            acc[...] += nn(d, block_of(wa_buf.at[slot]))
            pl.when(i == 3)(lambda: reduction.tick(clock + 10))

        stream(6, dx_feeds, dx_body)
        done = clock + 11

    def narrow(at):
        da[at, :] = acc[at, :].astype(BF16)

    row_tiles(rows, narrow)
    dx_store = load(0, da, dx_out)
    dx_store.start()
    dx_store.wait()

    def rest(t, _):
        reduction.tick(t)
        return 0

    lax.fori_loop(done, total + LAST_TICK, rest, 0)


def backward(upstream, weights, hot, mask, vectors, saved):
    rows, width = upstream.shape
    layers = len(saved)
    total = layers * GROUPS
    anywhere = pl.BlockSpec(memory_space=pl.ANY)
    in_vmem = pl.BlockSpec(memory_space=pltpu.VMEM)
    low = lambda *shape: pltpu.VMEM(shape, BF16)
    dma = lambda *shape: pltpu.SemaphoreType.DMA(shape)
    return pl.pallas_call(
        functools.partial(backward_kernel, layers),
        out_shape=(
            jax.ShapeDtypeStruct((total, 512, width), BF16),
            jax.ShapeDtypeStruct((total, 512, width), BF16),
            jax.ShapeDtypeStruct((rows, width), BF16),
            jax.ShapeDtypeStruct((layers, 2, FF_GROUPS, 1, 512), F32),
            jax.ShapeDtypeStruct((layers, 3, 2, 1, 512), F32),
            jax.ShapeDtypeStruct((layers, 8, width), F32),
        ),
        in_specs=[anywhere] * 4 + [in_vmem] + [anywhere] * (PER_LAYER * layers),
        out_specs=(anywhere, anywhere, anywhere, in_vmem, in_vmem, in_vmem),
        scratch_shapes=[
            pltpu.VMEM((rows, width), F32),
            pltpu.VMEM((rows, width), F32),
            low(rows, width),
            low(rows, width),
            low(rows, width),
            low(rows, width),
            low(2 * FF_GROUPS, rows, 512),
            low(FF_GROUPS, rows, 512),
            low(rows, width),
            low(3, rows, width),
            low(3, rows, 512),
            low(2, rows, width),
            low(2, rows, width),
            low(2, 2, 256, width),
            low(2, 2, 256, width),
            pltpu.VMEM((rows, width), F32),
            low(2, rows, 512),
            low(2, rows, 512),
            low(2, rows, 512),
            low(rows, width),
            low(rows, width),
            low(2, 4, 2 * rows, 128),
            pltpu.VMEM((2, 2, rows), F32),
            low(2, 2, 2 * rows, 128),
            low(rows, 128),
            low(512, width),
            low(SLOTS, 256, width),
            low(SLOTS, 128, width),
            low(SLOTS, 64, width),
            low(SLOTS, 32, width),
            low(SLOTS, 256, width),
            low(2, 256, width),
            dma(8, 2),
            dma(5),
            dma(1),
            dma(4),
            dma(4),
            dma(FF_GROUPS),
            dma(FF_GROUPS),
            dma(8, SLOTS),
            dma(8, SLOTS),
            dma(2),
            dma(SLOTS),
            pltpu.SemaphoreType.REGULAR((4,)),
            pltpu.SemaphoreType.REGULAR((3,)),
        ],
        compiler_params=pltpu.CompilerParams(
            collective_id=1, has_side_effects=True, vmem_limit_bytes=60 << 20
        ),
        cost_estimate=pl.CostEstimate(flops=60 << 30, bytes_accessed=300 << 20, transcendentals=1 << 24),
        name="backward",
    )(upstream, weights, hot, mask, vectors, *[ref for one in saved for ref in one])


def flip_order(values, axis, bits):
    for i, bit in enumerate(bits):
        values = jnp.where(bit == 0, values, jnp.flip(values, axis + i))
    return values


def sum_everywhere(values):
    for bit in (FLIP_C, FLIP_Y, FLIP_X, FLIP_Z0, FLIP_Z1):
        values = values + flip(values, bit)
    return values


def sequence_shards(
    block_input, segment_ids, random_blocks, w_qkv, b_qv, w_out, b_out, w_in, b_in, w_down, b_down,
    ln_gain, ln_bias, cotangent,
):
    y = lax.axis_index("tensor")
    dp = lax.axis_index("dp")
    core, x_bit, z0, z1 = dp % 2, (dp // 2) % 2, (dp // 4) % 2, dp // 8
    code = core * 8 + x_bit * 4 + z0 * 2 + z1
    code_arg = code.reshape(1).astype(jnp.int32)
    device_bits = (core, x_bit, z0, z1)

    rows, _, width = block_input.shape
    layers = w_qkv.shape[0]
    blocks = random_blocks.shape[2]
    own_blocks = blocks // 2
    heads = random_blocks.shape[1] * 2

    stream_low = swap_core_and_y(block_input[:, 0].astype(BF16))
    upstream_low = swap_core_and_y(cotangent[:, 0].astype(BF16))

    chosen = random_blocks[0]
    packed = jnp.concatenate(
        [chosen.reshape(-1), flip(chosen, FLIP_Y).reshape(-1), segment_ids[0]]
    )
    packed = jnp.where(core == y, packed, flip(packed, FLIP_C))
    chosen = packed[: 2 * chosen.size].reshape(2, heads // 2, blocks, -1)
    segments = packed[2 * random_blocks.size :]
    chosen = flip_order(chosen.reshape(2, 2, 2, 2, blocks, -1), 1, device_bits[:3])
    chosen = chosen.transpose(1, 0, 2, 3, 4, 5).reshape(heads, blocks, -1)
    segments = segments.reshape(2, rows)
    segments = jnp.where(core == 0, segments, segments[::-1]).reshape(-1)
    query_block = core * own_blocks + jnp.arange(own_blocks)
    key_block = jnp.arange(blocks) ^ (core * own_blocks)
    allowed = (
        (jnp.abs(query_block[:, None] - key_block[None, :]) <= 1)
        | (key_block[None, :] == 0)
        | (key_block[None, :] == blocks - 1)
        | (query_block[:, None] == 0)
        | (query_block[:, None] == blocks - 1)
    )
    chosen = lax.dynamic_slice_in_dim(chosen, core * own_blocks, own_blocks, axis=1)
    allowed = allowed[None] | jnp.any(chosen[:, :, None, :] == key_block[None, None, :, None], axis=3)
    block_rows = rows // own_blocks
    block_part = jnp.where(allowed, 0.0, BIG).astype(BF16).transpose(0, 2, 1)
    block_part = jnp.repeat(block_part, block_rows, axis=1)
    documents = jnp.arange(128 - own_blocks)
    document_part = jnp.where(
        (segments[:, None] == documents[None, :]) | (documents[None, :] > 7), 0.0, BIG
    ).astype(BF16)
    mask = jnp.concatenate(
        [block_part, jnp.broadcast_to(document_part[None], (heads,) + document_part.shape)], axis=2
    )
    hot = jnp.concatenate(
        [
            jnp.repeat(jnp.eye(own_blocks, dtype=BF16), block_rows, axis=0),
            (segments[:rows, None] == documents[None, :]).astype(BF16),
        ],
        axis=1,
    )

    bias_pack = jnp.concatenate(
        [
            flip_order(b_qv.reshape(layers * 2, 2, 2, 2, 2, -1), 1, device_bits).reshape(-1),
            flip_order(b_in.reshape(layers * FF_GROUPS, 2, 2, 2, 2, -1), 1, device_bits).reshape(-1),
        ]
    )
    bias_far = flip(bias_pack, FLIP_Y)
    n_qv = b_qv.size

    def local_bias(near, far, count):
        near, far = near.reshape(count, 2, 1, 256), far.reshape(count, 2, 1, 256)
        return jnp.concatenate([near, far], axis=2).reshape(count, 2, 512)

    bias_qv = local_bias(bias_pack[:n_qv], bias_far[:n_qv], layers * 2).reshape(layers, 2, 2, 1, 512)
    bias_qkv = jnp.stack([bias_qv[:, 0], jnp.zeros_like(bias_qv[:, 0]), bias_qv[:, 1]], axis=1)
    bias_in = local_bias(bias_pack[n_qv:], bias_far[n_qv:], layers * FF_GROUPS)
    bias_in = bias_in.reshape(layers, FF_GROUPS, 2, 1, 512).swapaxes(1, 2)

    total = layers * GROUPS
    weights = None
    for layer in range(layers):
        first = layer * GROUPS
        put = functools.partial(convert, total=total, code=code_arg)
        weights = put(
            w_qkv, (1, 1, width, 512), lambda i, l=layer: (l, i, 0, 0), True, 3, lambda i, f=first: f + i, weights
        )
        weights = put(
            w_out, (1, 512, width), lambda i, l=layer: (l, 0, 0), False, 1, lambda i, f=first: f + OUT_GROUP, weights
        )
        weights = put(
            w_in, (1, width, 512), lambda i, l=layer: (l, 0, i), True, FF_GROUPS,
            lambda i, f=first: f + in_group(i), weights,
        )
        weights = put(
            w_down, (1, 512, width), lambda i, l=layer: (l, i, 0), False, FF_GROUPS,
            lambda i, f=first: f + down_group(i), weights,
        )
    weights = spread_weights(weights, tuple(range(total)))

    vectors = [
        jnp.stack(
            [
                b_out[l], ln_gain[l, 0], ln_bias[l, 0], b_down[l], ln_gain[l, 1], ln_bias[l, 1],
                b_out[l], b_out[l],
            ]
        )
        for l in range(layers)
    ]
    stream, stream_now = stream_low.astype(F32), stream_low
    saved = []
    half = width // 2
    for layer in range(layers):
        first = layer * GROUPS
        xb = stream_now
        qkv = project_qkv(xb, weights, bias_qkv[layer], first)
        q, k, v = qkv[0], qkv[1], qkv[2]
        k_sib, v_sib = flip((k, v), FLIP_C)
        ctx, lse = attend(q, k, v, k_sib, v_sib, hot, mask)
        r1, hidden, g, slope, r2, stream, stream_now = forward_tail(
            ctx, stream, weights, bias_in[layer], vectors[layer], first
        )
        xb_sib, hidden_sib = flip((xb, hidden), FLIP_C)
        ctx_sib = flip(ctx[:, half:], FLIP_C)
        g_sib = flip(g[:, 4 * half :], FLIP_C)
        kv_sib = jnp.stack([k_sib, v_sib])
        saved.append((qkv, kv_sib, ctx, ctx_sib, lse, r1, r2, hidden, hidden_sib, g, g_sib, slope, xb, xb_sib))
    block_output = swap_core_and_y(stream_now).astype(F32)[:, None]

    _, grads, dx_low, d_b_in, qkv_sums, rows_small = backward(
        upstream_low, weights, hot, mask, jnp.stack(vectors), saved
    )
    input_grad = swap_core_and_y(dx_low).astype(F32)[:, None]

    placed = [None] * 4
    for layer in range(layers):
        first = (layers - 1 - layer) * GROUPS
        put = functools.partial(place, grads, code=code_arg)
        placed[0] = put(
            w_qkv.shape, (1, 1, width, 512), lambda i, l=layer: (l, i, 0, 0), True, 3,
            lambda i, f=first: f + 2 * FF_GROUPS + 1 + i, placed[0],
        )
        placed[1] = put(
            w_out.shape, (1, 512, width), lambda i, l=layer: (l, 0, 0), False, 1,
            lambda i, f=first: f + 2 * FF_GROUPS, placed[1],
        )
        placed[2] = put(
            w_in.shape, (1, width, 512), lambda i, l=layer: (l, 0, i), True, FF_GROUPS,
            lambda i, f=first: f + FF_GROUPS + i, placed[2],
        )
        placed[3] = put(
            w_down.shape, (1, 512, width), lambda i, l=layer: (l, i, 0), False, FF_GROUPS,
            lambda i, f=first: f + i, placed[3],
        )
    stacks = [
        jnp.stack([qkv_sums[:, 0], qkv_sums[:, 2]], axis=1),
        rows_small[:, 5],
        d_b_in.swapaxes(1, 2),
        rows_small[:, 2],
        jnp.stack([rows_small[:, 3], rows_small[:, 0]], axis=1),
        jnp.stack([rows_small[:, 4], rows_small[:, 1]], axis=1),
    ]

    def global_order(values, lead):
        values = values.reshape(lead, 2, 2, 2, 2, 2, 32).swapaxes(1, 2)
        values = flip_order(values, 1, (y,) + device_bits)
        return values.swapaxes(0, 1).reshape(2, -1)

    stacks[0] = global_order(stacks[0], layers * 2)
    stacks[2] = global_order(stacks[2], layers * FF_GROUPS)
    summed = sum_everywhere(jnp.concatenate([s.reshape(-1) for s in stacks]))
    parts, at = [], 0
    for s in stacks:
        parts.append(summed[at : at + s.size].reshape(s.shape))
        at += s.size
    g_b_qv = lax.dynamic_index_in_dim(parts[0], y, axis=0, keepdims=False).reshape(b_qv.shape)
    g_b_in = lax.dynamic_index_in_dim(parts[2], y, axis=0, keepdims=False).reshape(b_in.shape)
    return (
        block_output,
        input_grad,
        placed[0],
        g_b_qv,
        placed[1],
        parts[1],
        placed[2],
        g_b_in,
        placed[3],
        parts[3],
        parts[4],
        parts[5],
    )


def as_sent(array):

    def short(part):
        return part.astype(jnp.bfloat16) if part.dtype == jnp.float32 else part

    return jax.tree.map(short, array)


def norm_rows(values, gain_row, shift_row):
    row_mean = jnp.mean(values, axis=-1, keepdims=True)
    centred = values - row_mean
    variance = jnp.mean(centred * centred, axis=-1, keepdims=True)
    return centred * lax.rsqrt(variance + 1e-06) * gain_row + shift_row


def gelu_exact(values):
    return jax.nn.gelu(values, approximate=False)


def block_mask(chosen_blocks, segment_rows):
    nblocks = chosen_blocks.shape[2]
    block_index = jnp.arange(nblocks)
    near_blocks = jnp.abs(block_index[:, None] - block_index[None, :]) <= 1
    edge_blocks = (
        (block_index[None, :] == 0)
        | (block_index[None, :] == nblocks - 1)
        | (block_index[:, None] == 0)
        | (block_index[:, None] == nblocks - 1)
    )
    picked_blocks = jnp.any(chosen_blocks[..., None] == block_index, axis=3)
    allowed = near_blocks | edge_blocks | picked_blocks
    block_rows = segment_rows.shape[1] // nblocks
    allowed = jnp.repeat(jnp.repeat(allowed, block_rows, axis=2), block_rows, axis=3)
    same_doc = segment_rows[:, :, None] == segment_rows[:, None, :]
    return allowed & same_doc[:, None]


def masked_scores(queries, key_rows, allowed, score_scale):
    scores = (
        jnp.einsum("qshd,kshd->shqk", queries, key_rows, preferred_element_type=jnp.float32)
        * score_scale
    )
    return jnp.where(allowed, scores, -1e30)


def shards(
    block_input,
    segment_ids,
    random_blocks,
    w_qkv,
    b_qv,
    w_out,
    b_out,
    w_in,
    b_in,
    w_down,
    b_down,
    ln_gain,
    ln_bias,
    cotangent,
):
    score_scale = HEAD_DIM ** (-0.5)
    shard_rows, seq_count, model_width = block_input.shape
    layers = w_qkv.shape[0]
    local_width = w_qkv.shape[3]
    local_heads = local_width // HEAD_DIM
    allowed = block_mask(random_blocks, segment_ids)
    saved_acts = []
    stream = block_input
    for layer_index in range(layers):
        w_proj = w_qkv[layer_index].astype(jnp.bfloat16)
        w_mix = w_out[layer_index].astype(jnp.bfloat16)
        rows_low = stream.astype(jnp.bfloat16)
        full_rows = lax.all_gather(rows_low, "tensor", axis=0, tiled=True)
        length = full_rows.shape[0]
        projected = jnp.einsum(
            "lsd,tdc->tlsc", full_rows, w_proj, preferred_element_type=jnp.float32
        )
        qkv_bias = jnp.stack(
            [b_qv[layer_index, 0], jnp.zeros_like(b_qv[layer_index, 0]), b_qv[layer_index, 1]]
        )
        qkv_low = (projected + qkv_bias[:, None, None, :]).astype(jnp.bfloat16)
        head_view = qkv_low.reshape(3, length, seq_count, local_heads, HEAD_DIM)
        scores = masked_scores(head_view[0], head_view[1], allowed, score_scale)
        row_top = jnp.max(scores, axis=-1, keepdims=True)
        log_total = row_top + jnp.log(jnp.sum(jnp.exp(scores - row_top), axis=-1, keepdims=True))
        probs_low = jnp.exp(scores - log_total).astype(jnp.bfloat16)
        context = jnp.einsum(
            "shqk,kshd->qshd", probs_low, head_view[2], preferred_element_type=jnp.float32
        )
        context = context.reshape(length, seq_count, local_width).astype(jnp.bfloat16)
        mixed = lax.psum_scatter(
            jnp.einsum("lsc,cd->lsd", context, w_mix, preferred_element_type=jnp.float32).astype(
                jnp.bfloat16
            ),
            "tensor",
            scatter_dimension=0,
            tiled=True,
        ).astype(jnp.float32)
        first_sum = stream + mixed + b_out[layer_index]
        hidden_rows = norm_rows(first_sum, ln_gain[layer_index, 0], ln_bias[layer_index, 0])
        hidden_low = hidden_rows.astype(jnp.bfloat16)
        up_weight = w_in[layer_index].astype(jnp.bfloat16)
        backward_weight = w_down[layer_index].astype(jnp.bfloat16)
        hidden_full = lax.all_gather(hidden_low, "tensor", axis=0, tiled=True)
        preactivation = (
            jnp.einsum("twn,nj->twj", hidden_full, up_weight, preferred_element_type=jnp.float32)
            + b_in[layer_index]
        )
        activation_reduced = gelu_exact(preactivation).astype(jnp.bfloat16)
        grown = lax.psum_scatter(
            jnp.einsum(
                "unj,jp->unp",
                activation_reduced,
                backward_weight,
                preferred_element_type=jnp.float32,
            ).astype(jnp.bfloat16),
            "tensor",
            scatter_dimension=0,
            tiled=True,
        ).astype(jnp.float32)
        second_sum = hidden_rows + grown + b_down[layer_index]
        stream = norm_rows(second_sum, ln_gain[layer_index, 1], ln_bias[layer_index, 1])
        keep_rows, keep_hidden = (full_rows, hidden_full)
        saved_acts.append(
            (
                keep_rows,
                head_view,
                log_total,
                context,
                first_sum,
                keep_hidden,
                preactivation,
                activation_reduced,
                second_sum,
                up_weight,
                backward_weight,
            )
        )
    upstream = cotangent
    grads_by_layer = [None] * layers
    for layer_index in reversed(range(layers)):
        (
            keep_rows,
            head_view,
            log_total,
            context,
            first_sum,
            keep_hidden,
            preactivation,
            activation_reduced,
            second_sum,
            up_weight,
            backward_weight,
        ) = saved_acts[layer_index]
        full_rows, hidden_full = (keep_rows, keep_hidden)
        length = full_rows.shape[0]
        w_proj = w_qkv[layer_index].astype(jnp.bfloat16)
        w_mix = w_out[layer_index].astype(jnp.bfloat16)
        _, pull_second = jax.vjp(
            norm_rows, second_sum, ln_gain[layer_index, 1], ln_bias[layer_index, 1]
        )
        d_second, d_gain_two, d_shift_two = pull_second(upstream)
        _, pull_gelu = jax.vjp(gelu_exact, preactivation)
        widened_full = lax.all_gather(d_second.astype(jnp.bfloat16), "tensor", axis=0, tiled=True)
        down_gradient = jnp.einsum(
            "uxc,uxw->cw", activation_reduced, widened_full, preferred_element_type=jnp.float32
        )
        activation_gradient = jnp.einsum(
            "mra,xa->mrx", widened_full, backward_weight, preferred_element_type=jnp.float32
        )
        preactivation_gradient_reduced = pull_gelu(activation_gradient)[0].astype(jnp.bfloat16)
        up_gradient = jnp.einsum(
            "kmx,kmt->xt",
            hidden_full,
            preactivation_gradient_reduced,
            preferred_element_type=jnp.float32,
        )
        g_up_bias = jnp.sum(preactivation_gradient_reduced.astype(jnp.float32), axis=(0, 1))
        d_hidden = d_second + lax.psum_scatter(
            jnp.einsum(
                "hmp,tp->hmt",
                preactivation_gradient_reduced,
                up_weight,
                preferred_element_type=jnp.float32,
            ).astype(jnp.bfloat16),
            "tensor",
            scatter_dimension=0,
            tiled=True,
        ).astype(jnp.float32)
        _, pull_first = jax.vjp(
            norm_rows, first_sum, ln_gain[layer_index, 0], ln_bias[layer_index, 0]
        )
        d_first, d_gain_one, d_shift_one = pull_first(d_hidden)
        full_mixed = lax.all_gather(d_first.astype(jnp.bfloat16), "tensor", axis=0, tiled=True)
        g_out = jnp.einsum("lsc,lsd->cd", context, full_mixed, preferred_element_type=jnp.float32)
        d_context = jnp.einsum(
            "lsd,cd->lsc", full_mixed, w_mix, preferred_element_type=jnp.float32
        ).astype(jnp.bfloat16)
        d_context = d_context.reshape(length, seq_count, local_heads, HEAD_DIM)
        queries, key_rows, value_rows = (head_view[0], head_view[1], head_view[2])
        scores = masked_scores(queries, key_rows, allowed, score_scale)
        attn_probs = jnp.exp(scores - log_total)
        probs_low = attn_probs.astype(jnp.bfloat16)
        d_probs = jnp.einsum(
            "qshd,kshd->shqk", d_context, value_rows, preferred_element_type=jnp.float32
        )
        d_scores = attn_probs * (d_probs - jnp.sum(d_probs * attn_probs, axis=-1, keepdims=True))
        d_scores = d_scores.astype(jnp.bfloat16)
        d_query = (
            jnp.einsum("shqk,kshd->qshd", d_scores, key_rows, preferred_element_type=jnp.float32)
            * score_scale
        )
        d_key = (
            jnp.einsum("shqk,qshd->kshd", d_scores, queries, preferred_element_type=jnp.float32)
            * score_scale
        )
        d_value = jnp.einsum(
            "shqk,qshd->kshd", probs_low, d_context, preferred_element_type=jnp.float32
        )
        d_qkv = (
            jnp.stack([d_query, d_key, d_value])
            .reshape(3, length, seq_count, local_width)
            .astype(jnp.bfloat16)
        )
        g_proj = jnp.einsum("lsd,tlsc->tdc", full_rows, d_qkv, preferred_element_type=jnp.float32)
        qkv_sums = jnp.sum(d_qkv.astype(jnp.float32), axis=(1, 2))
        g_bias = jnp.stack([qkv_sums[0], qkv_sums[2]])
        upstream = d_first + lax.psum_scatter(
            jnp.einsum("tlsc,tdc->lsd", d_qkv, w_proj, preferred_element_type=jnp.float32).astype(
                jnp.bfloat16
            ),
            "tensor",
            scatter_dimension=0,
            tiled=True,
        ).astype(jnp.float32)
        weight_grads = (g_proj, g_bias, g_out, up_gradient, g_up_bias, down_gradient)
        small_grads = (
            jnp.sum(d_first, axis=(0, 1)),
            jnp.sum(d_second, axis=(0, 1)),
            jnp.stack([d_gain_one, d_gain_two]),
            jnp.stack([d_shift_one, d_shift_two]),
        )
        grads_by_layer[layer_index] = (weight_grads, small_grads)
    weight_stack = tuple(
        (
            jnp.stack([grads_by_layer[layer_index][0][member] for layer_index in range(layers)])
            for member in range(6)
        )
    )
    small_stack = tuple(
        (
            jnp.stack([grads_by_layer[layer_index][1][member] for layer_index in range(layers)])
            for member in range(4)
        )
    )
    weight_stack = jax.tree.map(
        lambda part: part.astype(jnp.float32), lax.psum(as_sent(weight_stack), "dp")
    )
    small_stack = lax.psum(small_stack, ("dp", "tensor"))
    return (
        stream,
        upstream,
        weight_stack[0],
        weight_stack[1],
        weight_stack[2],
        small_stack[0],
        weight_stack[3],
        weight_stack[4],
        weight_stack[5],
        small_stack[1],
        small_stack[2],
        small_stack[3],
    )


def solution(mesh):
    by_sequence = mesh.shape["tensor"] == 2 and mesh.shape["dp"] == 16
    return jax.shard_map(
        sequence_shards if by_sequence else shards,
        mesh=mesh,
        in_specs=(
            P("tensor", "dp", None),
            P("dp", None),
            P("dp", "tensor", None, None),
            P(None, None, None, "tensor"),
            P(None, None, "tensor"),
            P(None, "tensor", None),
            P(),
            P(None, None, "tensor"),
            P(None, "tensor"),
            P(None, "tensor", None),
            P(),
            P(),
            P(),
            P("tensor", "dp", None),
        ),
        out_specs=(
            P("tensor", "dp", None),
            P("tensor", "dp", None),
            P(None, None, None, "tensor"),
            P(None, None, "tensor"),
            P(None, "tensor", None),
            P(),
            P(None, None, "tensor"),
            P(None, "tensor"),
            P(None, "tensor", None),
            P(),
            P(),
            P(),
        ),
        check_vma=False,
    )
```

```python
import functools

import jax
import jax.numpy as jnp
from jax import lax
from jax.experimental import pallas as pl
from jax.experimental.pallas import tpu as pltpu
from jax.sharding import PartitionSpec as P

HEAD_DIM = 64
BIG = -1e30
BF16 = jnp.bfloat16
F32 = jnp.float32
MESH = pl.DeviceIdType.MESH
VMEM_LIMIT = 56 << 20

FLIP_Y, FLIP_C, FLIP_X, FLIP_Z0, FLIP_Z1 = 1, 2, 4, 8, 16
SWAP = FLIP_Y + FLIP_C
DEVICES = 32

GROUPS = 12
OUT_GROUP = 3
FF_GROUPS = 4


def in_group(s):
    return 4 + 2 * s


def down_group(s):
    return 5 + 2 * s


def flip(values, bit):
    pairs = [(i, i ^ bit) for i in range(DEVICES)]
    return jax.tree.map(lambda v: lax.ppermute(v, ("dp", "tensor"), pairs), values)


def nt(a, b):
    return lax.dot_general(a, b, (((1,), (1,)), ((), ())), preferred_element_type=F32)


def nn(a, b):
    return lax.dot_general(a, b, (((1,), (0,)), ((), ())), preferred_element_type=F32)


def tn(a, b):
    return lax.dot_general(a, b, (((0,), (0,)), ((), ())), preferred_element_type=F32)


def block_of(ref):
    width = ref.shape[-1]
    return ref[...].reshape(-1, width)


def place_kernel(transposed, code_ref, g_ref, *refs):
    o_ref, t_ref = refs[-2:]
    code = code_ref[0]
    for j in range(16):
        start = pl.multiple_of((j ^ code) * 32, 32)
        t_ref[j * 32 : (j + 1) * 32, :] = g_ref[0, pl.ds(start, 32), :].astype(F32)
    placed = t_ref[...].T if transposed else t_ref[...]
    o_ref[...] = placed.reshape(o_ref.shape)


def place(grads, shape, block, index, transposed, count, group, into, code):
    width = grads.shape[-1]
    more = [] if into is None else [into]
    return pl.pallas_call(
        functools.partial(place_kernel, transposed),
        out_shape=jax.ShapeDtypeStruct(shape, F32),
        grid_spec=pltpu.PrefetchScalarGridSpec(
            num_scalar_prefetch=1,
            grid=(count,),
            in_specs=[pl.BlockSpec((1, 512, width), lambda i, code: (group(i), 0, 0))]
            + [pl.BlockSpec(memory_space=pl.ANY) for _ in more],
            out_specs=pl.BlockSpec(block, lambda i, code: index(i)),
            scratch_shapes=[pltpu.VMEM((512, width), F32)],
        ),
        input_output_aliases={2: 0} if more else {},
        compiler_params=pltpu.CompilerParams(vmem_limit_bytes=VMEM_LIMIT),
        cost_estimate=pl.CostEstimate(flops=0, bytes_accessed=count * 512 * width * 6, transcendentals=0),
        name="place",
    )(code, grads, *more)


def partner(bits):
    dp, y = lax.axis_index("dp"), lax.axis_index("tensor")
    other = dp
    for step in (1, 2, 4, 8):
        if bits & (2 * step):
            other = other + step * (1 - 2 * ((dp // step) % 2))
    return (other, 1 - y if bits & FLIP_Y else y)


def greet(bits):
    barrier = pltpu.get_barrier_semaphore()
    for bit in bits:
        pl.semaphore_signal(barrier, inc=1, device_id=partner(bit), device_id_type=MESH)
    pl.semaphore_wait(barrier, len(bits))


def add_rows(into, other, rows):
    def step(i, _):
        at = pl.ds(pl.multiple_of(i * 32, 32), 32)
        into[at, :] = (into[at, :].astype(F32) + other[at, :].astype(F32)).astype(BF16)
        return 0

    lax.fori_loop(0, rows // 32, step, 0)


SLOTS = 8
LAST_TICK = 10


class Reduction:
    def __init__(self, grads, sums, count, bufs, sems):
        self.grads, self.sums, self.count = grads, sums, count
        self.y_buf, self.x_buf, self.z0_buf, self.z1_buf, self.all_buf, self.keep_buf = bufs
        self.send_sem, self.recv_sem, self.core_send, self.core_recv = sems[:4]
        self.keep_sem, self.out_sem, self.in_free, self.out_free = sems[4:]

    def copy(self, step, i):
        slot = lax.rem(i, SLOTS)
        ys, al = self.y_buf.at[slot], self.all_buf.at[slot]
        bit, source, target = (
            (FLIP_Y, self.grads.at[i, pl.ds(256, 256)], ys),
            (FLIP_X, ys.at[pl.ds(128, 128)], self.x_buf.at[slot]),
            (FLIP_Z0, ys.at[pl.ds(64, 64)], self.z0_buf.at[slot]),
            (FLIP_Z1, ys.at[pl.ds(32, 32)], self.z1_buf.at[slot]),
            (FLIP_Z1, al.at[pl.ds(0, 32)], al.at[pl.ds(32, 32)]),
            (FLIP_Z0, al.at[pl.ds(0, 64)], al.at[pl.ds(64, 64)]),
            (FLIP_X, al.at[pl.ds(0, 128)], al.at[pl.ds(128, 128)]),
            (FLIP_C, al, self.sums.at[i, pl.ds(256, 256)]),
        )[step]
        return pltpu.make_async_remote_copy(
            src_ref=source,
            dst_ref=target,
            send_sem=self.send_sem.at[step, slot] if step < 7 else self.core_send.at[i],
            recv_sem=self.recv_sem.at[step, slot] if step < 7 else self.core_recv.at[i],
            device_id=partner(bit),
            device_id_type=MESH,
        )

    def keep(self, i):
        slot = lax.rem(i, 2)
        return pltpu.make_async_copy(
            self.grads.at[i, pl.ds(0, 256)], self.keep_buf.at[slot], self.keep_sem.at[slot]
        )

    def out(self, i):
        slot = lax.rem(i, SLOTS)
        return pltpu.make_async_copy(
            self.all_buf.at[slot], self.sums.at[i, pl.ds(0, 256)], self.out_sem.at[slot]
        )

    def take(self, sem, i):
        @pl.when(i >= SLOTS)
        def _():
            pl.semaphore_wait(sem, 1)

    def give(self, sem, bit, i):
        @pl.when(i + SLOTS < self.count)
        def _():
            pl.semaphore_signal(sem, inc=1, device_id=partner(bit), device_id_type=MESH)

    def tick(self, t):
        def at(offset, body):
            i = t - offset
            pl.when((i >= 0) & (i < self.count))(lambda: body(i, lax.rem(i, SLOTS)))

        def set_out(i, slot):
            self.take(self.in_free.at[0], i)
            self.copy(0, i).start()
            self.keep(i).start()

        def finish(i, slot):
            self.copy(7, i).wait()
            self.out(i).wait()
            for n, bit in enumerate((FLIP_X, FLIP_Z0, FLIP_Z1)):
                self.give(self.out_free.at[n], bit, i)

        def to_core(i, slot):
            self.copy(6, i).wait()
            self.copy(7, i).start()
            self.out(i).start()

        def back_x(i, slot):
            self.copy(5, i).wait()
            self.take(self.out_free.at[0], i)
            self.copy(6, i).start()

        def back_z0(i, slot):
            self.copy(4, i).wait()
            self.take(self.out_free.at[1], i)
            self.copy(5, i).start()

        def back_z1(i, slot):
            self.copy(3, i).wait()
            add_rows(self.y_buf.at[slot], self.z1_buf.at[slot], 32)
            self.all_buf[slot, 0:32, :] = self.y_buf[slot, 0:32, :]
            for n, bit in enumerate((FLIP_Y, FLIP_X, FLIP_Z0, FLIP_Z1)):
                self.give(self.in_free.at[n], bit, i)
            self.take(self.out_free.at[2], i)
            self.copy(4, i).start()

        def on_z1(i, slot):
            self.copy(2, i).wait()
            add_rows(self.y_buf.at[slot], self.z0_buf.at[slot], 64)
            self.take(self.in_free.at[3], i)
            self.copy(3, i).start()

        def on_z0(i, slot):
            self.copy(1, i).wait()
            add_rows(self.y_buf.at[slot], self.x_buf.at[slot], 128)
            self.take(self.in_free.at[2], i)
            self.copy(2, i).start()

        def on_x(i, slot):
            self.copy(0, i).wait()
            self.keep(i).wait()
            add_rows(self.y_buf.at[slot], self.keep_buf.at[lax.rem(i, 2)], 256)
            self.take(self.in_free.at[1], i)
            self.copy(1, i).start()

        at(0, set_out)
        at(10, finish)
        at(9, to_core)
        at(7, back_x)
        at(6, back_z0)
        at(5, back_z1)
        at(4, on_z1)
        at(3, on_z0)
        at(1, on_x)


def stream(count, feeds, body):
    for copy in feeds(0, 0):
        copy.start()

    def step(i, _):
        slot = lax.rem(i, 2)

        @pl.when(i + 1 < count)
        def _():
            for copy in feeds(i + 1, 1 - slot):
                copy.start()

        for copy in feeds(i, slot):
            copy.wait()
        body(i, slot)
        return 0

    lax.fori_loop(0, count, step, 0)


def norm(r, gain, shift):
    centred = r - jnp.mean(r, axis=-1, keepdims=True)
    rstd = lax.rsqrt(jnp.mean(centred * centred, axis=-1, keepdims=True) + 1e-06)
    return centred * rstd * gain + shift


def norm_back(dy, r, gain):
    centred = r - jnp.mean(r, axis=-1, keepdims=True)
    rstd = lax.rsqrt(jnp.mean(centred * centred, axis=-1, keepdims=True) + 1e-06)
    unit = centred * rstd
    dunit = dy * gain
    dr = rstd * (
        dunit
        - jnp.mean(dunit, axis=-1, keepdims=True)
        - unit * jnp.mean(dunit * unit, axis=-1, keepdims=True)
    )
    return dr, dy * unit


def gelu_and_slope(u):
    cdf = 0.5 * (1.0 + lax.erf(u * (0.5**0.5)))
    pdf = jnp.exp(-0.5 * u * u) * 0.3989422804014327
    return u * cdf, cdf + u * pdf


TILE = 64


def row_tiles(rows, body):
    def step(i, _):
        body(pl.ds(pl.multiple_of(i * TILE, TILE), TILE))
        return 0

    lax.fori_loop(0, rows // TILE, step, 0)


def pair_lanes(values, e):
    lane = lax.broadcasted_iota(jnp.int32, values.shape, 1)
    return jnp.where(lane // HEAD_DIM == e, values, jnp.zeros_like(values))


def attend_pair(query, keys, values, hot, mask):
    scale = HEAD_DIM**-0.5
    rows = query.shape[0]
    query = query * jnp.asarray(scale, BF16)
    values_t = values.T
    tile = rows // 2
    contexts, lses = [], ([], [])
    for part in range(2):
        at = slice(part * tile, (part + 1) * tile)
        heads = []
        for e in range(2):
            right = jnp.concatenate([pair_lanes(query[at], e), hot[at]], axis=1)
            left = jnp.concatenate([keys, mask[e]], axis=1)
            s = nt(left, right)
            top = jnp.max(s, axis=0, keepdims=True)
            p = jnp.exp(s - top)
            total = jnp.sum(p, axis=0, keepdims=True)
            c = nn(values_t[e * HEAD_DIM : (e + 1) * HEAD_DIM, :], p.astype(BF16))
            heads.append(c * (1.0 / total))
            lses[e].append(top + jnp.log(total))
        contexts.append(jnp.concatenate(heads, axis=0).T)
    return jnp.concatenate(contexts, axis=0), [jnp.concatenate(parts, axis=1) for parts in lses]


def attend_back_pair(query, keys, values, hot, mask, ctx, lse, dctx):
    scale = HEAD_DIM**-0.5
    rows = query.shape[0]
    query = query * jnp.asarray(scale, BF16)
    keys_t = keys.T
    delta_t = (dctx.astype(F32) * ctx.astype(F32)).T
    tile = rows // 2
    dk, dv, dq = 0.0, 0.0, []
    for part in range(2):
        at = slice(part * tile, (part + 1) * tile)
        heads = []
        for e in range(2):
            lanes = slice(e * HEAD_DIM, (e + 1) * HEAD_DIM)
            query_e = pair_lanes(query[at], e)
            dctx_e = pair_lanes(dctx[at], e)
            right = jnp.concatenate([query_e, hot[at]], axis=1)
            left = jnp.concatenate([keys, mask[e]], axis=1)
            p = jnp.exp(nt(left, right) - lse[e : e + 1, at])
            dp = nt(values, dctx_e)
            delta = jnp.sum(delta_t[lanes, at], axis=0, keepdims=True)
            ds = (p * (dp - delta)).astype(BF16)
            dk = dk + nn(ds, query_e)
            dv = dv + nn(p.astype(BF16), dctx_e)
            heads.append(nn(keys_t[lanes, :], ds) * scale)
        dq.append(jnp.concatenate(heads, axis=0).T)
    return jnp.concatenate(dq, axis=0), dk, dv


class Spread:
    def __init__(self, weights, pairs, send_sem, recv_sem):
        self.weights, self.pairs, self.send_sem, self.recv_sem = weights, pairs, send_sem, recv_sem

    def copy(self, step, t):
        w = self.weights
        even, odd = 2 * t, 2 * t + 1
        bit, source, target = (
            (FLIP_Y, w.at[0, even, 0, pl.ds(0, 64)], w.at[0, even, 1, pl.ds(0, 64)]),
            (FLIP_Y, w.at[0, odd, 0, pl.ds(0, 64)], w.at[0, odd, 1, pl.ds(0, 64)]),
            (FLIP_X, w.at[0, even, 1, pl.ds(0, 64)], w.at[0, even, 1, pl.ds(128, 64)]),
            (FLIP_Z0, w.at[0, odd, 1, pl.ds(0, 64)], w.at[0, odd, 1, pl.ds(64, 64)]),
            (FLIP_Z0, w.at[0, even, 1, pl.ds(0, 64)], w.at[0, even, 1, pl.ds(64, 64)]),
            (FLIP_Z0, w.at[0, even, 1, pl.ds(128, 64)], w.at[0, even, 1, pl.ds(192, 64)]),
            (FLIP_X, w.at[0, odd, 1, pl.ds(0, 128)], w.at[0, odd, 1, pl.ds(128, 128)]),
            (FLIP_C, w.at[0, even, 1], w.at[1, even, 1]),
            (FLIP_C, w.at[0, odd, 1], w.at[1, odd, 1]),
        )[step]
        return pltpu.make_async_remote_copy(
            src_ref=source,
            dst_ref=target,
            send_sem=self.send_sem.at[step, t],
            recv_sem=self.recv_sem.at[step, t],
            device_id=partner(bit),
            device_id_type=MESH,
        )

    def tick(self, t):
        def at(offset, waits, starts):
            i = t - offset

            @pl.when((i >= 0) & (i < self.pairs))
            def _():
                for step in waits:
                    self.copy(step, i).wait()
                for step in starts:
                    self.copy(step, i).start()

        at(0, (), (0, 1))
        at(4, (7, 8), ())
        at(3, (4, 5, 6), (7, 8))
        at(2, (2, 3), (4, 5, 6))
        at(1, (0, 1), (2, 3))


SPREAD_TICKS = 4
PER_LAYER = 14


def forward_kernel(layers, *refs):
    refs = list(refs)
    x_ref, up_ref, wq_ref, wo_ref, wi_ref, wd_ref, hot_ref, mask_ref, bq_ref, bi_ref, vec_ref = refs[:11]
    w_ref, up_out, x_out = refs[11:14]
    saved = [refs[14 + PER_LAYER * l : 14 + PER_LAYER * (l + 1)] for l in range(layers)]
    (
        x, acc, r_buf, low, xb, qkv, kv_sib, ctx, lse, hl, g_all, slope_all,
        col_buf, row_buf, turn_buf, made_buf, wa_buf, wb_buf, mask_buf, hot_buf,
        feed_sem, load_sem, col_sem, row_sem, made_sem, store_sem, block_sem,
        core_send, core_recv, kv_send, kv_recv, g_send, g_recv, spread_send, spread_recv,
    ) = refs[14 + PER_LAYER * layers :]
    rows, width = acc.shape
    dp, y = lax.axis_index("dp"), lax.axis_index("tensor")
    core = dp % 2
    stays = core == y
    spread = Spread(w_ref, layers * GROUPS // 2, spread_send, spread_recv)
    greet((FLIP_Y, FLIP_X, FLIP_Z0, FLIP_C, SWAP))

    def feed(n, slot, source, target):
        return pltpu.make_async_copy(source, target, feed_sem.at[n, slot])

    def load(n, source, target):
        return pltpu.make_async_copy(source, target, load_sem.at[n])

    def store(n, source, target):
        return pltpu.make_async_copy(source, target, store_sem.at[n])

    def exchange(n, source, target, bits=FLIP_C):
        return pltpu.make_async_remote_copy(
            src_ref=source, dst_ref=target, send_sem=core_send.at[n], recv_sem=core_recv.at[n],
            device_id=partner(bits), device_id_type=MESH,
        )

    def columns(ref, i, size):
        return ref.at[:, pl.ds(pl.multiple_of(i * size, size), size)]

    def swap(n, source, target, begin):
        here = store(n, source, target)
        there = exchange(n, source, target, SWAP)

        @pl.when(stays)
        def _():
            here.start() if begin else here.wait()

        @pl.when(jnp.logical_not(stays))
        def _():
            there.start() if begin else there.wait()

    items = []
    for l in range(layers):
        items += [(True, wq_ref.at[l, t], l * GROUPS + t) for t in range(3)]
        items += [(False, wo_ref.at[l], l * GROUPS + OUT_GROUP)]
        for n in range(FF_GROUPS):
            items += [(True, wi_ref.at[l, :, pl.ds(n * 512, 512)], l * GROUPS + in_group(n))]
            items += [(False, wd_ref.at[l, pl.ds(n * 512, 512)], l * GROUPS + down_group(n))]
    fetches, counts, ahead = [], [0, 0], [[], []]
    for m, (turned, source, group) in enumerate(items):
        slot = counts[turned] % 2
        buf, sem = (col_buf, col_sem) if turned else (row_buf, row_sem)
        fetches.append((pltpu.make_async_copy(source, buf.at[slot], sem.at[slot]), slot))
        ahead[turned].append(m)
        counts[turned] += 1
    bits = [(dp // step) % 2 for step in (1, 2, 4, 8)]
    made = {}

    def convert(m):
        turned, _, group = items[m]
        copy, slot = fetches[m]
        copy.wait()
        if turned:

            def turn(i, _):
                turn_buf[pl.ds(pl.multiple_of(i * 128, 128), 128), :] = col_buf[
                    slot, :, pl.ds(pl.multiple_of(i * 128, 128), 128)
                ].T
                return 0

            lax.fori_loop(0, 4, turn, 0)
        if m >= 2:
            made[m - 2].wait()

        def block(j, _):
            where = 0
            for bit, weight in zip(bits, (8, 4, 2, 1)):
                own = (j // weight) % 2
                where = where + weight * (own + bit - 2 * own * bit)
            at = pl.ds(pl.multiple_of(where * 32, 32), 32)
            rows_32 = turn_buf[at, :] if turned else row_buf[slot, at, :]
            made_buf[m % 2, pl.ds(pl.multiple_of(j * 32, 32), 32), :] = rows_32.astype(BF16)
            return 0

        lax.fori_loop(0, 16, block, 0)
        later = [n for n in ahead[turned] if n > m]
        if len(later) > 1:
            fetches[later[1]][0].start()
        parts = [
            pltpu.make_async_copy(
                made_buf.at[m % 2, pl.ds(a * 256, 256)], w_ref.at[a, group, 0], made_sem.at[m % 2, a]
            )
            for a in range(2)
        ]

        class Both:
            def wait(self):
                for part in parts:
                    part.wait()

        for part in parts:
            part.start()
        made[m] = Both()

    load_x = load(0, x_ref.at[:, 0], x)
    load_x.start()
    load_up = load(1, up_ref.at[:, 0], acc)
    load_up.start()
    load_hot = load(2, hot_ref, hot_buf)
    load_hot.start()
    for kind in range(2):
        for m in ahead[kind][:2]:
            fetches[m][0].start()
    load_x.wait()

    def narrow_x(at):
        low[at, :] = x[at, :].astype(BF16)

    row_tiles(rows, narrow_x)
    swap(0, low, xb, True)
    load_up.wait()

    def narrow_up(at):
        hl[at, :] = acc[at, :].astype(BF16)

    row_tiles(rows, narrow_up)
    swap(1, hl, up_out, True)

    for m in range(len(items)):
        convert(m)
        if m % 4 == 3:
            spread.tick(m // 4)
    for m in range(len(items) - 2, len(items)):
        made[m].wait()
    swap(0, low, xb, False)
    swap(1, hl, up_out, False)
    load_hot.wait()

    def widen(at):
        x[at, :] = xb[at, :].astype(F32)

    row_tiles(rows, widen)

    pairs = width // 128
    for l in range(layers):
        (
            qkv_out, sib_out, ctx_out, ctx_sib_out, lse_out, r1_out, r2_out, hl_out, hl_sib_out,
            g_out, g_sib_out, slope_out, xb_out, xb_sib_out,
        ) = saved[l]
        first = l * GROUPS
        clock = 6 + 7 * l
        xb_store = store(0, xb, xb_out)
        xb_store.start()
        xb_copy = exchange(2 + 3 * l, xb, xb_sib_out)
        xb_copy.start()

        def give_kv(n, a):
            at = pl.ds(pl.multiple_of(a * 512, 512), 512)
            return pltpu.make_async_remote_copy(
                src_ref=qkv.at[1 + n, :, at], dst_ref=kv_sib.at[n, :, at],
                send_sem=kv_send.at[n, a], recv_sem=kv_recv.at[n, a],
                device_id=partner(FLIP_C), device_id_type=MESH,
            )

        def which(i):
            return (i // 2 + 1) % 3, i % 2

        def qkv_feeds(i, slot):
            t, a = which(i)
            return (feed(0, slot, w_ref.at[a, first + t], wa_buf.at[slot]),)

        def qkv_body(i, slot):
            t, a = which(i)
            at = pl.ds(pl.multiple_of(a * 512, 512), 512)
            qkv[t, :, at] = (nt(xb[...], block_of(wa_buf.at[slot])) + bq_ref[l, t, a]).astype(BF16)
            pl.when(i < 4)(lambda: give_kv(t - 1, a).start())
            pl.when(i == 3)(lambda: spread.tick(clock))

        stream(6, qkv_feeds, qkv_body)
        qkv_store = store(1, qkv, qkv_out)
        qkv_store.start()
        for n in range(2):
            for a in range(2):
                give_kv(n, a).wait()
        sib_store = store(2, kv_sib, sib_out)
        sib_store.start()

        def pair_feeds(p, slot):
            return (feed(1, slot, mask_ref.at[pl.ds(2 * p, 2)], mask_buf.at[slot]),)

        def pair_body(p, slot):
            far = lax.rem(p + pairs // 2, pairs)
            here = pl.ds(pl.multiple_of(p * 128, 128), 128)
            there = pl.ds(pl.multiple_of(far * 128, 128), 128)
            keys = jnp.concatenate([qkv[1, :, here], kv_sib[0, :, there]], axis=0)
            values = jnp.concatenate([qkv[2, :, here], kv_sib[1, :, there]], axis=0)
            context, parts = attend_pair(qkv[0, :, here], keys, values, hot_buf[...], mask_buf[slot])
            ctx[:, here] = context.astype(BF16)
            for e in range(2):
                lse[p, e : e + 1, :] = parts[e]
            pl.when(lax.rem(p, 3) == 1)(lambda: spread.tick(clock + 1 + lax.div(p, 3)))

        stream(pairs, pair_feeds, pair_body)
        ctx_store = store(3, ctx, ctx_out)
        ctx_store.start()
        lse_store = store(4, lse, lse_out)
        lse_store.start()
        ctx_copy = exchange(3 + 3 * l, ctx.at[:, pl.ds(512, 512)], ctx_sib_out)
        ctx_copy.start()

        def out_feeds(i, slot):
            return (feed(0, slot, w_ref.at[i, first + OUT_GROUP], wa_buf.at[slot]),)

        def out_body(i, slot):
            part = nn(ctx[:, pl.ds(pl.multiple_of(i * 512, 512), 512)], block_of(wa_buf.at[slot]))

            @pl.when(i == 0)
            def _():
                acc[...] = part

            @pl.when(i == 1)
            def _():
                acc[...] += part

        stream(2, out_feeds, out_body)
        sib_store.wait()

        def first_norm(at):
            r1 = x[at, :] + acc[at, :] + vec_ref[l, 0:1, :]
            r_buf[at, :] = r1
            h = norm(r1, vec_ref[l, 1:2, :], vec_ref[l, 2:3, :])
            hl[at, :] = h.astype(BF16)
            acc[at, :] = h + vec_ref[l, 3:4, :]

        row_tiles(rows, first_norm)
        r1_store = store(5, r_buf, r1_out)
        r1_store.start()
        hl_store = store(6, hl, hl_out)
        hl_store.start()
        hl_copy = exchange(4 + 3 * l, hl, hl_sib_out)
        hl_copy.start()

        def place_of(i):
            a = 1 - lax.div(i, FF_GROUPS)
            return a, lax.rem(i, FF_GROUPS)

        def ff_feeds(i, slot):
            a, n = place_of(i)
            return (
                feed(0, slot, w_ref.at[a, first + in_group(n)], wa_buf.at[slot]),
                feed(2, slot, w_ref.at[a, first + down_group(n)], wb_buf.at[slot]),
            )

        def g_store(j):
            return pltpu.make_async_copy(g_all.at[j], columns(g_out, j, 512), block_sem.at[0, j])

        def slope_store(j):
            return pltpu.make_async_copy(slope_all.at[j], columns(slope_out, j, 512), block_sem.at[1, j])

        def g_copy(n):
            return pltpu.make_async_remote_copy(
                src_ref=g_all.at[FF_GROUPS + n], dst_ref=columns(g_sib_out, n, 512),
                send_sem=g_send.at[l, n], recv_sem=g_recv.at[l, n],
                device_id=partner(FLIP_C), device_id_type=MESH,
            )

        def ff_body(i, slot):
            a, n = place_of(i)
            j = a * FF_GROUPS + n
            u = nt(hl[...], block_of(wa_buf.at[slot])) + bi_ref[l, a, n]
            g, slope = gelu_and_slope(u)
            g = g.astype(BF16)
            g_all[j] = g
            slope_all[j] = slope.astype(BF16)
            g_store(j).start()
            slope_store(j).start()
            pl.when(a == 1)(lambda: g_copy(n).start())
            acc[...] += nn(g, block_of(wb_buf.at[slot]))
            pl.when(lax.rem(i, 3) == 1)(lambda: spread.tick(clock + 4 + lax.div(i, 3)))

        stream(2 * FF_GROUPS, ff_feeds, ff_body)
        r1_store.wait()
        xb_store.wait()
        xb_copy.wait()

        def second_norm(at):
            r2 = acc[at, :]
            r_buf[at, :] = r2
            x2 = norm(r2, vec_ref[l, 4:5, :], vec_ref[l, 5:6, :])
            x[at, :] = x2
            xb[at, :] = x2.astype(BF16)

        row_tiles(rows, second_norm)
        r2_store = store(5, r_buf, r2_out)
        r2_store.start()
        if l == layers - 1:
            swap(10, xb, x_out, True)

        def settle(j, _):
            g_store(j).wait()
            slope_store(j).wait()
            return 0

        lax.fori_loop(0, 2 * FF_GROUPS, settle, 0)

        def settle_sent(n, _):
            g_copy(n).wait()
            return 0

        lax.fori_loop(0, FF_GROUPS, settle_sent, 0)
        for copy in (qkv_store, ctx_store, lse_store, ctx_copy, hl_store, hl_copy, r2_store):
            copy.wait()
    swap(10, xb, x_out, False)


def forward(block_input, cotangent, w_qkv, w_out, w_in, w_down, hot, mask, bias_qkv, bias_in, vectors):
    rows, _, width = block_input.shape
    layers = w_qkv.shape[0]
    total = layers * GROUPS
    anywhere = pl.BlockSpec(memory_space=pl.ANY)
    in_vmem = pl.BlockSpec(memory_space=pltpu.VMEM)
    low = lambda *shape: pltpu.VMEM(shape, BF16)
    full = lambda *shape: pltpu.VMEM(shape, F32)
    dma = lambda *shape: pltpu.SemaphoreType.DMA(shape)
    low_out = lambda *shape: jax.ShapeDtypeStruct(shape, BF16)
    full_out = lambda *shape: jax.ShapeDtypeStruct(shape, F32)
    layer_out = (
        low_out(3, rows, width),
        low_out(2, rows, width),
        low_out(rows, width),
        low_out(rows, width // 2),
        full_out(width // 128, 2, rows),
        full_out(rows, width),
        full_out(rows, width),
        low_out(rows, width),
        low_out(rows, width),
        low_out(rows, 4 * width),
        low_out(rows, 2 * width),
        low_out(rows, 4 * width),
        low_out(rows, width),
        low_out(rows, width),
    )
    outs = pl.pallas_call(
        functools.partial(forward_kernel, layers),
        out_shape=(low_out(2, total, 2, 256, width), low_out(rows, width), low_out(rows, width)) + layer_out * layers,
        in_specs=[anywhere] * 8 + [in_vmem] * 3,
        out_specs=(anywhere,) * (3 + PER_LAYER * layers),
        scratch_shapes=[
            full(rows, width),
            full(rows, width),
            full(rows, width),
            low(rows, width),
            low(rows, width),
            low(3, rows, width),
            low(2, rows, width),
            low(rows, width),
            full(width // 128, 2, rows),
            low(rows, width),
            low(2 * FF_GROUPS, rows, 512),
            low(2 * FF_GROUPS, rows, 512),
            full(2, width, 512),
            full(2, 512, width),
            full(512, width),
            low(2, 512, width),
            low(2, 2, 256, width),
            low(2, 2, 256, width),
            low(2, 2, 2 * rows, 128),
            low(rows, 128),
            dma(3, 2),
            dma(3),
            dma(2),
            dma(2),
            dma(2, 2),
            dma(11),
            dma(2, 2 * FF_GROUPS),
            dma(11),
            dma(11),
            dma(2, 2),
            dma(2, 2),
            dma(layers, FF_GROUPS),
            dma(layers, FF_GROUPS),
            dma(9, total // 2),
            dma(9, total // 2),
        ],
        compiler_params=pltpu.CompilerParams(collective_id=0, has_side_effects=True, vmem_limit_bytes=60 << 20),
        cost_estimate=pl.CostEstimate(flops=30 << 30, bytes_accessed=300 << 20, transcendentals=1 << 24),
        name="forward",
    )(block_input, cotangent, w_qkv, w_out, w_in, w_down, hot, mask, bias_qkv, bias_in, vectors)
    saved = [outs[3 + PER_LAYER * l : 3 + PER_LAYER * (l + 1)] for l in range(layers)]
    return outs[0], outs[1], outs[2], saved


def backward_kernel(layers, *refs):
    refs = list(refs)
    up_ref, w_ref, hot_ref, mask_ref, vec_ref = refs[:5]
    saved = [refs[5 + PER_LAYER * l : 5 + PER_LAYER * (l + 1)] for l in range(layers)]
    at_ref = 5 + PER_LAYER * layers
    grads, sums, dx_out, dbi_ref, qkv_sums_ref, small_ref = refs[at_ref : at_ref + 6]
    (
        acc, dr1, dm, dm_sib, da, da_sib, du, du_sib, dctx, dqkv, d_sib, kv_out, kv_far,
        wa_buf, wb_buf, r_buf, slope_buf, left_buf, left_sib_buf, right_buf, right_sib_buf,
        pair_buf, lse_buf, mask_buf, hot_buf, unit_buf,
        y_buf, x_buf, z0_buf, z1_buf, all_buf, keep_buf,
        feed_sem, load_sem, store_sem, core_send, core_recv, du_send, du_recv,
        send_sem, recv_sem, sum_send, sum_recv, keep_sem, out_sem, in_free, out_free,
    ) = refs[at_ref + 6 :]
    rows, width = acc.shape
    total = layers * GROUPS
    reduction = Reduction(
        grads, sums, total,
        (y_buf, x_buf, z0_buf, z1_buf, all_buf, keep_buf),
        (send_sem, recv_sem, sum_send, sum_recv, keep_sem, out_sem, in_free, out_free),
    )
    greet((FLIP_Y, FLIP_X, FLIP_Z0, FLIP_Z1, FLIP_C, SWAP))

    def feed(n, slot, source, target):
        return pltpu.make_async_copy(source, target, feed_sem.at[n, slot])

    def load(n, source, target):
        return pltpu.make_async_copy(source, target, load_sem.at[n])

    def exchange(n, source, target):
        return pltpu.make_async_remote_copy(
            src_ref=source, dst_ref=target, send_sem=core_send.at[n], recv_sem=core_recv.at[n],
            device_id=partner(FLIP_C), device_id_type=MESH,
        )

    def give_du(j, n):
        return pltpu.make_async_remote_copy(
            src_ref=du.at[j], dst_ref=du_sib.at[n], send_sem=du_send.at[n], recv_sem=du_recv.at[n],
            device_id=partner(FLIP_C), device_id_type=MESH,
        )

    def weight(a, group):
        return w_ref.at[a, group]

    def columns(ref, i, size):
        return ref.at[:, pl.ds(pl.multiple_of(i * size, size), size)]

    def unit(left, left_sib, right, right_sib, index):
        unit_buf[...] = (tn(left, right) + tn(left_sib, right_sib)).astype(BF16)
        store = pltpu.make_async_copy(unit_buf, grads.at[index], store_sem.at[0])
        store.start()
        store.wait()

    def add_small(l, row, value):
        small_ref[l, row : row + 1, :] += jnp.sum(value, axis=0, keepdims=True)

    start_up = load(0, up_ref, da)
    start_up.start()
    start_hot = load(1, hot_ref, hot_buf)
    start_hot.start()
    start_up.wait()
    start_hot.wait()
    small_ref[...] = jnp.zeros_like(small_ref)

    def widen(at):
        acc[at, :] = da[at, :].astype(F32)

    row_tiles(rows, widen)
    done = 0
    for l in reversed(range(layers)):
        qkv_ref, sib_ref, ctx_ref, ctx_sib_ref, lse_ref, r1_ref, r2_ref, hl_ref, hl_sib_ref, g_ref, g_sib_ref, slope_ref, xb_ref, xb_sib_ref = saved[l]
        first = l * GROUPS
        base = (layers - 1 - l) * GROUPS
        clock = 11 * (layers - 1 - l)

        r_load = load(0, r2_ref, r_buf)
        r_load.start()
        r_load.wait()

        def second(at):
            dy = acc[at, :]
            dr, part = norm_back(dy, r_buf[at, :], vec_ref[l, 4:5, :])
            acc[at, :] = dr
            dm[at, :] = dr.astype(BF16)
            add_small(l, 0, part)
            add_small(l, 1, dy)
            add_small(l, 2, dr)

        row_tiles(rows, second)
        dm_copy = exchange(0, dm, dm_sib)
        dm_copy.start()
        r_load = load(0, r1_ref, r_buf)
        r_load.start()
        right_load = load(1, hl_ref, right_buf)
        right_load.start()
        right_sib_load = load(2, hl_sib_ref, right_sib_buf)
        right_sib_load.start()
        dm_copy.wait()

        def down_feeds(i, slot):
            return (
                feed(0, slot, columns(g_ref, i, 512), left_buf.at[slot]),
                feed(1, slot, columns(g_sib_ref, i, 512), left_sib_buf.at[slot]),
            )

        def down_body(i, slot):
            unit(left_buf[slot], left_sib_buf[slot], dm[...], dm_sib[...], base + i)
            pl.when(lax.rem(i, 3) == 0)(lambda: reduction.tick(clock + lax.div(i, 3)))

        stream(FF_GROUPS, down_feeds, down_body)

        def place_of(i):
            a = 1 - lax.div(i, FF_GROUPS)
            return a, lax.rem(i, FF_GROUPS)

        def ff_feeds(i, slot):
            a, n = place_of(i)
            j = a * FF_GROUPS + n
            return (
                feed(0, slot, weight(a, first + down_group(n)), wa_buf.at[slot]),
                feed(1, slot, weight(a, first + in_group(n)), wb_buf.at[slot]),
                feed(2, slot, columns(slope_ref, j, 512), slope_buf.at[slot]),
            )

        def ff_body(i, slot):
            a, n = place_of(i)
            j = a * FF_GROUPS + n
            dg = nt(dm[...], block_of(wa_buf.at[slot]))
            d = (dg * slope_buf[slot].astype(F32)).astype(BF16)
            du[j] = d
            pl.when(a == 1)(lambda: give_du(j, n).start())
            dbi_ref[l, a, n] = jnp.sum(d.astype(F32), axis=0, keepdims=True)
            acc[...] += nn(d, block_of(wb_buf.at[slot]))
            pl.when(lax.rem(i, 3) == 2)(lambda: reduction.tick(clock + 2 + lax.div(i, 3)))

        stream(2 * FF_GROUPS, ff_feeds, ff_body)

        r_load.wait()

        def first_norm(at):
            dy = acc[at, :]
            dr, part = norm_back(dy, r_buf[at, :], vec_ref[l, 1:2, :])
            dr1[at, :] = dr
            da[at, :] = dr.astype(BF16)
            add_small(l, 3, part)
            add_small(l, 4, dy)
            add_small(l, 5, dr)

        row_tiles(rows, first_norm)
        da_copy = exchange(1, da, da_sib)
        da_copy.start()

        def out_feeds(i, slot):
            return (feed(0, slot, weight(i, first + OUT_GROUP), wa_buf.at[slot]),)

        def out_body(i, slot):
            dctx[:, pl.ds(pl.multiple_of(i * 512, 512), 512)] = nt(da[...], block_of(wa_buf.at[slot])).astype(BF16)

        stream(2, out_feeds, out_body)

        right_load.wait()
        right_sib_load.wait()

        def in_body(n, _):
            give_du(FF_GROUPS + n, n).wait()
            unit(du[n], du_sib[n], right_buf[...], right_sib_buf[...], base + FF_GROUPS + n)
            pl.when(lax.rem(n, 3) == 0)(lambda: reduction.tick(clock + 4 + lax.div(n, 3)))
            return 0

        lax.fori_loop(0, FF_GROUPS, in_body, 0)

        right_load = load(1, xb_ref, right_buf)
        right_load.start()
        right_sib_load = load(2, xb_sib_ref, right_sib_buf)
        right_sib_load.start()
        left_load = load(3, columns(ctx_ref, 0, 512), left_buf.at[0])
        left_load.start()
        left_sib_load = load(4, ctx_sib_ref, left_sib_buf.at[0])
        left_sib_load.start()
        da_copy.wait()
        left_load.wait()
        left_sib_load.wait()
        unit(left_buf[0], left_sib_buf[0], da[...], da_sib[...], base + 2 * FF_GROUPS)

        pairs = width // 128

        def pair_feeds(p, slot):
            far = lax.rem(p + pairs // 2, pairs)
            return (
                feed(0, slot, columns(qkv_ref.at[0], p, 128), pair_buf.at[slot, 0, pl.ds(0, rows)]),
                feed(1, slot, columns(qkv_ref.at[1], p, 128), pair_buf.at[slot, 1, pl.ds(0, rows)]),
                feed(2, slot, columns(sib_ref.at[0], far, 128), pair_buf.at[slot, 1, pl.ds(rows, rows)]),
                feed(3, slot, columns(qkv_ref.at[2], p, 128), pair_buf.at[slot, 2, pl.ds(0, rows)]),
                feed(4, slot, columns(sib_ref.at[1], far, 128), pair_buf.at[slot, 2, pl.ds(rows, rows)]),
                feed(5, slot, columns(ctx_ref, p, 128), pair_buf.at[slot, 3, pl.ds(0, rows)]),
                feed(6, slot, lse_ref.at[p], lse_buf.at[slot]),
                feed(7, slot, mask_ref.at[pl.ds(2 * p, 2)], mask_buf.at[slot]),
            )

        def pair_body(p, slot):
            far = lax.rem(p + pairs // 2, pairs)
            here = pl.ds(pl.multiple_of(p * 128, 128), 128)
            dq, dk, dv = attend_back_pair(
                pair_buf[slot, 0, 0:rows], pair_buf[slot, 1], pair_buf[slot, 2], hot_buf[...], mask_buf[slot],
                pair_buf[slot, 3, 0:rows], lse_buf[slot], dctx[:, here],
            )
            dqkv[0, :, here] = dq.astype(BF16)
            dqkv[1, :, here] = dk[:rows].astype(BF16)
            dqkv[2, :, here] = dv[:rows].astype(BF16)
            there = pl.ds(pl.multiple_of(far * 128, 128), 128)
            kv_out[0, :, there] = dk[rows:].astype(BF16)
            kv_out[1, :, there] = dv[rows:].astype(BF16)
            pl.when(lax.rem(p, 3) == 1)(lambda: reduction.tick(clock + 6 + lax.div(p, 3)))

        stream(pairs, pair_feeds, pair_body)
        kv_copy = exchange(2, kv_out, kv_far)
        kv_copy.start()
        kv_copy.wait()
        for n in range(2):
            add_rows(dqkv.at[1 + n], kv_far.at[n], rows)
        d_copy = exchange(3, dqkv.at[:, :, pl.ds(512, 512)], d_sib)
        d_copy.start()
        right_load.wait()
        right_sib_load.wait()
        d_copy.wait()

        def qkv_body(n, _):
            unit(dqkv[n, :, 0:512], d_sib[n], right_buf[...], right_sib_buf[...], base + 2 * FF_GROUPS + 1 + n)
            return 0

        lax.fori_loop(0, 3, qkv_body, 0)
        reduction.tick(clock + 9)

        def start_dx(at):
            acc[at, :] = dr1[at, :]

        row_tiles(rows, start_dx)

        def dx_feeds(i, slot):
            return (feed(0, slot, weight(lax.rem(i, 2), first + lax.div(i, 2)), wa_buf.at[slot]),)

        def dx_body(i, slot):
            a, n = lax.rem(i, 2), lax.div(i, 2)
            d = dqkv[n, :, pl.ds(pl.multiple_of(a * 512, 512), 512)]
            qkv_sums_ref[l, n, a] = jnp.sum(d.astype(F32), axis=0, keepdims=True)
            acc[...] += nn(d, block_of(wa_buf.at[slot]))
            pl.when(i == 3)(lambda: reduction.tick(clock + 10))

        stream(6, dx_feeds, dx_body)
        done = clock + 11

    def narrow(at):
        da[at, :] = acc[at, :].astype(BF16)

    row_tiles(rows, narrow)
    stays = lax.axis_index("dp") % 2 == lax.axis_index("tensor")
    dx_store = load(0, da, dx_out)
    dx_copy = pltpu.make_async_remote_copy(
        src_ref=da, dst_ref=dx_out, send_sem=core_send.at[4], recv_sem=core_recv.at[4],
        device_id=partner(SWAP), device_id_type=MESH,
    )
    pl.when(stays)(lambda: dx_store.start())
    pl.when(jnp.logical_not(stays))(lambda: dx_copy.start())

    def rest(t, _):
        reduction.tick(t)
        return 0

    lax.fori_loop(done, total + LAST_TICK, rest, 0)
    pl.when(stays)(lambda: dx_store.wait())
    pl.when(jnp.logical_not(stays))(lambda: dx_copy.wait())


def backward(upstream, weights, hot, mask, vectors, saved):
    rows, width = upstream.shape
    layers = len(saved)
    total = layers * GROUPS
    anywhere = pl.BlockSpec(memory_space=pl.ANY)
    in_vmem = pl.BlockSpec(memory_space=pltpu.VMEM)
    low = lambda *shape: pltpu.VMEM(shape, BF16)
    dma = lambda *shape: pltpu.SemaphoreType.DMA(shape)
    return pl.pallas_call(
        functools.partial(backward_kernel, layers),
        out_shape=(
            jax.ShapeDtypeStruct((total, 512, width), BF16),
            jax.ShapeDtypeStruct((total, 512, width), BF16),
            jax.ShapeDtypeStruct((rows, width), BF16),
            jax.ShapeDtypeStruct((layers, 2, FF_GROUPS, 1, 512), F32),
            jax.ShapeDtypeStruct((layers, 3, 2, 1, 512), F32),
            jax.ShapeDtypeStruct((layers, 8, width), F32),
        ),
        in_specs=[anywhere] * 4 + [in_vmem] + [anywhere] * (PER_LAYER * layers),
        out_specs=(anywhere, anywhere, anywhere, in_vmem, in_vmem, in_vmem),
        scratch_shapes=[
            pltpu.VMEM((rows, width), F32),
            pltpu.VMEM((rows, width), F32),
            low(rows, width),
            low(rows, width),
            low(rows, width),
            low(rows, width),
            low(2 * FF_GROUPS, rows, 512),
            low(FF_GROUPS, rows, 512),
            low(rows, width),
            low(3, rows, width),
            low(3, rows, 512),
            low(2, rows, width),
            low(2, rows, width),
            low(2, 2, 256, width),
            low(2, 2, 256, width),
            pltpu.VMEM((rows, width), F32),
            low(2, rows, 512),
            low(2, rows, 512),
            low(2, rows, 512),
            low(rows, width),
            low(rows, width),
            low(2, 4, 2 * rows, 128),
            pltpu.VMEM((2, 2, rows), F32),
            low(2, 2, 2 * rows, 128),
            low(rows, 128),
            low(512, width),
            low(SLOTS, 256, width),
            low(SLOTS, 128, width),
            low(SLOTS, 64, width),
            low(SLOTS, 32, width),
            low(SLOTS, 256, width),
            low(2, 256, width),
            dma(8, 2),
            dma(5),
            dma(1),
            dma(5),
            dma(5),
            dma(FF_GROUPS),
            dma(FF_GROUPS),
            dma(7, SLOTS),
            dma(7, SLOTS),
            dma(total),
            dma(total),
            dma(2),
            dma(SLOTS),
            pltpu.SemaphoreType.REGULAR((4,)),
            pltpu.SemaphoreType.REGULAR((3,)),
        ],
        compiler_params=pltpu.CompilerParams(
            collective_id=1, has_side_effects=True, vmem_limit_bytes=60 << 20
        ),
        cost_estimate=pl.CostEstimate(flops=60 << 30, bytes_accessed=300 << 20, transcendentals=1 << 24),
        name="backward",
    )(upstream, weights, hot, mask, vectors, *[ref for one in saved for ref in one])


def flip_order(values, axis, bits):
    for i, bit in enumerate(bits):
        values = jnp.where(bit == 0, values, jnp.flip(values, axis + i))
    return values


def sum_everywhere(values):
    for bit in (FLIP_C, FLIP_Y, FLIP_X, FLIP_Z0, FLIP_Z1):
        values = values + flip(values, bit)
    return values


def sequence_shards(
    block_input, segment_ids, random_blocks, w_qkv, b_qv, w_out, b_out, w_in, b_in, w_down, b_down,
    ln_gain, ln_bias, cotangent,
):
    y = lax.axis_index("tensor")
    dp = lax.axis_index("dp")
    core, x_bit, z0, z1 = dp % 2, (dp // 2) % 2, (dp // 4) % 2, dp // 8
    code = core * 8 + x_bit * 4 + z0 * 2 + z1
    code_arg = code.reshape(1).astype(jnp.int32)
    device_bits = (core, x_bit, z0, z1)

    rows, _, width = block_input.shape
    layers = w_qkv.shape[0]
    blocks = random_blocks.shape[2]
    own_blocks = blocks // 2
    heads = random_blocks.shape[1] * 2

    chosen = random_blocks[0]
    near = jnp.concatenate([chosen.reshape(-1), segment_ids[0]])
    sibling = flip(near, FLIP_C)
    across, diagonal = flip(chosen.reshape(-1), FLIP_Y), flip(chosen.reshape(-1), SWAP)
    mine = jnp.concatenate([near[: chosen.size], across, near[chosen.size :]])
    other = jnp.concatenate([sibling[: chosen.size], diagonal, sibling[chosen.size :]])
    packed = jnp.where(core == y, mine, other)
    chosen = packed[: 2 * chosen.size].reshape(2, heads // 2, blocks, -1)
    segments = packed[2 * random_blocks.size :]
    chosen = flip_order(chosen.reshape(2, 2, 2, 2, blocks, -1), 1, device_bits[:3])
    chosen = chosen.transpose(1, 0, 2, 3, 4, 5).reshape(heads, blocks, -1)
    segments = segments.reshape(2, rows)
    segments = jnp.where(core == 0, segments, segments[::-1]).reshape(-1)
    query_block = core * own_blocks + jnp.arange(own_blocks)
    key_block = jnp.arange(blocks) ^ (core * own_blocks)
    allowed = (
        (jnp.abs(query_block[:, None] - key_block[None, :]) <= 1)
        | (key_block[None, :] == 0)
        | (key_block[None, :] == blocks - 1)
        | (query_block[:, None] == 0)
        | (query_block[:, None] == blocks - 1)
    )
    chosen = lax.dynamic_slice_in_dim(chosen, core * own_blocks, own_blocks, axis=1)
    allowed = allowed[None] | jnp.any(chosen[:, :, None, :] == key_block[None, None, :, None], axis=3)
    block_rows = rows // own_blocks
    block_part = jnp.where(allowed, 0.0, BIG).astype(BF16).transpose(0, 2, 1)
    block_part = jnp.repeat(block_part, block_rows, axis=1)
    documents = jnp.arange(128 - own_blocks)
    document_part = jnp.where(
        (segments[:, None] == documents[None, :]) | (documents[None, :] > 7), 0.0, BIG
    ).astype(BF16)
    mask = jnp.concatenate(
        [block_part, jnp.broadcast_to(document_part[None], (heads,) + document_part.shape)], axis=2
    )
    hot = jnp.concatenate(
        [
            jnp.repeat(jnp.eye(own_blocks, dtype=BF16), block_rows, axis=0),
            (segments[:rows, None] == documents[None, :]).astype(BF16),
        ],
        axis=1,
    )

    bias_pack = jnp.concatenate(
        [
            flip_order(b_qv.reshape(layers * 2, 2, 2, 2, 2, -1), 1, device_bits).reshape(-1),
            flip_order(b_in.reshape(layers * FF_GROUPS, 2, 2, 2, 2, -1), 1, device_bits).reshape(-1),
        ]
    )
    bias_far = flip(bias_pack, FLIP_Y)
    n_qv = b_qv.size

    def local_bias(near, far, count):
        near, far = near.reshape(count, 2, 1, 256), far.reshape(count, 2, 1, 256)
        return jnp.concatenate([near, far], axis=2).reshape(count, 2, 512)

    bias_qv = local_bias(bias_pack[:n_qv], bias_far[:n_qv], layers * 2).reshape(layers, 2, 2, 1, 512)
    bias_qkv = jnp.stack([bias_qv[:, 0], jnp.zeros_like(bias_qv[:, 0]), bias_qv[:, 1]], axis=1)
    bias_in = local_bias(bias_pack[n_qv:], bias_far[n_qv:], layers * FF_GROUPS)
    bias_in = bias_in.reshape(layers, FF_GROUPS, 2, 1, 512).swapaxes(1, 2)

    vectors = [
        jnp.stack(
            [
                b_out[l], ln_gain[l, 0], ln_bias[l, 0], b_down[l], ln_gain[l, 1], ln_bias[l, 1],
                b_out[l], b_out[l],
            ]
        )
        for l in range(layers)
    ]
    vectors = jnp.stack(vectors)
    weights, upstream_low, stream_low, saved = forward(
        block_input, cotangent, w_qkv, w_out, w_in, w_down, hot, mask, bias_qkv, bias_in, vectors
    )
    block_output = stream_low.astype(F32)[:, None]
    _, grads, dx_low, d_b_in, qkv_sums, rows_small = backward(upstream_low, weights, hot, mask, vectors, saved)
    input_grad = dx_low.astype(F32)[:, None]

    placed = [None] * 4
    for layer in range(layers):
        first = (layers - 1 - layer) * GROUPS
        put = functools.partial(place, grads, code=code_arg)
        placed[0] = put(
            w_qkv.shape, (1, 1, width, 512), lambda i, l=layer: (l, i, 0, 0), True, 3,
            lambda i, f=first: f + 2 * FF_GROUPS + 1 + i, placed[0],
        )
        placed[1] = put(
            w_out.shape, (1, 512, width), lambda i, l=layer: (l, 0, 0), False, 1,
            lambda i, f=first: f + 2 * FF_GROUPS, placed[1],
        )
        placed[2] = put(
            w_in.shape, (1, width, 512), lambda i, l=layer: (l, 0, i), True, FF_GROUPS,
            lambda i, f=first: f + FF_GROUPS + i, placed[2],
        )
        placed[3] = put(
            w_down.shape, (1, 512, width), lambda i, l=layer: (l, i, 0), False, FF_GROUPS,
            lambda i, f=first: f + i, placed[3],
        )
    stacks = [
        jnp.stack([qkv_sums[:, 0], qkv_sums[:, 2]], axis=1),
        rows_small[:, 5],
        d_b_in.swapaxes(1, 2),
        rows_small[:, 2],
        jnp.stack([rows_small[:, 3], rows_small[:, 0]], axis=1),
        jnp.stack([rows_small[:, 4], rows_small[:, 1]], axis=1),
    ]

    def global_order(values, lead):
        values = values.reshape(lead, 2, 2, 2, 2, 2, 32).swapaxes(1, 2)
        values = flip_order(values, 1, (y,) + device_bits)
        return values.swapaxes(0, 1).reshape(2, -1)

    stacks[0] = global_order(stacks[0], layers * 2)
    stacks[2] = global_order(stacks[2], layers * FF_GROUPS)
    summed = sum_everywhere(jnp.concatenate([s.reshape(-1) for s in stacks]))
    parts, at = [], 0
    for s in stacks:
        parts.append(summed[at : at + s.size].reshape(s.shape))
        at += s.size
    g_b_qv = lax.dynamic_index_in_dim(parts[0], y, axis=0, keepdims=False).reshape(b_qv.shape)
    g_b_in = lax.dynamic_index_in_dim(parts[2], y, axis=0, keepdims=False).reshape(b_in.shape)
    return (
        block_output,
        input_grad,
        placed[0],
        g_b_qv,
        placed[1],
        parts[1],
        placed[2],
        g_b_in,
        placed[3],
        parts[3],
        parts[4],
        parts[5],
    )


def as_sent(array):

    def short(part):
        return part.astype(jnp.bfloat16) if part.dtype == jnp.float32 else part

    return jax.tree.map(short, array)


def norm_rows(values, gain_row, shift_row):
    row_mean = jnp.mean(values, axis=-1, keepdims=True)
    centred = values - row_mean
    variance = jnp.mean(centred * centred, axis=-1, keepdims=True)
    return centred * lax.rsqrt(variance + 1e-06) * gain_row + shift_row


def gelu_exact(values):
    return jax.nn.gelu(values, approximate=False)


def block_mask(chosen_blocks, segment_rows):
    nblocks = chosen_blocks.shape[2]
    block_index = jnp.arange(nblocks)
    near_blocks = jnp.abs(block_index[:, None] - block_index[None, :]) <= 1
    edge_blocks = (
        (block_index[None, :] == 0)
        | (block_index[None, :] == nblocks - 1)
        | (block_index[:, None] == 0)
        | (block_index[:, None] == nblocks - 1)
    )
    picked_blocks = jnp.any(chosen_blocks[..., None] == block_index, axis=3)
    allowed = near_blocks | edge_blocks | picked_blocks
    block_rows = segment_rows.shape[1] // nblocks
    allowed = jnp.repeat(jnp.repeat(allowed, block_rows, axis=2), block_rows, axis=3)
    same_doc = segment_rows[:, :, None] == segment_rows[:, None, :]
    return allowed & same_doc[:, None]


def masked_scores(queries, key_rows, allowed, score_scale):
    scores = (
        jnp.einsum("qshd,kshd->shqk", queries, key_rows, preferred_element_type=jnp.float32)
        * score_scale
    )
    return jnp.where(allowed, scores, -1e30)


def shards(
    block_input,
    segment_ids,
    random_blocks,
    w_qkv,
    b_qv,
    w_out,
    b_out,
    w_in,
    b_in,
    w_down,
    b_down,
    ln_gain,
    ln_bias,
    cotangent,
):
    score_scale = HEAD_DIM ** (-0.5)
    shard_rows, seq_count, model_width = block_input.shape
    layers = w_qkv.shape[0]
    local_width = w_qkv.shape[3]
    local_heads = local_width // HEAD_DIM
    allowed = block_mask(random_blocks, segment_ids)
    saved_acts = []
    stream = block_input
    for layer_index in range(layers):
        w_proj = w_qkv[layer_index].astype(jnp.bfloat16)
        w_mix = w_out[layer_index].astype(jnp.bfloat16)
        rows_low = stream.astype(jnp.bfloat16)
        full_rows = lax.all_gather(rows_low, "tensor", axis=0, tiled=True)
        length = full_rows.shape[0]
        projected = jnp.einsum(
            "lsd,tdc->tlsc", full_rows, w_proj, preferred_element_type=jnp.float32
        )
        qkv_bias = jnp.stack(
            [b_qv[layer_index, 0], jnp.zeros_like(b_qv[layer_index, 0]), b_qv[layer_index, 1]]
        )
        qkv_low = (projected + qkv_bias[:, None, None, :]).astype(jnp.bfloat16)
        head_view = qkv_low.reshape(3, length, seq_count, local_heads, HEAD_DIM)
        scores = masked_scores(head_view[0], head_view[1], allowed, score_scale)
        row_top = jnp.max(scores, axis=-1, keepdims=True)
        log_total = row_top + jnp.log(jnp.sum(jnp.exp(scores - row_top), axis=-1, keepdims=True))
        probs_low = jnp.exp(scores - log_total).astype(jnp.bfloat16)
        context = jnp.einsum(
            "shqk,kshd->qshd", probs_low, head_view[2], preferred_element_type=jnp.float32
        )
        context = context.reshape(length, seq_count, local_width).astype(jnp.bfloat16)
        mixed = lax.psum_scatter(
            jnp.einsum("lsc,cd->lsd", context, w_mix, preferred_element_type=jnp.float32).astype(
                jnp.bfloat16
            ),
            "tensor",
            scatter_dimension=0,
            tiled=True,
        ).astype(jnp.float32)
        first_sum = stream + mixed + b_out[layer_index]
        hidden_rows = norm_rows(first_sum, ln_gain[layer_index, 0], ln_bias[layer_index, 0])
        hidden_low = hidden_rows.astype(jnp.bfloat16)
        up_weight = w_in[layer_index].astype(jnp.bfloat16)
        backward_weight = w_down[layer_index].astype(jnp.bfloat16)
        hidden_full = lax.all_gather(hidden_low, "tensor", axis=0, tiled=True)
        preactivation = (
            jnp.einsum("twn,nj->twj", hidden_full, up_weight, preferred_element_type=jnp.float32)
            + b_in[layer_index]
        )
        activation_reduced = gelu_exact(preactivation).astype(jnp.bfloat16)
        grown = lax.psum_scatter(
            jnp.einsum(
                "unj,jp->unp",
                activation_reduced,
                backward_weight,
                preferred_element_type=jnp.float32,
            ).astype(jnp.bfloat16),
            "tensor",
            scatter_dimension=0,
            tiled=True,
        ).astype(jnp.float32)
        second_sum = hidden_rows + grown + b_down[layer_index]
        stream = norm_rows(second_sum, ln_gain[layer_index, 1], ln_bias[layer_index, 1])
        keep_rows, keep_hidden = (full_rows, hidden_full)
        saved_acts.append(
            (
                keep_rows,
                head_view,
                log_total,
                context,
                first_sum,
                keep_hidden,
                preactivation,
                activation_reduced,
                second_sum,
                up_weight,
                backward_weight,
            )
        )
    upstream = cotangent
    grads_by_layer = [None] * layers
    for layer_index in reversed(range(layers)):
        (
            keep_rows,
            head_view,
            log_total,
            context,
            first_sum,
            keep_hidden,
            preactivation,
            activation_reduced,
            second_sum,
            up_weight,
            backward_weight,
        ) = saved_acts[layer_index]
        full_rows, hidden_full = (keep_rows, keep_hidden)
        length = full_rows.shape[0]
        w_proj = w_qkv[layer_index].astype(jnp.bfloat16)
        w_mix = w_out[layer_index].astype(jnp.bfloat16)
        _, pull_second = jax.vjp(
            norm_rows, second_sum, ln_gain[layer_index, 1], ln_bias[layer_index, 1]
        )
        d_second, d_gain_two, d_shift_two = pull_second(upstream)
        _, pull_gelu = jax.vjp(gelu_exact, preactivation)
        widened_full = lax.all_gather(d_second.astype(jnp.bfloat16), "tensor", axis=0, tiled=True)
        down_gradient = jnp.einsum(
            "uxc,uxw->cw", activation_reduced, widened_full, preferred_element_type=jnp.float32
        )
        activation_gradient = jnp.einsum(
            "mra,xa->mrx", widened_full, backward_weight, preferred_element_type=jnp.float32
        )
        preactivation_gradient_reduced = pull_gelu(activation_gradient)[0].astype(jnp.bfloat16)
        up_gradient = jnp.einsum(
            "kmx,kmt->xt",
            hidden_full,
            preactivation_gradient_reduced,
            preferred_element_type=jnp.float32,
        )
        g_up_bias = jnp.sum(preactivation_gradient_reduced.astype(jnp.float32), axis=(0, 1))
        d_hidden = d_second + lax.psum_scatter(
            jnp.einsum(
                "hmp,tp->hmt",
                preactivation_gradient_reduced,
                up_weight,
                preferred_element_type=jnp.float32,
            ).astype(jnp.bfloat16),
            "tensor",
            scatter_dimension=0,
            tiled=True,
        ).astype(jnp.float32)
        _, pull_first = jax.vjp(
            norm_rows, first_sum, ln_gain[layer_index, 0], ln_bias[layer_index, 0]
        )
        d_first, d_gain_one, d_shift_one = pull_first(d_hidden)
        full_mixed = lax.all_gather(d_first.astype(jnp.bfloat16), "tensor", axis=0, tiled=True)
        g_out = jnp.einsum("lsc,lsd->cd", context, full_mixed, preferred_element_type=jnp.float32)
        d_context = jnp.einsum(
            "lsd,cd->lsc", full_mixed, w_mix, preferred_element_type=jnp.float32
        ).astype(jnp.bfloat16)
        d_context = d_context.reshape(length, seq_count, local_heads, HEAD_DIM)
        queries, key_rows, value_rows = (head_view[0], head_view[1], head_view[2])
        scores = masked_scores(queries, key_rows, allowed, score_scale)
        attn_probs = jnp.exp(scores - log_total)
        probs_low = attn_probs.astype(jnp.bfloat16)
        d_probs = jnp.einsum(
            "qshd,kshd->shqk", d_context, value_rows, preferred_element_type=jnp.float32
        )
        d_scores = attn_probs * (d_probs - jnp.sum(d_probs * attn_probs, axis=-1, keepdims=True))
        d_scores = d_scores.astype(jnp.bfloat16)
        d_query = (
            jnp.einsum("shqk,kshd->qshd", d_scores, key_rows, preferred_element_type=jnp.float32)
            * score_scale
        )
        d_key = (
            jnp.einsum("shqk,qshd->kshd", d_scores, queries, preferred_element_type=jnp.float32)
            * score_scale
        )
        d_value = jnp.einsum(
            "shqk,qshd->kshd", probs_low, d_context, preferred_element_type=jnp.float32
        )
        d_qkv = (
            jnp.stack([d_query, d_key, d_value])
            .reshape(3, length, seq_count, local_width)
            .astype(jnp.bfloat16)
        )
        g_proj = jnp.einsum("lsd,tlsc->tdc", full_rows, d_qkv, preferred_element_type=jnp.float32)
        qkv_sums = jnp.sum(d_qkv.astype(jnp.float32), axis=(1, 2))
        g_bias = jnp.stack([qkv_sums[0], qkv_sums[2]])
        upstream = d_first + lax.psum_scatter(
            jnp.einsum("tlsc,tdc->lsd", d_qkv, w_proj, preferred_element_type=jnp.float32).astype(
                jnp.bfloat16
            ),
            "tensor",
            scatter_dimension=0,
            tiled=True,
        ).astype(jnp.float32)
        weight_grads = (g_proj, g_bias, g_out, up_gradient, g_up_bias, down_gradient)
        small_grads = (
            jnp.sum(d_first, axis=(0, 1)),
            jnp.sum(d_second, axis=(0, 1)),
            jnp.stack([d_gain_one, d_gain_two]),
            jnp.stack([d_shift_one, d_shift_two]),
        )
        grads_by_layer[layer_index] = (weight_grads, small_grads)
    weight_stack = tuple(
        (
            jnp.stack([grads_by_layer[layer_index][0][member] for layer_index in range(layers)])
            for member in range(6)
        )
    )
    small_stack = tuple(
        (
            jnp.stack([grads_by_layer[layer_index][1][member] for layer_index in range(layers)])
            for member in range(4)
        )
    )
    weight_stack = jax.tree.map(
        lambda part: part.astype(jnp.float32), lax.psum(as_sent(weight_stack), "dp")
    )
    small_stack = lax.psum(small_stack, ("dp", "tensor"))
    return (
        stream,
        upstream,
        weight_stack[0],
        weight_stack[1],
        weight_stack[2],
        small_stack[0],
        weight_stack[3],
        weight_stack[4],
        weight_stack[5],
        small_stack[1],
        small_stack[2],
        small_stack[3],
    )


def solution(mesh):
    by_sequence = mesh.shape["tensor"] == 2 and mesh.shape["dp"] == 16
    return jax.shard_map(
        sequence_shards if by_sequence else shards,
        mesh=mesh,
        in_specs=(
            P("tensor", "dp", None),
            P("dp", None),
            P("dp", "tensor", None, None),
            P(None, None, None, "tensor"),
            P(None, None, "tensor"),
            P(None, "tensor", None),
            P(),
            P(None, None, "tensor"),
            P(None, "tensor"),
            P(None, "tensor", None),
            P(),
            P(),
            P(),
            P("tensor", "dp", None),
        ),
        out_specs=(
            P("tensor", "dp", None),
            P("tensor", "dp", None),
            P(None, None, None, "tensor"),
            P(None, None, "tensor"),
            P(None, "tensor", None),
            P(),
            P(None, None, "tensor"),
            P(None, "tensor"),
            P(None, "tensor", None),
            P(),
            P(),
            P(),
        ),
        check_vma=False,
    )
```

```python
import functools

import jax
import jax.numpy as jnp
from jax import lax
from jax.experimental import pallas as pl
from jax.experimental.pallas import tpu as pltpu
from jax.sharding import PartitionSpec as P

HEAD_DIM = 64
BIG = -1e30
BF16 = jnp.bfloat16
F32 = jnp.float32
MESH = pl.DeviceIdType.MESH
VMEM_LIMIT = 56 << 20

FLIP_Y, FLIP_C, FLIP_X, FLIP_Z0, FLIP_Z1 = 1, 2, 4, 8, 16
SWAP = FLIP_Y + FLIP_C
DEVICES = 32

GROUPS = 12
OUT_GROUP = 3
FF_GROUPS = 4


def in_group(s):
    return 4 + 2 * s


def down_group(s):
    return 5 + 2 * s


def flip(values, bit):
    pairs = [(i, i ^ bit) for i in range(DEVICES)]
    return jax.tree.map(lambda v: lax.ppermute(v, ("dp", "tensor"), pairs), values)


def nt(a, b):
    return lax.dot_general(a, b, (((1,), (1,)), ((), ())), preferred_element_type=F32)


def nn(a, b):
    return lax.dot_general(a, b, (((1,), (0,)), ((), ())), preferred_element_type=F32)


def tn(a, b):
    return lax.dot_general(a, b, (((0,), (0,)), ((), ())), preferred_element_type=F32)


def block_of(ref):
    width = ref.shape[-1]
    return ref[...].reshape(-1, width)


def place_kernel(turned, code_ref, g_ref, o_ref, *scratch):
    code = code_ref[0]
    for j in range(16):
        start = pl.multiple_of((j ^ code) * 32, 32)
        block = g_ref[0, pl.ds(start, 32), :].astype(F32)
        if turned:
            scratch[0][j * 32 : (j + 1) * 32, :] = block
        else:
            o_ref[0, j * 32 : (j + 1) * 32, :] = block
    if turned:
        o_ref[...] = scratch[0][...].T.reshape(o_ref.shape)


def place(sums, shape, block, index, turned, count, group, code):
    width = sums.shape[-1]
    return pl.pallas_call(
        functools.partial(place_kernel, turned),
        out_shape=jax.ShapeDtypeStruct(shape, F32),
        grid_spec=pltpu.PrefetchScalarGridSpec(
            num_scalar_prefetch=1,
            grid=(shape[0], count),
            in_specs=[pl.BlockSpec((1, 512, width), lambda l, i, code: (group(l, i), 0, 0))],
            out_specs=pl.BlockSpec(block, lambda l, i, code: index(l, i)),
            scratch_shapes=[pltpu.VMEM((512, width), F32)] if turned else [],
        ),
        compiler_params=pltpu.CompilerParams(vmem_limit_bytes=VMEM_LIMIT),
        cost_estimate=pl.CostEstimate(
            flops=0, bytes_accessed=shape[0] * count * 512 * width * 6, transcendentals=0
        ),
        name="place",
    )(code, sums)


def partner(bits):
    dp, y = lax.axis_index("dp"), lax.axis_index("tensor")
    other = dp
    for step in (1, 2, 4, 8):
        if bits & (2 * step):
            other = other + step * (1 - 2 * ((dp // step) % 2))
    return (other, 1 - y if bits & FLIP_Y else y)


def greet(bits):
    barrier = pltpu.get_barrier_semaphore()
    for bit in bits:
        pl.semaphore_signal(barrier, inc=1, device_id=partner(bit), device_id_type=MESH)
    pl.semaphore_wait(barrier, len(bits))


def add_rows(into, other, rows):
    def step(i, _):
        at = pl.ds(pl.multiple_of(i * 32, 32), 32)
        into[at, :] = (into[at, :].astype(F32) + other[at, :].astype(F32)).astype(BF16)
        return 0

    lax.fori_loop(0, rows // 32, step, 0)


SLOTS = 8
LAST_TICK = 10


class Reduction:
    def __init__(self, grads, sums, count, bufs, sems):
        self.grads, self.sums, self.count = grads, sums, count
        self.y_buf, self.x_buf, self.z0_buf, self.z1_buf, self.all_buf, self.keep_buf = bufs
        self.send_sem, self.recv_sem, self.core_send, self.core_recv = sems[:4]
        self.keep_sem, self.out_sem, self.in_free, self.out_free = sems[4:]

    def copy(self, step, i):
        slot = lax.rem(i, SLOTS)
        ys, al = self.y_buf.at[slot], self.all_buf.at[slot]
        bit, source, target = (
            (FLIP_Y, self.grads.at[i, pl.ds(256, 256)], ys),
            (FLIP_X, ys.at[pl.ds(128, 128)], self.x_buf.at[slot]),
            (FLIP_Z0, ys.at[pl.ds(64, 64)], self.z0_buf.at[slot]),
            (FLIP_Z1, ys.at[pl.ds(32, 32)], self.z1_buf.at[slot]),
            (FLIP_Z1, al.at[pl.ds(0, 32)], al.at[pl.ds(32, 32)]),
            (FLIP_Z0, al.at[pl.ds(0, 64)], al.at[pl.ds(64, 64)]),
            (FLIP_X, al.at[pl.ds(0, 128)], al.at[pl.ds(128, 128)]),
            (FLIP_C, al, self.sums.at[i, pl.ds(256, 256)]),
        )[step]
        return pltpu.make_async_remote_copy(
            src_ref=source,
            dst_ref=target,
            send_sem=self.send_sem.at[step, slot] if step < 7 else self.core_send.at[i],
            recv_sem=self.recv_sem.at[step, slot] if step < 7 else self.core_recv.at[i],
            device_id=partner(bit),
            device_id_type=MESH,
        )

    def keep(self, i):
        slot = lax.rem(i, 2)
        return pltpu.make_async_copy(
            self.grads.at[i, pl.ds(0, 256)], self.keep_buf.at[slot], self.keep_sem.at[slot]
        )

    def out(self, i):
        slot = lax.rem(i, SLOTS)
        return pltpu.make_async_copy(
            self.all_buf.at[slot], self.sums.at[i, pl.ds(0, 256)], self.out_sem.at[slot]
        )

    def take(self, sem, i):
        @pl.when(i >= SLOTS)
        def _():
            pl.semaphore_wait(sem, 1)

    def give(self, sem, bit, i):
        @pl.when(i + SLOTS < self.count)
        def _():
            pl.semaphore_signal(sem, inc=1, device_id=partner(bit), device_id_type=MESH)

    def tick(self, t):
        def at(offset, body):
            i = t - offset
            pl.when((i >= 0) & (i < self.count))(lambda: body(i, lax.rem(i, SLOTS)))

        def set_out(i, slot):
            self.take(self.in_free.at[0], i)
            self.copy(0, i).start()
            self.keep(i).start()

        def finish(i, slot):
            self.copy(7, i).wait()
            self.out(i).wait()
            for n, bit in enumerate((FLIP_X, FLIP_Z0, FLIP_Z1)):
                self.give(self.out_free.at[n], bit, i)

        def to_core(i, slot):
            self.copy(6, i).wait()
            self.copy(7, i).start()
            self.out(i).start()

        def back_x(i, slot):
            self.copy(5, i).wait()
            self.take(self.out_free.at[0], i)
            self.copy(6, i).start()

        def back_z0(i, slot):
            self.copy(4, i).wait()
            self.take(self.out_free.at[1], i)
            self.copy(5, i).start()

        def back_z1(i, slot):
            self.copy(3, i).wait()
            add_rows(self.y_buf.at[slot], self.z1_buf.at[slot], 32)
            self.all_buf[slot, 0:32, :] = self.y_buf[slot, 0:32, :]
            for n, bit in enumerate((FLIP_Y, FLIP_X, FLIP_Z0, FLIP_Z1)):
                self.give(self.in_free.at[n], bit, i)
            self.take(self.out_free.at[2], i)
            self.copy(4, i).start()

        def on_z1(i, slot):
            self.copy(2, i).wait()
            add_rows(self.y_buf.at[slot], self.z0_buf.at[slot], 64)
            self.take(self.in_free.at[3], i)
            self.copy(3, i).start()

        def on_z0(i, slot):
            self.copy(1, i).wait()
            add_rows(self.y_buf.at[slot], self.x_buf.at[slot], 128)
            self.take(self.in_free.at[2], i)
            self.copy(2, i).start()

        def on_x(i, slot):
            self.copy(0, i).wait()
            self.keep(i).wait()
            add_rows(self.y_buf.at[slot], self.keep_buf.at[lax.rem(i, 2)], 256)
            self.take(self.in_free.at[1], i)
            self.copy(1, i).start()

        at(0, set_out)
        at(10, finish)
        at(9, to_core)
        at(7, back_x)
        at(6, back_z0)
        at(5, back_z1)
        at(4, on_z1)
        at(1, on_x)
        at(3, on_z0)


def stream(count, feeds, body):
    for copy in feeds(0, 0):
        copy.start()

    def step(i, _):
        slot = lax.rem(i, 2)

        @pl.when(i + 1 < count)
        def _():
            for copy in feeds(i + 1, 1 - slot):
                copy.start()

        for copy in feeds(i, slot):
            copy.wait()
        body(i, slot)
        return 0

    lax.fori_loop(0, count, step, 0)


def norm(r, gain, shift):
    centred = r - jnp.mean(r, axis=-1, keepdims=True)
    rstd = lax.rsqrt(jnp.mean(centred * centred, axis=-1, keepdims=True) + 1e-06)
    return centred * rstd * gain + shift


def norm_back(dy, r, gain):
    centred = r - jnp.mean(r, axis=-1, keepdims=True)
    rstd = lax.rsqrt(jnp.mean(centred * centred, axis=-1, keepdims=True) + 1e-06)
    unit = centred * rstd
    dunit = dy * gain
    dr = rstd * (
        dunit
        - jnp.mean(dunit, axis=-1, keepdims=True)
        - unit * jnp.mean(dunit * unit, axis=-1, keepdims=True)
    )
    return dr, dy * unit


def gelu_and_slope(u):
    cdf = 0.5 * (1.0 + lax.erf(u * (0.5**0.5)))
    pdf = jnp.exp(-0.5 * u * u) * 0.3989422804014327
    return u * cdf, cdf + u * pdf


TILE = 64


def row_tiles(rows, body):
    def step(i, _):
        body(pl.ds(pl.multiple_of(i * TILE, TILE), TILE))
        return 0

    lax.fori_loop(0, rows // TILE, step, 0)


def pair_lanes(values, e):
    lane = lax.broadcasted_iota(jnp.int32, values.shape, 1)
    return jnp.where(lane // HEAD_DIM == e, values, jnp.zeros_like(values))


def spread_mask(block_part, document_part):
    blocks, lanes = block_part.shape
    each = document_part.shape[0] // blocks
    part = jnp.broadcast_to(block_part[:, None, :], (blocks, each, lanes)).reshape(blocks * each, lanes)
    return (part + document_part).astype(BF16)


def attend_pair(query, keys, values, hot, mask):
    scale = HEAD_DIM**-0.5
    rows = query.shape[0]
    query = query * jnp.asarray(scale, BF16)
    values_t = values.T
    tile = rows // 2
    contexts, lses = [], ([], [])
    for part in range(2):
        at = slice(part * tile, (part + 1) * tile)
        heads = []
        for e in range(2):
            right = jnp.concatenate([pair_lanes(query[at], e), hot[at]], axis=1)
            left = jnp.concatenate([keys, mask[e]], axis=1)
            s = nt(left, right)
            top = jnp.max(s, axis=0, keepdims=True)
            p = jnp.exp(s - top)
            total = jnp.sum(p, axis=0, keepdims=True)
            c = nn(values_t[e * HEAD_DIM : (e + 1) * HEAD_DIM, :], p.astype(BF16))
            heads.append(c * (1.0 / total))
            lses[e].append(top + jnp.log(total))
        contexts.append(jnp.concatenate(heads, axis=0).T)
    return jnp.concatenate(contexts, axis=0), [jnp.concatenate(parts, axis=1) for parts in lses]


def attend_back_pair(query, keys, values, hot, mask, ctx, lse, dctx):
    scale = HEAD_DIM**-0.5
    rows = query.shape[0]
    query = query * jnp.asarray(scale, BF16)
    keys_t = keys.T
    delta_t = (dctx.astype(F32) * ctx.astype(F32)).T
    tile = rows // 2
    dk, dv, dq = 0.0, 0.0, []
    for part in range(2):
        at = slice(part * tile, (part + 1) * tile)
        heads = []
        for e in range(2):
            lanes = slice(e * HEAD_DIM, (e + 1) * HEAD_DIM)
            query_e = pair_lanes(query[at], e)
            dctx_e = pair_lanes(dctx[at], e)
            right = jnp.concatenate([query_e, hot[at]], axis=1)
            left = jnp.concatenate([keys, mask[e]], axis=1)
            p = jnp.exp(nt(left, right) - lse[e : e + 1, at])
            dp = nt(values, dctx_e)
            delta = jnp.sum(delta_t[lanes, at], axis=0, keepdims=True)
            ds = (p * (dp - delta)).astype(BF16)
            dk = dk + nn(ds, query_e)
            dv = dv + nn(p.astype(BF16), dctx_e)
            heads.append(nn(keys_t[lanes, :], ds) * scale)
        dq.append(jnp.concatenate(heads, axis=0).T)
    return jnp.concatenate(dq, axis=0), dk, dv


class Spread:
    def __init__(self, weights, pairs, send_sem, recv_sem):
        self.weights, self.pairs, self.send_sem, self.recv_sem = weights, pairs, send_sem, recv_sem

    def copy(self, step, t):
        w = self.weights
        even, odd = 2 * t, 2 * t + 1
        bit, source, target = (
            (FLIP_Y, w.at[0, even, 0, pl.ds(0, 64)], w.at[0, even, 1, pl.ds(0, 64)]),
            (FLIP_Y, w.at[0, odd, 0, pl.ds(0, 64)], w.at[0, odd, 1, pl.ds(0, 64)]),
            (FLIP_X, w.at[0, even, 1, pl.ds(0, 64)], w.at[0, even, 1, pl.ds(128, 64)]),
            (FLIP_Z0, w.at[0, odd, 1, pl.ds(0, 64)], w.at[0, odd, 1, pl.ds(64, 64)]),
            (FLIP_Z0, w.at[0, even, 1, pl.ds(0, 64)], w.at[0, even, 1, pl.ds(64, 64)]),
            (FLIP_Z0, w.at[0, even, 1, pl.ds(128, 64)], w.at[0, even, 1, pl.ds(192, 64)]),
            (FLIP_X, w.at[0, odd, 1, pl.ds(0, 128)], w.at[0, odd, 1, pl.ds(128, 128)]),
            (FLIP_C, w.at[0, even, 1], w.at[1, even, 1]),
            (FLIP_C, w.at[0, odd, 1], w.at[1, odd, 1]),
        )[step]
        return pltpu.make_async_remote_copy(
            src_ref=source,
            dst_ref=target,
            send_sem=self.send_sem.at[step, t],
            recv_sem=self.recv_sem.at[step, t],
            device_id=partner(bit),
            device_id_type=MESH,
        )

    def tick(self, t):
        def at(offset, waits, starts):
            i = t - offset

            @pl.when((i >= 0) & (i < self.pairs))
            def _():
                for step in waits:
                    self.copy(step, i).wait()
                for step in starts:
                    self.copy(step, i).start()

        at(0, (), (0, 1))
        at(5, (7, 8), ())
        at(1, (0, 1), (2, 3))
        at(2, (2, 3), (4, 5, 6))
        at(4, (4, 5, 6), (7, 8))


PER_LAYER = 14
DEPTH = 3


def forward_kernel(layers, *refs):
    refs = list(refs)
    x_ref, up_ref, wq_ref, wo_ref, wi_ref, wd_ref = refs[:6]
    hot_buf, mask_ref, key_ref, bq_ref, bi_ref, vec_ref = refs[6:12]
    w_ref, up_out, x_out = refs[12:15]
    saved = [refs[15 + PER_LAYER * l : 15 + PER_LAYER * (l + 1)] for l in range(layers)]
    (
        x, acc, r_buf, low, xb, qkv, kv_sib, ctx, lse, hl, g_all, slope_all,
        col_buf, row_buf, turn_buf, made_buf, wa_buf, wb_buf,
        feed_sem, load_sem, col_sem, row_sem, made_sem, store_sem, block_sem,
        core_send, core_recv, kv_send, kv_recv, g_send, g_recv, spread_send, spread_recv,
    ) = refs[15 + PER_LAYER * layers :]
    rows, width = acc.shape
    dp, y = lax.axis_index("dp"), lax.axis_index("tensor")
    core = dp % 2
    stays = core == y
    spread = Spread(w_ref, layers * GROUPS // 2, spread_send, spread_recv)
    greet((FLIP_Y, FLIP_X, FLIP_Z0, FLIP_C, SWAP))

    def feed(n, slot, source, target):
        return pltpu.make_async_copy(source, target, feed_sem.at[n, slot])

    def load(n, source, target):
        return pltpu.make_async_copy(source, target, load_sem.at[n])

    def store(n, source, target):
        return pltpu.make_async_copy(source, target, store_sem.at[n])

    def exchange(n, source, target, bits=FLIP_C):
        return pltpu.make_async_remote_copy(
            src_ref=source, dst_ref=target, send_sem=core_send.at[n], recv_sem=core_recv.at[n],
            device_id=partner(bits), device_id_type=MESH,
        )

    def columns(ref, i, size):
        return ref.at[:, pl.ds(pl.multiple_of(i * size, size), size)]

    def swap(n, source, target, begin):
        here = store(n, source, target)
        there = exchange(n, source, target, SWAP)

        @pl.when(stays)
        def _():
            here.start() if begin else here.wait()

        @pl.when(jnp.logical_not(stays))
        def _():
            there.start() if begin else there.wait()

    items = []
    for l in range(layers):
        items += [(True, wq_ref.at[l, t], l * GROUPS + t) for t in range(3)]
        items += [(False, wo_ref.at[l], l * GROUPS + OUT_GROUP)]
        for n in range(FF_GROUPS):
            items += [(True, wi_ref.at[l, :, pl.ds(n * 512, 512)], l * GROUPS + in_group(n))]
            items += [(False, wd_ref.at[l, pl.ds(n * 512, 512)], l * GROUPS + down_group(n))]
    fetches, counts, ahead = [], [0, 0], [[], []]
    for m, (turned, source, group) in enumerate(items):
        slot = counts[turned] % DEPTH
        buf, sem = (col_buf, col_sem) if turned else (row_buf, row_sem)
        fetches.append((pltpu.make_async_copy(source, buf.at[slot], sem.at[slot]), slot))
        ahead[turned].append(m)
        counts[turned] += 1
    bits = [(dp // step) % 2 for step in (1, 2, 4, 8)]
    made = {}

    def convert(m):
        turned, _, group = items[m]
        copy, slot = fetches[m]
        copy.wait()
        if turned:

            def turn(i, _):
                turn_buf[pl.ds(pl.multiple_of(i * 128, 128), 128), :] = col_buf[
                    slot, :, pl.ds(pl.multiple_of(i * 128, 128), 128)
                ].T
                return 0

            lax.fori_loop(0, 4, turn, 0)
        if m >= 2:
            made[m - 2].wait()

        def block(j, _):
            where = 0
            for bit, weight in zip(bits, (8, 4, 2, 1)):
                own = (j // weight) % 2
                where = where + weight * (own + bit - 2 * own * bit)
            at = pl.ds(pl.multiple_of(where * 32, 32), 32)
            rows_32 = turn_buf[at, :] if turned else row_buf[slot, at, :]
            made_buf[m % 2, pl.ds(pl.multiple_of(j * 32, 32), 32), :] = rows_32.astype(BF16)
            return 0

        lax.fori_loop(0, 16, block, 0)
        later = [n for n in ahead[turned] if n > m]
        if len(later) >= DEPTH:
            fetches[later[DEPTH - 1]][0].start()
        parts = [
            pltpu.make_async_copy(
                made_buf.at[m % 2, pl.ds(a * 256, 256)], w_ref.at[a, group, 0], made_sem.at[m % 2, a]
            )
            for a in range(2)
        ]

        class Both:
            def wait(self):
                for part in parts:
                    part.wait()

        for part in parts:
            part.start()
        made[m] = Both()

    load_x = load(0, x_ref.at[:, 0], x)
    load_x.start()
    load_up = load(1, up_ref.at[:, 0], acc)
    load_up.start()
    for kind in range(2):
        for m in ahead[kind][:DEPTH]:
            fetches[m][0].start()
    load_x.wait()

    def narrow_x(at):
        low[at, :] = x[at, :].astype(BF16)

    row_tiles(rows, narrow_x)
    swap(0, low, xb, True)
    load_up.wait()

    def narrow_up(at):
        hl[at, :] = acc[at, :].astype(BF16)

    row_tiles(rows, narrow_up)
    swap(1, hl, up_out, True)

    for m in range(len(items)):
        convert(m)
        if m % 4 == 3:
            spread.tick(m // 4)
    for m in range(len(items) - 2, len(items)):
        made[m].wait()
    swap(0, low, xb, False)
    swap(1, hl, up_out, False)

    def widen(at):
        x[at, :] = xb[at, :].astype(F32)

    row_tiles(rows, widen)

    pairs = width // 128
    for l in range(layers):
        (
            qkv_out, sib_out, ctx_out, ctx_sib_out, lse_out, r1_out, r2_out, hl_out, hl_sib_out,
            g_out, g_sib_out, slope_out, xb_out, xb_sib_out,
        ) = saved[l]
        first = l * GROUPS
        clock = 6 + 6 * l
        xb_store = store(0, xb, xb_out)
        xb_store.start()
        xb_copy = exchange(2 + 3 * l, xb, xb_sib_out)
        xb_copy.start()

        def give_kv(n, a):
            at = pl.ds(pl.multiple_of(a * 512, 512), 512)
            return pltpu.make_async_remote_copy(
                src_ref=qkv.at[1 + n, :, at], dst_ref=kv_sib.at[n, :, at],
                send_sem=kv_send.at[n, a], recv_sem=kv_recv.at[n, a],
                device_id=partner(FLIP_C), device_id_type=MESH,
            )

        def which(i):
            n = lax.div(i, 2)
            return 1 - n + 3 * lax.div(n, 2), lax.rem(i, 2)

        def qkv_feeds(i, slot):
            t, a = which(i)
            return (feed(0, slot, w_ref.at[a, first + t], wa_buf.at[slot]),)

        def qkv_body(i, slot):
            t, a = which(i)
            at = pl.ds(pl.multiple_of(a * 512, 512), 512)
            qkv[t, :, at] = (nt(xb[...], block_of(wa_buf.at[slot])) + bq_ref[l, t, a]).astype(BF16)
            pl.when(t > 0)(lambda: give_kv(t - 1, a).start())
            pl.when(i == 2)(lambda: spread.tick(clock))

        stream(6, qkv_feeds, qkv_body)
        qkv_store = store(1, qkv, qkv_out)
        qkv_store.start()
        for n in range(2):
            for a in range(2):
                give_kv(n, a).wait()
        sib_store = store(2, kv_sib, sib_out)
        sib_store.start()

        def pair_body(p, _):
            far = lax.rem(p + pairs // 2, pairs)
            here = pl.ds(pl.multiple_of(p * 128, 128), 128)
            there = pl.ds(pl.multiple_of(far * 128, 128), 128)
            mask = [spread_mask(mask_ref[2 * p + e], key_ref[...]) for e in range(2)]
            keys = jnp.concatenate([qkv[1, :, here], kv_sib[0, :, there]], axis=0)
            values = jnp.concatenate([qkv[2, :, here], kv_sib[1, :, there]], axis=0)
            context, parts = attend_pair(qkv[0, :, here], keys, values, hot_buf[...], mask)
            ctx[:, here] = context.astype(BF16)
            for e in range(2):
                lse[p, e : e + 1, :] = parts[e]
            pl.when(lax.rem(p, 5) == 2)(lambda: spread.tick(clock + 1 + lax.div(p, 5)))
            return 0

        lax.fori_loop(0, pairs, pair_body, 0)
        ctx_store = store(3, ctx, ctx_out)
        ctx_store.start()
        lse_store = store(4, lse, lse_out)
        lse_store.start()
        ctx_copy = exchange(3 + 3 * l, ctx.at[:, pl.ds(512, 512)], ctx_sib_out)
        ctx_copy.start()

        def out_feeds(i, slot):
            return (feed(0, slot, w_ref.at[i, first + OUT_GROUP], wa_buf.at[slot]),)

        def out_body(i, slot):
            part = nn(ctx[:, pl.ds(pl.multiple_of(i * 512, 512), 512)], block_of(wa_buf.at[slot]))

            @pl.when(i == 0)
            def _():
                acc[...] = part

            @pl.when(i == 1)
            def _():
                acc[...] += part

        stream(2, out_feeds, out_body)
        sib_store.wait()

        def first_norm(at):
            r1 = x[at, :] + acc[at, :] + vec_ref[l, 0:1, :]
            r_buf[at, :] = r1
            h = norm(r1, vec_ref[l, 1:2, :], vec_ref[l, 2:3, :])
            hl[at, :] = h.astype(BF16)
            acc[at, :] = h + vec_ref[l, 3:4, :]

        row_tiles(rows, first_norm)
        r1_store = store(5, r_buf, r1_out)
        r1_store.start()
        hl_store = store(6, hl, hl_out)
        hl_store.start()
        hl_copy = exchange(4 + 3 * l, hl, hl_sib_out)
        hl_copy.start()

        def place_of(i):
            return 1 - lax.rem(i, 2), lax.div(i, 2)

        def ff_feeds(i, slot):
            a, n = place_of(i)
            return (
                feed(0, slot, w_ref.at[a, first + in_group(n)], wa_buf.at[slot]),
                feed(2, slot, w_ref.at[a, first + down_group(n)], wb_buf.at[slot]),
            )

        def g_store(j):
            return pltpu.make_async_copy(g_all.at[j], columns(g_out, j, 512), block_sem.at[0, j])

        def slope_store(j):
            return pltpu.make_async_copy(slope_all.at[j], columns(slope_out, j, 512), block_sem.at[1, j])

        def g_copy(n):
            return pltpu.make_async_remote_copy(
                src_ref=g_all.at[FF_GROUPS + n], dst_ref=columns(g_sib_out, n, 512),
                send_sem=g_send.at[l, n], recv_sem=g_recv.at[l, n],
                device_id=partner(FLIP_C), device_id_type=MESH,
            )

        def ff_body(i, slot):
            a, n = place_of(i)
            j = a * FF_GROUPS + n
            u = nt(hl[...], block_of(wa_buf.at[slot])) + bi_ref[l, a, n]
            g, slope = gelu_and_slope(u)
            g = g.astype(BF16)
            g_all[j] = g
            slope_all[j] = slope.astype(BF16)
            g_store(j).start()
            slope_store(j).start()
            pl.when(a == 1)(lambda: g_copy(n).start())
            acc[...] += nn(g, block_of(wb_buf.at[slot]))
            pl.when(lax.rem(i, 3) == 1)(lambda: spread.tick(clock + 3 + lax.div(i, 3)))

        stream(2 * FF_GROUPS, ff_feeds, ff_body)
        r1_store.wait()
        xb_store.wait()
        xb_copy.wait()

        def second_norm(at):
            r2 = acc[at, :]
            r_buf[at, :] = r2
            x2 = norm(r2, vec_ref[l, 4:5, :], vec_ref[l, 5:6, :])
            x[at, :] = x2
            xb[at, :] = x2.astype(BF16)

        row_tiles(rows, second_norm)
        r2_store = store(5, r_buf, r2_out)
        r2_store.start()
        if l == layers - 1:
            x_store = store(10, xb, x_out)
            x_store.start()

        def settle(j, _):
            g_store(j).wait()
            slope_store(j).wait()
            return 0

        lax.fori_loop(0, 2 * FF_GROUPS, settle, 0)

        def settle_sent(n, _):
            g_copy(n).wait()
            return 0

        lax.fori_loop(0, FF_GROUPS, settle_sent, 0)
        for copy in (qkv_store, ctx_store, lse_store, ctx_copy, hl_store, hl_copy, r2_store):
            copy.wait()
    x_store.wait()


def forward(block_input, cotangent, w_qkv, w_out, w_in, w_down, hot, mask, mask_rows, bias_qkv, bias_in, vectors):
    rows, _, width = block_input.shape
    layers = w_qkv.shape[0]
    total = layers * GROUPS
    anywhere = pl.BlockSpec(memory_space=pl.ANY)
    in_vmem = pl.BlockSpec(memory_space=pltpu.VMEM)
    low = lambda *shape: pltpu.VMEM(shape, BF16)
    full = lambda *shape: pltpu.VMEM(shape, F32)
    dma = lambda *shape: pltpu.SemaphoreType.DMA(shape)
    low_out = lambda *shape: jax.ShapeDtypeStruct(shape, BF16)
    full_out = lambda *shape: jax.ShapeDtypeStruct(shape, F32)
    layer_out = (
        low_out(3, rows, width),
        low_out(2, rows, width),
        low_out(rows, width),
        low_out(rows, width // 2),
        full_out(width // 128, 2, rows),
        full_out(rows, width),
        full_out(rows, width),
        low_out(rows, width),
        low_out(rows, width),
        low_out(rows, 4 * width),
        low_out(rows, 2 * width),
        low_out(rows, 4 * width),
        low_out(rows, width),
        low_out(rows, width),
    )
    outs = pl.pallas_call(
        functools.partial(forward_kernel, layers),
        out_shape=(low_out(2, total, 2, 256, width), low_out(rows, width), low_out(rows, width)) + layer_out * layers,
        in_specs=[anywhere] * 6 + [in_vmem] * 6,
        out_specs=(anywhere,) * (3 + PER_LAYER * layers),
        scratch_shapes=[
            full(rows, width),
            full(rows, width),
            full(rows, width),
            low(rows, width),
            low(rows, width),
            low(3, rows, width),
            low(2, rows, width),
            low(rows, width),
            full(width // 128, 2, rows),
            low(rows, width),
            low(2 * FF_GROUPS, rows, 512),
            low(2 * FF_GROUPS, rows, 512),
            full(DEPTH, width, 512),
            full(DEPTH, 512, width),
            full(512, width),
            low(2, 512, width),
            low(2, 2, 256, width),
            low(2, 2, 256, width),
            dma(3, 2),
            dma(3),
            dma(DEPTH),
            dma(DEPTH),
            dma(2, 2),
            dma(11),
            dma(2, 2 * FF_GROUPS),
            dma(11),
            dma(11),
            dma(2, 2),
            dma(2, 2),
            dma(layers, FF_GROUPS),
            dma(layers, FF_GROUPS),
            dma(9, total // 2),
            dma(9, total // 2),
        ],
        compiler_params=pltpu.CompilerParams(collective_id=0, has_side_effects=True, vmem_limit_bytes=60 << 20),
        cost_estimate=pl.CostEstimate(flops=30 << 30, bytes_accessed=300 << 20, transcendentals=1 << 24),
        name="forward",
    )(block_input, cotangent, w_qkv, w_out, w_in, w_down, hot, mask, mask_rows, bias_qkv, bias_in, vectors)
    saved = [outs[3 + PER_LAYER * l : 3 + PER_LAYER * (l + 1)] for l in range(layers)]
    return outs[0], outs[1], outs[2], saved


def backward_kernel(layers, *refs):
    refs = list(refs)
    up_ref, x_ref, w_ref, hot_buf, mask_ref, key_ref, vec_ref = refs[:7]
    saved = [refs[7 + PER_LAYER * l : 7 + PER_LAYER * (l + 1)] for l in range(layers)]
    at_ref = 7 + PER_LAYER * layers
    grads, sums, dx_out, x_out, dbi_ref, qkv_sums_ref, small_ref = refs[at_ref : at_ref + 7]
    (
        acc, dr1, dm, dm_sib, da, da_sib, du, du_sib, dctx, dqkv, d_sib, kv_out, kv_far,
        wa_buf, wb_buf, r_buf, slope_buf, left_buf, left_sib_buf, right_buf, right_sib_buf,
        pair_buf, lse_buf, unit_buf,
        y_buf, x_buf, z0_buf, z1_buf, all_buf, keep_buf,
        feed_sem, load_sem, store_sem, swap_sem, core_send, core_recv, du_send, du_recv,
        send_sem, recv_sem, sum_send, sum_recv, keep_sem, out_sem, in_free, out_free,
    ) = refs[at_ref + 7 :]
    rows, width = acc.shape
    total = layers * GROUPS
    reduction = Reduction(
        grads, sums, total,
        (y_buf, x_buf, z0_buf, z1_buf, all_buf, keep_buf),
        (send_sem, recv_sem, sum_send, sum_recv, keep_sem, out_sem, in_free, out_free),
    )
    greet((FLIP_Y, FLIP_X, FLIP_Z0, FLIP_Z1, FLIP_C, SWAP))

    def feed(n, slot, source, target):
        return pltpu.make_async_copy(source, target, feed_sem.at[n, slot])

    def load(n, source, target):
        return pltpu.make_async_copy(source, target, load_sem.at[n])

    def exchange(n, source, target):
        return pltpu.make_async_remote_copy(
            src_ref=source, dst_ref=target, send_sem=core_send.at[n], recv_sem=core_recv.at[n],
            device_id=partner(FLIP_C), device_id_type=MESH,
        )

    def give_du(j, n):
        return pltpu.make_async_remote_copy(
            src_ref=du.at[j], dst_ref=du_sib.at[n], send_sem=du_send.at[n], recv_sem=du_recv.at[n],
            device_id=partner(FLIP_C), device_id_type=MESH,
        )

    def weight(a, group):
        return w_ref.at[a, group]

    def columns(ref, i, size):
        return ref.at[:, pl.ds(pl.multiple_of(i * size, size), size)]

    def unit(left, left_sib, right, right_sib, index):
        unit_buf[...] = (tn(left, right) + tn(left_sib, right_sib)).astype(BF16)
        store = pltpu.make_async_copy(unit_buf, grads.at[index], store_sem.at[0])
        store.start()
        store.wait()

    def add_small(l, row, value):
        small_ref[l, row : row + 1, :] += jnp.sum(value, axis=0, keepdims=True)

    stays = lax.axis_index("dp") % 2 == lax.axis_index("tensor")

    def swap(n, source, target, begin):
        here = pltpu.make_async_copy(source, target, swap_sem.at[n])
        there = pltpu.make_async_remote_copy(
            src_ref=source, dst_ref=target, send_sem=core_send.at[4 + n], recv_sem=core_recv.at[4 + n],
            device_id=partner(SWAP), device_id_type=MESH,
        )

        @pl.when(stays)
        def _():
            here.start() if begin else here.wait()

        @pl.when(jnp.logical_not(stays))
        def _():
            there.start() if begin else there.wait()

    swap(1, x_ref, x_out, True)
    start_up = load(0, up_ref, da)
    start_up.start()
    start_up.wait()
    small_ref[...] = jnp.zeros_like(small_ref)

    def widen(at):
        acc[at, :] = da[at, :].astype(F32)

    row_tiles(rows, widen)
    done = 0
    for l in reversed(range(layers)):
        qkv_ref, sib_ref, ctx_ref, ctx_sib_ref, lse_ref, r1_ref, r2_ref, hl_ref, hl_sib_ref, g_ref, g_sib_ref, slope_ref, xb_ref, xb_sib_ref = saved[l]
        first = l * GROUPS
        base = (layers - 1 - l) * GROUPS
        clock = 11 * (layers - 1 - l)

        r_load = load(0, r2_ref, r_buf)
        r_load.start()
        r_load.wait()

        def second(at):
            dy = acc[at, :]
            dr, part = norm_back(dy, r_buf[at, :], vec_ref[l, 4:5, :])
            acc[at, :] = dr
            dm[at, :] = dr.astype(BF16)
            add_small(l, 0, part)
            add_small(l, 1, dy)
            add_small(l, 2, dr)

        row_tiles(rows, second)
        dm_copy = exchange(0, dm, dm_sib)
        dm_copy.start()
        r_load = load(0, r1_ref, r_buf)
        r_load.start()
        right_load = load(1, hl_ref, right_buf)
        right_load.start()
        right_sib_load = load(2, hl_sib_ref, right_sib_buf)
        right_sib_load.start()
        dm_copy.wait()

        def down_feeds(i, slot):
            return (
                feed(0, slot, columns(g_ref, i, 512), left_buf.at[slot]),
                feed(1, slot, columns(g_sib_ref, i, 512), left_sib_buf.at[slot]),
            )

        def down_body(i, slot):
            unit(left_buf[slot], left_sib_buf[slot], dm[...], dm_sib[...], base + i)
            pl.when(lax.rem(i, 3) == 0)(lambda: reduction.tick(clock + lax.div(i, 3)))

        stream(FF_GROUPS, down_feeds, down_body)

        def place_of(i):
            a = 1 - lax.div(i, FF_GROUPS)
            return a, lax.rem(i, FF_GROUPS)

        def ff_feeds(i, slot):
            a, n = place_of(i)
            j = a * FF_GROUPS + n
            return (
                feed(0, slot, weight(a, first + down_group(n)), wa_buf.at[slot]),
                feed(1, slot, weight(a, first + in_group(n)), wb_buf.at[slot]),
                feed(2, slot, columns(slope_ref, j, 512), slope_buf.at[slot]),
            )

        def ff_body(i, slot):
            a, n = place_of(i)
            j = a * FF_GROUPS + n
            dg = nt(dm[...], block_of(wa_buf.at[slot]))
            d = (dg * slope_buf[slot].astype(F32)).astype(BF16)
            du[j] = d
            pl.when(a == 1)(lambda: give_du(j, n).start())
            dbi_ref[l, a, n] = jnp.sum(d.astype(F32), axis=0, keepdims=True)
            acc[...] += nn(d, block_of(wb_buf.at[slot]))
            pl.when(lax.rem(i, 3) == 2)(lambda: reduction.tick(clock + 2 + lax.div(i, 3)))

        stream(2 * FF_GROUPS, ff_feeds, ff_body)

        r_load.wait()

        def first_norm(at):
            dy = acc[at, :]
            dr, part = norm_back(dy, r_buf[at, :], vec_ref[l, 1:2, :])
            dr1[at, :] = dr
            da[at, :] = dr.astype(BF16)
            add_small(l, 3, part)
            add_small(l, 4, dy)
            add_small(l, 5, dr)

        row_tiles(rows, first_norm)
        da_copy = exchange(1, da, da_sib)
        da_copy.start()

        def out_feeds(i, slot):
            return (feed(0, slot, weight(i, first + OUT_GROUP), wa_buf.at[slot]),)

        def out_body(i, slot):
            dctx[:, pl.ds(pl.multiple_of(i * 512, 512), 512)] = nt(da[...], block_of(wa_buf.at[slot])).astype(BF16)

        stream(2, out_feeds, out_body)

        right_load.wait()
        right_sib_load.wait()

        def in_body(n, _):
            give_du(FF_GROUPS + n, n).wait()
            unit(du[n], du_sib[n], right_buf[...], right_sib_buf[...], base + FF_GROUPS + n)
            pl.when(lax.rem(n, 3) == 0)(lambda: reduction.tick(clock + 4 + lax.div(n, 3)))
            return 0

        lax.fori_loop(0, FF_GROUPS, in_body, 0)

        right_load = load(1, xb_ref, right_buf)
        right_load.start()
        right_sib_load = load(2, xb_sib_ref, right_sib_buf)
        right_sib_load.start()
        left_load = load(3, columns(ctx_ref, 0, 512), left_buf.at[0])
        left_load.start()
        left_sib_load = load(4, ctx_sib_ref, left_sib_buf.at[0])
        left_sib_load.start()
        da_copy.wait()
        left_load.wait()
        left_sib_load.wait()
        unit(left_buf[0], left_sib_buf[0], da[...], da_sib[...], base + 2 * FF_GROUPS)

        pairs = width // 128

        def pair_feeds(p, slot):
            far = lax.rem(p + pairs // 2, pairs)
            return (
                feed(0, slot, columns(qkv_ref.at[0], p, 128), pair_buf.at[slot, 0, pl.ds(0, rows)]),
                feed(1, slot, columns(qkv_ref.at[1], p, 128), pair_buf.at[slot, 1, pl.ds(0, rows)]),
                feed(2, slot, columns(sib_ref.at[0], far, 128), pair_buf.at[slot, 1, pl.ds(rows, rows)]),
                feed(3, slot, columns(qkv_ref.at[2], p, 128), pair_buf.at[slot, 2, pl.ds(0, rows)]),
                feed(4, slot, columns(sib_ref.at[1], far, 128), pair_buf.at[slot, 2, pl.ds(rows, rows)]),
                feed(5, slot, columns(ctx_ref, p, 128), pair_buf.at[slot, 3, pl.ds(0, rows)]),
                feed(6, slot, lse_ref.at[p], lse_buf.at[slot]),
            )

        def pair_body(p, slot):
            far = lax.rem(p + pairs // 2, pairs)
            here = pl.ds(pl.multiple_of(p * 128, 128), 128)
            mask = [spread_mask(mask_ref[2 * p + e], key_ref[...]) for e in range(2)]
            dq, dk, dv = attend_back_pair(
                pair_buf[slot, 0, 0:rows], pair_buf[slot, 1], pair_buf[slot, 2], hot_buf[...], mask,
                pair_buf[slot, 3, 0:rows], lse_buf[slot], dctx[:, here],
            )
            dqkv[0, :, here] = dq.astype(BF16)
            dqkv[1, :, here] = dk[:rows].astype(BF16)
            dqkv[2, :, here] = dv[:rows].astype(BF16)
            there = pl.ds(pl.multiple_of(far * 128, 128), 128)
            kv_out[0, :, there] = dk[rows:].astype(BF16)
            kv_out[1, :, there] = dv[rows:].astype(BF16)
            pl.when(lax.rem(p, 3) == 1)(lambda: reduction.tick(clock + 6 + lax.div(p, 3)))

        stream(pairs, pair_feeds, pair_body)
        kv_copy = exchange(2, kv_out, kv_far)
        kv_copy.start()
        kv_copy.wait()
        for n in range(2):
            add_rows(dqkv.at[1 + n], kv_far.at[n], rows)
        d_copy = exchange(3, dqkv.at[:, :, pl.ds(512, 512)], d_sib)
        d_copy.start()
        right_load.wait()
        right_sib_load.wait()
        d_copy.wait()

        def qkv_body(n, _):
            unit(dqkv[n, :, 0:512], d_sib[n], right_buf[...], right_sib_buf[...], base + 2 * FF_GROUPS + 1 + n)
            return 0

        lax.fori_loop(0, 3, qkv_body, 0)
        reduction.tick(clock + 9)

        def start_dx(at):
            acc[at, :] = dr1[at, :]

        row_tiles(rows, start_dx)

        def dx_feeds(i, slot):
            return (feed(0, slot, weight(lax.rem(i, 2), first + lax.div(i, 2)), wa_buf.at[slot]),)

        def dx_body(i, slot):
            a, n = lax.rem(i, 2), lax.div(i, 2)
            d = dqkv[n, :, pl.ds(pl.multiple_of(a * 512, 512), 512)]
            qkv_sums_ref[l, n, a] = jnp.sum(d.astype(F32), axis=0, keepdims=True)
            acc[...] += nn(d, block_of(wa_buf.at[slot]))
            pl.when(i == 3)(lambda: reduction.tick(clock + 10))

        stream(6, dx_feeds, dx_body)
        done = clock + 11

    def narrow(at):
        da[at, :] = acc[at, :].astype(BF16)

    row_tiles(rows, narrow)
    swap(0, da, dx_out, True)

    def rest(t, _):
        reduction.tick(t)
        return 0

    lax.fori_loop(done, total + LAST_TICK, rest, 0)
    swap(0, da, dx_out, False)
    swap(1, x_ref, x_out, False)


def backward(upstream, stream_low, weights, hot, mask, mask_rows, vectors, saved):
    rows, width = upstream.shape
    layers = len(saved)
    total = layers * GROUPS
    anywhere = pl.BlockSpec(memory_space=pl.ANY)
    in_vmem = pl.BlockSpec(memory_space=pltpu.VMEM)
    low = lambda *shape: pltpu.VMEM(shape, BF16)
    dma = lambda *shape: pltpu.SemaphoreType.DMA(shape)
    return pl.pallas_call(
        functools.partial(backward_kernel, layers),
        out_shape=(
            jax.ShapeDtypeStruct((total, 512, width), BF16),
            jax.ShapeDtypeStruct((total, 512, width), BF16),
            jax.ShapeDtypeStruct((rows, width), BF16),
            jax.ShapeDtypeStruct((rows, width), BF16),
            jax.ShapeDtypeStruct((layers, 2, FF_GROUPS, 1, 512), F32),
            jax.ShapeDtypeStruct((layers, 3, 2, 1, 512), F32),
            jax.ShapeDtypeStruct((layers, 8, width), F32),
        ),
        in_specs=[anywhere] * 3 + [in_vmem] * 4 + [anywhere] * (PER_LAYER * layers),
        out_specs=(anywhere, anywhere, anywhere, anywhere, in_vmem, in_vmem, in_vmem),
        scratch_shapes=[
            pltpu.VMEM((rows, width), F32),
            pltpu.VMEM((rows, width), F32),
            low(rows, width),
            low(rows, width),
            low(rows, width),
            low(rows, width),
            low(2 * FF_GROUPS, rows, 512),
            low(FF_GROUPS, rows, 512),
            low(rows, width),
            low(3, rows, width),
            low(3, rows, 512),
            low(2, rows, width),
            low(2, rows, width),
            low(2, 2, 256, width),
            low(2, 2, 256, width),
            pltpu.VMEM((rows, width), F32),
            low(2, rows, 512),
            low(2, rows, 512),
            low(2, rows, 512),
            low(rows, width),
            low(rows, width),
            low(2, 4, 2 * rows, 128),
            pltpu.VMEM((2, 2, rows), F32),
            low(512, width),
            low(SLOTS, 256, width),
            low(SLOTS, 128, width),
            low(SLOTS, 64, width),
            low(SLOTS, 32, width),
            low(SLOTS, 256, width),
            low(2, 256, width),
            dma(8, 2),
            dma(5),
            dma(1),
            dma(2),
            dma(6),
            dma(6),
            dma(FF_GROUPS),
            dma(FF_GROUPS),
            dma(7, SLOTS),
            dma(7, SLOTS),
            dma(total),
            dma(total),
            dma(2),
            dma(SLOTS),
            pltpu.SemaphoreType.REGULAR((4,)),
            pltpu.SemaphoreType.REGULAR((3,)),
        ],
        compiler_params=pltpu.CompilerParams(
            collective_id=1, has_side_effects=True, vmem_limit_bytes=60 << 20
        ),
        cost_estimate=pl.CostEstimate(flops=60 << 30, bytes_accessed=300 << 20, transcendentals=1 << 24),
        name="backward",
    )(upstream, stream_low, weights, hot, mask, mask_rows, vectors, *[ref for one in saved for ref in one])


def flip_order(values, axis, bits):
    for i, bit in enumerate(bits):
        values = jnp.where(bit == 0, values, jnp.flip(values, axis + i))
    return values


def sequence_shards(
    block_input, segment_ids, random_blocks, w_qkv, b_qv, w_out, b_out, w_in, b_in, w_down, b_down,
    ln_gain, ln_bias, cotangent,
):
    y = lax.axis_index("tensor")
    dp = lax.axis_index("dp")
    core, x_bit, z0, z1 = dp % 2, (dp // 2) % 2, (dp // 4) % 2, dp // 8
    code = core * 8 + x_bit * 4 + z0 * 2 + z1
    code_arg = code.reshape(1).astype(jnp.int32)
    device_bits = (core, x_bit, z0, z1)

    rows, _, width = block_input.shape
    layers = w_qkv.shape[0]
    blocks = random_blocks.shape[2]
    own_blocks = blocks // 2
    heads = random_blocks.shape[1] * 2

    chosen = random_blocks[0]
    near = jnp.concatenate([chosen.reshape(-1), segment_ids[0]])
    sibling = flip(near, FLIP_C)
    across, diagonal = flip(chosen.reshape(-1), FLIP_Y), flip(chosen.reshape(-1), SWAP)
    mine = jnp.concatenate([near[: chosen.size], across, near[chosen.size :]])
    other = jnp.concatenate([sibling[: chosen.size], diagonal, sibling[chosen.size :]])
    packed = jnp.where(core == y, mine, other)
    chosen = packed[: 2 * chosen.size].reshape(2, heads // 2, blocks, -1)
    segments = packed[2 * random_blocks.size :]
    chosen = flip_order(chosen.reshape(2, 2, 2, 2, blocks, -1), 1, device_bits[:3])
    chosen = chosen.transpose(1, 0, 2, 3, 4, 5).reshape(heads, blocks, -1)
    segments = segments.reshape(2, rows)
    segments = jnp.where(core == 0, segments, segments[::-1]).reshape(-1)
    query_block = core * own_blocks + jnp.arange(own_blocks)
    key_block = jnp.arange(blocks) ^ (core * own_blocks)
    allowed = (
        (jnp.abs(query_block[:, None] - key_block[None, :]) <= 1)
        | (key_block[None, :] == 0)
        | (key_block[None, :] == blocks - 1)
        | (query_block[:, None] == 0)
        | (query_block[:, None] == blocks - 1)
    )
    chosen = lax.dynamic_slice_in_dim(chosen, core * own_blocks, own_blocks, axis=1)
    allowed = allowed[None] | jnp.any(chosen[:, :, None, :] == key_block[None, None, :, None], axis=3)
    block_rows = rows // own_blocks
    documents = jnp.arange(128 - own_blocks)
    mask = jnp.pad(
        jnp.where(allowed, 0.0, BIG).astype(F32).transpose(0, 2, 1), ((0, 0), (0, 0), (0, 128 - own_blocks))
    )
    document_part = jnp.where(
        (segments[:, None] == documents[None, :]) | (documents[None, :] > 7), 0.0, BIG
    ).astype(F32)
    mask_rows = jnp.pad(document_part, ((0, 0), (own_blocks, 0)))
    block_rows = rows // own_blocks
    hot = jnp.concatenate(
        [
            jnp.repeat(jnp.eye(own_blocks, dtype=BF16), block_rows, axis=0),
            (segments[:rows, None] == documents[None, :]).astype(BF16),
        ],
        axis=1,
    )

    bias_pack = jnp.concatenate(
        [
            flip_order(b_qv.reshape(layers * 2, 2, 2, 2, 2, -1), 1, device_bits).reshape(-1),
            flip_order(b_in.reshape(layers * FF_GROUPS, 2, 2, 2, 2, -1), 1, device_bits).reshape(-1),
        ]
    )
    bias_far = flip(bias_pack, FLIP_Y)
    n_qv = b_qv.size

    def local_bias(near, far, count):
        near, far = near.reshape(count, 2, 1, 256), far.reshape(count, 2, 1, 256)
        return jnp.concatenate([near, far], axis=2).reshape(count, 2, 512)

    bias_qv = local_bias(bias_pack[:n_qv], bias_far[:n_qv], layers * 2).reshape(layers, 2, 2, 1, 512)
    bias_qkv = jnp.stack([bias_qv[:, 0], jnp.zeros_like(bias_qv[:, 0]), bias_qv[:, 1]], axis=1)
    bias_in = local_bias(bias_pack[n_qv:], bias_far[n_qv:], layers * FF_GROUPS)
    bias_in = bias_in.reshape(layers, FF_GROUPS, 2, 1, 512).swapaxes(1, 2)

    vectors = [
        jnp.stack(
            [
                b_out[l], ln_gain[l, 0], ln_bias[l, 0], b_down[l], ln_gain[l, 1], ln_bias[l, 1],
                b_out[l], b_out[l],
            ]
        )
        for l in range(layers)
    ]
    vectors = jnp.stack(vectors)
    weights, upstream_low, stream_low, saved = forward(
        block_input, cotangent, w_qkv, w_out, w_in, w_down, hot, mask, mask_rows, bias_qkv, bias_in, vectors
    )
    _, grads, dx_low, x_low, d_b_in, qkv_sums, rows_small = backward(
        upstream_low, stream_low, weights, hot, mask, mask_rows, vectors, saved
    )
    block_output = x_low.astype(F32)[:, None]
    input_grad = dx_low.astype(F32)[:, None]

    stacks = [
        jnp.stack([qkv_sums[:, 0], qkv_sums[:, 2]], axis=1),
        rows_small[:, 5],
        d_b_in.swapaxes(1, 2),
        rows_small[:, 2],
        jnp.stack([rows_small[:, 3], rows_small[:, 0]], axis=1),
        jnp.stack([rows_small[:, 4], rows_small[:, 1]], axis=1),
    ]

    def global_order(values, lead):
        values = values.reshape(lead, 2, 2, 2, 2, 2, 32).swapaxes(1, 2)
        values = flip_order(values, 1, (y,) + device_bits)
        return values.swapaxes(0, 1).reshape(2, -1)

    stacks[0] = global_order(stacks[0], layers * 2)
    stacks[2] = global_order(stacks[2], layers * FF_GROUPS)
    def placing(shape, block, index, turned, count, start):
        return lambda values: place(
            values, shape, block, index, turned, count, lambda l, i: (layers - 1 - l) * GROUPS + start + i, code_arg
        )

    summed = jnp.concatenate([s.reshape(-1) for s in stacks])
    summed = summed + flip(summed, FLIP_C)
    placed = []
    for bit, put in (
        (FLIP_Y, placing(w_down.shape, (1, 512, width), lambda l, i: (l, i, 0), False, FF_GROUPS, 0)),
        (FLIP_X, placing(w_in.shape, (1, width, 512), lambda l, i: (l, 0, i), True, FF_GROUPS, FF_GROUPS)),
        (FLIP_Z0, placing(w_qkv.shape, (1, 1, width, 512), lambda l, i: (l, i, 0, 0), True, 3, 2 * FF_GROUPS + 1)),
        (FLIP_Z1, placing(w_out.shape, (1, 512, width), lambda l, i: (l, 0, 0), False, 1, 2 * FF_GROUPS)),
    ):
        summed, grads = lax.optimization_barrier((summed, grads))
        far = flip(summed, bit)
        done, summed, far = lax.optimization_barrier((put(grads), summed, far))
        placed.append(done)
        summed = summed + far
    parts, at = [], 0
    for s in stacks:
        parts.append(summed[at : at + s.size].reshape(s.shape))
        at += s.size
    g_b_qv = lax.dynamic_index_in_dim(parts[0], y, axis=0, keepdims=False).reshape(b_qv.shape)
    g_b_in = lax.dynamic_index_in_dim(parts[2], y, axis=0, keepdims=False).reshape(b_in.shape)
    return (
        block_output,
        input_grad,
        placed[2],
        g_b_qv,
        placed[3],
        parts[1],
        placed[1],
        g_b_in,
        placed[0],
        parts[3],
        parts[4],
        parts[5],
    )


def as_sent(array):

    def short(part):
        return part.astype(jnp.bfloat16) if part.dtype == jnp.float32 else part

    return jax.tree.map(short, array)


def norm_rows(values, gain_row, shift_row):
    row_mean = jnp.mean(values, axis=-1, keepdims=True)
    centred = values - row_mean
    variance = jnp.mean(centred * centred, axis=-1, keepdims=True)
    return centred * lax.rsqrt(variance + 1e-06) * gain_row + shift_row


def gelu_exact(values):
    return jax.nn.gelu(values, approximate=False)


def block_mask(chosen_blocks, segment_rows):
    nblocks = chosen_blocks.shape[2]
    block_index = jnp.arange(nblocks)
    near_blocks = jnp.abs(block_index[:, None] - block_index[None, :]) <= 1
    edge_blocks = (
        (block_index[None, :] == 0)
        | (block_index[None, :] == nblocks - 1)
        | (block_index[:, None] == 0)
        | (block_index[:, None] == nblocks - 1)
    )
    picked_blocks = jnp.any(chosen_blocks[..., None] == block_index, axis=3)
    allowed = near_blocks | edge_blocks | picked_blocks
    block_rows = segment_rows.shape[1] // nblocks
    allowed = jnp.repeat(jnp.repeat(allowed, block_rows, axis=2), block_rows, axis=3)
    same_doc = segment_rows[:, :, None] == segment_rows[:, None, :]
    return allowed & same_doc[:, None]


def masked_scores(queries, key_rows, allowed, score_scale):
    scores = (
        jnp.einsum("qshd,kshd->shqk", queries, key_rows, preferred_element_type=jnp.float32)
        * score_scale
    )
    return jnp.where(allowed, scores, -1e30)


def shards(
    block_input,
    segment_ids,
    random_blocks,
    w_qkv,
    b_qv,
    w_out,
    b_out,
    w_in,
    b_in,
    w_down,
    b_down,
    ln_gain,
    ln_bias,
    cotangent,
):
    score_scale = HEAD_DIM ** (-0.5)
    shard_rows, seq_count, model_width = block_input.shape
    layers = w_qkv.shape[0]
    local_width = w_qkv.shape[3]
    local_heads = local_width // HEAD_DIM
    allowed = block_mask(random_blocks, segment_ids)
    saved_acts = []
    stream = block_input
    for layer_index in range(layers):
        w_proj = w_qkv[layer_index].astype(jnp.bfloat16)
        w_mix = w_out[layer_index].astype(jnp.bfloat16)
        rows_low = stream.astype(jnp.bfloat16)
        full_rows = lax.all_gather(rows_low, "tensor", axis=0, tiled=True)
        length = full_rows.shape[0]
        projected = jnp.einsum(
            "lsd,tdc->tlsc", full_rows, w_proj, preferred_element_type=jnp.float32
        )
        qkv_bias = jnp.stack(
            [b_qv[layer_index, 0], jnp.zeros_like(b_qv[layer_index, 0]), b_qv[layer_index, 1]]
        )
        qkv_low = (projected + qkv_bias[:, None, None, :]).astype(jnp.bfloat16)
        head_view = qkv_low.reshape(3, length, seq_count, local_heads, HEAD_DIM)
        scores = masked_scores(head_view[0], head_view[1], allowed, score_scale)
        row_top = jnp.max(scores, axis=-1, keepdims=True)
        log_total = row_top + jnp.log(jnp.sum(jnp.exp(scores - row_top), axis=-1, keepdims=True))
        probs_low = jnp.exp(scores - log_total).astype(jnp.bfloat16)
        context = jnp.einsum(
            "shqk,kshd->qshd", probs_low, head_view[2], preferred_element_type=jnp.float32
        )
        context = context.reshape(length, seq_count, local_width).astype(jnp.bfloat16)
        mixed = lax.psum_scatter(
            jnp.einsum("lsc,cd->lsd", context, w_mix, preferred_element_type=jnp.float32).astype(
                jnp.bfloat16
            ),
            "tensor",
            scatter_dimension=0,
            tiled=True,
        ).astype(jnp.float32)
        first_sum = stream + mixed + b_out[layer_index]
        hidden_rows = norm_rows(first_sum, ln_gain[layer_index, 0], ln_bias[layer_index, 0])
        hidden_low = hidden_rows.astype(jnp.bfloat16)
        up_weight = w_in[layer_index].astype(jnp.bfloat16)
        backward_weight = w_down[layer_index].astype(jnp.bfloat16)
        hidden_full = lax.all_gather(hidden_low, "tensor", axis=0, tiled=True)
        preactivation = (
            jnp.einsum("twn,nj->twj", hidden_full, up_weight, preferred_element_type=jnp.float32)
            + b_in[layer_index]
        )
        activation_reduced = gelu_exact(preactivation).astype(jnp.bfloat16)
        grown = lax.psum_scatter(
            jnp.einsum(
                "unj,jp->unp",
                activation_reduced,
                backward_weight,
                preferred_element_type=jnp.float32,
            ).astype(jnp.bfloat16),
            "tensor",
            scatter_dimension=0,
            tiled=True,
        ).astype(jnp.float32)
        second_sum = hidden_rows + grown + b_down[layer_index]
        stream = norm_rows(second_sum, ln_gain[layer_index, 1], ln_bias[layer_index, 1])
        keep_rows, keep_hidden = (full_rows, hidden_full)
        saved_acts.append(
            (
                keep_rows,
                head_view,
                log_total,
                context,
                first_sum,
                keep_hidden,
                preactivation,
                activation_reduced,
                second_sum,
                up_weight,
                backward_weight,
            )
        )
    upstream = cotangent
    grads_by_layer = [None] * layers
    for layer_index in reversed(range(layers)):
        (
            keep_rows,
            head_view,
            log_total,
            context,
            first_sum,
            keep_hidden,
            preactivation,
            activation_reduced,
            second_sum,
            up_weight,
            backward_weight,
        ) = saved_acts[layer_index]
        full_rows, hidden_full = (keep_rows, keep_hidden)
        length = full_rows.shape[0]
        w_proj = w_qkv[layer_index].astype(jnp.bfloat16)
        w_mix = w_out[layer_index].astype(jnp.bfloat16)
        _, pull_second = jax.vjp(
            norm_rows, second_sum, ln_gain[layer_index, 1], ln_bias[layer_index, 1]
        )
        d_second, d_gain_two, d_shift_two = pull_second(upstream)
        _, pull_gelu = jax.vjp(gelu_exact, preactivation)
        widened_full = lax.all_gather(d_second.astype(jnp.bfloat16), "tensor", axis=0, tiled=True)
        down_gradient = jnp.einsum(
            "uxc,uxw->cw", activation_reduced, widened_full, preferred_element_type=jnp.float32
        )
        activation_gradient = jnp.einsum(
            "mra,xa->mrx", widened_full, backward_weight, preferred_element_type=jnp.float32
        )
        preactivation_gradient_reduced = pull_gelu(activation_gradient)[0].astype(jnp.bfloat16)
        up_gradient = jnp.einsum(
            "kmx,kmt->xt",
            hidden_full,
            preactivation_gradient_reduced,
            preferred_element_type=jnp.float32,
        )
        g_up_bias = jnp.sum(preactivation_gradient_reduced.astype(jnp.float32), axis=(0, 1))
        d_hidden = d_second + lax.psum_scatter(
            jnp.einsum(
                "hmp,tp->hmt",
                preactivation_gradient_reduced,
                up_weight,
                preferred_element_type=jnp.float32,
            ).astype(jnp.bfloat16),
            "tensor",
            scatter_dimension=0,
            tiled=True,
        ).astype(jnp.float32)
        _, pull_first = jax.vjp(
            norm_rows, first_sum, ln_gain[layer_index, 0], ln_bias[layer_index, 0]
        )
        d_first, d_gain_one, d_shift_one = pull_first(d_hidden)
        full_mixed = lax.all_gather(d_first.astype(jnp.bfloat16), "tensor", axis=0, tiled=True)
        g_out = jnp.einsum("lsc,lsd->cd", context, full_mixed, preferred_element_type=jnp.float32)
        d_context = jnp.einsum(
            "lsd,cd->lsc", full_mixed, w_mix, preferred_element_type=jnp.float32
        ).astype(jnp.bfloat16)
        d_context = d_context.reshape(length, seq_count, local_heads, HEAD_DIM)
        queries, key_rows, value_rows = (head_view[0], head_view[1], head_view[2])
        scores = masked_scores(queries, key_rows, allowed, score_scale)
        attn_probs = jnp.exp(scores - log_total)
        probs_low = attn_probs.astype(jnp.bfloat16)
        d_probs = jnp.einsum(
            "qshd,kshd->shqk", d_context, value_rows, preferred_element_type=jnp.float32
        )
        d_scores = attn_probs * (d_probs - jnp.sum(d_probs * attn_probs, axis=-1, keepdims=True))
        d_scores = d_scores.astype(jnp.bfloat16)
        d_query = (
            jnp.einsum("shqk,kshd->qshd", d_scores, key_rows, preferred_element_type=jnp.float32)
            * score_scale
        )
        d_key = (
            jnp.einsum("shqk,qshd->kshd", d_scores, queries, preferred_element_type=jnp.float32)
            * score_scale
        )
        d_value = jnp.einsum(
            "shqk,qshd->kshd", probs_low, d_context, preferred_element_type=jnp.float32
        )
        d_qkv = (
            jnp.stack([d_query, d_key, d_value])
            .reshape(3, length, seq_count, local_width)
            .astype(jnp.bfloat16)
        )
        g_proj = jnp.einsum("lsd,tlsc->tdc", full_rows, d_qkv, preferred_element_type=jnp.float32)
        qkv_sums = jnp.sum(d_qkv.astype(jnp.float32), axis=(1, 2))
        g_bias = jnp.stack([qkv_sums[0], qkv_sums[2]])
        upstream = d_first + lax.psum_scatter(
            jnp.einsum("tlsc,tdc->lsd", d_qkv, w_proj, preferred_element_type=jnp.float32).astype(
                jnp.bfloat16
            ),
            "tensor",
            scatter_dimension=0,
            tiled=True,
        ).astype(jnp.float32)
        weight_grads = (g_proj, g_bias, g_out, up_gradient, g_up_bias, down_gradient)
        small_grads = (
            jnp.sum(d_first, axis=(0, 1)),
            jnp.sum(d_second, axis=(0, 1)),
            jnp.stack([d_gain_one, d_gain_two]),
            jnp.stack([d_shift_one, d_shift_two]),
        )
        grads_by_layer[layer_index] = (weight_grads, small_grads)
    weight_stack = tuple(
        (
            jnp.stack([grads_by_layer[layer_index][0][member] for layer_index in range(layers)])
            for member in range(6)
        )
    )
    small_stack = tuple(
        (
            jnp.stack([grads_by_layer[layer_index][1][member] for layer_index in range(layers)])
            for member in range(4)
        )
    )
    weight_stack = jax.tree.map(
        lambda part: part.astype(jnp.float32), lax.psum(as_sent(weight_stack), "dp")
    )
    small_stack = lax.psum(small_stack, ("dp", "tensor"))
    return (
        stream,
        upstream,
        weight_stack[0],
        weight_stack[1],
        weight_stack[2],
        small_stack[0],
        weight_stack[3],
        weight_stack[4],
        weight_stack[5],
        small_stack[1],
        small_stack[2],
        small_stack[3],
    )


def solution(mesh):
    by_sequence = mesh.shape["tensor"] == 2 and mesh.shape["dp"] == 16
    return jax.shard_map(
        sequence_shards if by_sequence else shards,
        mesh=mesh,
        in_specs=(
            P("tensor", "dp", None),
            P("dp", None),
            P("dp", "tensor", None, None),
            P(None, None, None, "tensor"),
            P(None, None, "tensor"),
            P(None, "tensor", None),
            P(),
            P(None, None, "tensor"),
            P(None, "tensor"),
            P(None, "tensor", None),
            P(),
            P(),
            P(),
            P("tensor", "dp", None),
        ),
        out_specs=(
            P("tensor", "dp", None),
            P("tensor", "dp", None),
            P(None, None, None, "tensor"),
            P(None, None, "tensor"),
            P(None, "tensor", None),
            P(),
            P(None, None, "tensor"),
            P(None, "tensor"),
            P(None, "tensor", None),
            P(),
            P(),
            P(),
        ),
        check_vma=False,
    )
```

```python
import functools

import jax
import jax.numpy as jnp
from jax import lax
from jax.experimental import pallas as pl
from jax.experimental.pallas import tpu as pltpu
from jax.sharding import PartitionSpec as P

HEAD_DIM = 64
BIG = -1e30
BF16 = jnp.bfloat16
F32 = jnp.float32
MESH = pl.DeviceIdType.MESH
VMEM_LIMIT = 56 << 20

FLIP_Y, FLIP_C, FLIP_X, FLIP_Z0, FLIP_Z1 = 1, 2, 4, 8, 16
SWAP = FLIP_Y + FLIP_C
DEVICES = 32

GROUPS = 12
OUT_GROUP = 3
FF_GROUPS = 4


def in_group(s):
    return 4 + 2 * s


def down_group(s):
    return 5 + 2 * s


def flip(values, bit):
    pairs = [(i, i ^ bit) for i in range(DEVICES)]
    return jax.tree.map(lambda v: lax.ppermute(v, ("dp", "tensor"), pairs), values)


def nt(a, b):
    return lax.dot_general(a, b, (((1,), (1,)), ((), ())), preferred_element_type=F32)


def nn(a, b):
    return lax.dot_general(a, b, (((1,), (0,)), ((), ())), preferred_element_type=F32)


def tn(a, b):
    return lax.dot_general(a, b, (((0,), (0,)), ((), ())), preferred_element_type=F32)


def block_of(ref):
    width = ref.shape[-1]
    return ref[...].reshape(-1, width)


def place_kernel(turned, code_ref, g_ref, o_ref, *scratch):
    code = code_ref[0]
    for j in range(16):
        start = pl.multiple_of((j ^ code) * 32, 32)
        block = g_ref[0, pl.ds(start, 32), :].astype(F32)
        if turned:
            scratch[0][j * 32 : (j + 1) * 32, :] = block
        else:
            o_ref[0, j * 32 : (j + 1) * 32, :] = block
    if turned:
        o_ref[...] = scratch[0][...].T.reshape(o_ref.shape)


def place(sums, shape, block, index, turned, count, group, code):
    width = sums.shape[-1]
    return pl.pallas_call(
        functools.partial(place_kernel, turned),
        out_shape=jax.ShapeDtypeStruct(shape, F32),
        grid_spec=pltpu.PrefetchScalarGridSpec(
            num_scalar_prefetch=1,
            grid=(shape[0], count),
            in_specs=[pl.BlockSpec((1, 512, width), lambda l, i, code: (group(l, i), 0, 0))],
            out_specs=pl.BlockSpec(block, lambda l, i, code: index(l, i)),
            scratch_shapes=[pltpu.VMEM((512, width), F32)] if turned else [],
        ),
        compiler_params=pltpu.CompilerParams(vmem_limit_bytes=VMEM_LIMIT),
        cost_estimate=pl.CostEstimate(
            flops=0, bytes_accessed=shape[0] * count * 512 * width * 6, transcendentals=0
        ),
        name="place",
    )(code, sums)


def widen_kernel(a_ref, b_ref, a_out, b_out, a_buf, b_buf, sem):
    copies = []
    for n, (source, target, buf) in enumerate(((a_ref, a_out, a_buf), (b_ref, b_out, b_buf))):
        buf[...] = source[...].astype(F32)
        copies.append(pltpu.make_async_copy(buf, target.at[:, 0], sem.at[n]))
        copies[-1].start()
    for copy in copies:
        copy.wait()


def widen_rows(a, b):
    rows, width = a.shape
    out = jax.ShapeDtypeStruct((rows, 1, width), F32)
    return pl.pallas_call(
        widen_kernel,
        out_shape=(out, out),
        in_specs=[pl.BlockSpec(memory_space=pltpu.VMEM)] * 2,
        out_specs=(pl.BlockSpec(memory_space=pl.ANY),) * 2,
        scratch_shapes=[pltpu.VMEM((rows, width), F32), pltpu.VMEM((rows, width), F32), pltpu.SemaphoreType.DMA((2,))],
        name="widen_rows",
    )(a, b)


def partner(bits):
    dp, y = lax.axis_index("dp"), lax.axis_index("tensor")
    other = dp
    for step in (1, 2, 4, 8):
        if bits & (2 * step):
            other = other + step * (1 - 2 * ((dp // step) % 2))
    return (other, 1 - y if bits & FLIP_Y else y)


def greet(bits):
    barrier = pltpu.get_barrier_semaphore()
    for bit in bits:
        pl.semaphore_signal(barrier, inc=1, device_id=partner(bit), device_id_type=MESH)
    pl.semaphore_wait(barrier, len(bits))


def add_into(into, other, count):
    def step(i, _):
        into[i] = (into[i].astype(F32) + other[i].astype(F32)).astype(BF16)
        return 0

    lax.fori_loop(0, count, step, 0)


def add_rows(into, other, rows):
    def step(i, _):
        at = pl.ds(pl.multiple_of(i * 32, 32), 32)
        into[at, :] = (into[at, :].astype(F32) + other[at, :].astype(F32)).astype(BF16)
        return 0

    lax.fori_loop(0, rows // 32, step, 0)


SLOTS = 12
LAST_TICK = 10


class Reduction:
    def __init__(self, grads, sums, count, bufs, sems):
        self.grads, self.sums, self.count = grads, sums, count
        self.y_buf, self.x_buf, self.z0_buf, self.z1_buf, self.all_buf, self.keep_buf = bufs
        self.send_sem, self.recv_sem, self.core_send, self.core_recv = sems[:4]
        self.keep_sem, self.out_sem, self.in_free, self.out_free = sems[4:]

    def blocks(self, ref, i, first):
        part = pl.ds(pl.multiple_of(lax.rem(i, 2) * 16, 16), 16)
        return ref.at[lax.div(i, 2), pl.ds(first, 8), part]

    def copy(self, step, i):
        slot = lax.rem(i, SLOTS)
        ys, al = self.y_buf.at[slot], self.all_buf.at[slot]
        bit, source, target = (
            (FLIP_Y, self.blocks(self.grads, i, 8), ys),
            (FLIP_X, ys.at[pl.ds(4, 4)], self.x_buf.at[slot]),
            (FLIP_Z0, ys.at[pl.ds(2, 2)], self.z0_buf.at[slot]),
            (FLIP_Z1, ys.at[pl.ds(1, 1)], self.z1_buf.at[slot]),
            (FLIP_Z1, al.at[pl.ds(0, 1)], al.at[pl.ds(1, 1)]),
            (FLIP_Z0, al.at[pl.ds(0, 2)], al.at[pl.ds(2, 2)]),
            (FLIP_X, al.at[pl.ds(0, 4)], al.at[pl.ds(4, 4)]),
            (FLIP_C, al, self.blocks(self.sums, i, 8)),
        )[step]
        return pltpu.make_async_remote_copy(
            src_ref=source,
            dst_ref=target,
            send_sem=self.send_sem.at[step, slot] if step < 7 else self.core_send.at[i],
            recv_sem=self.recv_sem.at[step, slot] if step < 7 else self.core_recv.at[i],
            device_id=partner(bit),
            device_id_type=MESH,
        )

    def keep(self, i):
        slot = lax.rem(i, 2)
        return pltpu.make_async_copy(
            self.blocks(self.grads, i, 0), self.keep_buf.at[slot], self.keep_sem.at[slot]
        )

    def out(self, i):
        slot = lax.rem(i, SLOTS)
        return pltpu.make_async_copy(
            self.all_buf.at[slot], self.blocks(self.sums, i, 0), self.out_sem.at[slot]
        )

    def take(self, sem, i):
        @pl.when(i >= SLOTS)
        def _():
            pl.semaphore_wait(sem, 1)

    def give(self, sem, bit, i):
        @pl.when(i + SLOTS < self.count)
        def _():
            pl.semaphore_signal(sem, inc=1, device_id=partner(bit), device_id_type=MESH)

    def tick(self, t):
        def at(offset, body):
            i = t - offset
            pl.when((i >= 0) & (i < self.count))(lambda: body(i, lax.rem(i, SLOTS)))

        def set_out(i, slot):
            self.take(self.in_free.at[0], i)
            self.copy(0, i).start()
            self.keep(i).start()

        def finish(i, slot):
            self.copy(7, i).wait()
            self.out(i).wait()
            for n, bit in enumerate((FLIP_X, FLIP_Z0, FLIP_Z1)):
                self.give(self.out_free.at[n], bit, i)

        def to_core(i, slot):
            self.copy(6, i).wait()
            self.copy(7, i).start()
            self.out(i).start()

        def back_x(i, slot):
            self.copy(5, i).wait()
            self.take(self.out_free.at[0], i)
            self.copy(6, i).start()

        def back_z0(i, slot):
            self.copy(4, i).wait()
            self.take(self.out_free.at[1], i)
            self.copy(5, i).start()

        def back_z1(i, slot):
            self.copy(3, i).wait()
            add_into(self.y_buf.at[slot], self.z1_buf.at[slot], 1)
            self.all_buf[slot, 0] = self.y_buf[slot, 0]
            for n, bit in enumerate((FLIP_Y, FLIP_X, FLIP_Z0, FLIP_Z1)):
                self.give(self.in_free.at[n], bit, i)
            self.take(self.out_free.at[2], i)
            self.copy(4, i).start()

        def on_z1(i, slot):
            self.copy(2, i).wait()
            add_into(self.y_buf.at[slot], self.z0_buf.at[slot], 2)
            self.take(self.in_free.at[3], i)
            self.copy(3, i).start()

        def on_z0(i, slot):
            self.copy(1, i).wait()
            add_into(self.y_buf.at[slot], self.x_buf.at[slot], 4)
            self.take(self.in_free.at[2], i)
            self.copy(2, i).start()

        def on_x(i, slot):
            self.copy(0, i).wait()
            self.keep(i).wait()
            add_into(self.y_buf.at[slot], self.keep_buf.at[lax.rem(i, 2)], 8)
            self.take(self.in_free.at[1], i)
            self.copy(1, i).start()

        at(0, set_out)
        at(10, finish)
        at(9, to_core)
        at(7, back_x)
        at(6, back_z0)
        at(5, back_z1)
        at(4, on_z1)
        at(1, on_x)
        at(3, on_z0)


def stream(count, feeds, body):
    for copy in feeds(0, 0):
        copy.start()

    def step(i, _):
        slot = lax.rem(i, 2)

        @pl.when(i + 1 < count)
        def _():
            for copy in feeds(i + 1, 1 - slot):
                copy.start()

        for copy in feeds(i, slot):
            copy.wait()
        body(i, slot)
        return 0

    lax.fori_loop(0, count, step, 0)


def norm(r, gain, shift):
    centred = r - jnp.mean(r, axis=-1, keepdims=True)
    rstd = lax.rsqrt(jnp.mean(centred * centred, axis=-1, keepdims=True) + 1e-06)
    return centred * rstd * gain + shift


def norm_back(dy, r, gain):
    centred = r - jnp.mean(r, axis=-1, keepdims=True)
    rstd = lax.rsqrt(jnp.mean(centred * centred, axis=-1, keepdims=True) + 1e-06)
    unit = centred * rstd
    dunit = dy * gain
    dr = rstd * (
        dunit
        - jnp.mean(dunit, axis=-1, keepdims=True)
        - unit * jnp.mean(dunit * unit, axis=-1, keepdims=True)
    )
    return dr, dy * unit


def gelu_and_slope(u):
    cdf = 0.5 * (1.0 + lax.erf(u * (0.5**0.5)))
    pdf = jnp.exp(-0.5 * u * u) * 0.3989422804014327
    return u * cdf, cdf + u * pdf


TILE = 64


def row_tiles(rows, body):
    def step(i, _):
        body(pl.ds(pl.multiple_of(i * TILE, TILE), TILE))
        return 0

    lax.fori_loop(0, rows // TILE, step, 0)


def pair_lanes(values, e):
    lane = lax.broadcasted_iota(jnp.int32, values.shape, 1)
    return jnp.where(lane // HEAD_DIM == e, values, jnp.zeros_like(values))


def spread_mask(block_part, document_part):
    blocks, lanes = block_part.shape
    each = document_part.shape[0] // blocks
    part = jnp.broadcast_to(block_part[:, None, :], (blocks, each, lanes)).reshape(blocks * each, lanes)
    return (part + document_part).astype(BF16)


def attend_pair(query, keys, values, hot, mask):
    scale = HEAD_DIM**-0.5
    rows = query.shape[0]
    query = query * jnp.asarray(scale, BF16)
    values_t = values.T
    tile = rows // 2
    contexts, lses = [], ([], [])
    for part in range(2):
        at = slice(part * tile, (part + 1) * tile)
        heads = []
        for e in range(2):
            right = jnp.concatenate([pair_lanes(query[at], e), hot[at]], axis=1)
            left = jnp.concatenate([keys, mask[e]], axis=1)
            s = nt(left, right)
            top = jnp.max(s, axis=0, keepdims=True)
            p = jnp.exp(s - top)
            total = jnp.sum(p, axis=0, keepdims=True)
            c = nn(values_t[e * HEAD_DIM : (e + 1) * HEAD_DIM, :], p.astype(BF16))
            heads.append(c * (1.0 / total))
            lses[e].append(top + jnp.log(total))
        contexts.append(jnp.concatenate(heads, axis=0).T)
    return jnp.concatenate(contexts, axis=0), [jnp.concatenate(parts, axis=1) for parts in lses]


def attend_back_pair(query, keys, values, hot, mask, ctx, lse, dctx):
    scale = HEAD_DIM**-0.5
    rows = query.shape[0]
    query = query * jnp.asarray(scale, BF16)
    keys_t = keys.T
    delta_t = (dctx.astype(F32) * ctx.astype(F32)).T
    tile = rows // 2
    dk, dv, dq = 0.0, 0.0, []
    for part in range(2):
        at = slice(part * tile, (part + 1) * tile)
        heads = []
        for e in range(2):
            lanes = slice(e * HEAD_DIM, (e + 1) * HEAD_DIM)
            query_e = pair_lanes(query[at], e)
            dctx_e = pair_lanes(dctx[at], e)
            right = jnp.concatenate([query_e, hot[at]], axis=1)
            left = jnp.concatenate([keys, mask[e]], axis=1)
            p = jnp.exp(nt(left, right) - lse[e : e + 1, at])
            dp = nt(values, dctx_e)
            delta = jnp.sum(delta_t[lanes, at], axis=0, keepdims=True)
            ds = (p * (dp - delta)).astype(BF16)
            dk = dk + nn(ds, query_e)
            dv = dv + nn(p.astype(BF16), dctx_e)
            heads.append(nn(keys_t[lanes, :], ds) * scale)
        dq.append(jnp.concatenate(heads, axis=0).T)
    return jnp.concatenate(dq, axis=0), dk, dv


class Spread:
    def __init__(self, weights, pairs, send_sem, recv_sem):
        self.weights, self.pairs, self.send_sem, self.recv_sem = weights, pairs, send_sem, recv_sem

    def copy(self, step, t):
        w = self.weights
        even, odd = 2 * t, 2 * t + 1
        bit, source, target = (
            (FLIP_Y, w.at[0, even, 0, pl.ds(0, 64)], w.at[0, even, 1, pl.ds(0, 64)]),
            (FLIP_Y, w.at[0, odd, 0, pl.ds(0, 64)], w.at[0, odd, 1, pl.ds(0, 64)]),
            (FLIP_X, w.at[0, even, 1, pl.ds(0, 64)], w.at[0, even, 1, pl.ds(128, 64)]),
            (FLIP_Z0, w.at[0, odd, 1, pl.ds(0, 64)], w.at[0, odd, 1, pl.ds(64, 64)]),
            (FLIP_Z0, w.at[0, even, 1, pl.ds(0, 64)], w.at[0, even, 1, pl.ds(64, 64)]),
            (FLIP_Z0, w.at[0, even, 1, pl.ds(128, 64)], w.at[0, even, 1, pl.ds(192, 64)]),
            (FLIP_X, w.at[0, odd, 1, pl.ds(0, 128)], w.at[0, odd, 1, pl.ds(128, 128)]),
            (FLIP_C, w.at[0, even, 1], w.at[1, even, 1]),
            (FLIP_C, w.at[0, odd, 1], w.at[1, odd, 1]),
        )[step]
        return pltpu.make_async_remote_copy(
            src_ref=source,
            dst_ref=target,
            send_sem=self.send_sem.at[step, t],
            recv_sem=self.recv_sem.at[step, t],
            device_id=partner(bit),
            device_id_type=MESH,
        )

    def tick(self, t):
        def at(offset, waits, starts):
            i = t - offset

            @pl.when((i >= 0) & (i < self.pairs))
            def _():
                for step in waits:
                    self.copy(step, i).wait()
                for step in starts:
                    self.copy(step, i).start()

        at(0, (), (0, 1))
        at(5, (7, 8), ())
        at(1, (0, 1), (2, 3))
        at(2, (2, 3), (4, 5, 6))
        at(4, (4, 5, 6), (7, 8))


PER_LAYER = 14
DEPTH = 3


def forward_kernel(layers, *refs):
    refs = list(refs)
    x_ref, up_ref, wq_ref, wo_ref, wi_ref, wd_ref = refs[:6]
    hot_buf, mask_ref, key_ref, bq_ref, bi_ref, vec_ref = refs[6:12]
    w_ref, up_out, x_out = refs[12:15]
    saved = [refs[15 + PER_LAYER * l : 15 + PER_LAYER * (l + 1)] for l in range(layers)]
    (
        x, acc, r_buf, low, xb, qkv, kv_sib, ctx, lse, hl, g_all, slope_all,
        col_buf, row_buf, turn_buf, made_buf, wa_buf, wb_buf,
        feed_sem, load_sem, col_sem, row_sem, made_sem, store_sem, block_sem,
        core_send, core_recv, kv_send, kv_recv, g_send, g_recv, spread_send, spread_recv,
    ) = refs[15 + PER_LAYER * layers :]
    rows, width = acc.shape
    dp, y = lax.axis_index("dp"), lax.axis_index("tensor")
    core = dp % 2
    stays = core == y
    spread = Spread(w_ref, layers * GROUPS // 2, spread_send, spread_recv)
    greet((FLIP_Y, FLIP_X, FLIP_Z0, FLIP_C, SWAP))

    def feed(n, slot, source, target):
        return pltpu.make_async_copy(source, target, feed_sem.at[n, slot])

    def load(n, source, target):
        return pltpu.make_async_copy(source, target, load_sem.at[n])

    def store(n, source, target):
        return pltpu.make_async_copy(source, target, store_sem.at[n])

    def exchange(n, source, target, bits=FLIP_C):
        return pltpu.make_async_remote_copy(
            src_ref=source, dst_ref=target, send_sem=core_send.at[n], recv_sem=core_recv.at[n],
            device_id=partner(bits), device_id_type=MESH,
        )

    def columns(ref, i, size):
        return ref.at[:, pl.ds(pl.multiple_of(i * size, size), size)]

    def swap(n, source, target, begin):
        here = store(n, source, target)
        there = exchange(n, source, target, SWAP)

        @pl.when(stays)
        def _():
            here.start() if begin else here.wait()

        @pl.when(jnp.logical_not(stays))
        def _():
            there.start() if begin else there.wait()

    items = []
    for l in range(layers):
        items += [(True, wq_ref.at[l, t], l * GROUPS + t) for t in range(3)]
        items += [(False, wo_ref.at[l], l * GROUPS + OUT_GROUP)]
        for n in range(FF_GROUPS):
            items += [(True, wi_ref.at[l, :, pl.ds(n * 512, 512)], l * GROUPS + in_group(n))]
            items += [(False, wd_ref.at[l, pl.ds(n * 512, 512)], l * GROUPS + down_group(n))]
    fetches, counts, ahead = [], [0, 0], [[], []]
    for m, (turned, source, group) in enumerate(items):
        slot = counts[turned] % DEPTH
        buf, sem = (col_buf, col_sem) if turned else (row_buf, row_sem)
        fetches.append((pltpu.make_async_copy(source, buf.at[slot], sem.at[slot]), slot))
        ahead[turned].append(m)
        counts[turned] += 1
    bits = [(dp // step) % 2 for step in (1, 2, 4, 8)]
    made = {}

    def convert(m):
        turned, _, group = items[m]
        copy, slot = fetches[m]
        copy.wait()
        if turned:

            def turn(i, _):
                turn_buf[pl.ds(pl.multiple_of(i * 128, 128), 128), :] = col_buf[
                    slot, :, pl.ds(pl.multiple_of(i * 128, 128), 128)
                ].T
                return 0

            lax.fori_loop(0, 4, turn, 0)
        if m >= 2:
            made[m - 2].wait()

        def block(j, _):
            where = 0
            for bit, weight in zip(bits, (8, 4, 2, 1)):
                own = (j // weight) % 2
                where = where + weight * (own + bit - 2 * own * bit)
            at = pl.ds(pl.multiple_of(where * 32, 32), 32)
            rows_32 = turn_buf[at, :] if turned else row_buf[slot, at, :]
            made_buf[m % 2, pl.ds(pl.multiple_of(j * 32, 32), 32), :] = rows_32.astype(BF16)
            return 0

        lax.fori_loop(0, 16, block, 0)
        later = [n for n in ahead[turned] if n > m]
        if len(later) >= DEPTH:
            fetches[later[DEPTH - 1]][0].start()
        parts = [
            pltpu.make_async_copy(
                made_buf.at[m % 2, pl.ds(a * 256, 256)], w_ref.at[a, group, 0], made_sem.at[m % 2, a]
            )
            for a in range(2)
        ]

        class Both:
            def wait(self):
                for part in parts:
                    part.wait()

        for part in parts:
            part.start()
        made[m] = Both()

    load_x = load(0, x_ref.at[:, 0], x)
    load_x.start()
    load_up = load(1, up_ref.at[:, 0], acc)
    load_up.start()
    for kind in range(2):
        for m in ahead[kind][:DEPTH]:
            fetches[m][0].start()
    load_x.wait()

    def narrow_x(at):
        low[at, :] = x[at, :].astype(BF16)

    row_tiles(rows, narrow_x)
    swap(0, low, xb, True)
    load_up.wait()

    def narrow_up(at):
        hl[at, :] = acc[at, :].astype(BF16)

    row_tiles(rows, narrow_up)
    swap(1, hl, up_out, True)

    for m in range(len(items)):
        convert(m)
        if m % 4 == 3:
            spread.tick(m // 4)
    for m in range(len(items) - 2, len(items)):
        made[m].wait()
    swap(0, low, xb, False)
    swap(1, hl, up_out, False)

    def widen(at):
        x[at, :] = xb[at, :].astype(F32)

    row_tiles(rows, widen)

    pairs = width // 128
    for l in range(layers):
        (
            qkv_out, sib_out, ctx_out, ctx_sib_out, lse_out, r1_out, r2_out, hl_out, hl_sib_out,
            g_out, g_sib_out, slope_out, xb_out, xb_sib_out,
        ) = saved[l]
        first = l * GROUPS
        clock = 6 + 6 * l
        xb_store = store(0, xb, xb_out)
        xb_store.start()
        xb_copy = exchange(2 + 3 * l, xb, xb_sib_out)
        xb_copy.start()

        def give_kv(n, a):
            at = pl.ds(pl.multiple_of(a * 512, 512), 512)
            return pltpu.make_async_remote_copy(
                src_ref=qkv.at[1 + n, :, at], dst_ref=kv_sib.at[n, :, at],
                send_sem=kv_send.at[n, a], recv_sem=kv_recv.at[n, a],
                device_id=partner(FLIP_C), device_id_type=MESH,
            )

        def which(i):
            n = lax.div(i, 2)
            return 1 - n + 3 * lax.div(n, 2), lax.rem(i, 2)

        def qkv_feeds(i, slot):
            t, a = which(i)
            return (feed(0, slot, w_ref.at[a, first + t], wa_buf.at[slot]),)

        def qkv_body(i, slot):
            t, a = which(i)
            at = pl.ds(pl.multiple_of(a * 512, 512), 512)
            qkv[t, :, at] = (nt(xb[...], block_of(wa_buf.at[slot])) + bq_ref[l, t, a]).astype(BF16)
            pl.when(t > 0)(lambda: give_kv(t - 1, a).start())
            pl.when(i == 2)(lambda: spread.tick(clock))

        stream(6, qkv_feeds, qkv_body)
        qkv_store = store(1, qkv, qkv_out)
        qkv_store.start()
        for n in range(2):
            for a in range(2):
                give_kv(n, a).wait()
        sib_store = store(2, kv_sib, sib_out)
        sib_store.start()

        def pair_body(p, _):
            far = lax.rem(p + pairs // 2, pairs)
            here = pl.ds(pl.multiple_of(p * 128, 128), 128)
            there = pl.ds(pl.multiple_of(far * 128, 128), 128)
            mask = [spread_mask(mask_ref[2 * p + e], key_ref[...]) for e in range(2)]
            keys = jnp.concatenate([qkv[1, :, here], kv_sib[0, :, there]], axis=0)
            values = jnp.concatenate([qkv[2, :, here], kv_sib[1, :, there]], axis=0)
            context, parts = attend_pair(qkv[0, :, here], keys, values, hot_buf[...], mask)
            ctx[:, here] = context.astype(BF16)
            for e in range(2):
                lse[p, e : e + 1, :] = parts[e]
            pl.when(lax.rem(p, 5) == 2)(lambda: spread.tick(clock + 1 + lax.div(p, 5)))
            return 0

        lax.fori_loop(0, pairs, pair_body, 0)
        ctx_store = store(3, ctx, ctx_out)
        ctx_store.start()
        lse_store = store(4, lse, lse_out)
        lse_store.start()
        ctx_copy = exchange(3 + 3 * l, ctx.at[:, pl.ds(512, 512)], ctx_sib_out)
        ctx_copy.start()

        def out_feeds(i, slot):
            return (feed(0, slot, w_ref.at[i, first + OUT_GROUP], wa_buf.at[slot]),)

        def out_body(i, slot):
            part = nn(ctx[:, pl.ds(pl.multiple_of(i * 512, 512), 512)], block_of(wa_buf.at[slot]))

            @pl.when(i == 0)
            def _():
                acc[...] = part

            @pl.when(i == 1)
            def _():
                acc[...] += part

        stream(2, out_feeds, out_body)
        sib_store.wait()

        def first_norm(at):
            r1 = x[at, :] + acc[at, :] + vec_ref[l, 0:1, :]
            r_buf[at, :] = r1
            h = norm(r1, vec_ref[l, 1:2, :], vec_ref[l, 2:3, :])
            hl[at, :] = h.astype(BF16)
            acc[at, :] = h + vec_ref[l, 3:4, :]

        row_tiles(rows, first_norm)
        r1_store = store(5, r_buf, r1_out)
        r1_store.start()
        hl_store = store(6, hl, hl_out)
        hl_store.start()
        hl_copy = exchange(4 + 3 * l, hl, hl_sib_out)
        hl_copy.start()

        def place_of(i):
            return 1 - lax.rem(i, 2), lax.div(i, 2)

        def ff_feeds(i, slot):
            a, n = place_of(i)
            return (
                feed(0, slot, w_ref.at[a, first + in_group(n)], wa_buf.at[slot]),
                feed(2, slot, w_ref.at[a, first + down_group(n)], wb_buf.at[slot]),
            )

        def g_store(j):
            return pltpu.make_async_copy(g_all.at[j], columns(g_out, j, 512), block_sem.at[0, j])

        def slope_store(j):
            return pltpu.make_async_copy(slope_all.at[j], columns(slope_out, j, 512), block_sem.at[1, j])

        def g_copy(n):
            return pltpu.make_async_remote_copy(
                src_ref=g_all.at[FF_GROUPS + n], dst_ref=columns(g_sib_out, n, 512),
                send_sem=g_send.at[l, n], recv_sem=g_recv.at[l, n],
                device_id=partner(FLIP_C), device_id_type=MESH,
            )

        def ff_body(i, slot):
            a, n = place_of(i)
            j = a * FF_GROUPS + n
            u = nt(hl[...], block_of(wa_buf.at[slot])) + bi_ref[l, a, n]
            g, slope = gelu_and_slope(u)
            g = g.astype(BF16)
            g_all[j] = g
            slope_all[j] = slope.astype(BF16)
            g_store(j).start()
            slope_store(j).start()
            pl.when(a == 1)(lambda: g_copy(n).start())
            acc[...] += nn(g, block_of(wb_buf.at[slot]))
            pl.when(lax.rem(i, 3) == 1)(lambda: spread.tick(clock + 3 + lax.div(i, 3)))

        stream(2 * FF_GROUPS, ff_feeds, ff_body)
        r1_store.wait()
        xb_store.wait()
        xb_copy.wait()

        def second_norm(at):
            r2 = acc[at, :]
            r_buf[at, :] = r2
            x2 = norm(r2, vec_ref[l, 4:5, :], vec_ref[l, 5:6, :])
            x[at, :] = x2
            xb[at, :] = x2.astype(BF16)

        row_tiles(rows, second_norm)
        r2_store = store(5, r_buf, r2_out)
        r2_store.start()
        if l == layers - 1:
            x_store = store(10, xb, x_out)
            x_store.start()

        def settle(j, _):
            g_store(j).wait()
            slope_store(j).wait()
            return 0

        lax.fori_loop(0, 2 * FF_GROUPS, settle, 0)

        def settle_sent(n, _):
            g_copy(n).wait()
            return 0

        lax.fori_loop(0, FF_GROUPS, settle_sent, 0)
        for copy in (qkv_store, ctx_store, lse_store, ctx_copy, hl_store, hl_copy, r2_store):
            copy.wait()
    x_store.wait()


def forward(block_input, cotangent, w_qkv, w_out, w_in, w_down, hot, mask, mask_rows, bias_qkv, bias_in, vectors):
    rows, _, width = block_input.shape
    layers = w_qkv.shape[0]
    total = layers * GROUPS
    anywhere = pl.BlockSpec(memory_space=pl.ANY)
    in_vmem = pl.BlockSpec(memory_space=pltpu.VMEM)
    low = lambda *shape: pltpu.VMEM(shape, BF16)
    full = lambda *shape: pltpu.VMEM(shape, F32)
    dma = lambda *shape: pltpu.SemaphoreType.DMA(shape)
    low_out = lambda *shape: jax.ShapeDtypeStruct(shape, BF16)
    full_out = lambda *shape: jax.ShapeDtypeStruct(shape, F32)
    layer_out = (
        low_out(3, rows, width),
        low_out(2, rows, width),
        low_out(rows, width),
        low_out(rows, width // 2),
        full_out(width // 128, 2, rows),
        full_out(rows, width),
        full_out(rows, width),
        low_out(rows, width),
        low_out(rows, width),
        low_out(rows, 4 * width),
        low_out(rows, 2 * width),
        low_out(rows, 4 * width),
        low_out(rows, width),
        low_out(rows, width),
    )
    outs = pl.pallas_call(
        functools.partial(forward_kernel, layers),
        out_shape=(low_out(2, total, 2, 256, width), low_out(rows, width), low_out(rows, width)) + layer_out * layers,
        in_specs=[anywhere] * 6 + [in_vmem] * 6,
        out_specs=(anywhere,) * (3 + PER_LAYER * layers),
        scratch_shapes=[
            full(rows, width),
            full(rows, width),
            full(rows, width),
            low(rows, width),
            low(rows, width),
            low(3, rows, width),
            low(2, rows, width),
            low(rows, width),
            full(width // 128, 2, rows),
            low(rows, width),
            low(2 * FF_GROUPS, rows, 512),
            low(2 * FF_GROUPS, rows, 512),
            full(DEPTH, width, 512),
            full(DEPTH, 512, width),
            full(512, width),
            low(2, 512, width),
            low(2, 2, 256, width),
            low(2, 2, 256, width),
            dma(3, 2),
            dma(3),
            dma(DEPTH),
            dma(DEPTH),
            dma(2, 2),
            dma(11),
            dma(2, 2 * FF_GROUPS),
            dma(11),
            dma(11),
            dma(2, 2),
            dma(2, 2),
            dma(layers, FF_GROUPS),
            dma(layers, FF_GROUPS),
            dma(9, total // 2),
            dma(9, total // 2),
        ],
        compiler_params=pltpu.CompilerParams(collective_id=0, has_side_effects=True, vmem_limit_bytes=60 << 20),
        cost_estimate=pl.CostEstimate(flops=30 << 30, bytes_accessed=300 << 20, transcendentals=1 << 24),
        name="forward",
    )(block_input, cotangent, w_qkv, w_out, w_in, w_down, hot, mask, mask_rows, bias_qkv, bias_in, vectors)
    saved = [outs[3 + PER_LAYER * l : 3 + PER_LAYER * (l + 1)] for l in range(layers)]
    return outs[0], outs[1], outs[2], saved


def backward_kernel(layers, *refs):
    refs = list(refs)
    up_ref, x_ref, w_ref, hot_buf, mask_ref, key_ref, vec_ref = refs[:7]
    saved = [refs[7 + PER_LAYER * l : 7 + PER_LAYER * (l + 1)] for l in range(layers)]
    at_ref = 7 + PER_LAYER * layers
    grads, sums, dx_out, x_out, dbi_ref, qkv_sums_ref, small_ref = refs[at_ref : at_ref + 7]
    (
        acc, dr1, dm, dm_sib, da, da_sib, du, du_sib, dctx, dqkv, d_sib, kv_out, kv_far,
        wa_buf, wb_buf, r_buf, slope_buf, left_buf, left_sib_buf, right_buf, right_sib_buf,
        pair_buf, lse_buf, unit_buf,
        y_buf, x_buf, z0_buf, z1_buf, all_buf, keep_buf,
        feed_sem, load_sem, store_sem, swap_sem, core_send, core_recv, du_send, du_recv,
        send_sem, recv_sem, sum_send, sum_recv, keep_sem, out_sem, in_free, out_free,
    ) = refs[at_ref + 7 :]
    rows, width = acc.shape
    total = layers * GROUPS
    reduction = Reduction(
        grads, sums, 2 * total,
        (y_buf, x_buf, z0_buf, z1_buf, all_buf, keep_buf),
        (send_sem, recv_sem, sum_send, sum_recv, keep_sem, out_sem, in_free, out_free),
    )
    greet((FLIP_Y, FLIP_X, FLIP_Z0, FLIP_Z1, FLIP_C, SWAP))

    def feed(n, slot, source, target):
        return pltpu.make_async_copy(source, target, feed_sem.at[n, slot])

    def load(n, source, target):
        return pltpu.make_async_copy(source, target, load_sem.at[n])

    def exchange(n, source, target):
        return pltpu.make_async_remote_copy(
            src_ref=source, dst_ref=target, send_sem=core_send.at[n], recv_sem=core_recv.at[n],
            device_id=partner(FLIP_C), device_id_type=MESH,
        )

    def give_du(j, n):
        return pltpu.make_async_remote_copy(
            src_ref=du.at[j], dst_ref=du_sib.at[n], send_sem=du_send.at[n], recv_sem=du_recv.at[n],
            device_id=partner(FLIP_C), device_id_type=MESH,
        )

    def weight(a, group):
        return w_ref.at[a, group]

    def columns(ref, i, size):
        return ref.at[:, pl.ds(pl.multiple_of(i * size, size), size)]

    def unit(left, left_sib, right, right_sib, index):
        made = (tn(left, right) + tn(left_sib, right_sib)).astype(BF16)
        unit_buf[...] = made.reshape(unit_buf.shape)
        store = pltpu.make_async_copy(unit_buf, grads.at[index], store_sem.at[0])
        store.start()
        store.wait()

    def add_small(l, row, value):
        small_ref[l, row : row + 1, :] += jnp.sum(value, axis=0, keepdims=True)

    stays = lax.axis_index("dp") % 2 == lax.axis_index("tensor")

    def swap(n, source, target, begin):
        here = pltpu.make_async_copy(source, target, swap_sem.at[n])
        there = pltpu.make_async_remote_copy(
            src_ref=source, dst_ref=target, send_sem=core_send.at[4 + n], recv_sem=core_recv.at[4 + n],
            device_id=partner(SWAP), device_id_type=MESH,
        )

        @pl.when(stays)
        def _():
            here.start() if begin else here.wait()

        @pl.when(jnp.logical_not(stays))
        def _():
            there.start() if begin else there.wait()

    swap(1, x_ref, x_out, True)
    start_up = load(0, up_ref, da)
    start_up.start()
    start_up.wait()
    small_ref[...] = jnp.zeros_like(small_ref)

    def widen(at):
        acc[at, :] = da[at, :].astype(F32)

    row_tiles(rows, widen)
    done = 0
    for l in reversed(range(layers)):
        qkv_ref, sib_ref, ctx_ref, ctx_sib_ref, lse_ref, r1_ref, r2_ref, hl_ref, hl_sib_ref, g_ref, g_sib_ref, slope_ref, xb_ref, xb_sib_ref = saved[l]
        first = l * GROUPS
        base = (layers - 1 - l) * GROUPS
        clock = 22 * (layers - 1 - l)

        r_load = load(0, r2_ref, r_buf)
        r_load.start()
        r_load.wait()

        def second(at):
            dy = acc[at, :]
            dr, part = norm_back(dy, r_buf[at, :], vec_ref[l, 4:5, :])
            acc[at, :] = dr
            dm[at, :] = dr.astype(BF16)
            add_small(l, 0, part)
            add_small(l, 1, dy)
            add_small(l, 2, dr)

        row_tiles(rows, second)
        dm_copy = exchange(0, dm, dm_sib)
        dm_copy.start()
        r_load = load(0, r1_ref, r_buf)
        r_load.start()
        right_load = load(1, hl_ref, right_buf)
        right_load.start()
        right_sib_load = load(2, hl_sib_ref, right_sib_buf)
        right_sib_load.start()
        dm_copy.wait()

        def down_feeds(i, slot):
            return (
                feed(0, slot, columns(g_ref, i, 512), left_buf.at[slot]),
                feed(1, slot, columns(g_sib_ref, i, 512), left_sib_buf.at[slot]),
            )

        def down_body(i, slot):
            unit(left_buf[slot], left_sib_buf[slot], dm[...], dm_sib[...], base + i)
            reduction.tick(clock + i)

        stream(FF_GROUPS, down_feeds, down_body)

        def place_of(i):
            a = 1 - lax.div(i, FF_GROUPS)
            return a, lax.rem(i, FF_GROUPS)

        def ff_feeds(i, slot):
            a, n = place_of(i)
            j = a * FF_GROUPS + n
            return (
                feed(0, slot, weight(a, first + down_group(n)), wa_buf.at[slot]),
                feed(1, slot, weight(a, first + in_group(n)), wb_buf.at[slot]),
                feed(2, slot, columns(slope_ref, j, 512), slope_buf.at[slot]),
            )

        def ff_body(i, slot):
            a, n = place_of(i)
            j = a * FF_GROUPS + n
            dg = nt(dm[...], block_of(wa_buf.at[slot]))
            d = (dg * slope_buf[slot].astype(F32)).astype(BF16)
            du[j] = d
            pl.when(a == 1)(lambda: give_du(j, n).start())
            dbi_ref[l, a, n] = jnp.sum(d.astype(F32), axis=0, keepdims=True)
            acc[...] += nn(d, block_of(wb_buf.at[slot]))
            pl.when(lax.rem(i, 2) == 1)(lambda: reduction.tick(clock + 4 + lax.div(i, 2)))

        stream(2 * FF_GROUPS, ff_feeds, ff_body)

        r_load.wait()

        def first_norm(at):
            dy = acc[at, :]
            dr, part = norm_back(dy, r_buf[at, :], vec_ref[l, 1:2, :])
            dr1[at, :] = dr
            da[at, :] = dr.astype(BF16)
            add_small(l, 3, part)
            add_small(l, 4, dy)
            add_small(l, 5, dr)

        row_tiles(rows, first_norm)
        da_copy = exchange(1, da, da_sib)
        da_copy.start()

        def out_feeds(i, slot):
            return (feed(0, slot, weight(i, first + OUT_GROUP), wa_buf.at[slot]),)

        def out_body(i, slot):
            dctx[:, pl.ds(pl.multiple_of(i * 512, 512), 512)] = nt(da[...], block_of(wa_buf.at[slot])).astype(BF16)

        stream(2, out_feeds, out_body)

        right_load.wait()
        right_sib_load.wait()

        def in_body(n, _):
            give_du(FF_GROUPS + n, n).wait()
            unit(du[n], du_sib[n], right_buf[...], right_sib_buf[...], base + FF_GROUPS + n)
            reduction.tick(clock + 8 + n)
            return 0

        lax.fori_loop(0, FF_GROUPS, in_body, 0)

        right_load = load(1, xb_ref, right_buf)
        right_load.start()
        right_sib_load = load(2, xb_sib_ref, right_sib_buf)
        right_sib_load.start()
        left_load = load(3, columns(ctx_ref, 0, 512), left_buf.at[0])
        left_load.start()
        left_sib_load = load(4, ctx_sib_ref, left_sib_buf.at[0])
        left_sib_load.start()
        da_copy.wait()
        left_load.wait()
        left_sib_load.wait()
        unit(left_buf[0], left_sib_buf[0], da[...], da_sib[...], base + 2 * FF_GROUPS)

        pairs = width // 128

        def pair_feeds(p, slot):
            far = lax.rem(p + pairs // 2, pairs)
            return (
                feed(0, slot, columns(qkv_ref.at[0], p, 128), pair_buf.at[slot, 0, pl.ds(0, rows)]),
                feed(1, slot, columns(qkv_ref.at[1], p, 128), pair_buf.at[slot, 1, pl.ds(0, rows)]),
                feed(2, slot, columns(sib_ref.at[0], far, 128), pair_buf.at[slot, 1, pl.ds(rows, rows)]),
                feed(3, slot, columns(qkv_ref.at[2], p, 128), pair_buf.at[slot, 2, pl.ds(0, rows)]),
                feed(4, slot, columns(sib_ref.at[1], far, 128), pair_buf.at[slot, 2, pl.ds(rows, rows)]),
                feed(5, slot, columns(ctx_ref, p, 128), pair_buf.at[slot, 3, pl.ds(0, rows)]),
                feed(6, slot, lse_ref.at[p], lse_buf.at[slot]),
            )

        def pair_body(p, slot):
            far = lax.rem(p + pairs // 2, pairs)
            here = pl.ds(pl.multiple_of(p * 128, 128), 128)
            mask = [spread_mask(mask_ref[2 * p + e], key_ref[...]) for e in range(2)]
            dq, dk, dv = attend_back_pair(
                pair_buf[slot, 0, 0:rows], pair_buf[slot, 1], pair_buf[slot, 2], hot_buf[...], mask,
                pair_buf[slot, 3, 0:rows], lse_buf[slot], dctx[:, here],
            )
            dqkv[0, :, here] = dq.astype(BF16)
            dqkv[1, :, here] = dk[:rows].astype(BF16)
            dqkv[2, :, here] = dv[:rows].astype(BF16)
            there = pl.ds(pl.multiple_of(far * 128, 128), 128)
            kv_out[0, :, there] = dk[rows:].astype(BF16)
            kv_out[1, :, there] = dv[rows:].astype(BF16)
            pl.when(lax.rem(p, 4) < 3)(lambda: reduction.tick(clock + 12 + 3 * lax.div(p, 4) + lax.rem(p, 4)))

        stream(pairs, pair_feeds, pair_body)
        kv_copy = exchange(2, kv_out, kv_far)
        kv_copy.start()
        kv_copy.wait()
        for n in range(2):
            add_rows(dqkv.at[1 + n], kv_far.at[n], rows)
        d_copy = exchange(3, dqkv.at[:, :, pl.ds(512, 512)], d_sib)
        d_copy.start()
        right_load.wait()
        right_sib_load.wait()
        d_copy.wait()

        def qkv_body(n, _):
            unit(dqkv[n, :, 0:512], d_sib[n], right_buf[...], right_sib_buf[...], base + 2 * FF_GROUPS + 1 + n)
            pl.when(n > 0)(lambda: reduction.tick(clock + 17 + n))
            return 0

        lax.fori_loop(0, 3, qkv_body, 0)

        def start_dx(at):
            acc[at, :] = dr1[at, :]

        row_tiles(rows, start_dx)

        def dx_feeds(i, slot):
            return (feed(0, slot, weight(lax.rem(i, 2), first + lax.div(i, 2)), wa_buf.at[slot]),)

        def dx_body(i, slot):
            a, n = lax.rem(i, 2), lax.div(i, 2)
            d = dqkv[n, :, pl.ds(pl.multiple_of(a * 512, 512), 512)]
            qkv_sums_ref[l, n, a] = jnp.sum(d.astype(F32), axis=0, keepdims=True)
            acc[...] += nn(d, block_of(wa_buf.at[slot]))
            pl.when(lax.rem(i, 3) == 2)(lambda: reduction.tick(clock + 20 + lax.div(i, 3)))

        stream(6, dx_feeds, dx_body)
        done = clock + 22

    def narrow(at):
        da[at, :] = acc[at, :].astype(BF16)

    row_tiles(rows, narrow)
    swap(0, da, dx_out, True)

    def rest(t, _):
        reduction.tick(t)
        return 0

    lax.fori_loop(done, 2 * total + LAST_TICK, rest, 0)
    swap(0, da, dx_out, False)
    swap(1, x_ref, x_out, False)


def backward(upstream, stream_low, weights, hot, mask, mask_rows, vectors, saved):
    rows, width = upstream.shape
    layers = len(saved)
    total = layers * GROUPS
    anywhere = pl.BlockSpec(memory_space=pl.ANY)
    in_vmem = pl.BlockSpec(memory_space=pltpu.VMEM)
    low = lambda *shape: pltpu.VMEM(shape, BF16)
    dma = lambda *shape: pltpu.SemaphoreType.DMA(shape)
    return pl.pallas_call(
        functools.partial(backward_kernel, layers),
        out_shape=(
            jax.ShapeDtypeStruct((total, 16, 32, width), BF16),
            jax.ShapeDtypeStruct((total, 16, 32, width), BF16),
            jax.ShapeDtypeStruct((rows, width), BF16),
            jax.ShapeDtypeStruct((rows, width), BF16),
            jax.ShapeDtypeStruct((layers, 2, FF_GROUPS, 1, 512), F32),
            jax.ShapeDtypeStruct((layers, 3, 2, 1, 512), F32),
            jax.ShapeDtypeStruct((layers, 8, width), F32),
        ),
        in_specs=[anywhere] * 3 + [in_vmem] * 4 + [anywhere] * (PER_LAYER * layers),
        out_specs=(anywhere, anywhere, anywhere, anywhere, in_vmem, in_vmem, in_vmem),
        scratch_shapes=[
            pltpu.VMEM((rows, width), F32),
            pltpu.VMEM((rows, width), F32),
            low(rows, width),
            low(rows, width),
            low(rows, width),
            low(rows, width),
            low(2 * FF_GROUPS, rows, 512),
            low(FF_GROUPS, rows, 512),
            low(rows, width),
            low(3, rows, width),
            low(3, rows, 512),
            low(2, rows, width),
            low(2, rows, width),
            low(2, 2, 256, width),
            low(2, 2, 256, width),
            pltpu.VMEM((rows, width), F32),
            low(2, rows, 512),
            low(2, rows, 512),
            low(2, rows, 512),
            low(rows, width),
            low(rows, width),
            low(2, 4, 2 * rows, 128),
            pltpu.VMEM((2, 2, rows), F32),
            low(16, 32, width),
            low(SLOTS, 8, 16, width),
            low(SLOTS, 4, 16, width),
            low(SLOTS, 2, 16, width),
            low(SLOTS, 1, 16, width),
            low(SLOTS, 8, 16, width),
            low(2, 8, 16, width),
            dma(8, 2),
            dma(5),
            dma(1),
            dma(2),
            dma(6),
            dma(6),
            dma(FF_GROUPS),
            dma(FF_GROUPS),
            dma(7, SLOTS),
            dma(7, SLOTS),
            dma(2 * total),
            dma(2 * total),
            dma(2),
            dma(SLOTS),
            pltpu.SemaphoreType.REGULAR((4,)),
            pltpu.SemaphoreType.REGULAR((3,)),
        ],
        compiler_params=pltpu.CompilerParams(
            collective_id=1, has_side_effects=True, vmem_limit_bytes=60 << 20
        ),
        cost_estimate=pl.CostEstimate(flops=60 << 30, bytes_accessed=300 << 20, transcendentals=1 << 24),
        name="backward",
    )(upstream, stream_low, weights, hot, mask, mask_rows, vectors, *[ref for one in saved for ref in one])


def flip_order(values, axis, bits):
    for i, bit in enumerate(bits):
        values = jnp.where(bit == 0, values, jnp.flip(values, axis + i))
    return values


def sequence_shards(
    block_input, segment_ids, random_blocks, w_qkv, b_qv, w_out, b_out, w_in, b_in, w_down, b_down,
    ln_gain, ln_bias, cotangent,
):
    y = lax.axis_index("tensor")
    dp = lax.axis_index("dp")
    core, x_bit, z0, z1 = dp % 2, (dp // 2) % 2, (dp // 4) % 2, dp // 8
    code = core * 8 + x_bit * 4 + z0 * 2 + z1
    code_arg = code.reshape(1).astype(jnp.int32)
    device_bits = (core, x_bit, z0, z1)

    rows, _, width = block_input.shape
    layers = w_qkv.shape[0]
    blocks = random_blocks.shape[2]
    own_blocks = blocks // 2
    heads = random_blocks.shape[1] * 2

    chosen = random_blocks[0]
    near = jnp.concatenate([chosen.reshape(-1), segment_ids[0]])
    sibling = flip(near, FLIP_C)
    across, diagonal = flip(chosen.reshape(-1), FLIP_Y), flip(chosen.reshape(-1), SWAP)
    mine = jnp.concatenate([near[: chosen.size], across, near[chosen.size :]])
    other = jnp.concatenate([sibling[: chosen.size], diagonal, sibling[chosen.size :]])
    packed = jnp.where(core == y, mine, other)
    chosen = packed[: 2 * chosen.size].reshape(2, heads // 2, blocks, -1)
    segments = packed[2 * random_blocks.size :]
    chosen = flip_order(chosen.reshape(2, 2, 2, 2, blocks, -1), 1, device_bits[:3])
    chosen = chosen.transpose(1, 0, 2, 3, 4, 5).reshape(heads, blocks, -1)
    segments = segments.reshape(2, rows)
    segments = jnp.where(core == 0, segments, segments[::-1]).reshape(-1)
    query_block = core * own_blocks + jnp.arange(own_blocks)
    key_block = jnp.arange(blocks) ^ (core * own_blocks)
    allowed = (
        (jnp.abs(query_block[:, None] - key_block[None, :]) <= 1)
        | (key_block[None, :] == 0)
        | (key_block[None, :] == blocks - 1)
        | (query_block[:, None] == 0)
        | (query_block[:, None] == blocks - 1)
    )
    chosen = lax.dynamic_slice_in_dim(chosen, core * own_blocks, own_blocks, axis=1)
    allowed = allowed[None] | jnp.any(chosen[:, :, None, :] == key_block[None, None, :, None], axis=3)
    block_rows = rows // own_blocks
    documents = jnp.arange(128 - own_blocks)
    mask = jnp.pad(
        jnp.where(allowed, 0.0, BIG).astype(F32).transpose(0, 2, 1), ((0, 0), (0, 0), (0, 128 - own_blocks))
    )
    document_part = jnp.where(
        (segments[:, None] == documents[None, :]) | (documents[None, :] > 7), 0.0, BIG
    ).astype(F32)
    mask_rows = jnp.pad(document_part, ((0, 0), (own_blocks, 0)))
    block_rows = rows // own_blocks
    hot = jnp.concatenate(
        [
            jnp.repeat(jnp.eye(own_blocks, dtype=BF16), block_rows, axis=0),
            (segments[:rows, None] == documents[None, :]).astype(BF16),
        ],
        axis=1,
    )

    bias_pack = jnp.concatenate(
        [
            flip_order(b_qv.reshape(layers * 2, 2, 2, 2, 2, -1), 1, device_bits).reshape(-1),
            flip_order(b_in.reshape(layers * FF_GROUPS, 2, 2, 2, 2, -1), 1, device_bits).reshape(-1),
        ]
    )
    bias_far = flip(bias_pack, FLIP_Y)
    n_qv = b_qv.size

    def local_bias(near, far, count):
        near, far = near.reshape(count, 2, 1, 256), far.reshape(count, 2, 1, 256)
        return jnp.concatenate([near, far], axis=2).reshape(count, 2, 512)

    bias_qv = local_bias(bias_pack[:n_qv], bias_far[:n_qv], layers * 2).reshape(layers, 2, 2, 1, 512)
    bias_qkv = jnp.stack([bias_qv[:, 0], jnp.zeros_like(bias_qv[:, 0]), bias_qv[:, 1]], axis=1)
    bias_in = local_bias(bias_pack[n_qv:], bias_far[n_qv:], layers * FF_GROUPS)
    bias_in = bias_in.reshape(layers, FF_GROUPS, 2, 1, 512).swapaxes(1, 2)

    vectors = [
        jnp.stack(
            [
                b_out[l], ln_gain[l, 0], ln_bias[l, 0], b_down[l], ln_gain[l, 1], ln_bias[l, 1],
                b_out[l], b_out[l],
            ]
        )
        for l in range(layers)
    ]
    vectors = jnp.stack(vectors)
    weights, upstream_low, stream_low, saved = forward(
        block_input, cotangent, w_qkv, w_out, w_in, w_down, hot, mask, mask_rows, bias_qkv, bias_in, vectors
    )
    _, grads, dx_low, x_low, d_b_in, qkv_sums, rows_small = backward(
        upstream_low, stream_low, weights, hot, mask, mask_rows, vectors, saved
    )
    grads = grads.reshape(layers * GROUPS, 512, width)
    block_output, input_grad = widen_rows(x_low, dx_low)

    stacks = [
        jnp.stack([qkv_sums[:, 0], qkv_sums[:, 2]], axis=1),
        rows_small[:, 5],
        d_b_in.swapaxes(1, 2),
        rows_small[:, 2],
        jnp.stack([rows_small[:, 3], rows_small[:, 0]], axis=1),
        jnp.stack([rows_small[:, 4], rows_small[:, 1]], axis=1),
    ]

    def global_order(values, lead):
        values = values.reshape(lead, 2, 2, 2, 2, 2, 32).swapaxes(1, 2)
        values = flip_order(values, 1, (y,) + device_bits)
        return values.swapaxes(0, 1).reshape(2, -1)

    stacks[0] = global_order(stacks[0], layers * 2)
    stacks[2] = global_order(stacks[2], layers * FF_GROUPS)
    def placing(shape, block, index, turned, count, start):
        return lambda values: place(
            values, shape, block, index, turned, count, lambda l, i: (layers - 1 - l) * GROUPS + start + i, code_arg
        )

    summed = jnp.concatenate([s.reshape(-1) for s in stacks])
    summed = summed + flip(summed, FLIP_C)
    placed = []
    for bit, put in (
        (FLIP_Y, placing(w_down.shape, (1, 512, width), lambda l, i: (l, i, 0), False, FF_GROUPS, 0)),
        (FLIP_X, placing(w_in.shape, (1, width, 512), lambda l, i: (l, 0, i), True, FF_GROUPS, FF_GROUPS)),
        (FLIP_Z0, placing(w_qkv.shape, (1, 1, width, 512), lambda l, i: (l, i, 0, 0), True, 3, 2 * FF_GROUPS + 1)),
        (FLIP_Z1, placing(w_out.shape, (1, 512, width), lambda l, i: (l, 0, 0), False, 1, 2 * FF_GROUPS)),
    ):
        summed, grads = lax.optimization_barrier((summed, grads))
        far = flip(summed, bit)
        done, summed, far = lax.optimization_barrier((put(grads), summed, far))
        placed.append(done)
        summed = summed + far
    parts, at = [], 0
    for s in stacks:
        parts.append(summed[at : at + s.size].reshape(s.shape))
        at += s.size
    g_b_qv = lax.dynamic_index_in_dim(parts[0], y, axis=0, keepdims=False).reshape(b_qv.shape)
    g_b_in = lax.dynamic_index_in_dim(parts[2], y, axis=0, keepdims=False).reshape(b_in.shape)
    return (
        block_output,
        input_grad,
        placed[2],
        g_b_qv,
        placed[3],
        parts[1],
        placed[1],
        g_b_in,
        placed[0],
        parts[3],
        parts[4],
        parts[5],
    )


def as_sent(array):

    def short(part):
        return part.astype(jnp.bfloat16) if part.dtype == jnp.float32 else part

    return jax.tree.map(short, array)


def norm_rows(values, gain_row, shift_row):
    row_mean = jnp.mean(values, axis=-1, keepdims=True)
    centred = values - row_mean
    variance = jnp.mean(centred * centred, axis=-1, keepdims=True)
    return centred * lax.rsqrt(variance + 1e-06) * gain_row + shift_row


def gelu_exact(values):
    return jax.nn.gelu(values, approximate=False)


def block_mask(chosen_blocks, segment_rows):
    nblocks = chosen_blocks.shape[2]
    block_index = jnp.arange(nblocks)
    near_blocks = jnp.abs(block_index[:, None] - block_index[None, :]) <= 1
    edge_blocks = (
        (block_index[None, :] == 0)
        | (block_index[None, :] == nblocks - 1)
        | (block_index[:, None] == 0)
        | (block_index[:, None] == nblocks - 1)
    )
    picked_blocks = jnp.any(chosen_blocks[..., None] == block_index, axis=3)
    allowed = near_blocks | edge_blocks | picked_blocks
    block_rows = segment_rows.shape[1] // nblocks
    allowed = jnp.repeat(jnp.repeat(allowed, block_rows, axis=2), block_rows, axis=3)
    same_doc = segment_rows[:, :, None] == segment_rows[:, None, :]
    return allowed & same_doc[:, None]


def masked_scores(queries, key_rows, allowed, score_scale):
    scores = (
        jnp.einsum("qshd,kshd->shqk", queries, key_rows, preferred_element_type=jnp.float32)
        * score_scale
    )
    return jnp.where(allowed, scores, -1e30)


def shards(
    block_input,
    segment_ids,
    random_blocks,
    w_qkv,
    b_qv,
    w_out,
    b_out,
    w_in,
    b_in,
    w_down,
    b_down,
    ln_gain,
    ln_bias,
    cotangent,
):
    score_scale = HEAD_DIM ** (-0.5)
    shard_rows, seq_count, model_width = block_input.shape
    layers = w_qkv.shape[0]
    local_width = w_qkv.shape[3]
    local_heads = local_width // HEAD_DIM
    allowed = block_mask(random_blocks, segment_ids)
    saved_acts = []
    stream = block_input
    for layer_index in range(layers):
        w_proj = w_qkv[layer_index].astype(jnp.bfloat16)
        w_mix = w_out[layer_index].astype(jnp.bfloat16)
        rows_low = stream.astype(jnp.bfloat16)
        full_rows = lax.all_gather(rows_low, "tensor", axis=0, tiled=True)
        length = full_rows.shape[0]
        projected = jnp.einsum(
            "lsd,tdc->tlsc", full_rows, w_proj, preferred_element_type=jnp.float32
        )
        qkv_bias = jnp.stack(
            [b_qv[layer_index, 0], jnp.zeros_like(b_qv[layer_index, 0]), b_qv[layer_index, 1]]
        )
        qkv_low = (projected + qkv_bias[:, None, None, :]).astype(jnp.bfloat16)
        head_view = qkv_low.reshape(3, length, seq_count, local_heads, HEAD_DIM)
        scores = masked_scores(head_view[0], head_view[1], allowed, score_scale)
        row_top = jnp.max(scores, axis=-1, keepdims=True)
        log_total = row_top + jnp.log(jnp.sum(jnp.exp(scores - row_top), axis=-1, keepdims=True))
        probs_low = jnp.exp(scores - log_total).astype(jnp.bfloat16)
        context = jnp.einsum(
            "shqk,kshd->qshd", probs_low, head_view[2], preferred_element_type=jnp.float32
        )
        context = context.reshape(length, seq_count, local_width).astype(jnp.bfloat16)
        mixed = lax.psum_scatter(
            jnp.einsum("lsc,cd->lsd", context, w_mix, preferred_element_type=jnp.float32).astype(
                jnp.bfloat16
            ),
            "tensor",
            scatter_dimension=0,
            tiled=True,
        ).astype(jnp.float32)
        first_sum = stream + mixed + b_out[layer_index]
        hidden_rows = norm_rows(first_sum, ln_gain[layer_index, 0], ln_bias[layer_index, 0])
        hidden_low = hidden_rows.astype(jnp.bfloat16)
        up_weight = w_in[layer_index].astype(jnp.bfloat16)
        backward_weight = w_down[layer_index].astype(jnp.bfloat16)
        hidden_full = lax.all_gather(hidden_low, "tensor", axis=0, tiled=True)
        preactivation = (
            jnp.einsum("twn,nj->twj", hidden_full, up_weight, preferred_element_type=jnp.float32)
            + b_in[layer_index]
        )
        activation_reduced = gelu_exact(preactivation).astype(jnp.bfloat16)
        grown = lax.psum_scatter(
            jnp.einsum(
                "unj,jp->unp",
                activation_reduced,
                backward_weight,
                preferred_element_type=jnp.float32,
            ).astype(jnp.bfloat16),
            "tensor",
            scatter_dimension=0,
            tiled=True,
        ).astype(jnp.float32)
        second_sum = hidden_rows + grown + b_down[layer_index]
        stream = norm_rows(second_sum, ln_gain[layer_index, 1], ln_bias[layer_index, 1])
        keep_rows, keep_hidden = (full_rows, hidden_full)
        saved_acts.append(
            (
                keep_rows,
                head_view,
                log_total,
                context,
                first_sum,
                keep_hidden,
                preactivation,
                activation_reduced,
                second_sum,
                up_weight,
                backward_weight,
            )
        )
    upstream = cotangent
    grads_by_layer = [None] * layers
    for layer_index in reversed(range(layers)):
        (
            keep_rows,
            head_view,
            log_total,
            context,
            first_sum,
            keep_hidden,
            preactivation,
            activation_reduced,
            second_sum,
            up_weight,
            backward_weight,
        ) = saved_acts[layer_index]
        full_rows, hidden_full = (keep_rows, keep_hidden)
        length = full_rows.shape[0]
        w_proj = w_qkv[layer_index].astype(jnp.bfloat16)
        w_mix = w_out[layer_index].astype(jnp.bfloat16)
        _, pull_second = jax.vjp(
            norm_rows, second_sum, ln_gain[layer_index, 1], ln_bias[layer_index, 1]
        )
        d_second, d_gain_two, d_shift_two = pull_second(upstream)
        _, pull_gelu = jax.vjp(gelu_exact, preactivation)
        widened_full = lax.all_gather(d_second.astype(jnp.bfloat16), "tensor", axis=0, tiled=True)
        down_gradient = jnp.einsum(
            "uxc,uxw->cw", activation_reduced, widened_full, preferred_element_type=jnp.float32
        )
        activation_gradient = jnp.einsum(
            "mra,xa->mrx", widened_full, backward_weight, preferred_element_type=jnp.float32
        )
        preactivation_gradient_reduced = pull_gelu(activation_gradient)[0].astype(jnp.bfloat16)
        up_gradient = jnp.einsum(
            "kmx,kmt->xt",
            hidden_full,
            preactivation_gradient_reduced,
            preferred_element_type=jnp.float32,
        )
        g_up_bias = jnp.sum(preactivation_gradient_reduced.astype(jnp.float32), axis=(0, 1))
        d_hidden = d_second + lax.psum_scatter(
            jnp.einsum(
                "hmp,tp->hmt",
                preactivation_gradient_reduced,
                up_weight,
                preferred_element_type=jnp.float32,
            ).astype(jnp.bfloat16),
            "tensor",
            scatter_dimension=0,
            tiled=True,
        ).astype(jnp.float32)
        _, pull_first = jax.vjp(
            norm_rows, first_sum, ln_gain[layer_index, 0], ln_bias[layer_index, 0]
        )
        d_first, d_gain_one, d_shift_one = pull_first(d_hidden)
        full_mixed = lax.all_gather(d_first.astype(jnp.bfloat16), "tensor", axis=0, tiled=True)
        g_out = jnp.einsum("lsc,lsd->cd", context, full_mixed, preferred_element_type=jnp.float32)
        d_context = jnp.einsum(
            "lsd,cd->lsc", full_mixed, w_mix, preferred_element_type=jnp.float32
        ).astype(jnp.bfloat16)
        d_context = d_context.reshape(length, seq_count, local_heads, HEAD_DIM)
        queries, key_rows, value_rows = (head_view[0], head_view[1], head_view[2])
        scores = masked_scores(queries, key_rows, allowed, score_scale)
        attn_probs = jnp.exp(scores - log_total)
        probs_low = attn_probs.astype(jnp.bfloat16)
        d_probs = jnp.einsum(
            "qshd,kshd->shqk", d_context, value_rows, preferred_element_type=jnp.float32
        )
        d_scores = attn_probs * (d_probs - jnp.sum(d_probs * attn_probs, axis=-1, keepdims=True))
        d_scores = d_scores.astype(jnp.bfloat16)
        d_query = (
            jnp.einsum("shqk,kshd->qshd", d_scores, key_rows, preferred_element_type=jnp.float32)
            * score_scale
        )
        d_key = (
            jnp.einsum("shqk,qshd->kshd", d_scores, queries, preferred_element_type=jnp.float32)
            * score_scale
        )
        d_value = jnp.einsum(
            "shqk,qshd->kshd", probs_low, d_context, preferred_element_type=jnp.float32
        )
        d_qkv = (
            jnp.stack([d_query, d_key, d_value])
            .reshape(3, length, seq_count, local_width)
            .astype(jnp.bfloat16)
        )
        g_proj = jnp.einsum("lsd,tlsc->tdc", full_rows, d_qkv, preferred_element_type=jnp.float32)
        qkv_sums = jnp.sum(d_qkv.astype(jnp.float32), axis=(1, 2))
        g_bias = jnp.stack([qkv_sums[0], qkv_sums[2]])
        upstream = d_first + lax.psum_scatter(
            jnp.einsum("tlsc,tdc->lsd", d_qkv, w_proj, preferred_element_type=jnp.float32).astype(
                jnp.bfloat16
            ),
            "tensor",
            scatter_dimension=0,
            tiled=True,
        ).astype(jnp.float32)
        weight_grads = (g_proj, g_bias, g_out, up_gradient, g_up_bias, down_gradient)
        small_grads = (
            jnp.sum(d_first, axis=(0, 1)),
            jnp.sum(d_second, axis=(0, 1)),
            jnp.stack([d_gain_one, d_gain_two]),
            jnp.stack([d_shift_one, d_shift_two]),
        )
        grads_by_layer[layer_index] = (weight_grads, small_grads)
    weight_stack = tuple(
        (
            jnp.stack([grads_by_layer[layer_index][0][member] for layer_index in range(layers)])
            for member in range(6)
        )
    )
    small_stack = tuple(
        (
            jnp.stack([grads_by_layer[layer_index][1][member] for layer_index in range(layers)])
            for member in range(4)
        )
    )
    weight_stack = jax.tree.map(
        lambda part: part.astype(jnp.float32), lax.psum(as_sent(weight_stack), "dp")
    )
    small_stack = lax.psum(small_stack, ("dp", "tensor"))
    return (
        stream,
        upstream,
        weight_stack[0],
        weight_stack[1],
        weight_stack[2],
        small_stack[0],
        weight_stack[3],
        weight_stack[4],
        weight_stack[5],
        small_stack[1],
        small_stack[2],
        small_stack[3],
    )


def solution(mesh):
    by_sequence = mesh.shape["tensor"] == 2 and mesh.shape["dp"] == 16
    return jax.shard_map(
        sequence_shards if by_sequence else shards,
        mesh=mesh,
        in_specs=(
            P("tensor", "dp", None),
            P("dp", None),
            P("dp", "tensor", None, None),
            P(None, None, None, "tensor"),
            P(None, None, "tensor"),
            P(None, "tensor", None),
            P(),
            P(None, None, "tensor"),
            P(None, "tensor"),
            P(None, "tensor", None),
            P(),
            P(),
            P(),
            P("tensor", "dp", None),
        ),
        out_specs=(
            P("tensor", "dp", None),
            P("tensor", "dp", None),
            P(None, None, None, "tensor"),
            P(None, None, "tensor"),
            P(None, "tensor", None),
            P(),
            P(None, None, "tensor"),
            P(None, "tensor"),
            P(None, "tensor", None),
            P(),
            P(),
            P(),
        ),
        check_vma=False,
    )
```

```python
import functools

import jax
import jax.numpy as jnp
from jax import lax
from jax.experimental import pallas as pl
from jax.experimental.pallas import tpu as pltpu
from jax.sharding import PartitionSpec as P

HEAD_DIM = 64
BIG = -1e30
BF16 = jnp.bfloat16
F32 = jnp.float32
MESH = pl.DeviceIdType.MESH
VMEM_LIMIT = 56 << 20

FLIP_Y, FLIP_C, FLIP_X, FLIP_Z0, FLIP_Z1 = 1, 2, 4, 8, 16
SWAP = FLIP_Y + FLIP_C
DEVICES = 32

GROUPS = 12
OUT_GROUP = 3
FF_GROUPS = 4


def in_group(s):
    return 4 + 2 * s


def down_group(s):
    return 5 + 2 * s


def flip(values, bit):
    pairs = [(i, i ^ bit) for i in range(DEVICES)]
    return jax.tree.map(lambda v: lax.ppermute(v, ("dp", "tensor"), pairs), values)


def nt(a, b):
    return lax.dot_general(a, b, (((1,), (1,)), ((), ())), preferred_element_type=F32)


def nn(a, b):
    return lax.dot_general(a, b, (((1,), (0,)), ((), ())), preferred_element_type=F32)


def tn(a, b):
    return lax.dot_general(a, b, (((0,), (0,)), ((), ())), preferred_element_type=F32)


def block_of(ref):
    width = ref.shape[-1]
    return ref[...].reshape(-1, width)


def place_kernel(turned, code_ref, g_ref, o_ref, *scratch):
    code = code_ref[0]
    for j in range(16):
        start = pl.multiple_of((j ^ code) * 32, 32)
        block = g_ref[0, pl.ds(start, 32), :].astype(F32)
        if turned:
            scratch[0][j * 32 : (j + 1) * 32, :] = block
        else:
            o_ref[0, j * 32 : (j + 1) * 32, :] = block
    if turned:
        o_ref[...] = scratch[0][...].T.reshape(o_ref.shape)


def place(sums, shape, block, index, turned, count, group, code):
    width = sums.shape[-1]
    return pl.pallas_call(
        functools.partial(place_kernel, turned),
        out_shape=jax.ShapeDtypeStruct(shape, F32),
        grid_spec=pltpu.PrefetchScalarGridSpec(
            num_scalar_prefetch=1,
            grid=(shape[0], count),
            in_specs=[pl.BlockSpec((1, 512, width), lambda l, i, code: (group(l, i), 0, 0))],
            out_specs=pl.BlockSpec(block, lambda l, i, code: index(l, i)),
            scratch_shapes=[pltpu.VMEM((512, width), F32)] if turned else [],
        ),
        compiler_params=pltpu.CompilerParams(vmem_limit_bytes=VMEM_LIMIT),
        cost_estimate=pl.CostEstimate(
            flops=0, bytes_accessed=shape[0] * count * 512 * width * 6, transcendentals=0
        ),
        name="place",
    )(code, sums)


def widen_kernel(a_ref, b_ref, a_out, b_out, a_buf, b_buf, sem):
    copies = []
    for n, (source, target, buf) in enumerate(((a_ref, a_out, a_buf), (b_ref, b_out, b_buf))):
        buf[...] = source[...].astype(F32)
        copies.append(pltpu.make_async_copy(buf, target.at[:, 0], sem.at[n]))
        copies[-1].start()
    for copy in copies:
        copy.wait()


def widen_rows(a, b):
    rows, width = a.shape
    out = jax.ShapeDtypeStruct((rows, 1, width), F32)
    return pl.pallas_call(
        widen_kernel,
        out_shape=(out, out),
        in_specs=[pl.BlockSpec(memory_space=pltpu.VMEM)] * 2,
        out_specs=(pl.BlockSpec(memory_space=pl.ANY),) * 2,
        scratch_shapes=[pltpu.VMEM((rows, width), F32), pltpu.VMEM((rows, width), F32), pltpu.SemaphoreType.DMA((2,))],
        name="widen_rows",
    )(a, b)


def partner(bits):
    dp, y = lax.axis_index("dp"), lax.axis_index("tensor")
    other = dp
    for step in (1, 2, 4, 8):
        if bits & (2 * step):
            other = other + step * (1 - 2 * ((dp // step) % 2))
    return (other, 1 - y if bits & FLIP_Y else y)


def greet(bits):
    barrier = pltpu.get_barrier_semaphore()
    for bit in bits:
        pl.semaphore_signal(barrier, inc=1, device_id=partner(bit), device_id_type=MESH)
    pl.semaphore_wait(barrier, len(bits))


def add_into(into, other, count):
    def step(i, _):
        into[i] = (into[i].astype(F32) + other[i].astype(F32)).astype(BF16)
        return 0

    lax.fori_loop(0, count, step, 0)


def add_rows(into, other, rows):
    def step(i, _):
        at = pl.ds(pl.multiple_of(i * 32, 32), 32)
        into[at, :] = (into[at, :].astype(F32) + other[at, :].astype(F32)).astype(BF16)
        return 0

    lax.fori_loop(0, rows // 32, step, 0)


SLOTS = 12
LAST_TICK = 8


class Reduction:
    def __init__(self, grads, sums, count, bufs, sems):
        self.grads, self.sums, self.count = grads, sums, count
        self.y_buf, self.x_buf, self.z0_buf, self.z1_buf, self.all_buf, self.keep_buf = bufs
        self.send_sem, self.recv_sem, self.core_send, self.core_recv = sems[:4]
        self.keep_sem, self.out_sem, self.in_free, self.out_free = sems[4:]

    def blocks(self, ref, i, first):
        part = pl.ds(pl.multiple_of(lax.rem(i, 2) * 16, 16), 16)
        return ref.at[lax.div(i, 2), pl.ds(first, 8), part]

    def copy(self, step, i):
        slot = lax.rem(i, SLOTS)
        ys, al = self.y_buf.at[slot], self.all_buf.at[slot]
        bit, source, target = (
            (FLIP_Y, self.blocks(self.grads, i, 8), ys),
            (FLIP_X, ys.at[pl.ds(4, 4)], self.x_buf.at[slot]),
            (FLIP_Z0, ys.at[pl.ds(2, 2)], self.z0_buf.at[slot]),
            (FLIP_Z1, ys.at[pl.ds(1, 1)], self.z1_buf.at[slot]),
            (FLIP_Z1, al.at[pl.ds(0, 1)], al.at[pl.ds(1, 1)]),
            (FLIP_Z0, al.at[pl.ds(0, 2)], al.at[pl.ds(2, 2)]),
            (FLIP_X, al.at[pl.ds(0, 4)], al.at[pl.ds(4, 4)]),
            (FLIP_C, al, self.blocks(self.sums, i, 8)),
        )[step]
        return pltpu.make_async_remote_copy(
            src_ref=source,
            dst_ref=target,
            send_sem=self.send_sem.at[step, slot] if step < 7 else self.core_send.at[i],
            recv_sem=self.recv_sem.at[step, slot] if step < 7 else self.core_recv.at[i],
            device_id=partner(bit),
            device_id_type=MESH,
        )

    def keep(self, i):
        slot = lax.rem(i, 2)
        return pltpu.make_async_copy(
            self.blocks(self.grads, i, 0), self.keep_buf.at[slot], self.keep_sem.at[slot]
        )

    def out(self, i):
        slot = lax.rem(i, SLOTS)
        return pltpu.make_async_copy(
            self.all_buf.at[slot], self.blocks(self.sums, i, 0), self.out_sem.at[slot]
        )

    def take(self, sem, i):
        @pl.when(i >= SLOTS)
        def _():
            pl.semaphore_wait(sem, 1)

    def give(self, sem, bit, i):
        @pl.when(i + SLOTS < self.count)
        def _():
            pl.semaphore_signal(sem, inc=1, device_id=partner(bit), device_id_type=MESH)

    def tick(self, t):
        def at(offset, body):
            i = t - offset
            pl.when((i >= 0) & (i < self.count))(lambda: body(i, lax.rem(i, SLOTS)))

        def set_out(i, slot):
            self.take(self.in_free.at[0], i)
            self.copy(0, i).start()
            self.keep(i).start()

        def finish(i, slot):
            self.copy(7, i).wait()
            self.out(i).wait()
            for n, bit in enumerate((FLIP_X, FLIP_Z0, FLIP_Z1)):
                self.give(self.out_free.at[n], bit, i)

        def to_core(i, slot):
            self.copy(6, i).wait()
            self.copy(7, i).start()
            self.out(i).start()

        def back_x(i, slot):
            self.copy(5, i).wait()
            self.take(self.out_free.at[0], i)
            self.copy(6, i).start()

        def back_z0(i, slot):
            self.copy(4, i).wait()
            self.take(self.out_free.at[1], i)
            self.copy(5, i).start()

        def back_z1(i, slot):
            self.copy(3, i).wait()
            add_into(self.y_buf.at[slot], self.z1_buf.at[slot], 1)
            self.all_buf[slot, 0] = self.y_buf[slot, 0]
            for n, bit in enumerate((FLIP_Y, FLIP_X, FLIP_Z0, FLIP_Z1)):
                self.give(self.in_free.at[n], bit, i)
            self.take(self.out_free.at[2], i)
            self.copy(4, i).start()

        def on_z1(i, slot):
            self.copy(2, i).wait()
            add_into(self.y_buf.at[slot], self.z0_buf.at[slot], 2)
            self.take(self.in_free.at[3], i)
            self.copy(3, i).start()

        def on_z0(i, slot):
            self.copy(1, i).wait()
            add_into(self.y_buf.at[slot], self.x_buf.at[slot], 4)
            self.take(self.in_free.at[2], i)
            self.copy(2, i).start()

        def on_x(i, slot):
            self.copy(0, i).wait()
            self.keep(i).wait()
            add_into(self.y_buf.at[slot], self.keep_buf.at[lax.rem(i, 2)], 8)
            self.take(self.in_free.at[1], i)
            self.copy(1, i).start()

        at(0, set_out)
        at(8, finish)
        at(7, to_core)
        at(6, back_x)
        at(5, back_z0)
        at(4, back_z1)
        at(3, on_z1)
        at(2, on_z0)
        at(1, on_x)


def begin(feeds):
    for copy in feeds(0, 0):
        copy.start()


def stream(count, feeds, body):
    def step(i, _):
        slot = lax.rem(i, 2)

        @pl.when(i + 1 < count)
        def _():
            for copy in feeds(i + 1, 1 - slot):
                copy.start()

        for copy in feeds(i, slot):
            copy.wait()
        body(i, slot)
        return 0

    lax.fori_loop(0, count, step, 0)


def norm(r, gain, shift):
    centred = r - jnp.mean(r, axis=-1, keepdims=True)
    rstd = lax.rsqrt(jnp.mean(centred * centred, axis=-1, keepdims=True) + 1e-06)
    return centred * rstd * gain + shift


def norm_back(dy, r, gain):
    centred = r - jnp.mean(r, axis=-1, keepdims=True)
    rstd = lax.rsqrt(jnp.mean(centred * centred, axis=-1, keepdims=True) + 1e-06)
    unit = centred * rstd
    dunit = dy * gain
    dr = rstd * (
        dunit
        - jnp.mean(dunit, axis=-1, keepdims=True)
        - unit * jnp.mean(dunit * unit, axis=-1, keepdims=True)
    )
    return dr, dy * unit


def gelu_and_slope(u):
    cdf = 0.5 * (1.0 + lax.erf(u * (0.5**0.5)))
    pdf = jnp.exp(-0.5 * u * u) * 0.3989422804014327
    return u * cdf, cdf + u * pdf


TILE = 64


def row_tiles(rows, body):
    def step(i, _):
        body(pl.ds(pl.multiple_of(i * TILE, TILE), TILE))
        return 0

    lax.fori_loop(0, rows // TILE, step, 0)


def pair_lanes(values, e):
    lane = lax.broadcasted_iota(jnp.int32, values.shape, 1)
    return jnp.where(lane // HEAD_DIM == e, values, jnp.zeros_like(values))


def spread_mask(block_part, document_part):
    blocks, lanes = block_part.shape
    each = document_part.shape[0] // blocks
    part = jnp.broadcast_to(block_part[:, None, :], (blocks, each, lanes)).reshape(blocks * each, lanes)
    return (part + document_part).astype(BF16)


def attend_pair(query, keys, values, hot, mask):
    scale = HEAD_DIM**-0.5
    rows = query.shape[0]
    query = query * jnp.asarray(scale, BF16)
    values_t = values.T
    tile = rows // 2
    contexts, lses = [], ([], [])
    for part in range(2):
        at = slice(part * tile, (part + 1) * tile)
        heads = []
        for e in range(2):
            right = jnp.concatenate([pair_lanes(query[at], e), hot[at]], axis=1)
            left = jnp.concatenate([keys, mask[e]], axis=1)
            s = nt(left, right)
            top = jnp.max(s, axis=0, keepdims=True)
            p = jnp.exp(s - top)
            total = jnp.sum(p, axis=0, keepdims=True)
            c = nn(values_t[e * HEAD_DIM : (e + 1) * HEAD_DIM, :], p.astype(BF16))
            heads.append(c * (1.0 / total))
            lses[e].append(top + jnp.log(total))
        contexts.append(jnp.concatenate(heads, axis=0).T)
    return jnp.concatenate(contexts, axis=0), [jnp.concatenate(parts, axis=1) for parts in lses]


def attend_back_pair(query, keys, values, hot, mask, ctx, lse, dctx):
    scale = HEAD_DIM**-0.5
    rows = query.shape[0]
    query = query * jnp.asarray(scale, BF16)
    keys_t = keys.T
    delta_t = (dctx.astype(F32) * ctx.astype(F32)).T
    tile = rows // 2
    dk, dv, dq = 0.0, 0.0, []
    for part in range(2):
        at = slice(part * tile, (part + 1) * tile)
        heads = []
        for e in range(2):
            lanes = slice(e * HEAD_DIM, (e + 1) * HEAD_DIM)
            query_e = pair_lanes(query[at], e)
            dctx_e = pair_lanes(dctx[at], e)
            right = jnp.concatenate([query_e, hot[at]], axis=1)
            left = jnp.concatenate([keys, mask[e]], axis=1)
            p = jnp.exp(nt(left, right) - lse[e : e + 1, at])
            dp = nt(values, dctx_e)
            delta = jnp.sum(delta_t[lanes, at], axis=0, keepdims=True)
            ds = (p * (dp - delta)).astype(BF16)
            dk = dk + nn(ds, query_e)
            dv = dv + nn(p.astype(BF16), dctx_e)
            heads.append(nn(keys_t[lanes, :], ds) * scale)
        dq.append(jnp.concatenate(heads, axis=0).T)
    return jnp.concatenate(dq, axis=0), dk, dv


class Spread:
    def __init__(self, weights, pairs, send_sem, recv_sem):
        self.weights, self.pairs, self.send_sem, self.recv_sem = weights, pairs, send_sem, recv_sem

    def copy(self, step, t):
        w = self.weights
        even, odd = 2 * t, 2 * t + 1
        bit, source, target = (
            (FLIP_Y, w.at[0, even, 0, pl.ds(0, 64)], w.at[0, even, 1, pl.ds(0, 64)]),
            (FLIP_Y, w.at[0, odd, 0, pl.ds(0, 64)], w.at[0, odd, 1, pl.ds(0, 64)]),
            (FLIP_X, w.at[0, even, 1, pl.ds(0, 64)], w.at[0, even, 1, pl.ds(128, 64)]),
            (FLIP_Z0, w.at[0, odd, 1, pl.ds(0, 64)], w.at[0, odd, 1, pl.ds(64, 64)]),
            (FLIP_Z0, w.at[0, even, 1, pl.ds(0, 64)], w.at[0, even, 1, pl.ds(64, 64)]),
            (FLIP_Z0, w.at[0, even, 1, pl.ds(128, 64)], w.at[0, even, 1, pl.ds(192, 64)]),
            (FLIP_X, w.at[0, odd, 1, pl.ds(0, 128)], w.at[0, odd, 1, pl.ds(128, 128)]),
            (FLIP_C, w.at[0, even, 1], w.at[1, even, 1]),
            (FLIP_C, w.at[0, odd, 1], w.at[1, odd, 1]),
        )[step]
        return pltpu.make_async_remote_copy(
            src_ref=source,
            dst_ref=target,
            send_sem=self.send_sem.at[step, t],
            recv_sem=self.recv_sem.at[step, t],
            device_id=partner(bit),
            device_id_type=MESH,
        )

    def tick(self, t):
        def at(offset, waits, starts):
            i = t - offset

            @pl.when((i >= 0) & (i < self.pairs))
            def _():
                for step in waits:
                    self.copy(step, i).wait()
                for step in starts:
                    self.copy(step, i).start()

        at(0, (), (0, 1))
        at(5, (7, 8), ())
        at(1, (0, 1), (2, 3))
        at(2, (2, 3), (4, 5, 6))
        at(4, (4, 5, 6), (7, 8))


PER_LAYER = 14
DEPTH = 3


def forward_kernel(layers, *refs):
    refs = list(refs)
    x_ref, up_ref, wq_ref, wo_ref, wi_ref, wd_ref = refs[:6]
    hot_buf, mask_ref, key_ref, bq_ref, bi_ref, vec_ref = refs[6:12]
    w_ref, up_out, x_out = refs[12:15]
    saved = [refs[15 + PER_LAYER * l : 15 + PER_LAYER * (l + 1)] for l in range(layers)]
    (
        x, acc, r_buf, low, xb, qkv, kv_sib, ctx, lse, hl, g_all, slope_all,
        col_buf, row_buf, turn_buf, made_buf, wa_buf, wb_buf,
        feed_sem, load_sem, col_sem, row_sem, made_sem, store_sem, block_sem,
        core_send, core_recv, kv_send, kv_recv, g_send, g_recv, spread_send, spread_recv,
    ) = refs[15 + PER_LAYER * layers :]
    rows, width = acc.shape
    dp, y = lax.axis_index("dp"), lax.axis_index("tensor")
    core = dp % 2
    stays = core == y
    spread = Spread(w_ref, layers * GROUPS // 2, spread_send, spread_recv)
    greet((FLIP_Y, FLIP_X, FLIP_Z0, FLIP_C, SWAP))

    def feed(n, slot, source, target):
        return pltpu.make_async_copy(source, target, feed_sem.at[n, slot])

    def load(n, source, target):
        return pltpu.make_async_copy(source, target, load_sem.at[n])

    def store(n, source, target):
        return pltpu.make_async_copy(source, target, store_sem.at[n])

    def exchange(n, source, target, bits=FLIP_C):
        return pltpu.make_async_remote_copy(
            src_ref=source, dst_ref=target, send_sem=core_send.at[n], recv_sem=core_recv.at[n],
            device_id=partner(bits), device_id_type=MESH,
        )

    def columns(ref, i, size):
        return ref.at[:, pl.ds(pl.multiple_of(i * size, size), size)]

    def swap(n, source, target, begin):
        here = store(n, source, target)
        there = exchange(n, source, target, SWAP)

        @pl.when(stays)
        def _():
            here.start() if begin else here.wait()

        @pl.when(jnp.logical_not(stays))
        def _():
            there.start() if begin else there.wait()

    items = []
    for l in range(layers):
        items += [(True, wq_ref.at[l, (t + 1) % 3], l * GROUPS + t) for t in range(3)]
        items += [(False, wo_ref.at[l], l * GROUPS + OUT_GROUP)]
        for n in range(FF_GROUPS):
            items += [(True, wi_ref.at[l, :, pl.ds(n * 512, 512)], l * GROUPS + in_group(n))]
            items += [(False, wd_ref.at[l, pl.ds(n * 512, 512)], l * GROUPS + down_group(n))]
    fetches, counts, ahead = [], [0, 0], [[], []]
    for m, (turned, source, group) in enumerate(items):
        slot = counts[turned] % DEPTH
        buf, sem = (col_buf, col_sem) if turned else (row_buf, row_sem)
        fetches.append((pltpu.make_async_copy(source, buf.at[slot], sem.at[slot]), slot))
        ahead[turned].append(m)
        counts[turned] += 1
    bits = [(dp // step) % 2 for step in (1, 2, 4, 8)]
    made = {}

    def convert(m):
        turned, _, group = items[m]
        copy, slot = fetches[m]
        copy.wait()
        if turned:

            def turn(i, _):
                turn_buf[pl.ds(pl.multiple_of(i * 128, 128), 128), :] = col_buf[
                    slot, :, pl.ds(pl.multiple_of(i * 128, 128), 128)
                ].T
                return 0

            lax.fori_loop(0, 4, turn, 0)
        if m >= 2:
            made[m - 2].wait()

        def block(j, _):
            where = 0
            for bit, weight in zip(bits, (8, 4, 2, 1)):
                own = (j // weight) % 2
                where = where + weight * (own + bit - 2 * own * bit)
            at = pl.ds(pl.multiple_of(where * 32, 32), 32)
            rows_32 = turn_buf[at, :] if turned else row_buf[slot, at, :]
            made_buf[m % 2, pl.ds(pl.multiple_of(j * 32, 32), 32), :] = rows_32.astype(BF16)
            return 0

        lax.fori_loop(0, 16, block, 0)
        later = [n for n in ahead[turned] if n > m]
        if len(later) >= DEPTH:
            fetches[later[DEPTH - 1]][0].start()
        parts = [
            pltpu.make_async_copy(
                made_buf.at[m % 2, pl.ds(a * 256, 256)], w_ref.at[a, group, 0], made_sem.at[m % 2, a]
            )
            for a in range(2)
        ]

        class Both:
            def wait(self):
                for part in parts:
                    part.wait()

        for part in parts:
            part.start()
        made[m] = Both()

    load_x = load(0, x_ref.at[:, 0], x)
    load_x.start()
    load_up = load(1, up_ref.at[:, 0], acc)
    load_up.start()
    for kind in range(2):
        for m in ahead[kind][:DEPTH]:
            fetches[m][0].start()
    load_x.wait()

    def narrow_x(at):
        low[at, :] = x[at, :].astype(BF16)

    row_tiles(rows, narrow_x)
    swap(0, low, xb, True)
    load_up.wait()

    def narrow_up(at):
        hl[at, :] = acc[at, :].astype(BF16)

    row_tiles(rows, narrow_up)
    swap(1, hl, up_out, True)

    for m in range(len(items)):
        convert(m)
        if m % 4 == 3:
            spread.tick(m // 4)
    for m in range(len(items) - 2, len(items)):
        made[m].wait()
    swap(0, low, xb, False)
    swap(1, hl, up_out, False)

    def widen(at):
        x[at, :] = xb[at, :].astype(F32)

    row_tiles(rows, widen)

    pairs = width // 128
    for l in range(layers):
        (
            qkv_out, sib_out, ctx_out, ctx_sib_out, lse_out, r1_out, r2_out, hl_out, hl_sib_out,
            g_out, g_sib_out, slope_out, xb_out, xb_sib_out,
        ) = saved[l]
        first = l * GROUPS
        clock = 6 + 6 * l
        xb_store = store(0, xb, xb_out)
        xb_store.start()
        xb_copy = exchange(2 + 3 * l, xb, xb_sib_out)
        xb_copy.start()

        def give_kv(n, a):
            at = pl.ds(pl.multiple_of(a * 512, 512), 512)
            return pltpu.make_async_remote_copy(
                src_ref=qkv.at[1 + n, :, at], dst_ref=kv_sib.at[n, :, at],
                send_sem=kv_send.at[n, a], recv_sem=kv_recv.at[n, a],
                device_id=partner(FLIP_C), device_id_type=MESH,
            )

        def which(i):
            n = lax.div(i, 2)
            return lax.rem(n + 1, 3), n, lax.rem(i, 2)

        def qkv_feeds(i, slot):
            _, n, a = which(i)
            return (feed(0, slot, w_ref.at[a, first + n], wa_buf.at[slot]),)

        def qkv_body(i, slot):
            t, _, a = which(i)
            at = pl.ds(pl.multiple_of(a * 512, 512), 512)
            qkv[t, :, at] = (nt(xb[...], block_of(wa_buf.at[slot])) + bq_ref[l, t, a]).astype(BF16)
            pl.when(t > 0)(lambda: give_kv(t - 1, a).start())
            pl.when(i == 2)(lambda: spread.tick(clock))

        if l == 0:
            begin(qkv_feeds)
        stream(6, qkv_feeds, qkv_body)
        qkv_store = store(1, qkv, qkv_out)
        qkv_store.start()
        for n in range(2):
            for a in range(2):
                give_kv(n, a).wait()
        sib_store = store(2, kv_sib, sib_out)
        sib_store.start()

        feed(2, 0, w_ref.at[0, first + OUT_GROUP], wb_buf.at[0]).start()

        def pair_body(p, _):
            far = lax.rem(p + pairs // 2, pairs)
            here = pl.ds(pl.multiple_of(p * 128, 128), 128)
            there = pl.ds(pl.multiple_of(far * 128, 128), 128)
            mask = [spread_mask(mask_ref[2 * p + e], key_ref[...]) for e in range(2)]
            keys = jnp.concatenate([qkv[1, :, here], kv_sib[0, :, there]], axis=0)
            values = jnp.concatenate([qkv[2, :, here], kv_sib[1, :, there]], axis=0)
            context, parts = attend_pair(qkv[0, :, here], keys, values, hot_buf[...], mask)
            ctx[:, here] = context.astype(BF16)
            for e in range(2):
                lse[p, e : e + 1, :] = parts[e]
            pl.when(lax.rem(p, 5) == 2)(lambda: spread.tick(clock + 1 + lax.div(p, 5)))
            return 0

        lax.fori_loop(0, pairs, pair_body, 0)
        ctx_store = store(3, ctx, ctx_out)
        ctx_store.start()
        lse_store = store(4, lse, lse_out)
        lse_store.start()
        ctx_copy = exchange(3 + 3 * l, ctx.at[:, pl.ds(512, 512)], ctx_sib_out)
        ctx_copy.start()

        def place_of(i):
            return 1 - lax.rem(i, 2), lax.div(i, 2)

        def ff_feeds(i, slot):
            a, n = place_of(i)
            return (
                feed(0, slot, w_ref.at[a, first + in_group(n)], wa_buf.at[slot]),
                feed(2, slot, w_ref.at[a, first + down_group(n)], wb_buf.at[slot]),
            )

        ff_feeds(0, 0)[0].start()

        def out_feeds(i, slot):
            return (feed(2, slot, w_ref.at[i, first + OUT_GROUP], wb_buf.at[slot]),)

        def out_body(i, slot):
            part = nn(ctx[:, pl.ds(pl.multiple_of(i * 512, 512), 512)], block_of(wb_buf.at[slot]))

            @pl.when(i == 0)
            def _():
                acc[...] = part

            @pl.when(i == 1)
            def _():
                acc[...] += part

        stream(2, out_feeds, out_body)
        ff_feeds(0, 0)[1].start()
        sib_store.wait()

        def first_norm(at):
            r1 = x[at, :] + acc[at, :] + vec_ref[l, 0:1, :]
            r_buf[at, :] = r1
            h = norm(r1, vec_ref[l, 1:2, :], vec_ref[l, 2:3, :])
            hl[at, :] = h.astype(BF16)
            acc[at, :] = h + vec_ref[l, 3:4, :]

        row_tiles(rows, first_norm)
        r1_store = store(5, r_buf, r1_out)
        r1_store.start()
        hl_store = store(6, hl, hl_out)
        hl_store.start()
        hl_copy = exchange(4 + 3 * l, hl, hl_sib_out)
        hl_copy.start()

        def g_store(j):
            return pltpu.make_async_copy(g_all.at[j], columns(g_out, j, 512), block_sem.at[0, j])

        def slope_store(j):
            return pltpu.make_async_copy(slope_all.at[j], columns(slope_out, j, 512), block_sem.at[1, j])

        def g_copy(n):
            return pltpu.make_async_remote_copy(
                src_ref=g_all.at[FF_GROUPS + n], dst_ref=columns(g_sib_out, n, 512),
                send_sem=g_send.at[l, n], recv_sem=g_recv.at[l, n],
                device_id=partner(FLIP_C), device_id_type=MESH,
            )

        def ff_body(i, slot):
            a, n = place_of(i)
            j = a * FF_GROUPS + n
            u = nt(hl[...], block_of(wa_buf.at[slot])) + bi_ref[l, a, n]
            g, slope = gelu_and_slope(u)
            g = g.astype(BF16)
            g_all[j] = g
            slope_all[j] = slope.astype(BF16)
            g_store(j).start()
            slope_store(j).start()
            pl.when(a == 1)(lambda: g_copy(n).start())
            acc[...] += nn(g, block_of(wb_buf.at[slot]))
            pl.when(lax.rem(i, 3) == 1)(lambda: spread.tick(clock + 3 + lax.div(i, 3)))

        stream(2 * FF_GROUPS, ff_feeds, ff_body)
        r1_store.wait()
        xb_store.wait()
        xb_copy.wait()
        if l + 1 < layers:
            feed(0, 0, w_ref.at[0, first + GROUPS], wa_buf.at[0]).start()

        def second_norm(at):
            r2 = acc[at, :]
            r_buf[at, :] = r2
            x2 = norm(r2, vec_ref[l, 4:5, :], vec_ref[l, 5:6, :])
            x[at, :] = x2
            xb[at, :] = x2.astype(BF16)

        row_tiles(rows, second_norm)
        r2_store = store(5, r_buf, r2_out)
        r2_store.start()
        if l == layers - 1:
            x_store = store(10, xb, x_out)
            x_store.start()

        def settle(j, _):
            g_store(j).wait()
            slope_store(j).wait()
            return 0

        lax.fori_loop(0, 2 * FF_GROUPS, settle, 0)

        def settle_sent(n, _):
            g_copy(n).wait()
            return 0

        lax.fori_loop(0, FF_GROUPS, settle_sent, 0)
        for copy in (qkv_store, ctx_store, lse_store, ctx_copy, hl_store, hl_copy, r2_store):
            copy.wait()
    x_store.wait()


def forward(block_input, cotangent, w_qkv, w_out, w_in, w_down, hot, mask, mask_rows, bias_qkv, bias_in, vectors):
    rows, _, width = block_input.shape
    layers = w_qkv.shape[0]
    total = layers * GROUPS
    anywhere = pl.BlockSpec(memory_space=pl.ANY)
    in_vmem = pl.BlockSpec(memory_space=pltpu.VMEM)
    low = lambda *shape: pltpu.VMEM(shape, BF16)
    full = lambda *shape: pltpu.VMEM(shape, F32)
    dma = lambda *shape: pltpu.SemaphoreType.DMA(shape)
    low_out = lambda *shape: jax.ShapeDtypeStruct(shape, BF16)
    full_out = lambda *shape: jax.ShapeDtypeStruct(shape, F32)
    layer_out = (
        low_out(3, rows, width),
        low_out(2, rows, width),
        low_out(rows, width),
        low_out(rows, width // 2),
        full_out(width // 128, 2, rows),
        full_out(rows, width),
        full_out(rows, width),
        low_out(rows, width),
        low_out(rows, width),
        low_out(rows, 4 * width),
        low_out(rows, 2 * width),
        low_out(rows, 4 * width),
        low_out(rows, width),
        low_out(rows, width),
    )
    outs = pl.pallas_call(
        functools.partial(forward_kernel, layers),
        out_shape=(low_out(2, total, 2, 256, width), low_out(rows, width), low_out(rows, width)) + layer_out * layers,
        in_specs=[anywhere] * 6 + [in_vmem] * 6,
        out_specs=(anywhere,) * (3 + PER_LAYER * layers),
        scratch_shapes=[
            full(rows, width),
            full(rows, width),
            full(rows, width),
            low(rows, width),
            low(rows, width),
            low(3, rows, width),
            low(2, rows, width),
            low(rows, width),
            full(width // 128, 2, rows),
            low(rows, width),
            low(2 * FF_GROUPS, rows, 512),
            low(2 * FF_GROUPS, rows, 512),
            full(DEPTH, width, 512),
            full(DEPTH, 512, width),
            full(512, width),
            low(2, 512, width),
            low(2, 2, 256, width),
            low(2, 2, 256, width),
            dma(3, 2),
            dma(3),
            dma(DEPTH),
            dma(DEPTH),
            dma(2, 2),
            dma(11),
            dma(2, 2 * FF_GROUPS),
            dma(11),
            dma(11),
            dma(2, 2),
            dma(2, 2),
            dma(layers, FF_GROUPS),
            dma(layers, FF_GROUPS),
            dma(9, total // 2),
            dma(9, total // 2),
        ],
        compiler_params=pltpu.CompilerParams(collective_id=0, has_side_effects=True, vmem_limit_bytes=60 << 20),
        cost_estimate=pl.CostEstimate(flops=30 << 30, bytes_accessed=300 << 20, transcendentals=1 << 24),
        name="forward",
    )(block_input, cotangent, w_qkv, w_out, w_in, w_down, hot, mask, mask_rows, bias_qkv, bias_in, vectors)
    saved = [outs[3 + PER_LAYER * l : 3 + PER_LAYER * (l + 1)] for l in range(layers)]
    return outs[0], outs[1], outs[2], saved


def backward_kernel(layers, *refs):
    refs = list(refs)
    up_ref, x_ref, w_ref, hot_buf, mask_ref, key_ref, vec_ref = refs[:7]
    saved = [refs[7 + PER_LAYER * l : 7 + PER_LAYER * (l + 1)] for l in range(layers)]
    at_ref = 7 + PER_LAYER * layers
    grads, sums, dx_out, x_out, dbi_ref, qkv_sums_ref, small_ref = refs[at_ref : at_ref + 7]
    (
        acc, dr1, dm, dm_sib, da, da_sib, du, du_sib, dctx, dqkv, d_sib, kv_out, kv_far,
        wa_buf, wb_buf, r_buf, slope_buf, left_buf, left_sib_buf, right_buf, right_sib_buf,
        pair_buf, lse_buf, unit_buf,
        y_buf, x_buf, z0_buf, z1_buf, all_buf, keep_buf,
        feed_sem, load_sem, store_sem, swap_sem, core_send, core_recv, du_send, du_recv, pair_send, pair_recv,
        send_sem, recv_sem, sum_send, sum_recv, keep_sem, out_sem, in_free, out_free,
    ) = refs[at_ref + 7 :]
    rows, width = acc.shape
    total = layers * GROUPS
    reduction = Reduction(
        grads, sums, 2 * total,
        (y_buf, x_buf, z0_buf, z1_buf, all_buf, keep_buf),
        (send_sem, recv_sem, sum_send, sum_recv, keep_sem, out_sem, in_free, out_free),
    )
    greet((FLIP_Y, FLIP_X, FLIP_Z0, FLIP_Z1, FLIP_C, SWAP))

    def feed(n, slot, source, target):
        return pltpu.make_async_copy(source, target, feed_sem.at[n, slot])

    def load(n, source, target):
        return pltpu.make_async_copy(source, target, load_sem.at[n])

    def exchange(n, source, target):
        return pltpu.make_async_remote_copy(
            src_ref=source, dst_ref=target, send_sem=core_send.at[n], recv_sem=core_recv.at[n],
            device_id=partner(FLIP_C), device_id_type=MESH,
        )

    def give_du(j, n):
        return pltpu.make_async_remote_copy(
            src_ref=du.at[j], dst_ref=du_sib.at[n], send_sem=du_send.at[n], recv_sem=du_recv.at[n],
            device_id=partner(FLIP_C), device_id_type=MESH,
        )

    def weight(a, group):
        return w_ref.at[a, group]

    def columns(ref, i, size):
        return ref.at[:, pl.ds(pl.multiple_of(i * size, size), size)]

    def unit_store(slot, index):
        return pltpu.make_async_copy(unit_buf.at[slot], grads.at[index], store_sem.at[0])

    def unit(left, left_sib, right, right_sib, slot, index, fresh=False):
        made = (tn(left, right) + tn(left_sib, right_sib)).astype(BF16)
        unit_buf[slot] = made.reshape(unit_buf.shape[1:])
        if fresh is not False:
            pl.when(jnp.logical_not(fresh))(lambda: unit_store(slot, index).wait())
        else:
            unit_store(slot, index).wait()
        unit_store(slot, index).start()

    def add_small(l, row, value):
        small_ref[l, row : row + 1, :] += jnp.sum(value, axis=0, keepdims=True)

    stays = lax.axis_index("dp") % 2 == lax.axis_index("tensor")

    def swap(n, source, target, begin):
        here = pltpu.make_async_copy(source, target, swap_sem.at[n])
        there = pltpu.make_async_remote_copy(
            src_ref=source, dst_ref=target, send_sem=core_send.at[4 + n], recv_sem=core_recv.at[4 + n],
            device_id=partner(SWAP), device_id_type=MESH,
        )

        @pl.when(stays)
        def _():
            here.start() if begin else here.wait()

        @pl.when(jnp.logical_not(stays))
        def _():
            there.start() if begin else there.wait()

    swap(1, x_ref, x_out, True)
    load(0, saved[-1][6], r_buf).start()
    start_up = load(1, up_ref, da)
    start_up.start()
    start_up.wait()
    small_ref[...] = jnp.zeros_like(small_ref)

    def widen(at):
        acc[at, :] = da[at, :].astype(F32)

    row_tiles(rows, widen)
    done = 0
    for l in reversed(range(layers)):
        qkv_ref, sib_ref, ctx_ref, ctx_sib_ref, lse_ref, r1_ref, r2_ref, hl_ref, hl_sib_ref, g_ref, g_sib_ref, slope_ref, xb_ref, xb_sib_ref = saved[l]
        first = l * GROUPS
        base = (layers - 1 - l) * GROUPS
        clock = 22 * (layers - 1 - l)

        def down_feeds(i, slot):
            return (
                feed(0, slot, columns(g_ref, i, 512), left_buf.at[slot]),
                feed(1, slot, columns(g_sib_ref, i, 512), left_sib_buf.at[slot]),
            )

        begin(down_feeds)
        load(0, r2_ref, r_buf).wait()

        def second(at):
            dy = acc[at, :]
            dr, part = norm_back(dy, r_buf[at, :], vec_ref[l, 4:5, :])
            acc[at, :] = dr
            dm[at, :] = dr.astype(BF16)
            add_small(l, 0, part)
            add_small(l, 1, dy)
            add_small(l, 2, dr)

        row_tiles(rows, second)
        dm_copy = exchange(0, dm, dm_sib)
        dm_copy.start()
        r_load = load(0, r1_ref, r_buf)
        r_load.start()
        right_load = load(1, hl_ref, right_buf)
        right_load.start()
        right_sib_load = load(2, hl_sib_ref, right_sib_buf)
        right_sib_load.start()
        dm_copy.wait()

        def down_body(i, slot):
            fresh = (i == 0) if l == layers - 1 else False
            unit(left_buf[slot], left_sib_buf[slot], dm[...], dm_sib[...], lax.rem(i, 2), base + i, fresh)
            pl.when(i > 0)(lambda: reduction.tick(clock + i - 1))

        def place_of(i):
            a = 1 - lax.div(i, FF_GROUPS)
            return a, lax.rem(i, FF_GROUPS)

        def ff_feeds(i, slot):
            a, n = place_of(i)
            j = a * FF_GROUPS + n
            return (
                feed(2, slot, weight(a, first + down_group(n)), wa_buf.at[slot]),
                feed(3, slot, weight(a, first + in_group(n)), wb_buf.at[slot]),
                feed(4, slot, columns(slope_ref, j, 512), slope_buf.at[slot]),
            )

        begin(ff_feeds)
        stream(FF_GROUPS, down_feeds, down_body)
        unit_store(1, base + FF_GROUPS - 1).wait()

        def ff_body(i, slot):
            a, n = place_of(i)
            j = a * FF_GROUPS + n
            dg = nt(dm[...], block_of(wa_buf.at[slot]))
            d = (dg * slope_buf[slot].astype(F32)).astype(BF16)
            du[j] = d
            pl.when(a == 1)(lambda: give_du(j, n).start())
            dbi_ref[l, a, n] = jnp.sum(d.astype(F32), axis=0, keepdims=True)
            acc[...] += nn(d, block_of(wb_buf.at[slot]))
            pl.when(lax.rem(i, 2) == 1)(lambda: reduction.tick(clock + 3 + lax.div(i, 2)))

        stream(2 * FF_GROUPS, ff_feeds, ff_body)

        def out_feeds(i, slot):
            return (feed(2, slot, weight(i, first + OUT_GROUP), wa_buf.at[slot]),)

        begin(out_feeds)
        r_load.wait()

        def first_norm(at):
            dy = acc[at, :]
            dr, part = norm_back(dy, r_buf[at, :], vec_ref[l, 1:2, :])
            dr1[at, :] = dr
            da[at, :] = dr.astype(BF16)
            add_small(l, 3, part)
            add_small(l, 4, dy)
            add_small(l, 5, dr)

        row_tiles(rows, first_norm)
        if l > 0:
            load(0, saved[l - 1][6], r_buf).start()
        da_copy = exchange(1, da, da_sib)
        da_copy.start()

        def out_body(i, slot):
            dctx[:, pl.ds(pl.multiple_of(i * 512, 512), 512)] = nt(da[...], block_of(wa_buf.at[slot])).astype(BF16)

        stream(2, out_feeds, out_body)

        pairs = width // 128

        def pair_feeds(p, slot):
            far = lax.rem(p + pairs // 2, pairs)
            return (
                feed(5, slot, columns(qkv_ref.at[0], p, 128), pair_buf.at[slot, 0, pl.ds(0, rows)]),
                feed(6, slot, columns(qkv_ref.at[1], p, 128), pair_buf.at[slot, 1, pl.ds(0, rows)]),
                feed(7, slot, columns(sib_ref.at[0], far, 128), pair_buf.at[slot, 1, pl.ds(rows, rows)]),
                feed(8, slot, columns(qkv_ref.at[2], p, 128), pair_buf.at[slot, 2, pl.ds(0, rows)]),
                feed(9, slot, columns(sib_ref.at[1], far, 128), pair_buf.at[slot, 2, pl.ds(rows, rows)]),
                feed(10, slot, columns(ctx_ref, p, 128), pair_buf.at[slot, 3, pl.ds(0, rows)]),
                feed(11, slot, lse_ref.at[p], lse_buf.at[slot]),
            )

        begin(pair_feeds)
        right_load.wait()
        right_sib_load.wait()

        def in_body(n, _):
            give_du(FF_GROUPS + n, n).wait()
            unit(du[n], du_sib[n], right_buf[...], right_sib_buf[...], lax.rem(n, 2), base + FF_GROUPS + n, n == 0)
            reduction.tick(clock + 7 + n)
            return 0

        lax.fori_loop(0, FF_GROUPS, in_body, 0)

        right_load = load(1, xb_ref, right_buf)
        right_load.start()
        right_sib_load = load(2, xb_sib_ref, right_sib_buf)
        right_sib_load.start()
        left_load = load(3, columns(ctx_ref, 0, 512), left_buf.at[0])
        left_load.start()
        left_sib_load = load(4, ctx_sib_ref, left_sib_buf.at[0])
        left_sib_load.start()
        da_copy.wait()
        left_load.wait()
        left_sib_load.wait()
        unit(left_buf[0], left_sib_buf[0], da[...], da_sib[...], 0, base + 2 * FF_GROUPS)
        reduction.tick(clock + 11)
        unit_store(0, base + 2 * FF_GROUPS).wait()

        def dx_feeds(i, slot):
            return (feed(3, slot, weight(lax.rem(i, 2), first + lax.rem(lax.div(i, 2) + 2, 3)), wa_buf.at[slot]),)

        begin(dx_feeds)

        def give_pair(p):
            far = lax.rem(p + pairs // 2, pairs)
            at = pl.ds(pl.multiple_of(far * 128, 128), 128)
            return pltpu.make_async_remote_copy(
                src_ref=kv_out.at[:, :, at], dst_ref=kv_far.at[:, :, at], send_sem=pair_send.at[p], recv_sem=pair_recv.at[far],
                device_id=partner(FLIP_C), device_id_type=MESH,
            )

        def pair_body(p, slot):
            far = lax.rem(p + pairs // 2, pairs)
            here = pl.ds(pl.multiple_of(p * 128, 128), 128)
            mask = [spread_mask(mask_ref[2 * p + e], key_ref[...]) for e in range(2)]
            dq, dk, dv = attend_back_pair(
                pair_buf[slot, 0, 0:rows], pair_buf[slot, 1], pair_buf[slot, 2], hot_buf[...], mask,
                pair_buf[slot, 3, 0:rows], lse_buf[slot], dctx[:, here],
            )
            dqkv[0, :, here] = dq.astype(BF16)
            dqkv[1, :, here] = dk[:rows].astype(BF16)
            dqkv[2, :, here] = dv[:rows].astype(BF16)
            there = pl.ds(pl.multiple_of(far * 128, 128), 128)
            kv_out[0, :, there] = dk[rows:].astype(BF16)
            kv_out[1, :, there] = dv[rows:].astype(BF16)
            give_pair(p).start()
            pl.when(lax.rem(p, 4) < 3)(lambda: reduction.tick(clock + 12 + 3 * lax.div(p, 4) + lax.rem(p, 4)))

        stream(pairs, pair_feeds, pair_body)

        def settle_pair(p, _):
            give_pair(p).wait()
            return 0

        lax.fori_loop(0, pairs, settle_pair, 0)
        for n in range(2):
            add_rows(dqkv.at[1 + n], kv_far.at[n], rows)
        d_copy = exchange(3, dqkv.at[:, :, pl.ds(512, 512)], d_sib)
        d_copy.start()
        right_load.wait()
        right_sib_load.wait()
        d_copy.wait()

        def qkv_body(n, _):
            unit(
                dqkv[n, :, 0:512], d_sib[n], right_buf[...], right_sib_buf[...],
                lax.rem(n + 1, 2), base + 2 * FF_GROUPS + 1 + n, n == 0,
            )
            pl.when(n > 0)(lambda: reduction.tick(clock + 17 + n))
            return 0

        lax.fori_loop(0, 3, qkv_body, 0)

        def start_dx(at):
            acc[at, :] = dr1[at, :]

        row_tiles(rows, start_dx)

        def dx_body(i, slot):
            a, n = lax.rem(i, 2), lax.div(i, 2)
            d = dqkv[n, :, pl.ds(pl.multiple_of(a * 512, 512), 512)]
            qkv_sums_ref[l, n, a] = jnp.sum(d.astype(F32), axis=0, keepdims=True)
            acc[...] += nn(d, block_of(wa_buf.at[slot]))
            pl.when(lax.rem(i, 3) == 2)(lambda: reduction.tick(clock + 20 + lax.div(i, 3)))

        stream(6, dx_feeds, dx_body)
        done = clock + 22

    def narrow(at):
        da[at, :] = acc[at, :].astype(BF16)

    row_tiles(rows, narrow)
    unit_store(1, total - 1).wait()
    swap(0, da, dx_out, True)

    def rest(t, _):
        reduction.tick(t)
        return 0

    lax.fori_loop(done, 2 * total + LAST_TICK, rest, 0)
    swap(0, da, dx_out, False)
    swap(1, x_ref, x_out, False)


def backward(upstream, stream_low, weights, hot, mask, mask_rows, vectors, saved):
    rows, width = upstream.shape
    layers = len(saved)
    total = layers * GROUPS
    anywhere = pl.BlockSpec(memory_space=pl.ANY)
    in_vmem = pl.BlockSpec(memory_space=pltpu.VMEM)
    low = lambda *shape: pltpu.VMEM(shape, BF16)
    dma = lambda *shape: pltpu.SemaphoreType.DMA(shape)
    return pl.pallas_call(
        functools.partial(backward_kernel, layers),
        out_shape=(
            jax.ShapeDtypeStruct((total, 16, 32, width), BF16),
            jax.ShapeDtypeStruct((total, 16, 32, width), BF16),
            jax.ShapeDtypeStruct((rows, width), BF16),
            jax.ShapeDtypeStruct((rows, width), BF16),
            jax.ShapeDtypeStruct((layers, 2, FF_GROUPS, 1, 512), F32),
            jax.ShapeDtypeStruct((layers, 3, 2, 1, 512), F32),
            jax.ShapeDtypeStruct((layers, 8, width), F32),
        ),
        in_specs=[anywhere] * 3 + [in_vmem] * 4 + [anywhere] * (PER_LAYER * layers),
        out_specs=(anywhere, anywhere, anywhere, anywhere, in_vmem, in_vmem, in_vmem),
        scratch_shapes=[
            pltpu.VMEM((rows, width), F32),
            pltpu.VMEM((rows, width), F32),
            low(rows, width),
            low(rows, width),
            low(rows, width),
            low(rows, width),
            low(2 * FF_GROUPS, rows, 512),
            low(FF_GROUPS, rows, 512),
            low(rows, width),
            low(3, rows, width),
            low(3, rows, 512),
            low(2, rows, width),
            low(2, rows, width),
            low(2, 2, 256, width),
            low(2, 2, 256, width),
            pltpu.VMEM((rows, width), F32),
            low(2, rows, 512),
            low(2, rows, 512),
            low(2, rows, 512),
            low(rows, width),
            low(rows, width),
            low(2, 4, 2 * rows, 128),
            pltpu.VMEM((2, 2, rows), F32),
            low(2, 16, 32, width),
            low(SLOTS, 8, 16, width),
            low(SLOTS, 4, 16, width),
            low(SLOTS, 2, 16, width),
            low(SLOTS, 1, 16, width),
            low(SLOTS, 8, 16, width),
            low(2, 8, 16, width),
            dma(12, 2),
            dma(5),
            dma(1),
            dma(2),
            dma(6),
            dma(6),
            dma(FF_GROUPS),
            dma(FF_GROUPS),
            dma(width // 128),
            dma(width // 128),
            dma(7, SLOTS),
            dma(7, SLOTS),
            dma(2 * total),
            dma(2 * total),
            dma(2),
            dma(SLOTS),
            pltpu.SemaphoreType.REGULAR((4,)),
            pltpu.SemaphoreType.REGULAR((3,)),
        ],
        compiler_params=pltpu.CompilerParams(
            collective_id=1, has_side_effects=True, vmem_limit_bytes=60 << 20
        ),
        cost_estimate=pl.CostEstimate(flops=60 << 30, bytes_accessed=300 << 20, transcendentals=1 << 24),
        name="backward",
    )(upstream, stream_low, weights, hot, mask, mask_rows, vectors, *[ref for one in saved for ref in one])


def flip_order(values, axis, bits):
    for i, bit in enumerate(bits):
        values = jnp.where(bit == 0, values, jnp.flip(values, axis + i))
    return values


def sequence_shards(
    block_input, segment_ids, random_blocks, w_qkv, b_qv, w_out, b_out, w_in, b_in, w_down, b_down,
    ln_gain, ln_bias, cotangent,
):
    y = lax.axis_index("tensor")
    dp = lax.axis_index("dp")
    core, x_bit, z0, z1 = dp % 2, (dp // 2) % 2, (dp // 4) % 2, dp // 8
    code = core * 8 + x_bit * 4 + z0 * 2 + z1
    code_arg = code.reshape(1).astype(jnp.int32)
    device_bits = (core, x_bit, z0, z1)

    rows, _, width = block_input.shape
    layers = w_qkv.shape[0]
    blocks = random_blocks.shape[2]
    own_blocks = blocks // 2
    heads = random_blocks.shape[1] * 2

    chosen = random_blocks[0]
    near = jnp.concatenate([chosen.reshape(-1), segment_ids[0]])
    sibling = flip(near, FLIP_C)
    across, diagonal = flip(chosen.reshape(-1), FLIP_Y), flip(chosen.reshape(-1), SWAP)
    mine = jnp.concatenate([near[: chosen.size], across, near[chosen.size :]])
    other = jnp.concatenate([sibling[: chosen.size], diagonal, sibling[chosen.size :]])
    packed = jnp.where(core == y, mine, other)
    chosen = packed[: 2 * chosen.size].reshape(2, heads // 2, blocks, -1)
    segments = packed[2 * random_blocks.size :]
    chosen = flip_order(chosen.reshape(2, 2, 2, 2, blocks, -1), 1, device_bits[:3])
    chosen = chosen.transpose(1, 0, 2, 3, 4, 5).reshape(heads, blocks, -1)
    segments = segments.reshape(2, rows)
    segments = jnp.where(core == 0, segments, segments[::-1]).reshape(-1)
    query_block = core * own_blocks + jnp.arange(own_blocks)
    key_block = jnp.arange(blocks) ^ (core * own_blocks)
    allowed = (
        (jnp.abs(query_block[:, None] - key_block[None, :]) <= 1)
        | (key_block[None, :] == 0)
        | (key_block[None, :] == blocks - 1)
        | (query_block[:, None] == 0)
        | (query_block[:, None] == blocks - 1)
    )
    chosen = lax.dynamic_slice_in_dim(chosen, core * own_blocks, own_blocks, axis=1)
    allowed = allowed[None] | jnp.any(chosen[:, :, None, :] == key_block[None, None, :, None], axis=3)
    block_rows = rows // own_blocks
    documents = jnp.arange(128 - own_blocks)
    mask = jnp.pad(
        jnp.where(allowed, 0.0, BIG).astype(F32).transpose(0, 2, 1), ((0, 0), (0, 0), (0, 128 - own_blocks))
    )
    document_part = jnp.where(
        (segments[:, None] == documents[None, :]) | (documents[None, :] > 7), 0.0, BIG
    ).astype(F32)
    mask_rows = jnp.pad(document_part, ((0, 0), (own_blocks, 0)))
    block_rows = rows // own_blocks
    hot = jnp.concatenate(
        [
            jnp.repeat(jnp.eye(own_blocks, dtype=BF16), block_rows, axis=0),
            (segments[:rows, None] == documents[None, :]).astype(BF16),
        ],
        axis=1,
    )

    bias_pack = jnp.concatenate(
        [
            flip_order(b_qv.reshape(layers * 2, 2, 2, 2, 2, -1), 1, device_bits).reshape(-1),
            flip_order(b_in.reshape(layers * FF_GROUPS, 2, 2, 2, 2, -1), 1, device_bits).reshape(-1),
        ]
    )
    bias_far = flip(bias_pack, FLIP_Y)
    n_qv = b_qv.size

    def local_bias(near, far, count):
        near, far = near.reshape(count, 2, 1, 256), far.reshape(count, 2, 1, 256)
        return jnp.concatenate([near, far], axis=2).reshape(count, 2, 512)

    bias_qv = local_bias(bias_pack[:n_qv], bias_far[:n_qv], layers * 2).reshape(layers, 2, 2, 1, 512)
    bias_qkv = jnp.stack([bias_qv[:, 0], jnp.zeros_like(bias_qv[:, 0]), bias_qv[:, 1]], axis=1)
    bias_in = local_bias(bias_pack[n_qv:], bias_far[n_qv:], layers * FF_GROUPS)
    bias_in = bias_in.reshape(layers, FF_GROUPS, 2, 1, 512).swapaxes(1, 2)

    vectors = [
        jnp.stack(
            [
                b_out[l], ln_gain[l, 0], ln_bias[l, 0], b_down[l], ln_gain[l, 1], ln_bias[l, 1],
                b_out[l], b_out[l],
            ]
        )
        for l in range(layers)
    ]
    vectors = jnp.stack(vectors)
    weights, upstream_low, stream_low, saved = forward(
        block_input, cotangent, w_qkv, w_out, w_in, w_down, hot, mask, mask_rows, bias_qkv, bias_in, vectors
    )
    _, grads, dx_low, x_low, d_b_in, qkv_sums, rows_small = backward(
        upstream_low, stream_low, weights, hot, mask, mask_rows, vectors, saved
    )
    grads = grads.reshape(layers * GROUPS, 512, width)
    block_output, input_grad = widen_rows(x_low, dx_low)

    stacks = [
        jnp.stack([qkv_sums[:, 0], qkv_sums[:, 2]], axis=1),
        rows_small[:, 5],
        d_b_in.swapaxes(1, 2),
        rows_small[:, 2],
        jnp.stack([rows_small[:, 3], rows_small[:, 0]], axis=1),
        jnp.stack([rows_small[:, 4], rows_small[:, 1]], axis=1),
    ]

    def global_order(values, lead):
        values = values.reshape(lead, 2, 2, 2, 2, 2, 32).swapaxes(1, 2)
        values = flip_order(values, 1, (y,) + device_bits)
        return values.swapaxes(0, 1).reshape(2, -1)

    stacks[0] = global_order(stacks[0], layers * 2)
    stacks[2] = global_order(stacks[2], layers * FF_GROUPS)
    def placing(shape, block, index, turned, count, start):
        return lambda values: place(
            values, shape, block, index, turned, count, lambda l, i: (layers - 1 - l) * GROUPS + start + i, code_arg
        )

    summed = jnp.concatenate([s.reshape(-1) for s in stacks])
    summed = summed + flip(summed, FLIP_C)
    placed = []
    for bit, put in (
        (FLIP_Y, placing(w_down.shape, (1, 512, width), lambda l, i: (l, i, 0), False, FF_GROUPS, 0)),
        (FLIP_X, placing(w_in.shape, (1, width, 512), lambda l, i: (l, 0, i), True, FF_GROUPS, FF_GROUPS)),
        (FLIP_Z0, placing(w_qkv.shape, (1, 1, width, 512), lambda l, i: (l, i, 0, 0), True, 3, 2 * FF_GROUPS + 1)),
        (FLIP_Z1, placing(w_out.shape, (1, 512, width), lambda l, i: (l, 0, 0), False, 1, 2 * FF_GROUPS)),
    ):
        summed, grads = lax.optimization_barrier((summed, grads))
        far = flip(summed, bit)
        done, summed, far = lax.optimization_barrier((put(grads), summed, far))
        placed.append(done)
        summed = summed + far
    parts, at = [], 0
    for s in stacks:
        parts.append(summed[at : at + s.size].reshape(s.shape))
        at += s.size
    g_b_qv = lax.dynamic_index_in_dim(parts[0], y, axis=0, keepdims=False).reshape(b_qv.shape)
    g_b_in = lax.dynamic_index_in_dim(parts[2], y, axis=0, keepdims=False).reshape(b_in.shape)
    return (
        block_output,
        input_grad,
        placed[2],
        g_b_qv,
        placed[3],
        parts[1],
        placed[1],
        g_b_in,
        placed[0],
        parts[3],
        parts[4],
        parts[5],
    )


def as_sent(array):

    def short(part):
        return part.astype(jnp.bfloat16) if part.dtype == jnp.float32 else part

    return jax.tree.map(short, array)


def norm_rows(values, gain_row, shift_row):
    row_mean = jnp.mean(values, axis=-1, keepdims=True)
    centred = values - row_mean
    variance = jnp.mean(centred * centred, axis=-1, keepdims=True)
    return centred * lax.rsqrt(variance + 1e-06) * gain_row + shift_row


def gelu_exact(values):
    return jax.nn.gelu(values, approximate=False)


def block_mask(chosen_blocks, segment_rows):
    nblocks = chosen_blocks.shape[2]
    block_index = jnp.arange(nblocks)
    near_blocks = jnp.abs(block_index[:, None] - block_index[None, :]) <= 1
    edge_blocks = (
        (block_index[None, :] == 0)
        | (block_index[None, :] == nblocks - 1)
        | (block_index[:, None] == 0)
        | (block_index[:, None] == nblocks - 1)
    )
    picked_blocks = jnp.any(chosen_blocks[..., None] == block_index, axis=3)
    allowed = near_blocks | edge_blocks | picked_blocks
    block_rows = segment_rows.shape[1] // nblocks
    allowed = jnp.repeat(jnp.repeat(allowed, block_rows, axis=2), block_rows, axis=3)
    same_doc = segment_rows[:, :, None] == segment_rows[:, None, :]
    return allowed & same_doc[:, None]


def masked_scores(queries, key_rows, allowed, score_scale):
    scores = (
        jnp.einsum("qshd,kshd->shqk", queries, key_rows, preferred_element_type=jnp.float32)
        * score_scale
    )
    return jnp.where(allowed, scores, -1e30)


def shards(
    block_input,
    segment_ids,
    random_blocks,
    w_qkv,
    b_qv,
    w_out,
    b_out,
    w_in,
    b_in,
    w_down,
    b_down,
    ln_gain,
    ln_bias,
    cotangent,
):
    score_scale = HEAD_DIM ** (-0.5)
    shard_rows, seq_count, model_width = block_input.shape
    layers = w_qkv.shape[0]
    local_width = w_qkv.shape[3]
    local_heads = local_width // HEAD_DIM
    allowed = block_mask(random_blocks, segment_ids)
    saved_acts = []
    stream = block_input
    for layer_index in range(layers):
        w_proj = w_qkv[layer_index].astype(jnp.bfloat16)
        w_mix = w_out[layer_index].astype(jnp.bfloat16)
        rows_low = stream.astype(jnp.bfloat16)
        full_rows = lax.all_gather(rows_low, "tensor", axis=0, tiled=True)
        length = full_rows.shape[0]
        projected = jnp.einsum(
            "lsd,tdc->tlsc", full_rows, w_proj, preferred_element_type=jnp.float32
        )
        qkv_bias = jnp.stack(
            [b_qv[layer_index, 0], jnp.zeros_like(b_qv[layer_index, 0]), b_qv[layer_index, 1]]
        )
        qkv_low = (projected + qkv_bias[:, None, None, :]).astype(jnp.bfloat16)
        head_view = qkv_low.reshape(3, length, seq_count, local_heads, HEAD_DIM)
        scores = masked_scores(head_view[0], head_view[1], allowed, score_scale)
        row_top = jnp.max(scores, axis=-1, keepdims=True)
        log_total = row_top + jnp.log(jnp.sum(jnp.exp(scores - row_top), axis=-1, keepdims=True))
        probs_low = jnp.exp(scores - log_total).astype(jnp.bfloat16)
        context = jnp.einsum(
            "shqk,kshd->qshd", probs_low, head_view[2], preferred_element_type=jnp.float32
        )
        context = context.reshape(length, seq_count, local_width).astype(jnp.bfloat16)
        mixed = lax.psum_scatter(
            jnp.einsum("lsc,cd->lsd", context, w_mix, preferred_element_type=jnp.float32).astype(
                jnp.bfloat16
            ),
            "tensor",
            scatter_dimension=0,
            tiled=True,
        ).astype(jnp.float32)
        first_sum = stream + mixed + b_out[layer_index]
        hidden_rows = norm_rows(first_sum, ln_gain[layer_index, 0], ln_bias[layer_index, 0])
        hidden_low = hidden_rows.astype(jnp.bfloat16)
        up_weight = w_in[layer_index].astype(jnp.bfloat16)
        backward_weight = w_down[layer_index].astype(jnp.bfloat16)
        hidden_full = lax.all_gather(hidden_low, "tensor", axis=0, tiled=True)
        preactivation = (
            jnp.einsum("twn,nj->twj", hidden_full, up_weight, preferred_element_type=jnp.float32)
            + b_in[layer_index]
        )
        activation_reduced = gelu_exact(preactivation).astype(jnp.bfloat16)
        grown = lax.psum_scatter(
            jnp.einsum(
                "unj,jp->unp",
                activation_reduced,
                backward_weight,
                preferred_element_type=jnp.float32,
            ).astype(jnp.bfloat16),
            "tensor",
            scatter_dimension=0,
            tiled=True,
        ).astype(jnp.float32)
        second_sum = hidden_rows + grown + b_down[layer_index]
        stream = norm_rows(second_sum, ln_gain[layer_index, 1], ln_bias[layer_index, 1])
        keep_rows, keep_hidden = (full_rows, hidden_full)
        saved_acts.append(
            (
                keep_rows,
                head_view,
                log_total,
                context,
                first_sum,
                keep_hidden,
                preactivation,
                activation_reduced,
                second_sum,
                up_weight,
                backward_weight,
            )
        )
    upstream = cotangent
    grads_by_layer = [None] * layers
    for layer_index in reversed(range(layers)):
        (
            keep_rows,
            head_view,
            log_total,
            context,
            first_sum,
            keep_hidden,
            preactivation,
            activation_reduced,
            second_sum,
            up_weight,
            backward_weight,
        ) = saved_acts[layer_index]
        full_rows, hidden_full = (keep_rows, keep_hidden)
        length = full_rows.shape[0]
        w_proj = w_qkv[layer_index].astype(jnp.bfloat16)
        w_mix = w_out[layer_index].astype(jnp.bfloat16)
        _, pull_second = jax.vjp(
            norm_rows, second_sum, ln_gain[layer_index, 1], ln_bias[layer_index, 1]
        )
        d_second, d_gain_two, d_shift_two = pull_second(upstream)
        _, pull_gelu = jax.vjp(gelu_exact, preactivation)
        widened_full = lax.all_gather(d_second.astype(jnp.bfloat16), "tensor", axis=0, tiled=True)
        down_gradient = jnp.einsum(
            "uxc,uxw->cw", activation_reduced, widened_full, preferred_element_type=jnp.float32
        )
        activation_gradient = jnp.einsum(
            "mra,xa->mrx", widened_full, backward_weight, preferred_element_type=jnp.float32
        )
        preactivation_gradient_reduced = pull_gelu(activation_gradient)[0].astype(jnp.bfloat16)
        up_gradient = jnp.einsum(
            "kmx,kmt->xt",
            hidden_full,
            preactivation_gradient_reduced,
            preferred_element_type=jnp.float32,
        )
        g_up_bias = jnp.sum(preactivation_gradient_reduced.astype(jnp.float32), axis=(0, 1))
        d_hidden = d_second + lax.psum_scatter(
            jnp.einsum(
                "hmp,tp->hmt",
                preactivation_gradient_reduced,
                up_weight,
                preferred_element_type=jnp.float32,
            ).astype(jnp.bfloat16),
            "tensor",
            scatter_dimension=0,
            tiled=True,
        ).astype(jnp.float32)
        _, pull_first = jax.vjp(
            norm_rows, first_sum, ln_gain[layer_index, 0], ln_bias[layer_index, 0]
        )
        d_first, d_gain_one, d_shift_one = pull_first(d_hidden)
        full_mixed = lax.all_gather(d_first.astype(jnp.bfloat16), "tensor", axis=0, tiled=True)
        g_out = jnp.einsum("lsc,lsd->cd", context, full_mixed, preferred_element_type=jnp.float32)
        d_context = jnp.einsum(
            "lsd,cd->lsc", full_mixed, w_mix, preferred_element_type=jnp.float32
        ).astype(jnp.bfloat16)
        d_context = d_context.reshape(length, seq_count, local_heads, HEAD_DIM)
        queries, key_rows, value_rows = (head_view[0], head_view[1], head_view[2])
        scores = masked_scores(queries, key_rows, allowed, score_scale)
        attn_probs = jnp.exp(scores - log_total)
        probs_low = attn_probs.astype(jnp.bfloat16)
        d_probs = jnp.einsum(
            "qshd,kshd->shqk", d_context, value_rows, preferred_element_type=jnp.float32
        )
        d_scores = attn_probs * (d_probs - jnp.sum(d_probs * attn_probs, axis=-1, keepdims=True))
        d_scores = d_scores.astype(jnp.bfloat16)
        d_query = (
            jnp.einsum("shqk,kshd->qshd", d_scores, key_rows, preferred_element_type=jnp.float32)
            * score_scale
        )
        d_key = (
            jnp.einsum("shqk,qshd->kshd", d_scores, queries, preferred_element_type=jnp.float32)
            * score_scale
        )
        d_value = jnp.einsum(
            "shqk,qshd->kshd", probs_low, d_context, preferred_element_type=jnp.float32
        )
        d_qkv = (
            jnp.stack([d_query, d_key, d_value])
            .reshape(3, length, seq_count, local_width)
            .astype(jnp.bfloat16)
        )
        g_proj = jnp.einsum("lsd,tlsc->tdc", full_rows, d_qkv, preferred_element_type=jnp.float32)
        qkv_sums = jnp.sum(d_qkv.astype(jnp.float32), axis=(1, 2))
        g_bias = jnp.stack([qkv_sums[0], qkv_sums[2]])
        upstream = d_first + lax.psum_scatter(
            jnp.einsum("tlsc,tdc->lsd", d_qkv, w_proj, preferred_element_type=jnp.float32).astype(
                jnp.bfloat16
            ),
            "tensor",
            scatter_dimension=0,
            tiled=True,
        ).astype(jnp.float32)
        weight_grads = (g_proj, g_bias, g_out, up_gradient, g_up_bias, down_gradient)
        small_grads = (
            jnp.sum(d_first, axis=(0, 1)),
            jnp.sum(d_second, axis=(0, 1)),
            jnp.stack([d_gain_one, d_gain_two]),
            jnp.stack([d_shift_one, d_shift_two]),
        )
        grads_by_layer[layer_index] = (weight_grads, small_grads)
    weight_stack = tuple(
        (
            jnp.stack([grads_by_layer[layer_index][0][member] for layer_index in range(layers)])
            for member in range(6)
        )
    )
    small_stack = tuple(
        (
            jnp.stack([grads_by_layer[layer_index][1][member] for layer_index in range(layers)])
            for member in range(4)
        )
    )
    weight_stack = jax.tree.map(
        lambda part: part.astype(jnp.float32), lax.psum(as_sent(weight_stack), "dp")
    )
    small_stack = lax.psum(small_stack, ("dp", "tensor"))
    return (
        stream,
        upstream,
        weight_stack[0],
        weight_stack[1],
        weight_stack[2],
        small_stack[0],
        weight_stack[3],
        weight_stack[4],
        weight_stack[5],
        small_stack[1],
        small_stack[2],
        small_stack[3],
    )


def solution(mesh):
    by_sequence = mesh.shape["tensor"] == 2 and mesh.shape["dp"] == 16
    return jax.shard_map(
        sequence_shards if by_sequence else shards,
        mesh=mesh,
        in_specs=(
            P("tensor", "dp", None),
            P("dp", None),
            P("dp", "tensor", None, None),
            P(None, None, None, "tensor"),
            P(None, None, "tensor"),
            P(None, "tensor", None),
            P(),
            P(None, None, "tensor"),
            P(None, "tensor"),
            P(None, "tensor", None),
            P(),
            P(),
            P(),
            P("tensor", "dp", None),
        ),
        out_specs=(
            P("tensor", "dp", None),
            P("tensor", "dp", None),
            P(None, None, None, "tensor"),
            P(None, None, "tensor"),
            P(None, "tensor", None),
            P(),
            P(None, None, "tensor"),
            P(None, "tensor"),
            P(None, "tensor", None),
            P(),
            P(),
            P(),
        ),
        check_vma=False,
    )
```

```python
import functools

import jax
import jax.numpy as jnp
from jax import lax
from jax.experimental import pallas as pl
from jax.experimental.pallas import tpu as pltpu
from jax.sharding import PartitionSpec as P

HEAD_DIM = 64
BIG = -1e30
BF16 = jnp.bfloat16
F32 = jnp.float32
MESH = pl.DeviceIdType.MESH
VMEM_LIMIT = 56 << 20

FLIP_Y, FLIP_C, FLIP_X, FLIP_Z0, FLIP_Z1 = 1, 2, 4, 8, 16
SWAP = FLIP_Y + FLIP_C
DEVICES = 32

GROUPS = 12
OUT_GROUP = 3
FF_GROUPS = 4


def in_group(s):
    return 4 + 2 * s


def down_group(s):
    return 5 + 2 * s


def flip(values, bit):
    pairs = [(i, i ^ bit) for i in range(DEVICES)]
    return jax.tree.map(lambda v: lax.ppermute(v, ("dp", "tensor"), pairs), values)


def nt(a, b):
    return lax.dot_general(a, b, (((1,), (1,)), ((), ())), preferred_element_type=F32)


def nn(a, b):
    return lax.dot_general(a, b, (((1,), (0,)), ((), ())), preferred_element_type=F32)


def tn(a, b):
    return lax.dot_general(a, b, (((0,), (0,)), ((), ())), preferred_element_type=F32)


def block_of(ref):
    width = ref.shape[-1]
    return ref[...].reshape(-1, width)


def place_kernel(turned, code_ref, g_ref, o_ref, *scratch):
    code = code_ref[0]
    for j in range(16):
        start = pl.multiple_of((j ^ code) * 32, 32)
        block = g_ref[0, pl.ds(start, 32), :].astype(F32)
        if turned:
            scratch[0][j * 32 : (j + 1) * 32, :] = block
        else:
            o_ref[0, j * 32 : (j + 1) * 32, :] = block
    if turned:
        o_ref[...] = scratch[0][...].T.reshape(o_ref.shape)


def place(sums, shape, block, index, turned, count, group, code):
    width = sums.shape[-1]
    return pl.pallas_call(
        functools.partial(place_kernel, turned),
        out_shape=jax.ShapeDtypeStruct(shape, F32),
        grid_spec=pltpu.PrefetchScalarGridSpec(
            num_scalar_prefetch=1,
            grid=(shape[0], count),
            in_specs=[pl.BlockSpec((1, 512, width), lambda l, i, code: (group(l, i), 0, 0))],
            out_specs=pl.BlockSpec(block, lambda l, i, code: index(l, i)),
            scratch_shapes=[pltpu.VMEM((512, width), F32)] if turned else [],
        ),
        compiler_params=pltpu.CompilerParams(vmem_limit_bytes=VMEM_LIMIT),
        cost_estimate=pl.CostEstimate(
            flops=0, bytes_accessed=shape[0] * count * 512 * width * 6, transcendentals=0
        ),
        name="place",
    )(code, sums)


def widen_kernel(a_ref, b_ref, a_out, b_out, a_buf, b_buf, sem):
    copies = []
    for n, (source, target, buf) in enumerate(((a_ref, a_out, a_buf), (b_ref, b_out, b_buf))):
        buf[...] = source[...].astype(F32)
        copies.append(pltpu.make_async_copy(buf, target.at[:, 0], sem.at[n]))
        copies[-1].start()
    for copy in copies:
        copy.wait()


def widen_rows(a, b):
    rows, width = a.shape
    out = jax.ShapeDtypeStruct((rows, 1, width), F32)
    return pl.pallas_call(
        widen_kernel,
        out_shape=(out, out),
        in_specs=[pl.BlockSpec(memory_space=pltpu.VMEM)] * 2,
        out_specs=(pl.BlockSpec(memory_space=pl.ANY),) * 2,
        scratch_shapes=[pltpu.VMEM((rows, width), F32), pltpu.VMEM((rows, width), F32), pltpu.SemaphoreType.DMA((2,))],
        name="widen_rows",
    )(a, b)


def partner(bits):
    dp, y = lax.axis_index("dp"), lax.axis_index("tensor")
    other = dp
    for step in (1, 2, 4, 8):
        if bits & (2 * step):
            other = other + step * (1 - 2 * ((dp // step) % 2))
    return (other, 1 - y if bits & FLIP_Y else y)


def greet(bits):
    barrier = pltpu.get_barrier_semaphore()
    for bit in bits:
        pl.semaphore_signal(barrier, inc=1, device_id=partner(bit), device_id_type=MESH)
    pl.semaphore_wait(barrier, len(bits))


def add_into(into, other, count):
    def step(i, _):
        into[i] = (into[i].astype(F32) + other[i].astype(F32)).astype(BF16)
        return 0

    lax.fori_loop(0, count, step, 0)


def add_rows(into, other, rows):
    def step(i, _):
        at = pl.ds(pl.multiple_of(i * 32, 32), 32)
        into[at, :] = (into[at, :].astype(F32) + other[at, :].astype(F32)).astype(BF16)
        return 0

    lax.fori_loop(0, rows // 32, step, 0)


SLOTS = 6
LAST_TICK = 8


class Reduction:
    def __init__(self, grads, sums, count, bufs, sems):
        self.grads, self.sums, self.count = grads, sums, count
        self.y_buf, self.x_buf, self.z0_buf, self.z1_buf, self.all_buf, self.keep_buf = bufs
        self.send_sem, self.recv_sem, self.core_send, self.core_recv = sems[:4]
        self.keep_sem, self.out_sem, self.in_free, self.out_free = sems[4:]

    def copy(self, step, i):
        slot = lax.rem(i, SLOTS)
        ys, al = self.y_buf.at[slot], self.all_buf.at[slot]
        bit, source, target = (
            (FLIP_Y, self.grads.at[i, pl.ds(256, 256)], ys),
            (FLIP_X, ys.at[pl.ds(128, 128)], self.x_buf.at[slot]),
            (FLIP_Z0, ys.at[pl.ds(64, 64)], self.z0_buf.at[slot]),
            (FLIP_Z1, ys.at[pl.ds(32, 32)], self.z1_buf.at[slot]),
            (FLIP_Z1, al.at[pl.ds(0, 32)], al.at[pl.ds(32, 32)]),
            (FLIP_Z0, al.at[pl.ds(0, 64)], al.at[pl.ds(64, 64)]),
            (FLIP_X, al.at[pl.ds(0, 128)], al.at[pl.ds(128, 128)]),
            (FLIP_C, al, self.sums.at[i, pl.ds(256, 256)]),
        )[step]
        return pltpu.make_async_remote_copy(
            src_ref=source,
            dst_ref=target,
            send_sem=self.send_sem.at[step, slot] if step < 7 else self.core_send.at[i],
            recv_sem=self.recv_sem.at[step, slot] if step < 7 else self.core_recv.at[i],
            device_id=partner(bit),
            device_id_type=MESH,
        )

    def keep(self, i):
        slot = lax.rem(i, 2)
        return pltpu.make_async_copy(
            self.grads.at[i, pl.ds(0, 256)], self.keep_buf.at[slot], self.keep_sem.at[slot]
        )

    def out(self, i):
        slot = lax.rem(i, SLOTS)
        return pltpu.make_async_copy(
            self.all_buf.at[slot], self.sums.at[i, pl.ds(0, 256)], self.out_sem.at[slot]
        )

    def take(self, sem, i):
        @pl.when(i >= SLOTS)
        def _():
            pl.semaphore_wait(sem, 1)

    def give(self, sem, bit, i):
        @pl.when(i + SLOTS < self.count)
        def _():
            pl.semaphore_signal(sem, inc=1, device_id=partner(bit), device_id_type=MESH)

    def tick(self, t):
        def at(offset, body):
            i = t - offset
            pl.when((i >= 0) & (i < self.count))(lambda: body(i, lax.rem(i, SLOTS)))

        def set_out(i, slot):
            self.take(self.in_free.at[0], i)
            self.copy(0, i).start()
            self.keep(i).start()

        def finish(i, slot):
            self.copy(7, i).wait()
            self.out(i).wait()
            for n, bit in enumerate((FLIP_X, FLIP_Z0, FLIP_Z1)):
                self.give(self.out_free.at[n], bit, i)

        def to_core(i, slot):
            self.copy(6, i).wait()
            self.copy(7, i).start()
            self.out(i).start()

        def back_x(i, slot):
            self.copy(5, i).wait()
            self.take(self.out_free.at[0], i)
            self.copy(6, i).start()

        def back_z0(i, slot):
            self.copy(4, i).wait()
            self.take(self.out_free.at[1], i)
            self.copy(5, i).start()

        def back_z1(i, slot):
            self.copy(3, i).wait()
            add_rows(self.y_buf.at[slot], self.z1_buf.at[slot], 32)
            self.all_buf[slot, 0:32, :] = self.y_buf[slot, 0:32, :]
            for n, bit in enumerate((FLIP_Y, FLIP_X, FLIP_Z0, FLIP_Z1)):
                self.give(self.in_free.at[n], bit, i)
            self.take(self.out_free.at[2], i)
            self.copy(4, i).start()

        def on_z1(i, slot):
            self.copy(2, i).wait()
            add_rows(self.y_buf.at[slot], self.z0_buf.at[slot], 64)
            self.take(self.in_free.at[3], i)
            self.copy(3, i).start()

        def on_z0(i, slot):
            self.copy(1, i).wait()
            add_rows(self.y_buf.at[slot], self.x_buf.at[slot], 128)
            self.take(self.in_free.at[2], i)
            self.copy(2, i).start()

        def on_x(i, slot):
            self.copy(0, i).wait()
            self.keep(i).wait()
            add_rows(self.y_buf.at[slot], self.keep_buf.at[lax.rem(i, 2)], 256)
            self.take(self.in_free.at[1], i)
            self.copy(1, i).start()

        at(0, set_out)
        at(8, finish)
        at(7, to_core)
        at(6, back_x)
        at(5, back_z0)
        at(4, back_z1)
        at(3, on_z1)
        at(2, on_z0)
        at(1, on_x)


def begin(feeds):
    for copy in feeds(0, 0):
        copy.start()


def stream(count, feeds, body):
    def step(i, _):
        slot = lax.rem(i, 2)

        @pl.when(i + 1 < count)
        def _():
            for copy in feeds(i + 1, 1 - slot):
                copy.start()

        for copy in feeds(i, slot):
            copy.wait()
        body(i, slot)
        return 0

    lax.fori_loop(0, count, step, 0)


def norm(r, gain, shift):
    centred = r - jnp.mean(r, axis=-1, keepdims=True)
    rstd = lax.rsqrt(jnp.mean(centred * centred, axis=-1, keepdims=True) + 1e-06)
    return centred * rstd * gain + shift


def norm_back(dy, r, gain):
    centred = r - jnp.mean(r, axis=-1, keepdims=True)
    rstd = lax.rsqrt(jnp.mean(centred * centred, axis=-1, keepdims=True) + 1e-06)
    unit = centred * rstd
    dunit = dy * gain
    dr = rstd * (
        dunit
        - jnp.mean(dunit, axis=-1, keepdims=True)
        - unit * jnp.mean(dunit * unit, axis=-1, keepdims=True)
    )
    return dr, dy * unit


def gelu_and_slope(u):
    cdf = 0.5 * (1.0 + lax.erf(u * (0.5**0.5)))
    pdf = jnp.exp(-0.5 * u * u) * 0.3989422804014327
    return u * cdf, cdf + u * pdf


TILE = 64


def row_tiles(rows, body):
    def step(i, _):
        body(pl.ds(pl.multiple_of(i * TILE, TILE), TILE))
        return 0

    lax.fori_loop(0, rows // TILE, step, 0)


def pair_lanes(values, e):
    lane = lax.broadcasted_iota(jnp.int32, values.shape, 1)
    return jnp.where(lane // HEAD_DIM == e, values, jnp.zeros_like(values))


def spread_mask(block_part, document_part):
    blocks, lanes = block_part.shape
    each = document_part.shape[0] // blocks
    part = jnp.broadcast_to(block_part[:, None, :], (blocks, each, lanes)).reshape(blocks * each, lanes)
    return (part + document_part).astype(BF16)


def both_heads(values):
    return jnp.concatenate([pair_lanes(values, 0), pair_lanes(values, 1)], axis=0)


def attend_pair(query, keys, values, hot, mask):
    scale = HEAD_DIM**-0.5
    rows = query.shape[0]
    query = query * jnp.asarray(scale, BF16)
    right = jnp.concatenate([both_heads(query), both_heads(hot)], axis=1)
    s = nt(jnp.concatenate([keys, mask], axis=1), right)
    top = jnp.max(s, axis=0, keepdims=True)
    p = jnp.exp(s - top)
    total = jnp.sum(p, axis=0, keepdims=True)
    c = nn(values.T, p.astype(BF16)) * (1.0 / total)
    context = jnp.concatenate([c[:HEAD_DIM, :rows], c[HEAD_DIM:, rows:]], axis=0).T
    lse = top + jnp.log(total)
    return context, [lse[:, :rows], lse[:, rows:]]


def attend_back_pair(query, keys, values, hot, mask, ctx, lse, dctx):
    scale = HEAD_DIM**-0.5
    rows = query.shape[0]
    query = query * jnp.asarray(scale, BF16)
    keys_t = keys.T
    delta_t = (dctx.astype(F32) * ctx.astype(F32)).T
    left = jnp.concatenate([keys, mask], axis=1)
    tile = rows // 2
    dk, dv, dq = 0.0, 0.0, []
    for part in range(2):
        at = slice(part * tile, (part + 1) * tile)
        heads = []
        for e in range(2):
            lanes = slice(e * HEAD_DIM, (e + 1) * HEAD_DIM)
            query_e = pair_lanes(query[at], e)
            dctx_e = pair_lanes(dctx[at], e)
            right = jnp.concatenate([query_e, pair_lanes(hot[at], e)], axis=1)
            p = jnp.exp(nt(left, right) - lse[e : e + 1, at])
            dp = nt(values, dctx_e)
            delta = jnp.sum(delta_t[lanes, at], axis=0, keepdims=True)
            ds = (p * (dp - delta)).astype(BF16)
            dk = dk + nn(ds, query_e)
            dv = dv + nn(p.astype(BF16), dctx_e)
            heads.append(nn(keys_t[lanes, :], ds) * scale)
        dq.append(jnp.concatenate(heads, axis=0).T)
    return jnp.concatenate(dq, axis=0), dk, dv


class Spread:
    def __init__(self, weights, pairs, send_sem, recv_sem):
        self.weights, self.pairs, self.send_sem, self.recv_sem = weights, pairs, send_sem, recv_sem

    def copy(self, step, t):
        w = self.weights
        even, odd = 2 * t, 2 * t + 1
        bit, source, target = (
            (FLIP_Y, w.at[0, even, 0, pl.ds(0, 64)], w.at[0, even, 1, pl.ds(0, 64)]),
            (FLIP_Y, w.at[0, odd, 0, pl.ds(0, 64)], w.at[0, odd, 1, pl.ds(0, 64)]),
            (FLIP_X, w.at[0, even, 1, pl.ds(0, 64)], w.at[0, even, 1, pl.ds(128, 64)]),
            (FLIP_Z0, w.at[0, odd, 1, pl.ds(0, 64)], w.at[0, odd, 1, pl.ds(64, 64)]),
            (FLIP_Z0, w.at[0, even, 1, pl.ds(0, 64)], w.at[0, even, 1, pl.ds(64, 64)]),
            (FLIP_Z0, w.at[0, even, 1, pl.ds(128, 64)], w.at[0, even, 1, pl.ds(192, 64)]),
            (FLIP_X, w.at[0, odd, 1, pl.ds(0, 128)], w.at[0, odd, 1, pl.ds(128, 128)]),
            (FLIP_C, w.at[0, even, 1], w.at[1, even, 1]),
            (FLIP_C, w.at[0, odd, 1], w.at[1, odd, 1]),
        )[step]
        return pltpu.make_async_remote_copy(
            src_ref=source,
            dst_ref=target,
            send_sem=self.send_sem.at[step, t],
            recv_sem=self.recv_sem.at[step, t],
            device_id=partner(bit),
            device_id_type=MESH,
        )

    def tick(self, t):
        def at(offset, waits, starts):
            i = t - offset

            @pl.when((i >= 0) & (i < self.pairs))
            def _():
                for step in waits:
                    self.copy(step, i).wait()
                for step in starts:
                    self.copy(step, i).start()

        at(0, (), (0, 1))
        at(5, (7, 8), ())
        at(1, (0, 1), (2, 3))
        at(2, (2, 3), (4, 5, 6))
        at(4, (4, 5, 6), (7, 8))


PER_LAYER = 14
DEPTH = 3


def forward_kernel(layers, *refs):
    refs = list(refs)
    x_ref, up_ref, wq_ref, wo_ref, wi_ref, wd_ref = refs[:6]
    hot_buf, mask_ref, key_ref, bq_ref, bi_ref, vec_ref = refs[6:12]
    w_ref, up_out, x_out = refs[12:15]
    saved = [refs[15 + PER_LAYER * l : 15 + PER_LAYER * (l + 1)] for l in range(layers)]
    (
        x, acc, r_buf, low, xb, qkv, kv_sib, ctx, lse, hl, g_all, slope_all,
        col_buf, row_buf, turn_buf, made_buf, wa_buf, wb_buf,
        feed_sem, load_sem, col_sem, row_sem, made_sem, store_sem, block_sem,
        core_send, core_recv, kv_send, kv_recv, g_send, g_recv, spread_send, spread_recv,
    ) = refs[15 + PER_LAYER * layers :]
    rows, width = acc.shape
    dp, y = lax.axis_index("dp"), lax.axis_index("tensor")
    core = dp % 2
    stays = core == y
    spread = Spread(w_ref, layers * GROUPS // 2, spread_send, spread_recv)
    greet((FLIP_Y, FLIP_X, FLIP_Z0, FLIP_C, SWAP))

    def feed(n, slot, source, target):
        return pltpu.make_async_copy(source, target, feed_sem.at[n, slot])

    def load(n, source, target):
        return pltpu.make_async_copy(source, target, load_sem.at[n])

    def store(n, source, target):
        return pltpu.make_async_copy(source, target, store_sem.at[n])

    def exchange(n, source, target, bits=FLIP_C):
        return pltpu.make_async_remote_copy(
            src_ref=source, dst_ref=target, send_sem=core_send.at[n], recv_sem=core_recv.at[n],
            device_id=partner(bits), device_id_type=MESH,
        )

    def columns(ref, i, size):
        return ref.at[:, pl.ds(pl.multiple_of(i * size, size), size)]

    def swap(n, source, target, begin):
        here = store(n, source, target)
        there = exchange(n, source, target, SWAP)

        @pl.when(stays)
        def _():
            here.start() if begin else here.wait()

        @pl.when(jnp.logical_not(stays))
        def _():
            there.start() if begin else there.wait()

    items = []
    for l in range(layers):
        items += [(True, wq_ref.at[l, (t + 1) % 3], l * GROUPS + t) for t in range(3)]
        items += [(False, wo_ref.at[l], l * GROUPS + OUT_GROUP)]
        for n in range(FF_GROUPS):
            items += [(True, wi_ref.at[l, :, pl.ds(n * 512, 512)], l * GROUPS + in_group(n))]
            items += [(False, wd_ref.at[l, pl.ds(n * 512, 512)], l * GROUPS + down_group(n))]
    fetches, counts, ahead = [], [0, 0], [[], []]
    for m, (turned, source, group) in enumerate(items):
        slot = counts[turned] % DEPTH
        buf, sem = (col_buf, col_sem) if turned else (row_buf, row_sem)
        fetches.append((pltpu.make_async_copy(source, buf.at[slot], sem.at[slot]), slot))
        ahead[turned].append(m)
        counts[turned] += 1
    bits = [(dp // step) % 2 for step in (1, 2, 4, 8)]
    made = {}

    def convert(m):
        turned, _, group = items[m]
        copy, slot = fetches[m]
        copy.wait()
        if turned:

            def turn(i, _):
                strip = col_buf[slot, :, pl.ds(pl.multiple_of(i * 128, 128), 128)]
                turn_buf[pl.ds(pl.multiple_of(i * 128, 128), 128), :] = strip.astype(BF16).T
                return 0

            lax.fori_loop(0, 4, turn, 0)
        if m >= 2:
            made[m - 2].wait()

        def block(j, _):
            where = 0
            for bit, weight in zip(bits, (8, 4, 2, 1)):
                own = (j // weight) % 2
                where = where + weight * (own + bit - 2 * own * bit)
            at = pl.ds(pl.multiple_of(where * 32, 32), 32)
            rows_32 = turn_buf[at, :] if turned else row_buf[slot, at, :]
            made_buf[m % 2, pl.ds(pl.multiple_of(j * 32, 32), 32), :] = rows_32.astype(BF16)
            return 0

        lax.fori_loop(0, 16, block, 0)
        later = [n for n in ahead[turned] if n > m]
        if len(later) >= DEPTH:
            fetches[later[DEPTH - 1]][0].start()
        parts = [
            pltpu.make_async_copy(
                made_buf.at[m % 2, pl.ds(a * 256, 256)], w_ref.at[a, group, 0], made_sem.at[m % 2, a]
            )
            for a in range(2)
        ]

        class Both:
            def wait(self):
                for part in parts:
                    part.wait()

        for part in parts:
            part.start()
        made[m] = Both()

    load_x = load(0, x_ref.at[:, 0], x)
    load_x.start()
    load_up = load(1, up_ref.at[:, 0], acc)
    load_up.start()
    for kind in range(2):
        for m in ahead[kind][:DEPTH]:
            fetches[m][0].start()
    load_x.wait()

    def narrow_x(at):
        low[at, :] = x[at, :].astype(BF16)

    row_tiles(rows, narrow_x)
    swap(0, low, xb, True)
    load_up.wait()

    def narrow_up(at):
        hl[at, :] = acc[at, :].astype(BF16)

    row_tiles(rows, narrow_up)
    swap(1, hl, up_out, True)

    for m in range(len(items)):
        convert(m)
        if m % 4 == 3:
            spread.tick(m // 4)
    for m in range(len(items) - 2, len(items)):
        made[m].wait()
    swap(0, low, xb, False)
    swap(1, hl, up_out, False)

    def widen(at):
        x[at, :] = xb[at, :].astype(F32)

    row_tiles(rows, widen)

    pairs = width // 128
    for l in range(layers):
        (
            qkv_out, sib_out, ctx_out, ctx_sib_out, lse_out, r1_out, r2_out, hl_out, hl_sib_out,
            g_out, g_sib_out, slope_out, xb_out, xb_sib_out,
        ) = saved[l]
        first = l * GROUPS
        clock = 6 + 6 * l
        xb_store = store(0, xb, xb_out)
        xb_store.start()
        xb_copy = exchange(2 + 3 * l, xb, xb_sib_out)
        xb_copy.start()

        def give_kv(n, a):
            at = pl.ds(pl.multiple_of(a * 512, 512), 512)
            return pltpu.make_async_remote_copy(
                src_ref=qkv.at[1 + n, :, at], dst_ref=kv_sib.at[n, :, at],
                send_sem=kv_send.at[n, a], recv_sem=kv_recv.at[n, a],
                device_id=partner(FLIP_C), device_id_type=MESH,
            )

        def which(i):
            n = lax.div(i, 2)
            return lax.rem(n + 1, 3), n, lax.rem(i, 2)

        def qkv_feeds(i, slot):
            _, n, a = which(i)
            return (feed(0, slot, w_ref.at[a, first + n], wa_buf.at[slot]),)

        def qkv_body(i, slot):
            t, _, a = which(i)
            at = pl.ds(pl.multiple_of(a * 512, 512), 512)
            qkv[t, :, at] = (nt(xb[...], block_of(wa_buf.at[slot])) + bq_ref[l, t, a]).astype(BF16)
            pl.when(t > 0)(lambda: give_kv(t - 1, a).start())
            pl.when(i == 2)(lambda: spread.tick(clock))

        if l == 0:
            begin(qkv_feeds)
        stream(6, qkv_feeds, qkv_body)
        qkv_store = store(1, qkv, qkv_out)
        qkv_store.start()
        for n in range(2):
            for a in range(2):
                give_kv(n, a).wait()
        sib_store = store(2, kv_sib, sib_out)
        sib_store.start()

        feed(2, 0, w_ref.at[0, first + OUT_GROUP], wb_buf.at[0]).start()

        def pair_body(p, _):
            far = lax.rem(p + pairs // 2, pairs)
            here = pl.ds(pl.multiple_of(p * 128, 128), 128)
            there = pl.ds(pl.multiple_of(far * 128, 128), 128)
            mask = spread_mask(mask_ref[p], key_ref[...])
            keys = jnp.concatenate([qkv[1, :, here], kv_sib[0, :, there]], axis=0)
            values = jnp.concatenate([qkv[2, :, here], kv_sib[1, :, there]], axis=0)
            context, parts = attend_pair(qkv[0, :, here], keys, values, hot_buf[...], mask)
            ctx[:, here] = context.astype(BF16)
            for e in range(2):
                lse[p, e : e + 1, :] = parts[e]
            pl.when(lax.rem(p, 5) == 2)(lambda: spread.tick(clock + 1 + lax.div(p, 5)))
            return 0

        lax.fori_loop(0, pairs, pair_body, 0)
        ctx_store = store(3, ctx, ctx_out)
        ctx_store.start()
        lse_store = store(4, lse, lse_out)
        lse_store.start()
        ctx_copy = exchange(3 + 3 * l, ctx.at[:, pl.ds(512, 512)], ctx_sib_out)
        ctx_copy.start()

        def place_of(i):
            return 1 - lax.rem(i, 2), lax.div(i, 2)

        def ff_feeds(i, slot):
            a, n = place_of(i)
            return (
                feed(0, slot, w_ref.at[a, first + in_group(n)], wa_buf.at[slot]),
                feed(2, slot, w_ref.at[a, first + down_group(n)], wb_buf.at[slot]),
            )

        ff_feeds(0, 0)[0].start()

        def out_feeds(i, slot):
            return (feed(2, slot, w_ref.at[i, first + OUT_GROUP], wb_buf.at[slot]),)

        def out_body(i, slot):
            part = nn(ctx[:, pl.ds(pl.multiple_of(i * 512, 512), 512)], block_of(wb_buf.at[slot]))

            @pl.when(i == 0)
            def _():
                acc[...] = part

            @pl.when(i == 1)
            def _():
                acc[...] += part

        stream(2, out_feeds, out_body)
        ff_feeds(0, 0)[1].start()
        sib_store.wait()

        def first_norm(at):
            r1 = x[at, :] + acc[at, :] + vec_ref[l, 0:1, :]
            r_buf[at, :] = r1
            h = norm(r1, vec_ref[l, 1:2, :], vec_ref[l, 2:3, :])
            hl[at, :] = h.astype(BF16)
            acc[at, :] = h + vec_ref[l, 3:4, :]

        row_tiles(rows, first_norm)
        r1_store = store(5, r_buf, r1_out)
        r1_store.start()
        hl_store = store(6, hl, hl_out)
        hl_store.start()
        hl_copy = exchange(4 + 3 * l, hl, hl_sib_out)
        hl_copy.start()

        def g_store(j):
            return pltpu.make_async_copy(g_all.at[j], columns(g_out, j, 512), block_sem.at[0, j])

        def slope_store(j):
            return pltpu.make_async_copy(slope_all.at[j], columns(slope_out, j, 512), block_sem.at[1, j])

        def g_copy(n):
            return pltpu.make_async_remote_copy(
                src_ref=g_all.at[FF_GROUPS + n], dst_ref=columns(g_sib_out, n, 512),
                send_sem=g_send.at[l, n], recv_sem=g_recv.at[l, n],
                device_id=partner(FLIP_C), device_id_type=MESH,
            )

        def ff_body(i, slot):
            a, n = place_of(i)
            j = a * FF_GROUPS + n
            u = nt(hl[...], block_of(wa_buf.at[slot])) + bi_ref[l, a, n]
            g, slope = gelu_and_slope(u)
            g = g.astype(BF16)
            g_all[j] = g
            slope_all[j] = slope.astype(BF16)
            g_store(j).start()
            slope_store(j).start()
            pl.when(a == 1)(lambda: g_copy(n).start())
            acc[...] += nn(g, block_of(wb_buf.at[slot]))
            pl.when(lax.rem(i, 3) == 1)(lambda: spread.tick(clock + 3 + lax.div(i, 3)))

        stream(2 * FF_GROUPS, ff_feeds, ff_body)
        r1_store.wait()
        xb_store.wait()
        xb_copy.wait()
        if l + 1 < layers:
            feed(0, 0, w_ref.at[0, first + GROUPS], wa_buf.at[0]).start()

        def second_norm(at):
            r2 = acc[at, :]
            r_buf[at, :] = r2
            x2 = norm(r2, vec_ref[l, 4:5, :], vec_ref[l, 5:6, :])
            x[at, :] = x2
            xb[at, :] = x2.astype(BF16)

        row_tiles(rows, second_norm)
        r2_store = store(5, r_buf, r2_out)
        r2_store.start()
        if l == layers - 1:
            x_store = store(10, xb, x_out)
            x_store.start()

        def settle(j, _):
            g_store(j).wait()
            slope_store(j).wait()
            return 0

        lax.fori_loop(0, 2 * FF_GROUPS, settle, 0)

        def settle_sent(n, _):
            g_copy(n).wait()
            return 0

        lax.fori_loop(0, FF_GROUPS, settle_sent, 0)
        for copy in (qkv_store, ctx_store, lse_store, ctx_copy, hl_store, hl_copy, r2_store):
            copy.wait()
    x_store.wait()


def forward(block_input, cotangent, w_qkv, w_out, w_in, w_down, hot, mask, mask_rows, bias_qkv, bias_in, vectors):
    rows, _, width = block_input.shape
    layers = w_qkv.shape[0]
    total = layers * GROUPS
    anywhere = pl.BlockSpec(memory_space=pl.ANY)
    in_vmem = pl.BlockSpec(memory_space=pltpu.VMEM)
    low = lambda *shape: pltpu.VMEM(shape, BF16)
    full = lambda *shape: pltpu.VMEM(shape, F32)
    dma = lambda *shape: pltpu.SemaphoreType.DMA(shape)
    low_out = lambda *shape: jax.ShapeDtypeStruct(shape, BF16)
    full_out = lambda *shape: jax.ShapeDtypeStruct(shape, F32)
    layer_out = (
        low_out(3, rows, width),
        low_out(2, rows, width),
        low_out(rows, width),
        low_out(rows, width // 2),
        full_out(width // 128, 2, rows),
        full_out(rows, width),
        full_out(rows, width),
        low_out(rows, width),
        low_out(rows, width),
        low_out(rows, 4 * width),
        low_out(rows, 2 * width),
        low_out(rows, 4 * width),
        low_out(rows, width),
        low_out(rows, width),
    )
    outs = pl.pallas_call(
        functools.partial(forward_kernel, layers),
        out_shape=(low_out(2, total, 2, 256, width), low_out(rows, width), low_out(rows, width)) + layer_out * layers,
        in_specs=[anywhere] * 6 + [in_vmem] * 6,
        out_specs=(anywhere,) * (3 + PER_LAYER * layers),
        scratch_shapes=[
            full(rows, width),
            full(rows, width),
            full(rows, width),
            low(rows, width),
            low(rows, width),
            low(3, rows, width),
            low(2, rows, width),
            low(rows, width),
            full(width // 128, 2, rows),
            low(rows, width),
            low(2 * FF_GROUPS, rows, 512),
            low(2 * FF_GROUPS, rows, 512),
            full(DEPTH, width, 512),
            full(DEPTH, 512, width),
            low(512, width),
            low(2, 512, width),
            low(2, 2, 256, width),
            low(2, 2, 256, width),
            dma(3, 2),
            dma(3),
            dma(DEPTH),
            dma(DEPTH),
            dma(2, 2),
            dma(11),
            dma(2, 2 * FF_GROUPS),
            dma(11),
            dma(11),
            dma(2, 2),
            dma(2, 2),
            dma(layers, FF_GROUPS),
            dma(layers, FF_GROUPS),
            dma(9, total // 2),
            dma(9, total // 2),
        ],
        compiler_params=pltpu.CompilerParams(collective_id=0, has_side_effects=True, vmem_limit_bytes=60 << 20),
        cost_estimate=pl.CostEstimate(flops=30 << 30, bytes_accessed=300 << 20, transcendentals=1 << 24),
        name="forward",
    )(block_input, cotangent, w_qkv, w_out, w_in, w_down, hot, mask, mask_rows, bias_qkv, bias_in, vectors)
    saved = [outs[3 + PER_LAYER * l : 3 + PER_LAYER * (l + 1)] for l in range(layers)]
    return outs[0], outs[1], outs[2], saved


def backward_kernel(layers, *refs):
    refs = list(refs)
    up_ref, x_ref, w_ref, hot_buf, mask_ref, key_ref, vec_ref = refs[:7]
    saved = [refs[7 + PER_LAYER * l : 7 + PER_LAYER * (l + 1)] for l in range(layers)]
    at_ref = 7 + PER_LAYER * layers
    grads, sums, dx_out, x_out, dbi_ref, qkv_sums_ref, small_ref = refs[at_ref : at_ref + 7]
    (
        acc, dr1, dm, dm_sib, da, da_sib, du, du_sib, dctx, dqkv, d_sib, kv_out, kv_far,
        wa_buf, wb_buf, r_buf, slope_buf, left_buf, left_sib_buf, right_buf, right_sib_buf,
        pair_buf, lse_buf, unit_buf,
        y_buf, x_buf, z0_buf, z1_buf, all_buf, keep_buf,
        feed_sem, load_sem, store_sem, swap_sem, core_send, core_recv, du_send, du_recv, pair_send, pair_recv,
        send_sem, recv_sem, sum_send, sum_recv, keep_sem, out_sem, in_free, out_free,
    ) = refs[at_ref + 7 :]
    rows, width = acc.shape
    total = layers * GROUPS
    reduction = Reduction(
        grads, sums, total,
        (y_buf, x_buf, z0_buf, z1_buf, all_buf, keep_buf),
        (send_sem, recv_sem, sum_send, sum_recv, keep_sem, out_sem, in_free, out_free),
    )
    greet((FLIP_Y, FLIP_X, FLIP_Z0, FLIP_Z1, FLIP_C, SWAP))

    def feed(n, slot, source, target):
        return pltpu.make_async_copy(source, target, feed_sem.at[n, slot])

    def load(n, source, target):
        return pltpu.make_async_copy(source, target, load_sem.at[n])

    def exchange(n, source, target):
        return pltpu.make_async_remote_copy(
            src_ref=source, dst_ref=target, send_sem=core_send.at[n], recv_sem=core_recv.at[n],
            device_id=partner(FLIP_C), device_id_type=MESH,
        )

    def give_du(j, n):
        return pltpu.make_async_remote_copy(
            src_ref=du.at[j], dst_ref=du_sib.at[n], send_sem=du_send.at[n], recv_sem=du_recv.at[n],
            device_id=partner(FLIP_C), device_id_type=MESH,
        )

    def weight(a, group):
        return w_ref.at[a, group]

    def columns(ref, i, size):
        return ref.at[:, pl.ds(pl.multiple_of(i * size, size), size)]

    def unit_store(slot, index):
        return pltpu.make_async_copy(unit_buf.at[slot], grads.at[index], store_sem.at[0])

    def unit(left, left_sib, right, right_sib, slot, index, fresh=False):
        made = (tn(left, right) + tn(left_sib, right_sib)).astype(BF16)
        unit_buf[slot] = made
        if fresh is not False:
            pl.when(jnp.logical_not(fresh))(lambda: unit_store(slot, index).wait())
        else:
            unit_store(slot, index).wait()
        unit_store(slot, index).start()

    def add_small(l, row, value):
        small_ref[l, row : row + 1, :] += jnp.sum(value, axis=0, keepdims=True)

    stays = lax.axis_index("dp") % 2 == lax.axis_index("tensor")

    def swap(n, source, target, begin):
        here = pltpu.make_async_copy(source, target, swap_sem.at[n])
        there = pltpu.make_async_remote_copy(
            src_ref=source, dst_ref=target, send_sem=core_send.at[4 + n], recv_sem=core_recv.at[4 + n],
            device_id=partner(SWAP), device_id_type=MESH,
        )

        @pl.when(stays)
        def _():
            here.start() if begin else here.wait()

        @pl.when(jnp.logical_not(stays))
        def _():
            there.start() if begin else there.wait()

    swap(1, x_ref, x_out, True)
    load(0, saved[-1][6], r_buf).start()
    start_up = load(1, up_ref, da)
    start_up.start()
    start_up.wait()
    small_ref[...] = jnp.zeros_like(small_ref)

    def widen(at):
        acc[at, :] = da[at, :].astype(F32)

    row_tiles(rows, widen)
    done = 0
    for l in reversed(range(layers)):
        qkv_ref, sib_ref, ctx_ref, ctx_sib_ref, lse_ref, r1_ref, r2_ref, hl_ref, hl_sib_ref, g_ref, g_sib_ref, slope_ref, xb_ref, xb_sib_ref = saved[l]
        first = l * GROUPS
        base = (layers - 1 - l) * GROUPS
        clock = 11 * (layers - 1 - l)

        def down_feeds(i, slot):
            return (
                feed(0, slot, columns(g_ref, i, 512), left_buf.at[slot]),
                feed(1, slot, columns(g_sib_ref, i, 512), left_sib_buf.at[slot]),
            )

        begin(down_feeds)
        load(0, r2_ref, r_buf).wait()

        def second(at):
            dy = acc[at, :]
            dr, part = norm_back(dy, r_buf[at, :], vec_ref[l, 4:5, :])
            acc[at, :] = dr
            dm[at, :] = dr.astype(BF16)
            add_small(l, 0, part)
            add_small(l, 1, dy)
            add_small(l, 2, dr)

        row_tiles(rows, second)
        dm_copy = exchange(0, dm, dm_sib)
        dm_copy.start()
        r_load = load(0, r1_ref, r_buf)
        r_load.start()
        right_load = load(1, hl_ref, right_buf)
        right_load.start()
        right_sib_load = load(2, hl_sib_ref, right_sib_buf)
        right_sib_load.start()
        dm_copy.wait()

        def down_body(i, slot):
            fresh = (i == 0) if l == layers - 1 else False
            unit(left_buf[slot], left_sib_buf[slot], dm[...], dm_sib[...], lax.rem(i, 2), base + i, fresh)
            pl.when(lax.rem(i, 2) == 1)(lambda: reduction.tick(clock + lax.div(i, 2)))

        def place_of(i):
            a = 1 - lax.div(i, FF_GROUPS)
            return a, lax.rem(i, FF_GROUPS)

        def ff_feeds(i, slot):
            a, n = place_of(i)
            j = a * FF_GROUPS + n
            return (
                feed(2, slot, weight(a, first + down_group(n)), wa_buf.at[slot]),
                feed(3, slot, weight(a, first + in_group(n)), wb_buf.at[slot]),
                feed(4, slot, columns(slope_ref, j, 512), slope_buf.at[slot]),
            )

        begin(ff_feeds)
        stream(FF_GROUPS, down_feeds, down_body)
        unit_store(1, base + FF_GROUPS - 1).wait()

        def ff_body(i, slot):
            a, n = place_of(i)
            j = a * FF_GROUPS + n
            dg = nt(dm[...], block_of(wa_buf.at[slot]))
            d = (dg * slope_buf[slot].astype(F32)).astype(BF16)
            du[j] = d
            pl.when(a == 1)(lambda: give_du(j, n).start())
            dbi_ref[l, a, n] = jnp.sum(d.astype(F32), axis=0, keepdims=True)
            acc[...] += nn(d, block_of(wb_buf.at[slot]))
            pl.when(lax.rem(i, 4) == 3)(lambda: reduction.tick(clock + 2 + lax.div(i, 4)))

        stream(2 * FF_GROUPS, ff_feeds, ff_body)

        def out_feeds(i, slot):
            return (feed(2, slot, weight(i, first + OUT_GROUP), wa_buf.at[slot]),)

        begin(out_feeds)
        r_load.wait()

        def first_norm(at):
            dy = acc[at, :]
            dr, part = norm_back(dy, r_buf[at, :], vec_ref[l, 1:2, :])
            dr1[at, :] = dr
            da[at, :] = dr.astype(BF16)
            add_small(l, 3, part)
            add_small(l, 4, dy)
            add_small(l, 5, dr)

        row_tiles(rows, first_norm)
        if l > 0:
            load(0, saved[l - 1][6], r_buf).start()
        da_copy = exchange(1, da, da_sib)
        da_copy.start()

        def out_body(i, slot):
            dctx[:, pl.ds(pl.multiple_of(i * 512, 512), 512)] = nt(da[...], block_of(wa_buf.at[slot])).astype(BF16)

        stream(2, out_feeds, out_body)

        pairs = width // 128

        def pair_feeds(p, slot):
            far = lax.rem(p + pairs // 2, pairs)
            return (
                feed(5, slot, columns(qkv_ref.at[0], p, 128), pair_buf.at[slot, 0, pl.ds(0, rows)]),
                feed(6, slot, columns(qkv_ref.at[1], p, 128), pair_buf.at[slot, 1, pl.ds(0, rows)]),
                feed(7, slot, columns(sib_ref.at[0], far, 128), pair_buf.at[slot, 1, pl.ds(rows, rows)]),
                feed(8, slot, columns(qkv_ref.at[2], p, 128), pair_buf.at[slot, 2, pl.ds(0, rows)]),
                feed(9, slot, columns(sib_ref.at[1], far, 128), pair_buf.at[slot, 2, pl.ds(rows, rows)]),
                feed(10, slot, columns(ctx_ref, p, 128), pair_buf.at[slot, 3, pl.ds(0, rows)]),
                feed(11, slot, lse_ref.at[p], lse_buf.at[slot]),
            )

        begin(pair_feeds)
        right_load.wait()
        right_sib_load.wait()

        def in_body(n, _):
            give_du(FF_GROUPS + n, n).wait()
            unit(du[n], du_sib[n], right_buf[...], right_sib_buf[...], lax.rem(n, 2), base + FF_GROUPS + n, n == 0)
            pl.when(lax.rem(n, 2) == 1)(lambda: reduction.tick(clock + 4 + lax.div(n, 2)))
            return 0

        lax.fori_loop(0, FF_GROUPS, in_body, 0)

        right_load = load(1, xb_ref, right_buf)
        right_load.start()
        right_sib_load = load(2, xb_sib_ref, right_sib_buf)
        right_sib_load.start()
        left_load = load(3, columns(ctx_ref, 0, 512), left_buf.at[0])
        left_load.start()
        left_sib_load = load(4, ctx_sib_ref, left_sib_buf.at[0])
        left_sib_load.start()
        da_copy.wait()
        left_load.wait()
        left_sib_load.wait()
        unit(left_buf[0], left_sib_buf[0], da[...], da_sib[...], 0, base + 2 * FF_GROUPS)
        unit_store(0, base + 2 * FF_GROUPS).wait()

        def dx_feeds(i, slot):
            return (feed(3, slot, weight(lax.rem(i, 2), first + lax.rem(lax.div(i, 2) + 2, 3)), wa_buf.at[slot]),)

        begin(dx_feeds)

        def give_pair(p):
            far = lax.rem(p + pairs // 2, pairs)
            at = pl.ds(pl.multiple_of(far * 128, 128), 128)
            return pltpu.make_async_remote_copy(
                src_ref=kv_out.at[:, :, at], dst_ref=kv_far.at[:, :, at], send_sem=pair_send.at[p], recv_sem=pair_recv.at[far],
                device_id=partner(FLIP_C), device_id_type=MESH,
            )

        def pair_body(p, slot):
            far = lax.rem(p + pairs // 2, pairs)
            here = pl.ds(pl.multiple_of(p * 128, 128), 128)
            mask = spread_mask(mask_ref[p], key_ref[...])
            dq, dk, dv = attend_back_pair(
                pair_buf[slot, 0, 0:rows], pair_buf[slot, 1], pair_buf[slot, 2], hot_buf[...], mask,
                pair_buf[slot, 3, 0:rows], lse_buf[slot], dctx[:, here],
            )
            dqkv[0, :, here] = dq.astype(BF16)
            dqkv[1, :, here] = dk[:rows].astype(BF16)
            dqkv[2, :, here] = dv[:rows].astype(BF16)
            there = pl.ds(pl.multiple_of(far * 128, 128), 128)
            kv_out[0, :, there] = dk[rows:].astype(BF16)
            kv_out[1, :, there] = dv[rows:].astype(BF16)
            give_pair(p).start()
            pl.when(lax.rem(p, 3) == 1)(lambda: reduction.tick(clock + 6 + lax.div(p, 3)))

        stream(pairs, pair_feeds, pair_body)

        def settle_pair(p, _):
            give_pair(p).wait()
            return 0

        lax.fori_loop(0, pairs, settle_pair, 0)
        for n in range(2):
            add_rows(dqkv.at[1 + n], kv_far.at[n], rows)
        d_copy = exchange(3, dqkv.at[:, :, pl.ds(512, 512)], d_sib)
        d_copy.start()
        right_load.wait()
        right_sib_load.wait()
        d_copy.wait()

        def qkv_body(n, _):
            unit(
                dqkv[n, :, 0:512], d_sib[n], right_buf[...], right_sib_buf[...],
                lax.rem(n + 1, 2), base + 2 * FF_GROUPS + 1 + n, n == 0,
            )
            pl.when(n == 1)(lambda: reduction.tick(clock + 9))
            return 0

        lax.fori_loop(0, 3, qkv_body, 0)

        def start_dx(at):
            acc[at, :] = dr1[at, :]

        row_tiles(rows, start_dx)

        def dx_body(i, slot):
            a, n = lax.rem(i, 2), lax.div(i, 2)
            d = dqkv[n, :, pl.ds(pl.multiple_of(a * 512, 512), 512)]
            qkv_sums_ref[l, n, a] = jnp.sum(d.astype(F32), axis=0, keepdims=True)
            acc[...] += nn(d, block_of(wa_buf.at[slot]))
            pl.when(i == 3)(lambda: reduction.tick(clock + 10))

        stream(6, dx_feeds, dx_body)
        done = clock + 11

    def narrow(at):
        da[at, :] = acc[at, :].astype(BF16)

    row_tiles(rows, narrow)
    unit_store(1, total - 1).wait()
    swap(0, da, dx_out, True)

    def rest(t, _):
        reduction.tick(t)
        return 0

    lax.fori_loop(done, total + LAST_TICK, rest, 0)
    swap(0, da, dx_out, False)
    swap(1, x_ref, x_out, False)


def backward(upstream, stream_low, weights, hot, mask, mask_rows, vectors, saved):
    rows, width = upstream.shape
    layers = len(saved)
    total = layers * GROUPS
    anywhere = pl.BlockSpec(memory_space=pl.ANY)
    in_vmem = pl.BlockSpec(memory_space=pltpu.VMEM)
    low = lambda *shape: pltpu.VMEM(shape, BF16)
    dma = lambda *shape: pltpu.SemaphoreType.DMA(shape)
    return pl.pallas_call(
        functools.partial(backward_kernel, layers),
        out_shape=(
            jax.ShapeDtypeStruct((total, 512, width), BF16),
            jax.ShapeDtypeStruct((total, 512, width), BF16),
            jax.ShapeDtypeStruct((rows, width), BF16),
            jax.ShapeDtypeStruct((rows, width), BF16),
            jax.ShapeDtypeStruct((layers, 2, FF_GROUPS, 1, 512), F32),
            jax.ShapeDtypeStruct((layers, 3, 2, 1, 512), F32),
            jax.ShapeDtypeStruct((layers, 8, width), F32),
        ),
        in_specs=[anywhere] * 3 + [in_vmem] * 4 + [anywhere] * (PER_LAYER * layers),
        out_specs=(anywhere, anywhere, anywhere, anywhere, in_vmem, in_vmem, in_vmem),
        scratch_shapes=[
            pltpu.VMEM((rows, width), F32),
            pltpu.VMEM((rows, width), F32),
            low(rows, width),
            low(rows, width),
            low(rows, width),
            low(rows, width),
            low(2 * FF_GROUPS, rows, 512),
            low(FF_GROUPS, rows, 512),
            low(rows, width),
            low(3, rows, width),
            low(3, rows, 512),
            low(2, rows, width),
            low(2, rows, width),
            low(2, 2, 256, width),
            low(2, 2, 256, width),
            pltpu.VMEM((rows, width), F32),
            low(2, rows, 512),
            low(2, rows, 512),
            low(2, rows, 512),
            low(rows, width),
            low(rows, width),
            low(2, 4, 2 * rows, 128),
            pltpu.VMEM((2, 2, rows), F32),
            low(2, 512, width),
            low(SLOTS, 256, width),
            low(SLOTS, 128, width),
            low(SLOTS, 64, width),
            low(SLOTS, 32, width),
            low(SLOTS, 256, width),
            low(2, 256, width),
            dma(12, 2),
            dma(5),
            dma(1),
            dma(2),
            dma(6),
            dma(6),
            dma(FF_GROUPS),
            dma(FF_GROUPS),
            dma(width // 128),
            dma(width // 128),
            dma(7, SLOTS),
            dma(7, SLOTS),
            dma(total),
            dma(total),
            dma(2),
            dma(SLOTS),
            pltpu.SemaphoreType.REGULAR((4,)),
            pltpu.SemaphoreType.REGULAR((3,)),
        ],
        compiler_params=pltpu.CompilerParams(
            collective_id=1, has_side_effects=True, vmem_limit_bytes=60 << 20
        ),
        cost_estimate=pl.CostEstimate(flops=60 << 30, bytes_accessed=300 << 20, transcendentals=1 << 24),
        name="backward",
    )(upstream, stream_low, weights, hot, mask, mask_rows, vectors, *[ref for one in saved for ref in one])


def flip_order(values, axis, bits):
    for i, bit in enumerate(bits):
        values = jnp.where(bit == 0, values, jnp.flip(values, axis + i))
    return values


def sequence_shards(
    block_input, segment_ids, random_blocks, w_qkv, b_qv, w_out, b_out, w_in, b_in, w_down, b_down,
    ln_gain, ln_bias, cotangent,
):
    y = lax.axis_index("tensor")
    dp = lax.axis_index("dp")
    core, x_bit, z0, z1 = dp % 2, (dp // 2) % 2, (dp // 4) % 2, dp // 8
    code = core * 8 + x_bit * 4 + z0 * 2 + z1
    code_arg = code.reshape(1).astype(jnp.int32)
    device_bits = (core, x_bit, z0, z1)

    rows, _, width = block_input.shape
    layers = w_qkv.shape[0]
    blocks = random_blocks.shape[2]
    own_blocks = blocks // 2
    heads = random_blocks.shape[1] * 2

    chosen = random_blocks[0]
    near = jnp.concatenate([chosen.reshape(-1), segment_ids[0]])
    sibling = flip(near, FLIP_C)
    across, diagonal = flip(chosen.reshape(-1), FLIP_Y), flip(chosen.reshape(-1), SWAP)
    mine = jnp.concatenate([near[: chosen.size], across, near[chosen.size :]])
    other = jnp.concatenate([sibling[: chosen.size], diagonal, sibling[chosen.size :]])
    packed = jnp.where(core == y, mine, other)
    chosen = packed[: 2 * chosen.size].reshape(2, heads // 2, blocks, -1)
    segments = packed[2 * random_blocks.size :]
    chosen = flip_order(chosen.reshape(2, 2, 2, 2, blocks, -1), 1, device_bits[:3])
    chosen = chosen.transpose(1, 0, 2, 3, 4, 5).reshape(heads, blocks, -1)
    segments = segments.reshape(2, rows)
    segments = jnp.where(core == 0, segments, segments[::-1]).reshape(-1)
    query_block = core * own_blocks + jnp.arange(own_blocks)
    key_block = jnp.arange(blocks) ^ (core * own_blocks)
    allowed = (
        (jnp.abs(query_block[:, None] - key_block[None, :]) <= 1)
        | (key_block[None, :] == 0)
        | (key_block[None, :] == blocks - 1)
        | (query_block[:, None] == 0)
        | (query_block[:, None] == blocks - 1)
    )
    chosen = lax.dynamic_slice_in_dim(chosen, core * own_blocks, own_blocks, axis=1)
    allowed = allowed[None] | jnp.any(chosen[:, :, None, :] == key_block[None, None, :, None], axis=3)
    block_rows = rows // own_blocks
    documents = jnp.arange(HEAD_DIM - own_blocks)
    mask = jnp.pad(
        jnp.where(allowed, 0.0, BIG).astype(F32).transpose(0, 2, 1), ((0, 0), (0, 0), (0, HEAD_DIM - own_blocks))
    )
    mask = mask.reshape(heads // 2, 2, blocks, HEAD_DIM).transpose(0, 2, 1, 3).reshape(heads // 2, blocks, 2 * HEAD_DIM)
    document_part = jnp.where(
        (segments[:, None] == documents[None, :]) | (documents[None, :] > 7), 0.0, BIG
    ).astype(F32)
    mask_rows = jnp.pad(document_part, ((0, 0), (own_blocks, 0)))
    mask_rows = jnp.concatenate([mask_rows, mask_rows], axis=1)
    block_rows = rows // own_blocks
    hot = jnp.concatenate(
        [
            jnp.repeat(jnp.eye(own_blocks, dtype=BF16), block_rows, axis=0),
            (segments[:rows, None] == documents[None, :]).astype(BF16),
        ],
        axis=1,
    )
    hot = jnp.concatenate([hot, hot], axis=1)

    bias_pack = jnp.concatenate(
        [
            flip_order(b_qv.reshape(layers * 2, 2, 2, 2, 2, -1), 1, device_bits).reshape(-1),
            flip_order(b_in.reshape(layers * FF_GROUPS, 2, 2, 2, 2, -1), 1, device_bits).reshape(-1),
        ]
    )
    bias_far = flip(bias_pack, FLIP_Y)
    n_qv = b_qv.size

    def local_bias(near, far, count):
        near, far = near.reshape(count, 2, 1, 256), far.reshape(count, 2, 1, 256)
        return jnp.concatenate([near, far], axis=2).reshape(count, 2, 512)

    bias_qv = local_bias(bias_pack[:n_qv], bias_far[:n_qv], layers * 2).reshape(layers, 2, 2, 1, 512)
    bias_qkv = jnp.stack([bias_qv[:, 0], jnp.zeros_like(bias_qv[:, 0]), bias_qv[:, 1]], axis=1)
    bias_in = local_bias(bias_pack[n_qv:], bias_far[n_qv:], layers * FF_GROUPS)
    bias_in = bias_in.reshape(layers, FF_GROUPS, 2, 1, 512).swapaxes(1, 2)

    vectors = [
        jnp.stack(
            [
                b_out[l], ln_gain[l, 0], ln_bias[l, 0], b_down[l], ln_gain[l, 1], ln_bias[l, 1],
                b_out[l], b_out[l],
            ]
        )
        for l in range(layers)
    ]
    vectors = jnp.stack(vectors)
    weights, upstream_low, stream_low, saved = forward(
        block_input, cotangent, w_qkv, w_out, w_in, w_down, hot, mask, mask_rows, bias_qkv, bias_in, vectors
    )
    _, grads, dx_low, x_low, d_b_in, qkv_sums, rows_small = backward(
        upstream_low, stream_low, weights, hot, mask, mask_rows, vectors, saved
    )
    block_output, input_grad = widen_rows(x_low, dx_low)

    stacks = [
        jnp.stack([qkv_sums[:, 0], qkv_sums[:, 2]], axis=1),
        rows_small[:, 5],
        d_b_in.swapaxes(1, 2),
        rows_small[:, 2],
        jnp.stack([rows_small[:, 3], rows_small[:, 0]], axis=1),
        jnp.stack([rows_small[:, 4], rows_small[:, 1]], axis=1),
    ]

    def global_order(values, lead):
        values = values.reshape(lead, 2, 2, 2, 2, 2, 32).swapaxes(1, 2)
        values = flip_order(values, 1, (y,) + device_bits)
        return values.swapaxes(0, 1).reshape(2, -1)

    stacks[0] = global_order(stacks[0], layers * 2)
    stacks[2] = global_order(stacks[2], layers * FF_GROUPS)
    def placing(shape, block, index, turned, count, start):
        return lambda values: place(
            values, shape, block, index, turned, count, lambda l, i: (layers - 1 - l) * GROUPS + start + i, code_arg
        )

    summed = jnp.concatenate([s.reshape(-1) for s in stacks])
    summed = summed + flip(summed, FLIP_C)
    placed = []
    for bit, put in (
        (FLIP_Y, placing(w_down.shape, (1, 512, width), lambda l, i: (l, i, 0), False, FF_GROUPS, 0)),
        (FLIP_X, placing(w_in.shape, (1, width, 512), lambda l, i: (l, 0, i), True, FF_GROUPS, FF_GROUPS)),
        (FLIP_Z0, placing(w_qkv.shape, (1, 1, width, 512), lambda l, i: (l, i, 0, 0), True, 3, 2 * FF_GROUPS + 1)),
        (FLIP_Z1, placing(w_out.shape, (1, 512, width), lambda l, i: (l, 0, 0), False, 1, 2 * FF_GROUPS)),
    ):
        summed, grads = lax.optimization_barrier((summed, grads))
        far = flip(summed, bit)
        done, summed, far = lax.optimization_barrier((put(grads), summed, far))
        placed.append(done)
        summed = summed + far
    parts, at = [], 0
    for s in stacks:
        parts.append(summed[at : at + s.size].reshape(s.shape))
        at += s.size
    g_b_qv = lax.dynamic_index_in_dim(parts[0], y, axis=0, keepdims=False).reshape(b_qv.shape)
    g_b_in = lax.dynamic_index_in_dim(parts[2], y, axis=0, keepdims=False).reshape(b_in.shape)
    return (
        block_output,
        input_grad,
        placed[2],
        g_b_qv,
        placed[3],
        parts[1],
        placed[1],
        g_b_in,
        placed[0],
        parts[3],
        parts[4],
        parts[5],
    )


def as_sent(array):

    def short(part):
        return part.astype(jnp.bfloat16) if part.dtype == jnp.float32 else part

    return jax.tree.map(short, array)


def norm_rows(values, gain_row, shift_row):
    row_mean = jnp.mean(values, axis=-1, keepdims=True)
    centred = values - row_mean
    variance = jnp.mean(centred * centred, axis=-1, keepdims=True)
    return centred * lax.rsqrt(variance + 1e-06) * gain_row + shift_row


def gelu_exact(values):
    return jax.nn.gelu(values, approximate=False)


def block_mask(chosen_blocks, segment_rows):
    nblocks = chosen_blocks.shape[2]
    block_index = jnp.arange(nblocks)
    near_blocks = jnp.abs(block_index[:, None] - block_index[None, :]) <= 1
    edge_blocks = (
        (block_index[None, :] == 0)
        | (block_index[None, :] == nblocks - 1)
        | (block_index[:, None] == 0)
        | (block_index[:, None] == nblocks - 1)
    )
    picked_blocks = jnp.any(chosen_blocks[..., None] == block_index, axis=3)
    allowed = near_blocks | edge_blocks | picked_blocks
    block_rows = segment_rows.shape[1] // nblocks
    allowed = jnp.repeat(jnp.repeat(allowed, block_rows, axis=2), block_rows, axis=3)
    same_doc = segment_rows[:, :, None] == segment_rows[:, None, :]
    return allowed & same_doc[:, None]


def masked_scores(queries, key_rows, allowed, score_scale):
    scores = (
        jnp.einsum("qshd,kshd->shqk", queries, key_rows, preferred_element_type=jnp.float32)
        * score_scale
    )
    return jnp.where(allowed, scores, -1e30)


def shards(
    block_input,
    segment_ids,
    random_blocks,
    w_qkv,
    b_qv,
    w_out,
    b_out,
    w_in,
    b_in,
    w_down,
    b_down,
    ln_gain,
    ln_bias,
    cotangent,
):
    score_scale = HEAD_DIM ** (-0.5)
    shard_rows, seq_count, model_width = block_input.shape
    layers = w_qkv.shape[0]
    local_width = w_qkv.shape[3]
    local_heads = local_width // HEAD_DIM
    allowed = block_mask(random_blocks, segment_ids)
    saved_acts = []
    stream = block_input
    for layer_index in range(layers):
        w_proj = w_qkv[layer_index].astype(jnp.bfloat16)
        w_mix = w_out[layer_index].astype(jnp.bfloat16)
        rows_low = stream.astype(jnp.bfloat16)
        full_rows = lax.all_gather(rows_low, "tensor", axis=0, tiled=True)
        length = full_rows.shape[0]
        projected = jnp.einsum(
            "lsd,tdc->tlsc", full_rows, w_proj, preferred_element_type=jnp.float32
        )
        qkv_bias = jnp.stack(
            [b_qv[layer_index, 0], jnp.zeros_like(b_qv[layer_index, 0]), b_qv[layer_index, 1]]
        )
        qkv_low = (projected + qkv_bias[:, None, None, :]).astype(jnp.bfloat16)
        head_view = qkv_low.reshape(3, length, seq_count, local_heads, HEAD_DIM)
        scores = masked_scores(head_view[0], head_view[1], allowed, score_scale)
        row_top = jnp.max(scores, axis=-1, keepdims=True)
        log_total = row_top + jnp.log(jnp.sum(jnp.exp(scores - row_top), axis=-1, keepdims=True))
        probs_low = jnp.exp(scores - log_total).astype(jnp.bfloat16)
        context = jnp.einsum(
            "shqk,kshd->qshd", probs_low, head_view[2], preferred_element_type=jnp.float32
        )
        context = context.reshape(length, seq_count, local_width).astype(jnp.bfloat16)
        mixed = lax.psum_scatter(
            jnp.einsum("lsc,cd->lsd", context, w_mix, preferred_element_type=jnp.float32).astype(
                jnp.bfloat16
            ),
            "tensor",
            scatter_dimension=0,
            tiled=True,
        ).astype(jnp.float32)
        first_sum = stream + mixed + b_out[layer_index]
        hidden_rows = norm_rows(first_sum, ln_gain[layer_index, 0], ln_bias[layer_index, 0])
        hidden_low = hidden_rows.astype(jnp.bfloat16)
        up_weight = w_in[layer_index].astype(jnp.bfloat16)
        backward_weight = w_down[layer_index].astype(jnp.bfloat16)
        hidden_full = lax.all_gather(hidden_low, "tensor", axis=0, tiled=True)
        preactivation = (
            jnp.einsum("twn,nj->twj", hidden_full, up_weight, preferred_element_type=jnp.float32)
            + b_in[layer_index]
        )
        activation_reduced = gelu_exact(preactivation).astype(jnp.bfloat16)
        grown = lax.psum_scatter(
            jnp.einsum(
                "unj,jp->unp",
                activation_reduced,
                backward_weight,
                preferred_element_type=jnp.float32,
            ).astype(jnp.bfloat16),
            "tensor",
            scatter_dimension=0,
            tiled=True,
        ).astype(jnp.float32)
        second_sum = hidden_rows + grown + b_down[layer_index]
        stream = norm_rows(second_sum, ln_gain[layer_index, 1], ln_bias[layer_index, 1])
        keep_rows, keep_hidden = (full_rows, hidden_full)
        saved_acts.append(
            (
                keep_rows,
                head_view,
                log_total,
                context,
                first_sum,
                keep_hidden,
                preactivation,
                activation_reduced,
                second_sum,
                up_weight,
                backward_weight,
            )
        )
    upstream = cotangent
    grads_by_layer = [None] * layers
    for layer_index in reversed(range(layers)):
        (
            keep_rows,
            head_view,
            log_total,
            context,
            first_sum,
            keep_hidden,
            preactivation,
            activation_reduced,
            second_sum,
            up_weight,
            backward_weight,
        ) = saved_acts[layer_index]
        full_rows, hidden_full = (keep_rows, keep_hidden)
        length = full_rows.shape[0]
        w_proj = w_qkv[layer_index].astype(jnp.bfloat16)
        w_mix = w_out[layer_index].astype(jnp.bfloat16)
        _, pull_second = jax.vjp(
            norm_rows, second_sum, ln_gain[layer_index, 1], ln_bias[layer_index, 1]
        )
        d_second, d_gain_two, d_shift_two = pull_second(upstream)
        _, pull_gelu = jax.vjp(gelu_exact, preactivation)
        widened_full = lax.all_gather(d_second.astype(jnp.bfloat16), "tensor", axis=0, tiled=True)
        down_gradient = jnp.einsum(
            "uxc,uxw->cw", activation_reduced, widened_full, preferred_element_type=jnp.float32
        )
        activation_gradient = jnp.einsum(
            "mra,xa->mrx", widened_full, backward_weight, preferred_element_type=jnp.float32
        )
        preactivation_gradient_reduced = pull_gelu(activation_gradient)[0].astype(jnp.bfloat16)
        up_gradient = jnp.einsum(
            "kmx,kmt->xt",
            hidden_full,
            preactivation_gradient_reduced,
            preferred_element_type=jnp.float32,
        )
        g_up_bias = jnp.sum(preactivation_gradient_reduced.astype(jnp.float32), axis=(0, 1))
        d_hidden = d_second + lax.psum_scatter(
            jnp.einsum(
                "hmp,tp->hmt",
                preactivation_gradient_reduced,
                up_weight,
                preferred_element_type=jnp.float32,
            ).astype(jnp.bfloat16),
            "tensor",
            scatter_dimension=0,
            tiled=True,
        ).astype(jnp.float32)
        _, pull_first = jax.vjp(
            norm_rows, first_sum, ln_gain[layer_index, 0], ln_bias[layer_index, 0]
        )
        d_first, d_gain_one, d_shift_one = pull_first(d_hidden)
        full_mixed = lax.all_gather(d_first.astype(jnp.bfloat16), "tensor", axis=0, tiled=True)
        g_out = jnp.einsum("lsc,lsd->cd", context, full_mixed, preferred_element_type=jnp.float32)
        d_context = jnp.einsum(
            "lsd,cd->lsc", full_mixed, w_mix, preferred_element_type=jnp.float32
        ).astype(jnp.bfloat16)
        d_context = d_context.reshape(length, seq_count, local_heads, HEAD_DIM)
        queries, key_rows, value_rows = (head_view[0], head_view[1], head_view[2])
        scores = masked_scores(queries, key_rows, allowed, score_scale)
        attn_probs = jnp.exp(scores - log_total)
        probs_low = attn_probs.astype(jnp.bfloat16)
        d_probs = jnp.einsum(
            "qshd,kshd->shqk", d_context, value_rows, preferred_element_type=jnp.float32
        )
        d_scores = attn_probs * (d_probs - jnp.sum(d_probs * attn_probs, axis=-1, keepdims=True))
        d_scores = d_scores.astype(jnp.bfloat16)
        d_query = (
            jnp.einsum("shqk,kshd->qshd", d_scores, key_rows, preferred_element_type=jnp.float32)
            * score_scale
        )
        d_key = (
            jnp.einsum("shqk,qshd->kshd", d_scores, queries, preferred_element_type=jnp.float32)
            * score_scale
        )
        d_value = jnp.einsum(
            "shqk,qshd->kshd", probs_low, d_context, preferred_element_type=jnp.float32
        )
        d_qkv = (
            jnp.stack([d_query, d_key, d_value])
            .reshape(3, length, seq_count, local_width)
            .astype(jnp.bfloat16)
        )
        g_proj = jnp.einsum("lsd,tlsc->tdc", full_rows, d_qkv, preferred_element_type=jnp.float32)
        qkv_sums = jnp.sum(d_qkv.astype(jnp.float32), axis=(1, 2))
        g_bias = jnp.stack([qkv_sums[0], qkv_sums[2]])
        upstream = d_first + lax.psum_scatter(
            jnp.einsum("tlsc,tdc->lsd", d_qkv, w_proj, preferred_element_type=jnp.float32).astype(
                jnp.bfloat16
            ),
            "tensor",
            scatter_dimension=0,
            tiled=True,
        ).astype(jnp.float32)
        weight_grads = (g_proj, g_bias, g_out, up_gradient, g_up_bias, down_gradient)
        small_grads = (
            jnp.sum(d_first, axis=(0, 1)),
            jnp.sum(d_second, axis=(0, 1)),
            jnp.stack([d_gain_one, d_gain_two]),
            jnp.stack([d_shift_one, d_shift_two]),
        )
        grads_by_layer[layer_index] = (weight_grads, small_grads)
    weight_stack = tuple(
        (
            jnp.stack([grads_by_layer[layer_index][0][member] for layer_index in range(layers)])
            for member in range(6)
        )
    )
    small_stack = tuple(
        (
            jnp.stack([grads_by_layer[layer_index][1][member] for layer_index in range(layers)])
            for member in range(4)
        )
    )
    weight_stack = jax.tree.map(
        lambda part: part.astype(jnp.float32), lax.psum(as_sent(weight_stack), "dp")
    )
    small_stack = lax.psum(small_stack, ("dp", "tensor"))
    return (
        stream,
        upstream,
        weight_stack[0],
        weight_stack[1],
        weight_stack[2],
        small_stack[0],
        weight_stack[3],
        weight_stack[4],
        weight_stack[5],
        small_stack[1],
        small_stack[2],
        small_stack[3],
    )


def solution(mesh):
    by_sequence = mesh.shape["tensor"] == 2 and mesh.shape["dp"] == 16
    return jax.shard_map(
        sequence_shards if by_sequence else shards,
        mesh=mesh,
        in_specs=(
            P("tensor", "dp", None),
            P("dp", None),
            P("dp", "tensor", None, None),
            P(None, None, None, "tensor"),
            P(None, None, "tensor"),
            P(None, "tensor", None),
            P(),
            P(None, None, "tensor"),
            P(None, "tensor"),
            P(None, "tensor", None),
            P(),
            P(),
            P(),
            P("tensor", "dp", None),
        ),
        out_specs=(
            P("tensor", "dp", None),
            P("tensor", "dp", None),
            P(None, None, None, "tensor"),
            P(None, None, "tensor"),
            P(None, "tensor", None),
            P(),
            P(None, None, "tensor"),
            P(None, "tensor"),
            P(None, "tensor", None),
            P(),
            P(),
            P(),
        ),
        check_vma=False,
    )
```

```python
import functools

import jax
import jax.numpy as jnp
from jax import lax
from jax.experimental import pallas as pl
from jax.experimental.pallas import tpu as pltpu
from jax.sharding import PartitionSpec as P

HEAD_DIM = 64
BIG = -1e30
BF16 = jnp.bfloat16
F32 = jnp.float32
MESH = pl.DeviceIdType.MESH
VMEM_LIMIT = 56 << 20

FLIP_Y, FLIP_C, FLIP_X, FLIP_Z0, FLIP_Z1 = 1, 2, 4, 8, 16
SWAP = FLIP_Y + FLIP_C
DEVICES = 32

GROUPS = 12
OUT_GROUP = 3
FF_GROUPS = 4


def in_group(s):
    return 4 + 2 * s


def down_group(s):
    return 5 + 2 * s


def flip(values, bit):
    pairs = [(i, i ^ bit) for i in range(DEVICES)]
    return jax.tree.map(lambda v: lax.ppermute(v, ("dp", "tensor"), pairs), values)


def nt(a, b):
    return lax.dot_general(a, b, (((1,), (1,)), ((), ())), preferred_element_type=F32)


def nn(a, b):
    return lax.dot_general(a, b, (((1,), (0,)), ((), ())), preferred_element_type=F32)


def tn(a, b):
    return lax.dot_general(a, b, (((0,), (0,)), ((), ())), preferred_element_type=F32)


def block_of(ref):
    width = ref.shape[-1]
    return ref[...].reshape(-1, width)


def place_kernel(turned, code_ref, g_ref, o_ref, *scratch):
    code = code_ref[0]
    for j in range(16):
        start = pl.multiple_of((j ^ code) * 32, 32)
        block = g_ref[0, pl.ds(start, 32), :].astype(F32)
        if turned:
            scratch[0][j * 32 : (j + 1) * 32, :] = block
        else:
            o_ref[0, j * 32 : (j + 1) * 32, :] = block
    if turned:
        o_ref[...] = scratch[0][...].T.reshape(o_ref.shape)


def place(sums, shape, block, index, turned, count, group, code):
    width = sums.shape[-1]
    return pl.pallas_call(
        functools.partial(place_kernel, turned),
        out_shape=jax.ShapeDtypeStruct(shape, F32),
        grid_spec=pltpu.PrefetchScalarGridSpec(
            num_scalar_prefetch=1,
            grid=(shape[0], count),
            in_specs=[pl.BlockSpec((1, 512, width), lambda l, i, code: (group(l, i), 0, 0))],
            out_specs=pl.BlockSpec(block, lambda l, i, code: index(l, i)),
            scratch_shapes=[pltpu.VMEM((512, width), F32)] if turned else [],
        ),
        compiler_params=pltpu.CompilerParams(vmem_limit_bytes=VMEM_LIMIT),
        cost_estimate=pl.CostEstimate(
            flops=0, bytes_accessed=shape[0] * count * 512 * width * 6, transcendentals=0
        ),
        name="place",
    )(code, sums)


def widen_kernel(a_ref, b_ref, a_out, b_out, a_buf, b_buf, sem):
    copies = []
    for n, (source, target, buf) in enumerate(((a_ref, a_out, a_buf), (b_ref, b_out, b_buf))):
        buf[...] = source[...].astype(F32)
        copies.append(pltpu.make_async_copy(buf, target.at[:, 0], sem.at[n]))
        copies[-1].start()
    for copy in copies:
        copy.wait()


def widen_rows(a, b):
    rows, width = a.shape
    out = jax.ShapeDtypeStruct((rows, 1, width), F32)
    return pl.pallas_call(
        widen_kernel,
        out_shape=(out, out),
        in_specs=[pl.BlockSpec(memory_space=pltpu.VMEM)] * 2,
        out_specs=(pl.BlockSpec(memory_space=pl.ANY),) * 2,
        scratch_shapes=[pltpu.VMEM((rows, width), F32), pltpu.VMEM((rows, width), F32), pltpu.SemaphoreType.DMA((2,))],
        name="widen_rows",
    )(a, b)


def hand_out_kernel(layers, y_ref, packed, out, down, gain, shift, qv, hidden):
    y = y_ref[0]
    width = packed.shape[1]
    out[...] = packed[0:layers, :]
    down[...] = packed[layers : 2 * layers, :]
    for l in range(layers):
        for n in range(2):
            row = 2 * layers + 2 * l + n
            gain[l, n : n + 1, :] = packed[row : row + 1, :]
            row += 2 * layers
            shift[l, n : n + 1, :] = packed[row : row + 1, :]
            at = 8 * layers + 2 * l + n
            hidden[l : l + 1, n * width : (n + 1) * width] = jnp.where(
                y == 0, packed[at : at + 1, :], packed[at + 2 * layers : at + 2 * layers + 1, :]
            )
            half = slice(n * width // 2, (n + 1) * width // 2)
            at = 6 * layers + l
            qv[l, n : n + 1, :] = jnp.where(
                y == 0, packed[at : at + 1, half], packed[at + layers : at + layers + 1, half]
            )


def hand_out(packed, y, layers):
    width = packed.shape[1]
    full = lambda *shape: jax.ShapeDtypeStruct(shape, F32)
    in_vmem = pl.BlockSpec(memory_space=pltpu.VMEM)
    return pl.pallas_call(
        functools.partial(hand_out_kernel, layers),
        out_shape=(
            full(layers, width),
            full(layers, width),
            full(layers, 2, width),
            full(layers, 2, width),
            full(layers, 2, width // 2),
            full(layers, 2 * width),
        ),
        in_specs=[pl.BlockSpec(memory_space=pltpu.SMEM), in_vmem],
        out_specs=(in_vmem,) * 6,
        name="hand_out",
    )(y, packed)


def partner(bits):
    dp, y = lax.axis_index("dp"), lax.axis_index("tensor")
    other = dp
    for step in (1, 2, 4, 8):
        if bits & (2 * step):
            other = other + step * (1 - 2 * ((dp // step) % 2))
    return (other, 1 - y if bits & FLIP_Y else y)


def all_partners(bits):
    return {bit: partner(bit) for bit in bits}


def greet(partners):
    barrier = pltpu.get_barrier_semaphore()
    for other in partners.values():
        pl.semaphore_signal(barrier, inc=1, device_id=other, device_id_type=MESH)
    pl.semaphore_wait(barrier, len(partners))


def add_into(into, other, count):
    def step(i, _):
        into[i] = (into[i].astype(F32) + other[i].astype(F32)).astype(BF16)
        return 0

    lax.fori_loop(0, count, step, 0)


def add_rows(into, other, rows):
    def step(i, _):
        at = pl.ds(pl.multiple_of(i * 32, 32), 32)
        into[at, :] = (into[at, :].astype(F32) + other[at, :].astype(F32)).astype(BF16)
        return 0

    lax.fori_loop(0, rows // 32, step, 0)


SLOTS = 6
LAST_TICK = 8


class Reduction:
    def __init__(self, grads, sums, count, partners, bufs, sems):
        self.grads, self.sums, self.count, self.partners = grads, sums, count, partners
        self.y_buf, self.x_buf, self.z0_buf, self.z1_buf, self.all_buf, self.keep_buf = bufs
        self.send_sem, self.recv_sem, self.core_send, self.core_recv = sems[:4]
        self.keep_sem, self.out_sem, self.in_free, self.out_free = sems[4:]

    def copy(self, step, i):
        slot = lax.rem(i, SLOTS)
        ys, al = self.y_buf.at[slot], self.all_buf.at[slot]
        bit, source, target = (
            (FLIP_Y, self.grads.at[i, pl.ds(256, 256)], ys),
            (FLIP_X, ys.at[pl.ds(128, 128)], self.x_buf.at[slot]),
            (FLIP_Z0, ys.at[pl.ds(64, 64)], self.z0_buf.at[slot]),
            (FLIP_Z1, ys.at[pl.ds(32, 32)], self.z1_buf.at[slot]),
            (FLIP_Z1, al.at[pl.ds(0, 32)], al.at[pl.ds(32, 32)]),
            (FLIP_Z0, al.at[pl.ds(0, 64)], al.at[pl.ds(64, 64)]),
            (FLIP_X, al.at[pl.ds(0, 128)], al.at[pl.ds(128, 128)]),
            (FLIP_C, al, self.sums.at[i, pl.ds(256, 256)]),
        )[step]
        return pltpu.make_async_remote_copy(
            src_ref=source,
            dst_ref=target,
            send_sem=self.send_sem.at[step, slot] if step < 7 else self.core_send.at[i],
            recv_sem=self.recv_sem.at[step, slot] if step < 7 else self.core_recv.at[i],
            device_id=self.partners[bit],
            device_id_type=MESH,
        )

    def keep(self, i):
        slot = lax.rem(i, 2)
        return pltpu.make_async_copy(
            self.grads.at[i, pl.ds(0, 256)], self.keep_buf.at[slot], self.keep_sem.at[slot]
        )

    def out(self, i):
        slot = lax.rem(i, SLOTS)
        return pltpu.make_async_copy(
            self.all_buf.at[slot], self.sums.at[i, pl.ds(0, 256)], self.out_sem.at[slot]
        )

    def take(self, sem, i):
        @pl.when(i >= SLOTS)
        def _():
            pl.semaphore_wait(sem, 1)

    def give(self, sem, bit, i):
        @pl.when(i + SLOTS < self.count)
        def _():
            pl.semaphore_signal(sem, inc=1, device_id=self.partners[bit], device_id_type=MESH)

    def tick(self, t):
        def at(offset, body):
            i = t - offset
            pl.when((i >= 0) & (i < self.count))(lambda: body(i, lax.rem(i, SLOTS)))

        def set_out(i, slot):
            self.take(self.in_free.at[0], i)
            self.copy(0, i).start()
            self.keep(i).start()

        def finish(i, slot):
            self.copy(7, i).wait()
            self.out(i).wait()
            for n, bit in enumerate((FLIP_X, FLIP_Z0, FLIP_Z1)):
                self.give(self.out_free.at[n], bit, i)

        def to_core(i, slot):
            self.copy(6, i).wait()
            self.copy(7, i).start()
            self.out(i).start()

        def back_x(i, slot):
            self.copy(5, i).wait()
            self.take(self.out_free.at[0], i)
            self.copy(6, i).start()

        def back_z0(i, slot):
            self.copy(4, i).wait()
            self.take(self.out_free.at[1], i)
            self.copy(5, i).start()

        def back_z1(i, slot):
            self.copy(3, i).wait()
            add_rows(self.y_buf.at[slot], self.z1_buf.at[slot], 32)
            self.all_buf[slot, 0:32, :] = self.y_buf[slot, 0:32, :]
            for n, bit in enumerate((FLIP_Y, FLIP_X, FLIP_Z0, FLIP_Z1)):
                self.give(self.in_free.at[n], bit, i)
            self.take(self.out_free.at[2], i)
            self.copy(4, i).start()

        def on_z1(i, slot):
            self.copy(2, i).wait()
            add_rows(self.y_buf.at[slot], self.z0_buf.at[slot], 64)
            self.take(self.in_free.at[3], i)
            self.copy(3, i).start()

        def on_z0(i, slot):
            self.copy(1, i).wait()
            add_rows(self.y_buf.at[slot], self.x_buf.at[slot], 128)
            self.take(self.in_free.at[2], i)
            self.copy(2, i).start()

        def on_x(i, slot):
            self.copy(0, i).wait()
            self.keep(i).wait()
            add_rows(self.y_buf.at[slot], self.keep_buf.at[lax.rem(i, 2)], 256)
            self.take(self.in_free.at[1], i)
            self.copy(1, i).start()

        at(0, set_out)
        at(8, finish)
        at(7, to_core)
        at(6, back_x)
        at(5, back_z0)
        at(4, back_z1)
        at(3, on_z1)
        at(2, on_z0)
        at(1, on_x)


def unit_order(y, core_free_bits):
    taken = lax.broadcasted_iota(jnp.int32, (512, 512), 0)
    column = lax.broadcasted_iota(jnp.int32, (512, 512), 1)
    where = lax.rem(column, 32)
    for own, weight in zip((y,) + core_free_bits, (256, 128, 64, 32)):
        bit = lax.rem(lax.div(column, weight), 2)
        where = where + weight * (bit + own - 2 * own * bit)
    return (taken == where).astype(F32)


def begin(feeds):
    for copy in feeds(0, 0):
        copy.start()


def stream(count, feeds, body):
    def step(i, _):
        slot = lax.rem(i, 2)

        @pl.when(i + 1 < count)
        def _():
            for copy in feeds(i + 1, 1 - slot):
                copy.start()

        for copy in feeds(i, slot):
            copy.wait()
        body(i, slot)
        return 0

    lax.fori_loop(0, count, step, 0)


def norm(r, gain, shift):
    centred = r - jnp.mean(r, axis=-1, keepdims=True)
    rstd = lax.rsqrt(jnp.mean(centred * centred, axis=-1, keepdims=True) + 1e-06)
    return centred * rstd * gain + shift


def norm_back(dy, r, gain):
    centred = r - jnp.mean(r, axis=-1, keepdims=True)
    rstd = lax.rsqrt(jnp.mean(centred * centred, axis=-1, keepdims=True) + 1e-06)
    unit = centred * rstd
    dunit = dy * gain
    dr = rstd * (
        dunit
        - jnp.mean(dunit, axis=-1, keepdims=True)
        - unit * jnp.mean(dunit * unit, axis=-1, keepdims=True)
    )
    return dr, dy * unit


def gelu_and_slope(u):
    cdf = 0.5 * (1.0 + lax.erf(u * (0.5**0.5)))
    pdf = jnp.exp(-0.5 * u * u) * 0.3989422804014327
    return u * cdf, cdf + u * pdf


TILE = 64


def row_tiles(rows, body):
    def step(i, _):
        body(pl.ds(pl.multiple_of(i * TILE, TILE), TILE))
        return 0

    lax.fori_loop(0, rows // TILE, step, 0)


def pair_lanes(values, e):
    lane = lax.broadcasted_iota(jnp.int32, values.shape, 1)
    return jnp.where(lane // HEAD_DIM == e, values, jnp.zeros_like(values))


def spread_mask(block_part, document_part):
    blocks, lanes = block_part.shape
    each = document_part.shape[0] // blocks
    part = jnp.broadcast_to(block_part[:, None, :], (blocks, each, lanes)).reshape(blocks * each, lanes)
    return (part + document_part).astype(BF16)


def both_heads(values):
    return jnp.concatenate([pair_lanes(values, 0), pair_lanes(values, 1)], axis=0)


def attend_pair(query, keys, values, hot, mask):
    scale = HEAD_DIM**-0.5
    rows = query.shape[0]
    query = query * jnp.asarray(scale, BF16)
    right = jnp.concatenate([both_heads(query), both_heads(hot)], axis=1)
    s = nt(jnp.concatenate([keys, mask], axis=1), right)
    top = jnp.max(s, axis=0, keepdims=True)
    p = jnp.exp(s - top)
    total = jnp.sum(p, axis=0, keepdims=True)
    c = nn(values.T, p.astype(BF16)) * (1.0 / total)
    context = jnp.concatenate([c[:HEAD_DIM, :rows], c[HEAD_DIM:, rows:]], axis=0).T
    lse = top + jnp.log(total)
    return context, [lse[:, :rows], lse[:, rows:]]


def attend_back_pair(query, keys, values, hot, mask, ctx, lse, dctx):
    scale = HEAD_DIM**-0.5
    rows = query.shape[0]
    query = query * jnp.asarray(scale, BF16)
    keys_t = keys.T
    delta_t = (dctx.astype(F32) * ctx.astype(F32)).T
    left = jnp.concatenate([keys, mask], axis=1)
    tile = rows // 2
    dk, dv, dq = 0.0, 0.0, []
    for part in range(2):
        at = slice(part * tile, (part + 1) * tile)
        heads = []
        for e in range(2):
            lanes = slice(e * HEAD_DIM, (e + 1) * HEAD_DIM)
            query_e = pair_lanes(query[at], e)
            dctx_e = pair_lanes(dctx[at], e)
            right = jnp.concatenate([query_e, pair_lanes(hot[at], e)], axis=1)
            p = jnp.exp(nt(left, right) - lse[e : e + 1, at])
            dp = nt(values, dctx_e)
            delta = jnp.sum(delta_t[lanes, at], axis=0, keepdims=True)
            ds = (p * (dp - delta)).astype(BF16)
            dk = dk + nn(ds, query_e)
            dv = dv + nn(p.astype(BF16), dctx_e)
            heads.append(nn(keys_t[lanes, :], ds) * scale)
        dq.append(jnp.concatenate(heads, axis=0).T)
    return jnp.concatenate(dq, axis=0), dk, dv


class Spread:
    def __init__(self, weights, pairs, partners, send_sem, recv_sem):
        self.weights, self.pairs, self.partners = weights, pairs, partners
        self.send_sem, self.recv_sem = send_sem, recv_sem

    def copy(self, step, t):
        w = self.weights
        even, odd = 2 * t, 2 * t + 1
        bit, source, target = (
            (FLIP_Y, w.at[0, even, 0, pl.ds(0, 64)], w.at[0, even, 1, pl.ds(0, 64)]),
            (FLIP_Y, w.at[0, odd, 0, pl.ds(0, 64)], w.at[0, odd, 1, pl.ds(0, 64)]),
            (FLIP_X, w.at[0, even, 1, pl.ds(0, 64)], w.at[0, even, 1, pl.ds(128, 64)]),
            (FLIP_Z0, w.at[0, odd, 1, pl.ds(0, 64)], w.at[0, odd, 1, pl.ds(64, 64)]),
            (FLIP_Z0, w.at[0, even, 1, pl.ds(0, 64)], w.at[0, even, 1, pl.ds(64, 64)]),
            (FLIP_Z0, w.at[0, even, 1, pl.ds(128, 64)], w.at[0, even, 1, pl.ds(192, 64)]),
            (FLIP_X, w.at[0, odd, 1, pl.ds(0, 128)], w.at[0, odd, 1, pl.ds(128, 128)]),
            (FLIP_C, w.at[0, even, 1], w.at[1, even, 1]),
            (FLIP_C, w.at[0, odd, 1], w.at[1, odd, 1]),
        )[step]
        return pltpu.make_async_remote_copy(
            src_ref=source,
            dst_ref=target,
            send_sem=self.send_sem.at[step, t],
            recv_sem=self.recv_sem.at[step, t],
            device_id=self.partners[bit],
            device_id_type=MESH,
        )

    def tick(self, t):
        def at(offset, waits, starts):
            i = t - offset

            @pl.when((i >= 0) & (i < self.pairs))
            def _():
                for step in waits:
                    self.copy(step, i).wait()
                for step in starts:
                    self.copy(step, i).start()

        at(0, (), (0, 1))
        at(5, (7, 8), ())
        at(1, (0, 1), (2, 3))
        at(2, (2, 3), (4, 5, 6))
        at(4, (4, 5, 6), (7, 8))


PER_LAYER = 14
DEPTH = 3


def forward_kernel(layers, *refs):
    refs = list(refs)
    x_ref, up_ref, wq_ref, wo_ref, wi_ref, wd_ref = refs[:6]
    hot_buf, mask_ref, key_ref, bq_ref, bi_ref, vec_ref = refs[6:12]
    w_ref, up_out, x_out = refs[12:15]
    saved = [refs[15 + PER_LAYER * l : 15 + PER_LAYER * (l + 1)] for l in range(layers)]
    (
        x, acc, r_buf, low, xb, qkv, kv_sib, ctx, lse, hl, g_all, slope_all,
        col_buf, row_buf, turn_buf, made_buf, wa_buf, wb_buf,
        feed_sem, load_sem, col_sem, row_sem, made_sem, store_sem, block_sem,
        core_send, core_recv, kv_send, kv_recv, g_send, g_recv, spread_send, spread_recv,
    ) = refs[15 + PER_LAYER * layers :]
    rows, width = acc.shape
    dp, y = lax.axis_index("dp"), lax.axis_index("tensor")
    core = dp % 2
    stays = core == y
    partners = all_partners((FLIP_Y, FLIP_X, FLIP_Z0, FLIP_C, SWAP))
    spread = Spread(w_ref, layers * GROUPS // 2, partners, spread_send, spread_recv)
    greet(partners)

    def feed(n, slot, source, target):
        return pltpu.make_async_copy(source, target, feed_sem.at[n, slot])

    def load(n, source, target):
        return pltpu.make_async_copy(source, target, load_sem.at[n])

    def store(n, source, target):
        return pltpu.make_async_copy(source, target, store_sem.at[n])

    def exchange(n, source, target, bits=FLIP_C):
        return pltpu.make_async_remote_copy(
            src_ref=source, dst_ref=target, send_sem=core_send.at[n], recv_sem=core_recv.at[n],
            device_id=partners[bits], device_id_type=MESH,
        )

    def columns(ref, i, size):
        return ref.at[:, pl.ds(pl.multiple_of(i * size, size), size)]

    def swap(n, source, target, begin):
        here = store(n, source, target)
        there = exchange(n, source, target, SWAP)

        @pl.when(stays)
        def _():
            here.start() if begin else here.wait()

        @pl.when(jnp.logical_not(stays))
        def _():
            there.start() if begin else there.wait()

    items = []
    for l in range(layers):
        items += [(True, wq_ref.at[l, (t + 1) % 3], l * GROUPS + t) for t in range(3)]
        items += [(False, wo_ref.at[l], l * GROUPS + OUT_GROUP)]
        for n in range(FF_GROUPS):
            items += [(True, wi_ref.at[l, :, pl.ds(n * 512, 512)], l * GROUPS + in_group(n))]
            items += [(False, wd_ref.at[l, pl.ds(n * 512, 512)], l * GROUPS + down_group(n))]
    fetches, counts, ahead = [], [0, 0], [[], []]
    for m, (turned, source, group) in enumerate(items):
        slot = counts[turned] % DEPTH
        buf, sem = (col_buf, col_sem) if turned else (row_buf, row_sem)
        fetches.append((pltpu.make_async_copy(source, buf.at[slot], sem.at[slot]), slot))
        ahead[turned].append(m)
        counts[turned] += 1
    bits = [(dp // step) % 2 for step in (1, 2, 4, 8)]
    made = {}

    def convert(m):
        turned, _, group = items[m]
        copy, slot = fetches[m]
        copy.wait()
        if turned:

            def turn(i, _):
                strip = col_buf[slot, :, pl.ds(pl.multiple_of(i * 128, 128), 128)]
                turn_buf[pl.ds(pl.multiple_of(i * 128, 128), 128), :] = strip.astype(BF16).T
                return 0

            lax.fori_loop(0, 4, turn, 0)
        if m >= 2:
            made[m - 2].wait()

        def block(j, _):
            where = 0
            for bit, weight in zip(bits, (8, 4, 2, 1)):
                own = (j // weight) % 2
                where = where + weight * (own + bit - 2 * own * bit)
            at = pl.ds(pl.multiple_of(where * 32, 32), 32)
            rows_32 = turn_buf[at, :] if turned else row_buf[slot, at, :]
            made_buf[m % 2, pl.ds(pl.multiple_of(j * 32, 32), 32), :] = rows_32.astype(BF16)
            return 0

        lax.fori_loop(0, 16, block, 0)
        later = [n for n in ahead[turned] if n > m]
        if len(later) >= DEPTH:
            fetches[later[DEPTH - 1]][0].start()
        parts = [
            pltpu.make_async_copy(
                made_buf.at[m % 2, pl.ds(a * 256, 256)], w_ref.at[a, group, 0], made_sem.at[m % 2, a]
            )
            for a in range(2)
        ]

        class Both:
            def wait(self):
                for part in parts:
                    part.wait()

        for part in parts:
            part.start()
        made[m] = Both()

    load_x = load(0, x_ref.at[:, 0], x)
    load_x.start()
    load_up = load(1, up_ref.at[:, 0], acc)
    load_up.start()
    for kind in range(2):
        for m in ahead[kind][:DEPTH]:
            fetches[m][0].start()
    load_x.wait()

    def narrow_x(at):
        low[at, :] = x[at, :].astype(BF16)

    row_tiles(rows, narrow_x)
    swap(0, low, xb, True)
    load_up.wait()

    def narrow_up(at):
        hl[at, :] = acc[at, :].astype(BF16)

    row_tiles(rows, narrow_up)
    swap(1, hl, up_out, True)

    for m in range(len(items)):
        convert(m)
        if m % 4 == 3:
            spread.tick(m // 4)
    for m in range(len(items) - 2, len(items)):
        made[m].wait()
    swap(0, low, xb, False)
    swap(1, hl, up_out, False)

    def widen(at):
        x[at, :] = xb[at, :].astype(F32)

    row_tiles(rows, widen)

    pairs = width // 128
    for l in range(layers):
        (
            qkv_out, sib_out, ctx_out, ctx_sib_out, lse_out, r1_out, r2_out, hl_out, hl_sib_out,
            g_out, g_sib_out, slope_out, xb_out, xb_sib_out,
        ) = saved[l]
        first = l * GROUPS
        clock = 6 + 6 * l
        xb_store = store(0, xb, xb_out)
        xb_store.start()
        xb_copy = exchange(2 + 3 * l, xb, xb_sib_out)
        xb_copy.start()

        def give_kv(n, a):
            at = pl.ds(pl.multiple_of(a * 512, 512), 512)
            return pltpu.make_async_remote_copy(
                src_ref=qkv.at[1 + n, :, at], dst_ref=kv_sib.at[n, :, at],
                send_sem=kv_send.at[n, a], recv_sem=kv_recv.at[n, a],
                device_id=partners[FLIP_C], device_id_type=MESH,
            )

        def which(i):
            n = lax.div(i, 2)
            return lax.rem(n + 1, 3), n, lax.rem(i, 2)

        def qkv_feeds(i, slot):
            _, n, a = which(i)
            return (feed(0, slot, w_ref.at[a, first + n], wa_buf.at[slot]),)

        def qkv_body(i, slot):
            t, _, a = which(i)
            at = pl.ds(pl.multiple_of(a * 512, 512), 512)
            qkv[t, :, at] = (nt(xb[...], block_of(wa_buf.at[slot])) + bq_ref[l, t, a]).astype(BF16)
            pl.when(t > 0)(lambda: give_kv(t - 1, a).start())
            pl.when(i == 2)(lambda: spread.tick(clock))

        if l == 0:
            begin(qkv_feeds)
        stream(6, qkv_feeds, qkv_body)
        qkv_store = store(1, qkv, qkv_out)
        qkv_store.start()
        for n in range(2):
            for a in range(2):
                give_kv(n, a).wait()
        sib_store = store(2, kv_sib, sib_out)
        sib_store.start()

        feed(2, 0, w_ref.at[0, first + OUT_GROUP], wb_buf.at[0]).start()

        def pair_body(p, _):
            far = lax.rem(p + pairs // 2, pairs)
            here = pl.ds(pl.multiple_of(p * 128, 128), 128)
            there = pl.ds(pl.multiple_of(far * 128, 128), 128)
            mask = spread_mask(mask_ref[p], key_ref[...])
            keys = jnp.concatenate([qkv[1, :, here], kv_sib[0, :, there]], axis=0)
            values = jnp.concatenate([qkv[2, :, here], kv_sib[1, :, there]], axis=0)
            context, parts = attend_pair(qkv[0, :, here], keys, values, hot_buf[...], mask)
            ctx[:, here] = context.astype(BF16)
            for e in range(2):
                lse[p, e : e + 1, :] = parts[e]
            pl.when(lax.rem(p, 5) == 2)(lambda: spread.tick(clock + 1 + lax.div(p, 5)))
            return 0

        lax.fori_loop(0, pairs, pair_body, 0)
        ctx_store = store(3, ctx, ctx_out)
        ctx_store.start()
        lse_store = store(4, lse, lse_out)
        lse_store.start()
        ctx_copy = exchange(3 + 3 * l, ctx.at[:, pl.ds(512, 512)], ctx_sib_out)
        ctx_copy.start()

        def place_of(i):
            return 1 - lax.rem(i, 2), lax.div(i, 2)

        def ff_feeds(i, slot):
            a, n = place_of(i)
            return (
                feed(0, slot, w_ref.at[a, first + in_group(n)], wa_buf.at[slot]),
                feed(2, slot, w_ref.at[a, first + down_group(n)], wb_buf.at[slot]),
            )

        ff_feeds(0, 0)[0].start()

        def out_feeds(i, slot):
            return (feed(2, slot, w_ref.at[i, first + OUT_GROUP], wb_buf.at[slot]),)

        def out_body(i, slot):
            part = nn(ctx[:, pl.ds(pl.multiple_of(i * 512, 512), 512)], block_of(wb_buf.at[slot]))

            @pl.when(i == 0)
            def _():
                acc[...] = part

            @pl.when(i == 1)
            def _():
                acc[...] += part

        stream(2, out_feeds, out_body)
        ff_feeds(0, 0)[1].start()
        sib_store.wait()

        def first_norm(at):
            r1 = x[at, :] + acc[at, :] + vec_ref[l, 0:1, :]
            r_buf[at, :] = r1
            h = norm(r1, vec_ref[l, 1:2, :], vec_ref[l, 2:3, :])
            hl[at, :] = h.astype(BF16)
            acc[at, :] = h + vec_ref[l, 3:4, :]

        row_tiles(rows, first_norm)
        r1_store = store(5, r_buf, r1_out)
        r1_store.start()
        hl_store = store(6, hl, hl_out)
        hl_store.start()
        hl_copy = exchange(4 + 3 * l, hl, hl_sib_out)
        hl_copy.start()

        def g_store(j):
            return pltpu.make_async_copy(g_all.at[j], columns(g_out, j, 512), block_sem.at[0, j])

        def slope_store(j):
            return pltpu.make_async_copy(slope_all.at[j], columns(slope_out, j, 512), block_sem.at[1, j])

        def g_copy(n):
            return pltpu.make_async_remote_copy(
                src_ref=g_all.at[FF_GROUPS + n], dst_ref=columns(g_sib_out, n, 512),
                send_sem=g_send.at[l, n], recv_sem=g_recv.at[l, n],
                device_id=partners[FLIP_C], device_id_type=MESH,
            )

        def ff_body(i, slot):
            a, n = place_of(i)
            j = a * FF_GROUPS + n
            u = nt(hl[...], block_of(wa_buf.at[slot])) + bi_ref[l, a, n]
            g, slope = gelu_and_slope(u)
            g = g.astype(BF16)
            g_all[j] = g
            slope_all[j] = slope.astype(BF16)
            g_store(j).start()
            slope_store(j).start()
            pl.when(a == 1)(lambda: g_copy(n).start())
            acc[...] += nn(g, block_of(wb_buf.at[slot]))
            pl.when(lax.rem(i, 3) == 1)(lambda: spread.tick(clock + 3 + lax.div(i, 3)))

        stream(2 * FF_GROUPS, ff_feeds, ff_body)
        r1_store.wait()
        xb_store.wait()
        xb_copy.wait()
        if l + 1 < layers:
            feed(0, 0, w_ref.at[0, first + GROUPS], wa_buf.at[0]).start()

        def second_norm(at):
            r2 = acc[at, :]
            r_buf[at, :] = r2
            x2 = norm(r2, vec_ref[l, 4:5, :], vec_ref[l, 5:6, :])
            x[at, :] = x2
            xb[at, :] = x2.astype(BF16)

        row_tiles(rows, second_norm)
        r2_store = store(5, r_buf, r2_out)
        r2_store.start()
        if l == layers - 1:
            x_store = store(10, xb, x_out)
            x_store.start()

        def settle(j, _):
            g_store(j).wait()
            slope_store(j).wait()
            return 0

        lax.fori_loop(0, 2 * FF_GROUPS, settle, 0)

        def settle_sent(n, _):
            g_copy(n).wait()
            return 0

        lax.fori_loop(0, FF_GROUPS, settle_sent, 0)
        for copy in (qkv_store, ctx_store, lse_store, ctx_copy, hl_store, hl_copy, r2_store):
            copy.wait()
    x_store.wait()


def forward(block_input, cotangent, w_qkv, w_out, w_in, w_down, hot, mask, mask_rows, bias_qkv, bias_in, vectors):
    rows, _, width = block_input.shape
    layers = w_qkv.shape[0]
    total = layers * GROUPS
    anywhere = pl.BlockSpec(memory_space=pl.ANY)
    in_vmem = pl.BlockSpec(memory_space=pltpu.VMEM)
    low = lambda *shape: pltpu.VMEM(shape, BF16)
    full = lambda *shape: pltpu.VMEM(shape, F32)
    dma = lambda *shape: pltpu.SemaphoreType.DMA(shape)
    low_out = lambda *shape: jax.ShapeDtypeStruct(shape, BF16)
    full_out = lambda *shape: jax.ShapeDtypeStruct(shape, F32)
    layer_out = (
        low_out(3, rows, width),
        low_out(2, rows, width),
        low_out(rows, width),
        low_out(rows, width // 2),
        full_out(width // 128, 2, rows),
        full_out(rows, width),
        full_out(rows, width),
        low_out(rows, width),
        low_out(rows, width),
        low_out(rows, 4 * width),
        low_out(rows, 2 * width),
        low_out(rows, 4 * width),
        low_out(rows, width),
        low_out(rows, width),
    )
    outs = pl.pallas_call(
        functools.partial(forward_kernel, layers),
        out_shape=(low_out(2, total, 2, 256, width), low_out(rows, width), low_out(rows, width)) + layer_out * layers,
        in_specs=[anywhere] * 6 + [in_vmem] * 6,
        out_specs=(anywhere,) * (3 + PER_LAYER * layers),
        scratch_shapes=[
            full(rows, width),
            full(rows, width),
            full(rows, width),
            low(rows, width),
            low(rows, width),
            low(3, rows, width),
            low(2, rows, width),
            low(rows, width),
            full(width // 128, 2, rows),
            low(rows, width),
            low(2 * FF_GROUPS, rows, 512),
            low(2 * FF_GROUPS, rows, 512),
            full(DEPTH, width, 512),
            full(DEPTH, 512, width),
            low(512, width),
            low(2, 512, width),
            low(2, 2, 256, width),
            low(2, 2, 256, width),
            dma(3, 2),
            dma(3),
            dma(DEPTH),
            dma(DEPTH),
            dma(2, 2),
            dma(11),
            dma(2, 2 * FF_GROUPS),
            dma(11),
            dma(11),
            dma(2, 2),
            dma(2, 2),
            dma(layers, FF_GROUPS),
            dma(layers, FF_GROUPS),
            dma(9, total // 2),
            dma(9, total // 2),
        ],
        compiler_params=pltpu.CompilerParams(collective_id=0, has_side_effects=True, vmem_limit_bytes=60 << 20),
        cost_estimate=pl.CostEstimate(flops=30 << 30, bytes_accessed=300 << 20, transcendentals=1 << 24),
        name="forward",
    )(block_input, cotangent, w_qkv, w_out, w_in, w_down, hot, mask, mask_rows, bias_qkv, bias_in, vectors)
    saved = [outs[3 + PER_LAYER * l : 3 + PER_LAYER * (l + 1)] for l in range(layers)]
    return outs[0], outs[1], outs[2], saved


def backward_kernel(layers, *refs):
    refs = list(refs)
    up_ref, x_ref, w_ref, hot_buf, mask_ref, key_ref, vec_ref = refs[:7]
    saved = [refs[7 + PER_LAYER * l : 7 + PER_LAYER * (l + 1)] for l in range(layers)]
    at_ref = 7 + PER_LAYER * layers
    grads, sums, dx_out, x_out, packed = refs[at_ref : at_ref + 5]
    (
        acc, dr1, dm, dm_sib, da, da_sib, du, du_sib, dctx, dqkv, d_sib, kv_out, kv_far,
        wa_buf, wb_buf, r_buf, slope_buf, left_buf, left_sib_buf, right_buf, right_sib_buf,
        pair_buf, lse_buf, unit_buf,
        y_buf, x_buf, z0_buf, z1_buf, all_buf, keep_buf,
        feed_sem, load_sem, store_sem, swap_sem, core_send, core_recv, du_send, du_recv, pair_send, pair_recv,
        send_sem, recv_sem, sum_send, sum_recv, keep_sem, out_sem, in_free, out_free,
        dbi_ref, qkv_sums_ref, small_ref, far_buf, far_send, far_recv,
    ) = refs[at_ref + 5 :]
    rows, width = acc.shape
    total = layers * GROUPS
    partners = all_partners((FLIP_Y, FLIP_X, FLIP_Z0, FLIP_Z1, FLIP_C, SWAP))
    reduction = Reduction(
        grads, sums, total, partners,
        (y_buf, x_buf, z0_buf, z1_buf, all_buf, keep_buf),
        (send_sem, recv_sem, sum_send, sum_recv, keep_sem, out_sem, in_free, out_free),
    )
    greet(partners)

    def feed(n, slot, source, target):
        return pltpu.make_async_copy(source, target, feed_sem.at[n, slot])

    def load(n, source, target):
        return pltpu.make_async_copy(source, target, load_sem.at[n])

    def exchange(n, source, target):
        return pltpu.make_async_remote_copy(
            src_ref=source, dst_ref=target, send_sem=core_send.at[n], recv_sem=core_recv.at[n],
            device_id=partners[FLIP_C], device_id_type=MESH,
        )

    def give_du(j, n):
        return pltpu.make_async_remote_copy(
            src_ref=du.at[j], dst_ref=du_sib.at[n], send_sem=du_send.at[n], recv_sem=du_recv.at[n],
            device_id=partners[FLIP_C], device_id_type=MESH,
        )

    def weight(a, group):
        return w_ref.at[a, group]

    def columns(ref, i, size):
        return ref.at[:, pl.ds(pl.multiple_of(i * size, size), size)]

    def unit_store(slot, index):
        return pltpu.make_async_copy(unit_buf.at[slot], grads.at[index], store_sem.at[0])

    def unit(left, left_sib, right, right_sib, slot, index, fresh=False):
        made = (tn(left, right) + tn(left_sib, right_sib)).astype(BF16)
        unit_buf[slot] = made
        if fresh is not False:
            pl.when(jnp.logical_not(fresh))(lambda: unit_store(slot, index).wait())
        else:
            unit_store(slot, index).wait()
        unit_store(slot, index).start()

    def add_small(l, row, value):
        small_ref[l, row : row + 1, :] += jnp.sum(value, axis=0, keepdims=True)

    stays = lax.axis_index("dp") % 2 == lax.axis_index("tensor")

    def swap(n, source, target, begin):
        here = pltpu.make_async_copy(source, target, swap_sem.at[n])
        there = pltpu.make_async_remote_copy(
            src_ref=source, dst_ref=target, send_sem=core_send.at[4 + n], recv_sem=core_recv.at[4 + n],
            device_id=partners[SWAP], device_id_type=MESH,
        )

        @pl.when(stays)
        def _():
            here.start() if begin else here.wait()

        @pl.when(jnp.logical_not(stays))
        def _():
            there.start() if begin else there.wait()

    swap(1, x_ref, x_out, True)
    load(0, saved[-1][6], r_buf).start()
    start_up = load(1, up_ref, da)
    start_up.start()
    start_up.wait()
    small_ref[...] = jnp.zeros_like(small_ref)

    def widen(at):
        acc[at, :] = da[at, :].astype(F32)

    row_tiles(rows, widen)
    done = 0
    for l in reversed(range(layers)):
        qkv_ref, sib_ref, ctx_ref, ctx_sib_ref, lse_ref, r1_ref, r2_ref, hl_ref, hl_sib_ref, g_ref, g_sib_ref, slope_ref, xb_ref, xb_sib_ref = saved[l]
        first = l * GROUPS
        base = (layers - 1 - l) * GROUPS
        clock = 11 * (layers - 1 - l)

        def down_feeds(i, slot):
            return (
                feed(0, slot, columns(g_ref, i, 512), left_buf.at[slot]),
                feed(1, slot, columns(g_sib_ref, i, 512), left_sib_buf.at[slot]),
            )

        begin(down_feeds)
        load(0, r2_ref, r_buf).wait()

        def second(at):
            dy = acc[at, :]
            dr, part = norm_back(dy, r_buf[at, :], vec_ref[l, 4:5, :])
            acc[at, :] = dr
            dm[at, :] = dr.astype(BF16)
            add_small(l, 0, part)
            add_small(l, 1, dy)
            add_small(l, 2, dr)

        row_tiles(rows, second)
        dm_copy = exchange(0, dm, dm_sib)
        dm_copy.start()
        r_load = load(0, r1_ref, r_buf)
        r_load.start()
        right_load = load(1, hl_ref, right_buf)
        right_load.start()
        right_sib_load = load(2, hl_sib_ref, right_sib_buf)
        right_sib_load.start()
        dm_copy.wait()

        def down_body(i, slot):
            fresh = (i == 0) if l == layers - 1 else False
            unit(left_buf[slot], left_sib_buf[slot], dm[...], dm_sib[...], lax.rem(i, 2), base + i, fresh)
            pl.when(lax.rem(i, 2) == 1)(lambda: reduction.tick(clock + lax.div(i, 2)))

        def place_of(i):
            a = 1 - lax.div(i, FF_GROUPS)
            return a, lax.rem(i, FF_GROUPS)

        def ff_feeds(i, slot):
            a, n = place_of(i)
            j = a * FF_GROUPS + n
            return (
                feed(2, slot, weight(a, first + down_group(n)), wa_buf.at[slot]),
                feed(3, slot, weight(a, first + in_group(n)), wb_buf.at[slot]),
                feed(4, slot, columns(slope_ref, j, 512), slope_buf.at[slot]),
            )

        begin(ff_feeds)
        stream(FF_GROUPS, down_feeds, down_body)
        unit_store(1, base + FF_GROUPS - 1).wait()

        def ff_body(i, slot):
            a, n = place_of(i)
            j = a * FF_GROUPS + n
            dg = nt(dm[...], block_of(wa_buf.at[slot]))
            d = (dg * slope_buf[slot].astype(F32)).astype(BF16)
            du[j] = d
            pl.when(a == 1)(lambda: give_du(j, n).start())
            dbi_ref[l, a, n] = jnp.sum(d.astype(F32), axis=0, keepdims=True)
            acc[...] += nn(d, block_of(wb_buf.at[slot]))
            pl.when(lax.rem(i, 4) == 3)(lambda: reduction.tick(clock + 2 + lax.div(i, 4)))

        stream(2 * FF_GROUPS, ff_feeds, ff_body)

        def out_feeds(i, slot):
            return (feed(2, slot, weight(i, first + OUT_GROUP), wa_buf.at[slot]),)

        begin(out_feeds)
        r_load.wait()

        def first_norm(at):
            dy = acc[at, :]
            dr, part = norm_back(dy, r_buf[at, :], vec_ref[l, 1:2, :])
            dr1[at, :] = dr
            da[at, :] = dr.astype(BF16)
            add_small(l, 3, part)
            add_small(l, 4, dy)
            add_small(l, 5, dr)

        row_tiles(rows, first_norm)
        if l > 0:
            load(0, saved[l - 1][6], r_buf).start()
        da_copy = exchange(1, da, da_sib)
        da_copy.start()

        def out_body(i, slot):
            dctx[:, pl.ds(pl.multiple_of(i * 512, 512), 512)] = nt(da[...], block_of(wa_buf.at[slot])).astype(BF16)

        stream(2, out_feeds, out_body)

        pairs = width // 128

        def pair_feeds(p, slot):
            far = lax.rem(p + pairs // 2, pairs)
            return (
                feed(5, slot, columns(qkv_ref.at[0], p, 128), pair_buf.at[slot, 0, pl.ds(0, rows)]),
                feed(6, slot, columns(qkv_ref.at[1], p, 128), pair_buf.at[slot, 1, pl.ds(0, rows)]),
                feed(7, slot, columns(sib_ref.at[0], far, 128), pair_buf.at[slot, 1, pl.ds(rows, rows)]),
                feed(8, slot, columns(qkv_ref.at[2], p, 128), pair_buf.at[slot, 2, pl.ds(0, rows)]),
                feed(9, slot, columns(sib_ref.at[1], far, 128), pair_buf.at[slot, 2, pl.ds(rows, rows)]),
                feed(10, slot, columns(ctx_ref, p, 128), pair_buf.at[slot, 3, pl.ds(0, rows)]),
                feed(11, slot, lse_ref.at[p], lse_buf.at[slot]),
            )

        begin(pair_feeds)
        right_load.wait()
        right_sib_load.wait()

        def in_body(n, _):
            give_du(FF_GROUPS + n, n).wait()
            unit(du[n], du_sib[n], right_buf[...], right_sib_buf[...], lax.rem(n, 2), base + FF_GROUPS + n, n == 0)
            pl.when(lax.rem(n, 2) == 1)(lambda: reduction.tick(clock + 4 + lax.div(n, 2)))
            return 0

        lax.fori_loop(0, FF_GROUPS, in_body, 0)

        right_load = load(1, xb_ref, right_buf)
        right_load.start()
        right_sib_load = load(2, xb_sib_ref, right_sib_buf)
        right_sib_load.start()
        left_load = load(3, columns(ctx_ref, 0, 512), left_buf.at[0])
        left_load.start()
        left_sib_load = load(4, ctx_sib_ref, left_sib_buf.at[0])
        left_sib_load.start()
        da_copy.wait()
        left_load.wait()
        left_sib_load.wait()
        unit(left_buf[0], left_sib_buf[0], da[...], da_sib[...], 0, base + 2 * FF_GROUPS)
        unit_store(0, base + 2 * FF_GROUPS).wait()

        def dx_feeds(i, slot):
            return (feed(3, slot, weight(lax.rem(i, 2), first + lax.rem(lax.div(i, 2) + 2, 3)), wa_buf.at[slot]),)

        begin(dx_feeds)

        def give_pair(p):
            far = lax.rem(p + pairs // 2, pairs)
            at = pl.ds(pl.multiple_of(far * 128, 128), 128)
            return pltpu.make_async_remote_copy(
                src_ref=kv_out.at[:, :, at], dst_ref=kv_far.at[:, :, at], send_sem=pair_send.at[p], recv_sem=pair_recv.at[far],
                device_id=partners[FLIP_C], device_id_type=MESH,
            )

        def pair_body(p, slot):
            far = lax.rem(p + pairs // 2, pairs)
            here = pl.ds(pl.multiple_of(p * 128, 128), 128)
            mask = spread_mask(mask_ref[p], key_ref[...])
            dq, dk, dv = attend_back_pair(
                pair_buf[slot, 0, 0:rows], pair_buf[slot, 1], pair_buf[slot, 2], hot_buf[...], mask,
                pair_buf[slot, 3, 0:rows], lse_buf[slot], dctx[:, here],
            )
            dqkv[0, :, here] = dq.astype(BF16)
            dqkv[1, :, here] = dk[:rows].astype(BF16)
            dqkv[2, :, here] = dv[:rows].astype(BF16)
            there = pl.ds(pl.multiple_of(far * 128, 128), 128)
            kv_out[0, :, there] = dk[rows:].astype(BF16)
            kv_out[1, :, there] = dv[rows:].astype(BF16)
            give_pair(p).start()
            pl.when(lax.rem(p, 3) == 1)(lambda: reduction.tick(clock + 6 + lax.div(p, 3)))

        stream(pairs, pair_feeds, pair_body)

        def settle_pair(p, _):
            give_pair(p).wait()
            return 0

        lax.fori_loop(0, pairs, settle_pair, 0)
        for n in range(2):
            add_rows(dqkv.at[1 + n], kv_far.at[n], rows)
        d_copy = exchange(3, dqkv.at[:, :, pl.ds(512, 512)], d_sib)
        d_copy.start()
        right_load.wait()
        right_sib_load.wait()
        d_copy.wait()

        def qkv_body(n, _):
            unit(
                dqkv[n, :, 0:512], d_sib[n], right_buf[...], right_sib_buf[...],
                lax.rem(n + 1, 2), base + 2 * FF_GROUPS + 1 + n, n == 0,
            )
            pl.when(n == 1)(lambda: reduction.tick(clock + 9))
            return 0

        lax.fori_loop(0, 3, qkv_body, 0)

        def start_dx(at):
            acc[at, :] = dr1[at, :]

        row_tiles(rows, start_dx)

        def dx_body(i, slot):
            a, n = lax.rem(i, 2), lax.div(i, 2)
            d = dqkv[n, :, pl.ds(pl.multiple_of(a * 512, 512), 512)]
            qkv_sums_ref[l, n, a] = jnp.sum(d.astype(F32), axis=0, keepdims=True)
            acc[...] += nn(d, block_of(wa_buf.at[slot]))
            pl.when(i == 3)(lambda: reduction.tick(clock + 10))

        stream(6, dx_feeds, dx_body)
        done = clock + 11

    def narrow(at):
        da[at, :] = acc[at, :].astype(BF16)

    row_tiles(rows, narrow)
    unit_store(1, total - 1).wait()
    swap(0, da, dx_out, True)

    dp, y = lax.axis_index("dp"), lax.axis_index("tensor")
    core = dp % 2
    turned = unit_order(y, ((dp // 2) % 2, (dp // 4) % 2, (dp // 8) % 2))

    def in_order(pair):
        rows_ab = lax.dot_general(
            jnp.concatenate(pair, axis=0), turned, (((1,), (0,)), ((), ())),
            precision=lax.Precision.HIGHEST, preferred_element_type=F32,
        )
        near = jnp.where(core == 0, rows_ab[0:1], rows_ab[1:2])
        far = jnp.where(core == 0, rows_ab[1:2], rows_ab[0:1])
        return [
            jnp.concatenate([near[:, h * 256 : (h + 1) * 256], far[:, h * 256 : (h + 1) * 256]], axis=1)
            for h in range(2)
        ]

    for l in range(layers):
        for n, source in enumerate((5, 2, 3, 0, 4, 1)):
            row = n * layers + l if n < 2 else 2 * layers + (n // 2 - 1) * 2 * layers + 2 * l + n % 2
            packed[row : row + 1, :] = small_ref[l, source : source + 1, :]
        for n, t in enumerate((0, 2)):
            for h, part in enumerate(in_order([qkv_sums_ref[l, t, a] for a in range(2)])):
                packed[6 * layers + h * layers + l : 6 * layers + h * layers + l + 1, n * 512 : (n + 1) * 512] = part
        for n in range(FF_GROUPS):
            for h, part in enumerate(in_order([dbi_ref[l, a, n] for a in range(2)])):
                row = 8 * layers + h * 2 * layers + 2 * l + n // 2
                packed[row : row + 1, (n % 2) * 512 : (n % 2 + 1) * 512] = part

    tick_at = done
    for n, bit in enumerate((FLIP_C, FLIP_Y, FLIP_X, FLIP_Z0, FLIP_Z1)):
        cross = pltpu.make_async_remote_copy(
            src_ref=packed, dst_ref=far_buf.at[n], send_sem=far_send.at[n], recv_sem=far_recv.at[n],
            device_id=partners[bit], device_id_type=MESH,
        )
        cross.start()
        reduction.tick(tick_at)
        cross.wait()
        packed[...] += far_buf[n]
        tick_at += 1

    def rest(t, _):
        reduction.tick(t)
        return 0

    lax.fori_loop(tick_at, total + LAST_TICK, rest, 0)
    swap(0, da, dx_out, False)
    swap(1, x_ref, x_out, False)


def backward(upstream, stream_low, weights, hot, mask, mask_rows, vectors, saved):
    rows, width = upstream.shape
    layers = len(saved)
    total = layers * GROUPS
    anywhere = pl.BlockSpec(memory_space=pl.ANY)
    in_vmem = pl.BlockSpec(memory_space=pltpu.VMEM)
    low = lambda *shape: pltpu.VMEM(shape, BF16)
    dma = lambda *shape: pltpu.SemaphoreType.DMA(shape)
    return pl.pallas_call(
        functools.partial(backward_kernel, layers),
        out_shape=(
            jax.ShapeDtypeStruct((total, 512, width), BF16),
            jax.ShapeDtypeStruct((total, 512, width), BF16),
            jax.ShapeDtypeStruct((rows, width), BF16),
            jax.ShapeDtypeStruct((rows, width), BF16),
            jax.ShapeDtypeStruct((12 * layers, width), F32),
        ),
        in_specs=[anywhere] * 3 + [in_vmem] * 4 + [anywhere] * (PER_LAYER * layers),
        out_specs=(anywhere, anywhere, anywhere, anywhere, in_vmem),
        scratch_shapes=[
            pltpu.VMEM((rows, width), F32),
            pltpu.VMEM((rows, width), F32),
            low(rows, width),
            low(rows, width),
            low(rows, width),
            low(rows, width),
            low(2 * FF_GROUPS, rows, 512),
            low(FF_GROUPS, rows, 512),
            low(rows, width),
            low(3, rows, width),
            low(3, rows, 512),
            low(2, rows, width),
            low(2, rows, width),
            low(2, 2, 256, width),
            low(2, 2, 256, width),
            pltpu.VMEM((rows, width), F32),
            low(2, rows, 512),
            low(2, rows, 512),
            low(2, rows, 512),
            low(rows, width),
            low(rows, width),
            low(2, 4, 2 * rows, 128),
            pltpu.VMEM((2, 2, rows), F32),
            low(2, 512, width),
            low(SLOTS, 256, width),
            low(SLOTS, 128, width),
            low(SLOTS, 64, width),
            low(SLOTS, 32, width),
            low(SLOTS, 256, width),
            low(2, 256, width),
            dma(12, 2),
            dma(5),
            dma(1),
            dma(2),
            dma(6),
            dma(6),
            dma(FF_GROUPS),
            dma(FF_GROUPS),
            dma(width // 128),
            dma(width // 128),
            dma(7, SLOTS),
            dma(7, SLOTS),
            dma(total),
            dma(total),
            dma(2),
            dma(SLOTS),
            pltpu.SemaphoreType.REGULAR((4,)),
            pltpu.SemaphoreType.REGULAR((3,)),
            pltpu.VMEM((layers, 2, FF_GROUPS, 1, 512), F32),
            pltpu.VMEM((layers, 3, 2, 1, 512), F32),
            pltpu.VMEM((layers, 8, width), F32),
            pltpu.VMEM((5, 12 * layers, width), F32),
            dma(5),
            dma(5),
        ],
        compiler_params=pltpu.CompilerParams(
            collective_id=1, has_side_effects=True, vmem_limit_bytes=60 << 20
        ),
        cost_estimate=pl.CostEstimate(flops=60 << 30, bytes_accessed=300 << 20, transcendentals=1 << 24),
        name="backward",
    )(upstream, stream_low, weights, hot, mask, mask_rows, vectors, *[ref for one in saved for ref in one])


def flip_order(values, axis, bits):
    for i, bit in enumerate(bits):
        values = jnp.where(bit == 0, values, jnp.flip(values, axis + i))
    return values


def sequence_shards(
    block_input, segment_ids, random_blocks, w_qkv, b_qv, w_out, b_out, w_in, b_in, w_down, b_down,
    ln_gain, ln_bias, cotangent,
):
    y = lax.axis_index("tensor")
    dp = lax.axis_index("dp")
    core, x_bit, z0, z1 = dp % 2, (dp // 2) % 2, (dp // 4) % 2, dp // 8
    code = core * 8 + x_bit * 4 + z0 * 2 + z1
    code_arg = code.reshape(1).astype(jnp.int32)
    device_bits = (core, x_bit, z0, z1)

    rows, _, width = block_input.shape
    layers = w_qkv.shape[0]
    blocks = random_blocks.shape[2]
    own_blocks = blocks // 2
    heads = random_blocks.shape[1] * 2

    chosen = random_blocks[0]
    near = jnp.concatenate([chosen.reshape(-1), segment_ids[0]])
    sibling = flip(near, FLIP_C)
    across, diagonal = flip(chosen.reshape(-1), FLIP_Y), flip(chosen.reshape(-1), SWAP)
    mine = jnp.concatenate([near[: chosen.size], across, near[chosen.size :]])
    other = jnp.concatenate([sibling[: chosen.size], diagonal, sibling[chosen.size :]])
    packed = jnp.where(core == y, mine, other)
    chosen = packed[: 2 * chosen.size].reshape(2, heads // 2, blocks, -1)
    segments = packed[2 * random_blocks.size :]
    chosen = flip_order(chosen.reshape(2, 2, 2, 2, blocks, -1), 1, device_bits[:3])
    chosen = chosen.transpose(1, 0, 2, 3, 4, 5).reshape(heads, blocks, -1)
    segments = segments.reshape(2, rows)
    segments = jnp.where(core == 0, segments, segments[::-1]).reshape(-1)
    query_block = core * own_blocks + jnp.arange(own_blocks)
    key_block = jnp.arange(blocks) ^ (core * own_blocks)
    allowed = (
        (jnp.abs(query_block[:, None] - key_block[None, :]) <= 1)
        | (key_block[None, :] == 0)
        | (key_block[None, :] == blocks - 1)
        | (query_block[:, None] == 0)
        | (query_block[:, None] == blocks - 1)
    )
    chosen = lax.dynamic_slice_in_dim(chosen, core * own_blocks, own_blocks, axis=1)
    allowed = allowed[None] | jnp.any(chosen[:, :, None, :] == key_block[None, None, :, None], axis=3)
    block_rows = rows // own_blocks
    documents = jnp.arange(HEAD_DIM - own_blocks)
    mask = jnp.pad(
        jnp.where(allowed, 0.0, BIG).astype(F32).transpose(0, 2, 1), ((0, 0), (0, 0), (0, HEAD_DIM - own_blocks))
    )
    mask = mask.reshape(heads // 2, 2, blocks, HEAD_DIM).transpose(0, 2, 1, 3).reshape(heads // 2, blocks, 2 * HEAD_DIM)
    document_part = jnp.where(
        (segments[:, None] == documents[None, :]) | (documents[None, :] > 7), 0.0, BIG
    ).astype(F32)
    mask_rows = jnp.pad(document_part, ((0, 0), (own_blocks, 0)))
    mask_rows = jnp.concatenate([mask_rows, mask_rows], axis=1)
    block_rows = rows // own_blocks
    hot = jnp.concatenate(
        [
            jnp.repeat(jnp.eye(own_blocks, dtype=BF16), block_rows, axis=0),
            (segments[:rows, None] == documents[None, :]).astype(BF16),
        ],
        axis=1,
    )
    hot = jnp.concatenate([hot, hot], axis=1)

    bias_pack = jnp.concatenate(
        [
            flip_order(b_qv.reshape(layers * 2, 2, 2, 2, 2, -1), 1, device_bits).reshape(-1),
            flip_order(b_in.reshape(layers * FF_GROUPS, 2, 2, 2, 2, -1), 1, device_bits).reshape(-1),
        ]
    )
    bias_far = flip(bias_pack, FLIP_Y)
    n_qv = b_qv.size

    def local_bias(near, far, count):
        near, far = near.reshape(count, 2, 1, 256), far.reshape(count, 2, 1, 256)
        return jnp.concatenate([near, far], axis=2).reshape(count, 2, 512)

    bias_qv = local_bias(bias_pack[:n_qv], bias_far[:n_qv], layers * 2).reshape(layers, 2, 2, 1, 512)
    bias_qkv = jnp.stack([bias_qv[:, 0], jnp.zeros_like(bias_qv[:, 0]), bias_qv[:, 1]], axis=1)
    bias_in = local_bias(bias_pack[n_qv:], bias_far[n_qv:], layers * FF_GROUPS)
    bias_in = bias_in.reshape(layers, FF_GROUPS, 2, 1, 512).swapaxes(1, 2)

    vectors = [
        jnp.stack(
            [
                b_out[l], ln_gain[l, 0], ln_bias[l, 0], b_down[l], ln_gain[l, 1], ln_bias[l, 1],
                b_out[l], b_out[l],
            ]
        )
        for l in range(layers)
    ]
    vectors = jnp.stack(vectors)
    weights, upstream_low, stream_low, saved = forward(
        block_input, cotangent, w_qkv, w_out, w_in, w_down, hot, mask, mask_rows, bias_qkv, bias_in, vectors
    )
    _, grads, dx_low, x_low, packed = backward(
        upstream_low, stream_low, weights, hot, mask, mask_rows, vectors, saved
    )
    block_output, input_grad = widen_rows(x_low, dx_low)

    def placing(shape, block, index, turned, count, start):
        return place(
            grads, shape, block, index, turned, count, lambda l, i: (layers - 1 - l) * GROUPS + start + i, code_arg
        )

    g_b_out, g_b_down, g_gain, g_shift, g_b_qv, g_b_in = hand_out(packed, y.reshape(1).astype(jnp.int32), layers)
    g_down = placing(w_down.shape, (1, 512, width), lambda l, i: (l, i, 0), False, FF_GROUPS, 0)
    g_in = placing(w_in.shape, (1, width, 512), lambda l, i: (l, 0, i), True, FF_GROUPS, FF_GROUPS)
    g_qkv = placing(w_qkv.shape, (1, 1, width, 512), lambda l, i: (l, i, 0, 0), True, 3, 2 * FF_GROUPS + 1)
    g_out = placing(w_out.shape, (1, 512, width), lambda l, i: (l, 0, 0), False, 1, 2 * FF_GROUPS)
    return (
        block_output,
        input_grad,
        g_qkv,
        g_b_qv,
        g_out,
        g_b_out,
        g_in,
        g_b_in,
        g_down,
        g_b_down,
        g_gain,
        g_shift,
    )


def as_sent(array):

    def short(part):
        return part.astype(jnp.bfloat16) if part.dtype == jnp.float32 else part

    return jax.tree.map(short, array)


def norm_rows(values, gain_row, shift_row):
    row_mean = jnp.mean(values, axis=-1, keepdims=True)
    centred = values - row_mean
    variance = jnp.mean(centred * centred, axis=-1, keepdims=True)
    return centred * lax.rsqrt(variance + 1e-06) * gain_row + shift_row


def gelu_exact(values):
    return jax.nn.gelu(values, approximate=False)


def block_mask(chosen_blocks, segment_rows):
    nblocks = chosen_blocks.shape[2]
    block_index = jnp.arange(nblocks)
    near_blocks = jnp.abs(block_index[:, None] - block_index[None, :]) <= 1
    edge_blocks = (
        (block_index[None, :] == 0)
        | (block_index[None, :] == nblocks - 1)
        | (block_index[:, None] == 0)
        | (block_index[:, None] == nblocks - 1)
    )
    picked_blocks = jnp.any(chosen_blocks[..., None] == block_index, axis=3)
    allowed = near_blocks | edge_blocks | picked_blocks
    block_rows = segment_rows.shape[1] // nblocks
    allowed = jnp.repeat(jnp.repeat(allowed, block_rows, axis=2), block_rows, axis=3)
    same_doc = segment_rows[:, :, None] == segment_rows[:, None, :]
    return allowed & same_doc[:, None]


def masked_scores(queries, key_rows, allowed, score_scale):
    scores = (
        jnp.einsum("qshd,kshd->shqk", queries, key_rows, preferred_element_type=jnp.float32)
        * score_scale
    )
    return jnp.where(allowed, scores, -1e30)


def shards(
    block_input,
    segment_ids,
    random_blocks,
    w_qkv,
    b_qv,
    w_out,
    b_out,
    w_in,
    b_in,
    w_down,
    b_down,
    ln_gain,
    ln_bias,
    cotangent,
):
    score_scale = HEAD_DIM ** (-0.5)
    shard_rows, seq_count, model_width = block_input.shape
    layers = w_qkv.shape[0]
    local_width = w_qkv.shape[3]
    local_heads = local_width // HEAD_DIM
    allowed = block_mask(random_blocks, segment_ids)
    saved_acts = []
    stream = block_input
    for layer_index in range(layers):
        w_proj = w_qkv[layer_index].astype(jnp.bfloat16)
        w_mix = w_out[layer_index].astype(jnp.bfloat16)
        rows_low = stream.astype(jnp.bfloat16)
        full_rows = lax.all_gather(rows_low, "tensor", axis=0, tiled=True)
        length = full_rows.shape[0]
        projected = jnp.einsum(
            "lsd,tdc->tlsc", full_rows, w_proj, preferred_element_type=jnp.float32
        )
        qkv_bias = jnp.stack(
            [b_qv[layer_index, 0], jnp.zeros_like(b_qv[layer_index, 0]), b_qv[layer_index, 1]]
        )
        qkv_low = (projected + qkv_bias[:, None, None, :]).astype(jnp.bfloat16)
        head_view = qkv_low.reshape(3, length, seq_count, local_heads, HEAD_DIM)
        scores = masked_scores(head_view[0], head_view[1], allowed, score_scale)
        row_top = jnp.max(scores, axis=-1, keepdims=True)
        log_total = row_top + jnp.log(jnp.sum(jnp.exp(scores - row_top), axis=-1, keepdims=True))
        probs_low = jnp.exp(scores - log_total).astype(jnp.bfloat16)
        context = jnp.einsum(
            "shqk,kshd->qshd", probs_low, head_view[2], preferred_element_type=jnp.float32
        )
        context = context.reshape(length, seq_count, local_width).astype(jnp.bfloat16)
        mixed = lax.psum_scatter(
            jnp.einsum("lsc,cd->lsd", context, w_mix, preferred_element_type=jnp.float32).astype(
                jnp.bfloat16
            ),
            "tensor",
            scatter_dimension=0,
            tiled=True,
        ).astype(jnp.float32)
        first_sum = stream + mixed + b_out[layer_index]
        hidden_rows = norm_rows(first_sum, ln_gain[layer_index, 0], ln_bias[layer_index, 0])
        hidden_low = hidden_rows.astype(jnp.bfloat16)
        up_weight = w_in[layer_index].astype(jnp.bfloat16)
        backward_weight = w_down[layer_index].astype(jnp.bfloat16)
        hidden_full = lax.all_gather(hidden_low, "tensor", axis=0, tiled=True)
        preactivation = (
            jnp.einsum("twn,nj->twj", hidden_full, up_weight, preferred_element_type=jnp.float32)
            + b_in[layer_index]
        )
        activation_reduced = gelu_exact(preactivation).astype(jnp.bfloat16)
        grown = lax.psum_scatter(
            jnp.einsum(
                "unj,jp->unp",
                activation_reduced,
                backward_weight,
                preferred_element_type=jnp.float32,
            ).astype(jnp.bfloat16),
            "tensor",
            scatter_dimension=0,
            tiled=True,
        ).astype(jnp.float32)
        second_sum = hidden_rows + grown + b_down[layer_index]
        stream = norm_rows(second_sum, ln_gain[layer_index, 1], ln_bias[layer_index, 1])
        keep_rows, keep_hidden = (full_rows, hidden_full)
        saved_acts.append(
            (
                keep_rows,
                head_view,
                log_total,
                context,
                first_sum,
                keep_hidden,
                preactivation,
                activation_reduced,
                second_sum,
                up_weight,
                backward_weight,
            )
        )
    upstream = cotangent
    grads_by_layer = [None] * layers
    for layer_index in reversed(range(layers)):
        (
            keep_rows,
            head_view,
            log_total,
            context,
            first_sum,
            keep_hidden,
            preactivation,
            activation_reduced,
            second_sum,
            up_weight,
            backward_weight,
        ) = saved_acts[layer_index]
        full_rows, hidden_full = (keep_rows, keep_hidden)
        length = full_rows.shape[0]
        w_proj = w_qkv[layer_index].astype(jnp.bfloat16)
        w_mix = w_out[layer_index].astype(jnp.bfloat16)
        _, pull_second = jax.vjp(
            norm_rows, second_sum, ln_gain[layer_index, 1], ln_bias[layer_index, 1]
        )
        d_second, d_gain_two, d_shift_two = pull_second(upstream)
        _, pull_gelu = jax.vjp(gelu_exact, preactivation)
        widened_full = lax.all_gather(d_second.astype(jnp.bfloat16), "tensor", axis=0, tiled=True)
        down_gradient = jnp.einsum(
            "uxc,uxw->cw", activation_reduced, widened_full, preferred_element_type=jnp.float32
        )
        activation_gradient = jnp.einsum(
            "mra,xa->mrx", widened_full, backward_weight, preferred_element_type=jnp.float32
        )
        preactivation_gradient_reduced = pull_gelu(activation_gradient)[0].astype(jnp.bfloat16)
        up_gradient = jnp.einsum(
            "kmx,kmt->xt",
            hidden_full,
            preactivation_gradient_reduced,
            preferred_element_type=jnp.float32,
        )
        g_up_bias = jnp.sum(preactivation_gradient_reduced.astype(jnp.float32), axis=(0, 1))
        d_hidden = d_second + lax.psum_scatter(
            jnp.einsum(
                "hmp,tp->hmt",
                preactivation_gradient_reduced,
                up_weight,
                preferred_element_type=jnp.float32,
            ).astype(jnp.bfloat16),
            "tensor",
            scatter_dimension=0,
            tiled=True,
        ).astype(jnp.float32)
        _, pull_first = jax.vjp(
            norm_rows, first_sum, ln_gain[layer_index, 0], ln_bias[layer_index, 0]
        )
        d_first, d_gain_one, d_shift_one = pull_first(d_hidden)
        full_mixed = lax.all_gather(d_first.astype(jnp.bfloat16), "tensor", axis=0, tiled=True)
        g_out = jnp.einsum("lsc,lsd->cd", context, full_mixed, preferred_element_type=jnp.float32)
        d_context = jnp.einsum(
            "lsd,cd->lsc", full_mixed, w_mix, preferred_element_type=jnp.float32
        ).astype(jnp.bfloat16)
        d_context = d_context.reshape(length, seq_count, local_heads, HEAD_DIM)
        queries, key_rows, value_rows = (head_view[0], head_view[1], head_view[2])
        scores = masked_scores(queries, key_rows, allowed, score_scale)
        attn_probs = jnp.exp(scores - log_total)
        probs_low = attn_probs.astype(jnp.bfloat16)
        d_probs = jnp.einsum(
            "qshd,kshd->shqk", d_context, value_rows, preferred_element_type=jnp.float32
        )
        d_scores = attn_probs * (d_probs - jnp.sum(d_probs * attn_probs, axis=-1, keepdims=True))
        d_scores = d_scores.astype(jnp.bfloat16)
        d_query = (
            jnp.einsum("shqk,kshd->qshd", d_scores, key_rows, preferred_element_type=jnp.float32)
            * score_scale
        )
        d_key = (
            jnp.einsum("shqk,qshd->kshd", d_scores, queries, preferred_element_type=jnp.float32)
            * score_scale
        )
        d_value = jnp.einsum(
            "shqk,qshd->kshd", probs_low, d_context, preferred_element_type=jnp.float32
        )
        d_qkv = (
            jnp.stack([d_query, d_key, d_value])
            .reshape(3, length, seq_count, local_width)
            .astype(jnp.bfloat16)
        )
        g_proj = jnp.einsum("lsd,tlsc->tdc", full_rows, d_qkv, preferred_element_type=jnp.float32)
        qkv_sums = jnp.sum(d_qkv.astype(jnp.float32), axis=(1, 2))
        g_bias = jnp.stack([qkv_sums[0], qkv_sums[2]])
        upstream = d_first + lax.psum_scatter(
            jnp.einsum("tlsc,tdc->lsd", d_qkv, w_proj, preferred_element_type=jnp.float32).astype(
                jnp.bfloat16
            ),
            "tensor",
            scatter_dimension=0,
            tiled=True,
        ).astype(jnp.float32)
        weight_grads = (g_proj, g_bias, g_out, up_gradient, g_up_bias, down_gradient)
        small_grads = (
            jnp.sum(d_first, axis=(0, 1)),
            jnp.sum(d_second, axis=(0, 1)),
            jnp.stack([d_gain_one, d_gain_two]),
            jnp.stack([d_shift_one, d_shift_two]),
        )
        grads_by_layer[layer_index] = (weight_grads, small_grads)
    weight_stack = tuple(
        (
            jnp.stack([grads_by_layer[layer_index][0][member] for layer_index in range(layers)])
            for member in range(6)
        )
    )
    small_stack = tuple(
        (
            jnp.stack([grads_by_layer[layer_index][1][member] for layer_index in range(layers)])
            for member in range(4)
        )
    )
    weight_stack = jax.tree.map(
        lambda part: part.astype(jnp.float32), lax.psum(as_sent(weight_stack), "dp")
    )
    small_stack = lax.psum(small_stack, ("dp", "tensor"))
    return (
        stream,
        upstream,
        weight_stack[0],
        weight_stack[1],
        weight_stack[2],
        small_stack[0],
        weight_stack[3],
        weight_stack[4],
        weight_stack[5],
        small_stack[1],
        small_stack[2],
        small_stack[3],
    )


def solution(mesh):
    by_sequence = mesh.shape["tensor"] == 2 and mesh.shape["dp"] == 16
    return jax.shard_map(
        sequence_shards if by_sequence else shards,
        mesh=mesh,
        in_specs=(
            P("tensor", "dp", None),
            P("dp", None),
            P("dp", "tensor", None, None),
            P(None, None, None, "tensor"),
            P(None, None, "tensor"),
            P(None, "tensor", None),
            P(),
            P(None, None, "tensor"),
            P(None, "tensor"),
            P(None, "tensor", None),
            P(),
            P(),
            P(),
            P("tensor", "dp", None),
        ),
        out_specs=(
            P("tensor", "dp", None),
            P("tensor", "dp", None),
            P(None, None, None, "tensor"),
            P(None, None, "tensor"),
            P(None, "tensor", None),
            P(),
            P(None, None, "tensor"),
            P(None, "tensor"),
            P(None, "tensor", None),
            P(),
            P(),
            P(),
        ),
        check_vma=False,
    )
```

```python
import functools

import jax
import jax.numpy as jnp
from jax import lax
from jax.experimental import pallas as pl
from jax.experimental.pallas import tpu as pltpu
from jax.sharding import PartitionSpec as P

HEAD_DIM = 64
BIG = -1e30
BF16 = jnp.bfloat16
F32 = jnp.float32
MESH = pl.DeviceIdType.MESH
VMEM_LIMIT = 56 << 20

FLIP_Y, FLIP_C, FLIP_X, FLIP_Z0, FLIP_Z1 = 1, 2, 4, 8, 16
SWAP = FLIP_Y + FLIP_C
DEVICES = 32

GROUPS = 12
OUT_GROUP = 3
FF_GROUPS = 4


def in_group(s):
    return 4 + 2 * s


def down_group(s):
    return 5 + 2 * s


def flip(values, bit):
    pairs = [(i, i ^ bit) for i in range(DEVICES)]
    return jax.tree.map(lambda v: lax.ppermute(v, ("dp", "tensor"), pairs), values)


def nt(a, b):
    return lax.dot_general(a, b, (((1,), (1,)), ((), ())), preferred_element_type=F32)


def nn(a, b):
    return lax.dot_general(a, b, (((1,), (0,)), ((), ())), preferred_element_type=F32)


def tn(a, b):
    return lax.dot_general(a, b, (((0,), (0,)), ((), ())), preferred_element_type=F32)


def block_of(ref):
    width = ref.shape[-1]
    return ref[...].reshape(-1, width)


def place_kernel(turned, code_ref, g_ref, o_ref, *scratch):
    code = code_ref[0]
    for j in range(16):
        start = pl.multiple_of((j ^ code) * 32, 32)
        block = g_ref[0, pl.ds(start, 32), :].astype(F32)
        if turned:
            scratch[0][j * 32 : (j + 1) * 32, :] = block
        else:
            o_ref[0, j * 32 : (j + 1) * 32, :] = block
    if turned:
        o_ref[...] = scratch[0][...].T.reshape(o_ref.shape)


def place(sums, shape, block, index, turned, count, group, code):
    width = sums.shape[-1]
    return pl.pallas_call(
        functools.partial(place_kernel, turned),
        out_shape=jax.ShapeDtypeStruct(shape, F32),
        grid_spec=pltpu.PrefetchScalarGridSpec(
            num_scalar_prefetch=1,
            grid=(shape[0], count),
            in_specs=[pl.BlockSpec((1, 512, width), lambda l, i, code: (group(l, i), 0, 0))],
            out_specs=pl.BlockSpec(block, lambda l, i, code: index(l, i)),
            scratch_shapes=[pltpu.VMEM((512, width), F32)] if turned else [],
        ),
        compiler_params=pltpu.CompilerParams(vmem_limit_bytes=VMEM_LIMIT),
        cost_estimate=pl.CostEstimate(
            flops=0, bytes_accessed=shape[0] * count * 512 * width * 6, transcendentals=0
        ),
        name="place",
    )(code, sums)


def widen_kernel(a_ref, b_ref, a_out, b_out, a_buf, b_buf, sem):
    copies = []
    for n, (source, target, buf) in enumerate(((a_ref, a_out, a_buf), (b_ref, b_out, b_buf))):
        buf[...] = source[...].astype(F32)
        copies.append(pltpu.make_async_copy(buf, target.at[:, 0], sem.at[n]))
        copies[-1].start()
    for copy in copies:
        copy.wait()


def widen_rows(a, b):
    rows, width = a.shape
    out = jax.ShapeDtypeStruct((rows, 1, width), F32)
    return pl.pallas_call(
        widen_kernel,
        out_shape=(out, out),
        in_specs=[pl.BlockSpec(memory_space=pltpu.VMEM)] * 2,
        out_specs=(pl.BlockSpec(memory_space=pl.ANY),) * 2,
        scratch_shapes=[pltpu.VMEM((rows, width), F32), pltpu.VMEM((rows, width), F32), pltpu.SemaphoreType.DMA((2,))],
        name="widen_rows",
    )(a, b)


def hand_out_kernel(layers, y_ref, packed, out, down, gain, shift, qv, hidden):
    y = y_ref[0]
    width = packed.shape[1]
    out[...] = packed[0:layers, :]
    down[...] = packed[layers : 2 * layers, :]
    for l in range(layers):
        for n in range(2):
            row = 2 * layers + 2 * l + n
            gain[l, n : n + 1, :] = packed[row : row + 1, :]
            row += 2 * layers
            shift[l, n : n + 1, :] = packed[row : row + 1, :]
            at = 8 * layers + 2 * l + n
            hidden[l : l + 1, n * width : (n + 1) * width] = jnp.where(
                y == 0, packed[at : at + 1, :], packed[at + 2 * layers : at + 2 * layers + 1, :]
            )
            half = slice(n * width // 2, (n + 1) * width // 2)
            at = 6 * layers + l
            qv[l, n : n + 1, :] = jnp.where(
                y == 0, packed[at : at + 1, half], packed[at + layers : at + layers + 1, half]
            )


def hand_out(packed, y, layers):
    width = packed.shape[1]
    full = lambda *shape: jax.ShapeDtypeStruct(shape, F32)
    in_vmem = pl.BlockSpec(memory_space=pltpu.VMEM)
    return pl.pallas_call(
        functools.partial(hand_out_kernel, layers),
        out_shape=(
            full(layers, width),
            full(layers, width),
            full(layers, 2, width),
            full(layers, 2, width),
            full(layers, 2, width // 2),
            full(layers, 2 * width),
        ),
        in_specs=[pl.BlockSpec(memory_space=pltpu.SMEM), in_vmem],
        out_specs=(in_vmem,) * 6,
        name="hand_out",
    )(y, packed)


def partner(bits):
    dp, y = lax.axis_index("dp"), lax.axis_index("tensor")
    other = dp
    for step in (1, 2, 4, 8):
        if bits & (2 * step):
            other = other + step * (1 - 2 * ((dp // step) % 2))
    return (other, 1 - y if bits & FLIP_Y else y)


def all_partners(bits):
    return {bit: partner(bit) for bit in bits}


def greet(partners):
    barrier = pltpu.get_barrier_semaphore()
    for other in partners.values():
        pl.semaphore_signal(barrier, inc=1, device_id=other, device_id_type=MESH)
    pl.semaphore_wait(barrier, len(partners))


def add_into(into, other, count):
    def step(i, _):
        into[i] = (into[i].astype(F32) + other[i].astype(F32)).astype(BF16)
        return 0

    lax.fori_loop(0, count, step, 0)


def add_rows(into, other, rows):
    def step(i, _):
        at = pl.ds(pl.multiple_of(i * 32, 32), 32)
        into[at, :] = (into[at, :].astype(F32) + other[at, :].astype(F32)).astype(BF16)
        return 0

    lax.fori_loop(0, rows // 32, step, 0)


def add_into(into, other, count):
    def step(i, _):
        into[i] = (into[i].astype(F32) + other[i].astype(F32)).astype(BF16)
        return 0

    lax.fori_loop(0, count, step, 0)


SLOTS = 6
PARTED = 2
PARTS = 2
LAST_TICK = 8


class Reduction:
    def __init__(self, grads, sums, first, groups, parts, partners, bufs, sems):
        self.grads, self.sums, self.first, self.parts, self.partners = grads, sums, first, parts, partners
        self.count = groups * parts
        self.y_buf, self.x_buf, self.z0_buf, self.z1_buf, self.all_buf, self.keep_buf = bufs
        self.slots = self.y_buf.shape[0]
        self.send_sem, self.recv_sem, self.core_send, self.core_recv, self.keep_sem, self.out_sem = sems[:6]
        self.in_free, self.out_free = sems[6:] if len(sems) > 6 else (None, None)

    def blocks(self, ref, i, at):
        if self.parts == 1:
            return ref.at[self.first + i, pl.ds(at, 8)]
        size = 32 // self.parts
        part = pl.ds(pl.multiple_of(lax.rem(i, self.parts) * size, size), size)
        return ref.at[self.first + lax.div(i, self.parts), pl.ds(at, 8), part]

    def copy(self, step, i):
        slot = lax.rem(i, self.slots)
        ys, al = self.y_buf.at[slot], self.all_buf.at[slot]
        bit, source, target = (
            (FLIP_Y, self.blocks(self.grads, i, 8), ys),
            (FLIP_X, ys.at[pl.ds(4, 4)], self.x_buf.at[slot]),
            (FLIP_Z0, ys.at[pl.ds(2, 2)], self.z0_buf.at[slot]),
            (FLIP_Z1, ys.at[pl.ds(1, 1)], self.z1_buf.at[slot]),
            (FLIP_Z1, al.at[pl.ds(0, 1)], al.at[pl.ds(1, 1)]),
            (FLIP_Z0, al.at[pl.ds(0, 2)], al.at[pl.ds(2, 2)]),
            (FLIP_X, al.at[pl.ds(0, 4)], al.at[pl.ds(4, 4)]),
            (FLIP_C, al, self.blocks(self.sums, i, 8)),
        )[step]
        return pltpu.make_async_remote_copy(
            src_ref=source,
            dst_ref=target,
            send_sem=self.send_sem.at[step, slot] if step < 7 else self.core_send.at[i],
            recv_sem=self.recv_sem.at[step, slot] if step < 7 else self.core_recv.at[i],
            device_id=self.partners[bit],
            device_id_type=MESH,
        )

    def keep(self, i):
        slot = lax.rem(i, 2)
        return pltpu.make_async_copy(
            self.blocks(self.grads, i, 0), self.keep_buf.at[slot], self.keep_sem.at[slot]
        )

    def out(self, i):
        slot = lax.rem(i, self.slots)
        return pltpu.make_async_copy(
            self.all_buf.at[slot], self.blocks(self.sums, i, 0), self.out_sem.at[slot]
        )

    def take(self, sems, n, i):
        if sems is not None:
            pl.when(i >= self.slots)(lambda: pl.semaphore_wait(sems.at[n], 1))

    def give(self, sems, n, bit, i):
        if sems is not None:
            pl.when(i + self.slots < self.count)(
                lambda: pl.semaphore_signal(
                    sems.at[n], inc=1, device_id=self.partners[bit], device_id_type=MESH
                )
            )

    def tick(self, t):
        def at(offset, body):
            i = t - offset
            pl.when((i >= 0) & (i < self.count))(lambda: body(i, lax.rem(i, self.slots)))

        def set_out(i, slot):
            self.take(self.in_free, 0, i)
            self.copy(0, i).start()
            self.keep(i).start()

        def finish(i, slot):
            self.copy(7, i).wait()
            self.out(i).wait()
            for n, bit in enumerate((FLIP_X, FLIP_Z0, FLIP_Z1)):
                self.give(self.out_free, n, bit, i)

        def to_core(i, slot):
            self.copy(6, i).wait()
            self.copy(7, i).start()
            self.out(i).start()

        def back_x(i, slot):
            self.copy(5, i).wait()
            self.take(self.out_free, 0, i)
            self.copy(6, i).start()

        def back_z0(i, slot):
            self.copy(4, i).wait()
            self.take(self.out_free, 1, i)
            self.copy(5, i).start()

        def back_z1(i, slot):
            self.copy(3, i).wait()
            add_into(self.y_buf.at[slot], self.z1_buf.at[slot], 1)
            self.all_buf[slot, 0] = self.y_buf[slot, 0]
            for n, bit in enumerate((FLIP_Y, FLIP_X, FLIP_Z0, FLIP_Z1)):
                self.give(self.in_free, n, bit, i)
            self.take(self.out_free, 2, i)
            self.copy(4, i).start()

        def on_z1(i, slot):
            self.copy(2, i).wait()
            add_into(self.y_buf.at[slot], self.z0_buf.at[slot], 2)
            self.take(self.in_free, 3, i)
            self.copy(3, i).start()

        def on_z0(i, slot):
            self.copy(1, i).wait()
            add_into(self.y_buf.at[slot], self.x_buf.at[slot], 4)
            self.take(self.in_free, 2, i)
            self.copy(2, i).start()

        def on_x(i, slot):
            self.copy(0, i).wait()
            self.keep(i).wait()
            add_into(self.y_buf.at[slot], self.keep_buf.at[lax.rem(i, 2)], 8)
            self.take(self.in_free, 1, i)
            self.copy(1, i).start()

        at(0, set_out)
        at(8, finish)
        at(7, to_core)
        at(6, back_x)
        at(5, back_z0)
        at(4, back_z1)
        at(3, on_z1)
        at(2, on_z0)
        at(1, on_x)


def unit_order(y, core_free_bits):
    taken = lax.broadcasted_iota(jnp.int32, (512, 512), 0)
    column = lax.broadcasted_iota(jnp.int32, (512, 512), 1)
    where = lax.rem(column, 32)
    for own, weight in zip((y,) + core_free_bits, (256, 128, 64, 32)):
        bit = lax.rem(lax.div(column, weight), 2)
        where = where + weight * (bit + own - 2 * own * bit)
    return (taken == where).astype(F32)


def begin(feeds):
    for copy in feeds(0, 0):
        copy.start()


def stream(count, feeds, body):
    def step(i, _):
        slot = lax.rem(i, 2)

        @pl.when(i + 1 < count)
        def _():
            for copy in feeds(i + 1, 1 - slot):
                copy.start()

        for copy in feeds(i, slot):
            copy.wait()
        body(i, slot)
        return 0

    lax.fori_loop(0, count, step, 0)


def norm(r, gain, shift):
    centred = r - jnp.mean(r, axis=-1, keepdims=True)
    rstd = lax.rsqrt(jnp.mean(centred * centred, axis=-1, keepdims=True) + 1e-06)
    return centred * rstd * gain + shift


def norm_back(dy, r, gain):
    centred = r - jnp.mean(r, axis=-1, keepdims=True)
    rstd = lax.rsqrt(jnp.mean(centred * centred, axis=-1, keepdims=True) + 1e-06)
    unit = centred * rstd
    dunit = dy * gain
    dr = rstd * (
        dunit
        - jnp.mean(dunit, axis=-1, keepdims=True)
        - unit * jnp.mean(dunit * unit, axis=-1, keepdims=True)
    )
    return dr, dy * unit


def gelu_and_slope(u):
    cdf = 0.5 * (1.0 + lax.erf(u * (0.5**0.5)))
    pdf = jnp.exp(-0.5 * u * u) * 0.3989422804014327
    return u * cdf, cdf + u * pdf


TILE = 64


def row_tiles(rows, body):
    def step(i, _):
        body(pl.ds(pl.multiple_of(i * TILE, TILE), TILE))
        return 0

    lax.fori_loop(0, rows // TILE, step, 0)


def pair_lanes(values, e):
    lane = lax.broadcasted_iota(jnp.int32, values.shape, 1)
    return jnp.where(lane // HEAD_DIM == e, values, jnp.zeros_like(values))


def spread_mask(block_part, document_part):
    blocks, lanes = block_part.shape
    each = document_part.shape[0] // blocks
    part = jnp.broadcast_to(block_part[:, None, :], (blocks, each, lanes)).reshape(blocks * each, lanes)
    return (part + document_part).astype(BF16)


def both_heads(values):
    return jnp.concatenate([pair_lanes(values, 0), pair_lanes(values, 1)], axis=0)


def attend_pair(query, keys, values, hot, mask):
    scale = HEAD_DIM**-0.5
    rows = query.shape[0]
    query = query * jnp.asarray(scale, BF16)
    right = jnp.concatenate([both_heads(query), both_heads(hot)], axis=1)
    s = nt(jnp.concatenate([keys, mask], axis=1), right)
    top = jnp.max(s, axis=0, keepdims=True)
    p = jnp.exp(s - top)
    total = jnp.sum(p, axis=0, keepdims=True)
    c = nn(values.T, p.astype(BF16)) * (1.0 / total)
    context = jnp.concatenate([c[:HEAD_DIM, :rows], c[HEAD_DIM:, rows:]], axis=0).T
    lse = top + jnp.log(total)
    return context, [lse[:, :rows], lse[:, rows:]]


def attend_back_pair(query, keys, values, hot, mask, ctx, lse, dctx):
    scale = HEAD_DIM**-0.5
    rows = query.shape[0]
    query = query * jnp.asarray(scale, BF16)
    keys_t = keys.T
    delta_t = (dctx.astype(F32) * ctx.astype(F32)).T
    left = jnp.concatenate([keys, mask], axis=1)
    tile = rows // 2
    dk, dv, dq = 0.0, 0.0, []
    for part in range(2):
        at = slice(part * tile, (part + 1) * tile)
        heads = []
        for e in range(2):
            lanes = slice(e * HEAD_DIM, (e + 1) * HEAD_DIM)
            query_e = pair_lanes(query[at], e)
            dctx_e = pair_lanes(dctx[at], e)
            right = jnp.concatenate([query_e, pair_lanes(hot[at], e)], axis=1)
            p = jnp.exp(nt(left, right) - lse[e : e + 1, at])
            dp = nt(values, dctx_e)
            delta = jnp.sum(delta_t[lanes, at], axis=0, keepdims=True)
            ds = (p * (dp - delta)).astype(BF16)
            dk = dk + nn(ds, query_e)
            dv = dv + nn(p.astype(BF16), dctx_e)
            heads.append(nn(keys_t[lanes, :], ds) * scale)
        dq.append(jnp.concatenate(heads, axis=0).T)
    return jnp.concatenate(dq, axis=0), dk, dv


class Spread:
    def __init__(self, weights, pairs, partners, send_sem, recv_sem):
        self.weights, self.pairs, self.partners = weights, pairs, partners
        self.send_sem, self.recv_sem = send_sem, recv_sem

    def copy(self, step, t):
        w = self.weights
        even, odd = 2 * t, 2 * t + 1
        bit, source, target = (
            (FLIP_Y, w.at[0, even, 0, pl.ds(0, 64)], w.at[0, even, 1, pl.ds(0, 64)]),
            (FLIP_Y, w.at[0, odd, 0, pl.ds(0, 64)], w.at[0, odd, 1, pl.ds(0, 64)]),
            (FLIP_X, w.at[0, even, 1, pl.ds(0, 64)], w.at[0, even, 1, pl.ds(128, 64)]),
            (FLIP_Z0, w.at[0, odd, 1, pl.ds(0, 64)], w.at[0, odd, 1, pl.ds(64, 64)]),
            (FLIP_Z0, w.at[0, even, 1, pl.ds(0, 64)], w.at[0, even, 1, pl.ds(64, 64)]),
            (FLIP_Z0, w.at[0, even, 1, pl.ds(128, 64)], w.at[0, even, 1, pl.ds(192, 64)]),
            (FLIP_X, w.at[0, odd, 1, pl.ds(0, 128)], w.at[0, odd, 1, pl.ds(128, 128)]),
            (FLIP_C, w.at[0, even, 1], w.at[1, even, 1]),
            (FLIP_C, w.at[0, odd, 1], w.at[1, odd, 1]),
        )[step]
        return pltpu.make_async_remote_copy(
            src_ref=source,
            dst_ref=target,
            send_sem=self.send_sem.at[step, t],
            recv_sem=self.recv_sem.at[step, t],
            device_id=self.partners[bit],
            device_id_type=MESH,
        )

    def tick(self, t):
        def at(offset, waits, starts):
            i = t - offset

            @pl.when((i >= 0) & (i < self.pairs))
            def _():
                for step in waits:
                    self.copy(step, i).wait()
                for step in starts:
                    self.copy(step, i).start()

        at(0, (), (0, 1))
        at(5, (7, 8), ())
        at(1, (0, 1), (2, 3))
        at(2, (2, 3), (4, 5, 6))
        at(4, (4, 5, 6), (7, 8))


PER_LAYER = 14
DEPTH = 3


def forward_kernel(layers, *refs):
    refs = list(refs)
    x_ref, up_ref, wq_ref, wo_ref, wi_ref, wd_ref = refs[:6]
    hot_buf, mask_ref, key_ref, bq_ref, bi_ref, vec_ref = refs[6:12]
    w_ref, up_out, x_out = refs[12:15]
    saved = [refs[15 + PER_LAYER * l : 15 + PER_LAYER * (l + 1)] for l in range(layers)]
    (
        x, acc, r_buf, low, xb, qkv, kv_sib, ctx, lse, hl, g_all, slope_all,
        col_buf, row_buf, turn_buf, made_buf, wa_buf, wb_buf,
        feed_sem, load_sem, col_sem, row_sem, made_sem, store_sem, block_sem,
        core_send, core_recv, kv_send, kv_recv, g_send, g_recv, spread_send, spread_recv,
    ) = refs[15 + PER_LAYER * layers :]
    rows, width = acc.shape
    dp, y = lax.axis_index("dp"), lax.axis_index("tensor")
    core = dp % 2
    stays = core == y
    partners = all_partners((FLIP_Y, FLIP_X, FLIP_Z0, FLIP_C, SWAP))
    spread = Spread(w_ref, layers * GROUPS // 2, partners, spread_send, spread_recv)
    greet(partners)

    def feed(n, slot, source, target):
        return pltpu.make_async_copy(source, target, feed_sem.at[n, slot])

    def load(n, source, target):
        return pltpu.make_async_copy(source, target, load_sem.at[n])

    def store(n, source, target):
        return pltpu.make_async_copy(source, target, store_sem.at[n])

    def exchange(n, source, target, bits=FLIP_C):
        return pltpu.make_async_remote_copy(
            src_ref=source, dst_ref=target, send_sem=core_send.at[n], recv_sem=core_recv.at[n],
            device_id=partners[bits], device_id_type=MESH,
        )

    def columns(ref, i, size):
        return ref.at[:, pl.ds(pl.multiple_of(i * size, size), size)]

    def swap(n, source, target, begin):
        here = store(n, source, target)
        there = exchange(n, source, target, SWAP)

        @pl.when(stays)
        def _():
            here.start() if begin else here.wait()

        @pl.when(jnp.logical_not(stays))
        def _():
            there.start() if begin else there.wait()

    items = []
    for l in range(layers):
        items += [(True, wq_ref.at[l, (t + 1) % 3], l * GROUPS + t) for t in range(3)]
        items += [(False, wo_ref.at[l], l * GROUPS + OUT_GROUP)]
        for n in range(FF_GROUPS):
            items += [(True, wi_ref.at[l, :, pl.ds(n * 512, 512)], l * GROUPS + in_group(n))]
            items += [(False, wd_ref.at[l, pl.ds(n * 512, 512)], l * GROUPS + down_group(n))]
    fetches, counts, ahead = [], [0, 0], [[], []]
    for m, (turned, source, group) in enumerate(items):
        slot = counts[turned] % DEPTH
        buf, sem = (col_buf, col_sem) if turned else (row_buf, row_sem)
        fetches.append((pltpu.make_async_copy(source, buf.at[slot], sem.at[slot]), slot))
        ahead[turned].append(m)
        counts[turned] += 1
    bits = [(dp // step) % 2 for step in (1, 2, 4, 8)]
    made = {}

    def convert(m):
        turned, _, group = items[m]
        copy, slot = fetches[m]
        copy.wait()
        if turned:

            def turn(i, _):
                strip = col_buf[slot, :, pl.ds(pl.multiple_of(i * 128, 128), 128)]
                turn_buf[pl.ds(pl.multiple_of(i * 128, 128), 128), :] = strip.astype(BF16).T
                return 0

            lax.fori_loop(0, 4, turn, 0)
        if m >= 2:
            made[m - 2].wait()

        def block(j, _):
            where = 0
            for bit, weight in zip(bits, (8, 4, 2, 1)):
                own = (j // weight) % 2
                where = where + weight * (own + bit - 2 * own * bit)
            at = pl.ds(pl.multiple_of(where * 32, 32), 32)
            rows_32 = turn_buf[at, :] if turned else row_buf[slot, at, :]
            made_buf[m % 2, pl.ds(pl.multiple_of(j * 32, 32), 32), :] = rows_32.astype(BF16)
            return 0

        lax.fori_loop(0, 16, block, 0)
        later = [n for n in ahead[turned] if n > m]
        if len(later) >= DEPTH:
            fetches[later[DEPTH - 1]][0].start()
        parts = [
            pltpu.make_async_copy(
                made_buf.at[m % 2, pl.ds(a * 256, 256)], w_ref.at[a, group, 0], made_sem.at[m % 2, a]
            )
            for a in range(2)
        ]

        class Both:
            def wait(self):
                for part in parts:
                    part.wait()

        for part in parts:
            part.start()
        made[m] = Both()

    load_x = load(0, x_ref.at[:, 0], x)
    load_x.start()
    for kind in range(2):
        for m in ahead[kind][:DEPTH]:
            fetches[m][0].start()
    load_x.wait()

    def narrow_x(at):
        low[at, :] = x[at, :].astype(BF16)

    row_tiles(rows, narrow_x)
    swap(0, low, xb, True)
    for m in range(len(items)):
        convert(m)
        if m % 4 == 3:
            spread.tick(m // 4)
    for m in range(len(items) - 2, len(items)):
        made[m].wait()
    swap(0, low, xb, False)
    load_up = load(1, up_ref.at[:, 0], row_buf.at[0])
    load_up.start()

    def widen(at):
        x[at, :] = xb[at, :].astype(F32)

    row_tiles(rows, widen)

    pairs = width // 128
    for l in range(layers):
        (
            qkv_out, sib_out, ctx_out, ctx_sib_out, lse_out, r1_out, r2_out, hl_out, hl_sib_out,
            g_out, g_sib_out, slope_out, xb_out, xb_sib_out,
        ) = saved[l]
        first = l * GROUPS
        clock = 6 + 6 * l
        xb_store = store(0, xb, xb_out)
        xb_store.start()
        xb_copy = exchange(2 + 3 * l, xb, xb_sib_out)
        xb_copy.start()

        def give_kv(n, a):
            at = pl.ds(pl.multiple_of(a * 512, 512), 512)
            return pltpu.make_async_remote_copy(
                src_ref=qkv.at[1 + n, :, at], dst_ref=kv_sib.at[n, :, at],
                send_sem=kv_send.at[n, a], recv_sem=kv_recv.at[n, a],
                device_id=partners[FLIP_C], device_id_type=MESH,
            )

        def which(i):
            n = lax.div(i, 2)
            return lax.rem(n + 1, 3), n, lax.rem(i, 2)

        def qkv_feeds(i, slot):
            _, n, a = which(i)
            return (feed(0, slot, w_ref.at[a, first + n], wa_buf.at[slot]),)

        def qkv_body(i, slot):
            t, _, a = which(i)
            at = pl.ds(pl.multiple_of(a * 512, 512), 512)
            qkv[t, :, at] = (nt(xb[...], block_of(wa_buf.at[slot])) + bq_ref[l, t, a]).astype(BF16)
            pl.when(t > 0)(lambda: give_kv(t - 1, a).start())
            pl.when(i == 2)(lambda: spread.tick(clock))

        if l == 0:
            begin(qkv_feeds)
        stream(6, qkv_feeds, qkv_body)
        qkv_store = store(1, qkv, qkv_out)
        qkv_store.start()
        for n in range(2):
            for a in range(2):
                give_kv(n, a).wait()
        sib_store = store(2, kv_sib, sib_out)
        sib_store.start()

        feed(2, 0, w_ref.at[0, first + OUT_GROUP], wb_buf.at[0]).start()

        def pair_body(p, _):
            far = lax.rem(p + pairs // 2, pairs)
            here = pl.ds(pl.multiple_of(p * 128, 128), 128)
            there = pl.ds(pl.multiple_of(far * 128, 128), 128)
            mask = spread_mask(mask_ref[p], key_ref[...])
            keys = jnp.concatenate([qkv[1, :, here], kv_sib[0, :, there]], axis=0)
            values = jnp.concatenate([qkv[2, :, here], kv_sib[1, :, there]], axis=0)
            context, parts = attend_pair(qkv[0, :, here], keys, values, hot_buf[...], mask)
            ctx[:, here] = context.astype(BF16)
            for e in range(2):
                lse[p, e : e + 1, :] = parts[e]
            pl.when(lax.rem(p, 5) == 2)(lambda: spread.tick(clock + 1 + lax.div(p, 5)))
            return 0

        lax.fori_loop(0, pairs, pair_body, 0)
        ctx_store = store(3, ctx, ctx_out)
        ctx_store.start()
        lse_store = store(4, lse, lse_out)
        lse_store.start()
        ctx_copy = exchange(3 + 3 * l, ctx.at[:, pl.ds(512, 512)], ctx_sib_out)
        ctx_copy.start()

        def place_of(i):
            return 1 - lax.rem(i, 2), lax.div(i, 2)

        def ff_feeds(i, slot):
            a, n = place_of(i)
            return (
                feed(0, slot, w_ref.at[a, first + in_group(n)], wa_buf.at[slot]),
                feed(2, slot, w_ref.at[a, first + down_group(n)], wb_buf.at[slot]),
            )

        ff_feeds(0, 0)[0].start()

        def out_feeds(i, slot):
            return (feed(2, slot, w_ref.at[i, first + OUT_GROUP], wb_buf.at[slot]),)

        def out_body(i, slot):
            part = nn(ctx[:, pl.ds(pl.multiple_of(i * 512, 512), 512)], block_of(wb_buf.at[slot]))

            @pl.when(i == 0)
            def _():
                acc[...] = part

            @pl.when(i == 1)
            def _():
                acc[...] += part

        stream(2, out_feeds, out_body)
        ff_feeds(0, 0)[1].start()
        sib_store.wait()

        def first_norm(at):
            r1 = x[at, :] + acc[at, :] + vec_ref[l, 0:1, :]
            r_buf[at, :] = r1
            h = norm(r1, vec_ref[l, 1:2, :], vec_ref[l, 2:3, :])
            hl[at, :] = h.astype(BF16)
            acc[at, :] = h + vec_ref[l, 3:4, :]

        row_tiles(rows, first_norm)
        r1_store = store(5, r_buf, r1_out)
        r1_store.start()
        hl_store = store(6, hl, hl_out)
        hl_store.start()
        hl_copy = exchange(4 + 3 * l, hl, hl_sib_out)
        hl_copy.start()

        def g_store(j):
            return pltpu.make_async_copy(g_all.at[j], columns(g_out, j, 512), block_sem.at[0, j])

        def slope_store(j):
            return pltpu.make_async_copy(slope_all.at[j], columns(slope_out, j, 512), block_sem.at[1, j])

        def g_copy(n):
            return pltpu.make_async_remote_copy(
                src_ref=g_all.at[FF_GROUPS + n], dst_ref=columns(g_sib_out, n, 512),
                send_sem=g_send.at[l, n], recv_sem=g_recv.at[l, n],
                device_id=partners[FLIP_C], device_id_type=MESH,
            )

        def ff_body(i, slot):
            a, n = place_of(i)
            j = a * FF_GROUPS + n
            u = nt(hl[...], block_of(wa_buf.at[slot])) + bi_ref[l, a, n]
            g, slope = gelu_and_slope(u)
            g = g.astype(BF16)
            g_all[j] = g
            slope_all[j] = slope.astype(BF16)
            g_store(j).start()
            slope_store(j).start()
            pl.when(a == 1)(lambda: g_copy(n).start())
            acc[...] += nn(g, block_of(wb_buf.at[slot]))
            pl.when(lax.rem(i, 3) == 1)(lambda: spread.tick(clock + 3 + lax.div(i, 3)))

        stream(2 * FF_GROUPS, ff_feeds, ff_body)
        r1_store.wait()
        xb_store.wait()
        xb_copy.wait()
        if l + 1 < layers:
            feed(0, 0, w_ref.at[0, first + GROUPS], wa_buf.at[0]).start()
        if l == 0:
            load_up.wait()

            def narrow_up(at):
                low[at, :] = row_buf[0, at, :].astype(BF16)

            row_tiles(rows, narrow_up)
            swap(9, low, up_out, True)

        def second_norm(at):
            r2 = acc[at, :]
            r_buf[at, :] = r2
            x2 = norm(r2, vec_ref[l, 4:5, :], vec_ref[l, 5:6, :])
            x[at, :] = x2
            xb[at, :] = x2.astype(BF16)

        row_tiles(rows, second_norm)
        r2_store = store(5, r_buf, r2_out)
        r2_store.start()
        if l == layers - 1:
            x_store = store(10, xb, x_out)
            x_store.start()

        def settle(j, _):
            g_store(j).wait()
            slope_store(j).wait()
            return 0

        lax.fori_loop(0, 2 * FF_GROUPS, settle, 0)

        def settle_sent(n, _):
            g_copy(n).wait()
            return 0

        lax.fori_loop(0, FF_GROUPS, settle_sent, 0)
        for copy in (qkv_store, ctx_store, lse_store, ctx_copy, hl_store, hl_copy, r2_store):
            copy.wait()
    x_store.wait()
    swap(9, low, up_out, False)


def forward(block_input, cotangent, w_qkv, w_out, w_in, w_down, hot, mask, mask_rows, bias_qkv, bias_in, vectors):
    rows, _, width = block_input.shape
    layers = w_qkv.shape[0]
    total = layers * GROUPS
    anywhere = pl.BlockSpec(memory_space=pl.ANY)
    in_vmem = pl.BlockSpec(memory_space=pltpu.VMEM)
    low = lambda *shape: pltpu.VMEM(shape, BF16)
    full = lambda *shape: pltpu.VMEM(shape, F32)
    dma = lambda *shape: pltpu.SemaphoreType.DMA(shape)
    low_out = lambda *shape: jax.ShapeDtypeStruct(shape, BF16)
    full_out = lambda *shape: jax.ShapeDtypeStruct(shape, F32)
    layer_out = (
        low_out(3, rows, width),
        low_out(2, rows, width),
        low_out(rows, width),
        low_out(rows, width // 2),
        full_out(width // 128, 2, rows),
        full_out(rows, width),
        full_out(rows, width),
        low_out(rows, width),
        low_out(rows, width),
        low_out(rows, 4 * width),
        low_out(rows, 2 * width),
        low_out(rows, 4 * width),
        low_out(rows, width),
        low_out(rows, width),
    )
    outs = pl.pallas_call(
        functools.partial(forward_kernel, layers),
        out_shape=(low_out(2, total, 2, 256, width), low_out(rows, width), low_out(rows, width)) + layer_out * layers,
        in_specs=[anywhere] * 6 + [in_vmem] * 6,
        out_specs=(anywhere,) * (3 + PER_LAYER * layers),
        scratch_shapes=[
            full(rows, width),
            full(rows, width),
            full(rows, width),
            low(rows, width),
            low(rows, width),
            low(3, rows, width),
            low(2, rows, width),
            low(rows, width),
            full(width // 128, 2, rows),
            low(rows, width),
            low(2 * FF_GROUPS, rows, 512),
            low(2 * FF_GROUPS, rows, 512),
            full(DEPTH, width, 512),
            full(DEPTH, 512, width),
            low(512, width),
            low(2, 512, width),
            low(2, 2, 256, width),
            low(2, 2, 256, width),
            dma(3, 2),
            dma(3),
            dma(DEPTH),
            dma(DEPTH),
            dma(2, 2),
            dma(11),
            dma(2, 2 * FF_GROUPS),
            dma(11),
            dma(11),
            dma(2, 2),
            dma(2, 2),
            dma(layers, FF_GROUPS),
            dma(layers, FF_GROUPS),
            dma(9, total // 2),
            dma(9, total // 2),
        ],
        compiler_params=pltpu.CompilerParams(collective_id=0, has_side_effects=True, vmem_limit_bytes=60 << 20),
        cost_estimate=pl.CostEstimate(flops=30 << 30, bytes_accessed=300 << 20, transcendentals=1 << 24),
        name="forward",
    )(block_input, cotangent, w_qkv, w_out, w_in, w_down, hot, mask, mask_rows, bias_qkv, bias_in, vectors)
    saved = [outs[3 + PER_LAYER * l : 3 + PER_LAYER * (l + 1)] for l in range(layers)]
    return outs[0], outs[1], outs[2], saved


def backward_kernel(layers, *refs):
    refs = list(refs)
    up_ref, x_ref, w_ref, hot_buf, mask_ref, key_ref, vec_ref = refs[:7]
    saved = [refs[7 + PER_LAYER * l : 7 + PER_LAYER * (l + 1)] for l in range(layers)]
    at_ref = 7 + PER_LAYER * layers
    grads, sums, dx_out, x_out, packed = refs[at_ref : at_ref + 5]
    (
        acc, dr1, dm, dm_sib, da, da_sib, du, du_sib, dctx, dqkv, d_sib, kv_out, kv_far,
        wa_buf, wb_buf, r_buf, slope_buf, left_buf, left_sib_buf, right_buf, right_sib_buf,
        pair_buf, lse_buf, unit_buf,
        y_buf, x_buf, z0_buf, z1_buf, all_buf, keep_buf,
        feed_sem, load_sem, store_sem, swap_sem, core_send, core_recv, du_send, du_recv, pair_send, pair_recv,
        send_sem, recv_sem, sum_send, sum_recv, keep_sem, out_sem, in_free, out_free,
        dbi_ref, qkv_sums_ref, small_ref, far_buf, far_send, far_recv,
    ) = refs[at_ref + 5 : -12]
    part_bufs, part_sems = refs[-12:-6], refs[-6:]
    rows, width = acc.shape
    total = layers * GROUPS
    partners = all_partners((FLIP_Y, FLIP_X, FLIP_Z0, FLIP_Z1, FLIP_C, SWAP))
    whole = total - PARTED
    reduction = Reduction(
        grads, sums, 0, whole, 1, partners,
        (y_buf, x_buf, z0_buf, z1_buf, all_buf, keep_buf),
        (send_sem, recv_sem, sum_send, sum_recv, keep_sem, out_sem, in_free, out_free),
    )
    ending = Reduction(grads, sums, whole, PARTED, PARTS, partners, part_bufs, part_sems)
    greet(partners)

    def feed(n, slot, source, target):
        return pltpu.make_async_copy(source, target, feed_sem.at[n, slot])

    def load(n, source, target):
        return pltpu.make_async_copy(source, target, load_sem.at[n])

    def exchange(n, source, target):
        return pltpu.make_async_remote_copy(
            src_ref=source, dst_ref=target, send_sem=core_send.at[n], recv_sem=core_recv.at[n],
            device_id=partners[FLIP_C], device_id_type=MESH,
        )

    def give_du(j, n):
        return pltpu.make_async_remote_copy(
            src_ref=du.at[j], dst_ref=du_sib.at[n], send_sem=du_send.at[n], recv_sem=du_recv.at[n],
            device_id=partners[FLIP_C], device_id_type=MESH,
        )

    def weight(a, group):
        return w_ref.at[a, group]

    def columns(ref, i, size):
        return ref.at[:, pl.ds(pl.multiple_of(i * size, size), size)]

    def unit_store(slot, index):
        return pltpu.make_async_copy(unit_buf.at[slot], grads.at[index], store_sem.at[0])

    def unit(left, left_sib, right, right_sib, slot, index, fresh=False):
        made = (tn(left, right) + tn(left_sib, right_sib)).astype(BF16)
        unit_buf[slot] = made.reshape(unit_buf.shape[1:])
        if fresh is not False:
            pl.when(jnp.logical_not(fresh))(lambda: unit_store(slot, index).wait())
        else:
            unit_store(slot, index).wait()
        unit_store(slot, index).start()

    def add_small(l, row, value):
        small_ref[l, row : row + 1, :] += jnp.sum(value, axis=0, keepdims=True)

    stays = lax.axis_index("dp") % 2 == lax.axis_index("tensor")

    def swap(n, source, target, begin):
        here = pltpu.make_async_copy(source, target, swap_sem.at[n])
        there = pltpu.make_async_remote_copy(
            src_ref=source, dst_ref=target, send_sem=core_send.at[4 + n], recv_sem=core_recv.at[4 + n],
            device_id=partners[SWAP], device_id_type=MESH,
        )

        @pl.when(stays)
        def _():
            here.start() if begin else here.wait()

        @pl.when(jnp.logical_not(stays))
        def _():
            there.start() if begin else there.wait()

    load(0, saved[-1][6], r_buf).start()
    start_up = load(1, up_ref, da)
    start_up.start()
    start_up.wait()
    small_ref[...] = jnp.zeros_like(small_ref)

    def widen(at):
        acc[at, :] = da[at, :].astype(F32)

    row_tiles(rows, widen)
    done = 0
    for l in reversed(range(layers)):
        qkv_ref, sib_ref, ctx_ref, ctx_sib_ref, lse_ref, r1_ref, r2_ref, hl_ref, hl_sib_ref, g_ref, g_sib_ref, slope_ref, xb_ref, xb_sib_ref = saved[l]
        first = l * GROUPS
        base = (layers - 1 - l) * GROUPS
        clock = 11 * (layers - 1 - l)

        def down_feeds(i, slot):
            return (
                feed(0, slot, columns(g_ref, i, 512), left_buf.at[slot]),
                feed(1, slot, columns(g_sib_ref, i, 512), left_sib_buf.at[slot]),
            )

        begin(down_feeds)
        load(0, r2_ref, r_buf).wait()

        def second(at):
            dy = acc[at, :]
            dr, part = norm_back(dy, r_buf[at, :], vec_ref[l, 4:5, :])
            acc[at, :] = dr
            dm[at, :] = dr.astype(BF16)
            add_small(l, 0, part)
            add_small(l, 1, dy)
            add_small(l, 2, dr)

        row_tiles(rows, second)
        dm_copy = exchange(0, dm, dm_sib)
        dm_copy.start()
        r_load = load(0, r1_ref, r_buf)
        r_load.start()
        right_load = load(1, hl_ref, right_buf)
        right_load.start()
        right_sib_load = load(2, hl_sib_ref, right_sib_buf)
        right_sib_load.start()
        dm_copy.wait()

        def down_body(i, slot):
            fresh = (i == 0) if l == layers - 1 else False
            unit(left_buf[slot], left_sib_buf[slot], dm[...], dm_sib[...], lax.rem(i, 2), base + i, fresh)
            pl.when(lax.rem(i, 2) == 1)(lambda: reduction.tick(clock + lax.div(i, 2)))

        def place_of(i):
            a = 1 - lax.div(i, FF_GROUPS)
            return a, lax.rem(i, FF_GROUPS)

        def ff_feeds(i, slot):
            a, n = place_of(i)
            j = a * FF_GROUPS + n
            return (
                feed(2, slot, weight(a, first + down_group(n)), wa_buf.at[slot]),
                feed(3, slot, weight(a, first + in_group(n)), wb_buf.at[slot]),
                feed(4, slot, columns(slope_ref, j, 512), slope_buf.at[slot]),
            )

        begin(ff_feeds)
        stream(FF_GROUPS, down_feeds, down_body)
        unit_store(1, base + FF_GROUPS - 1).wait()

        def ff_body(i, slot):
            a, n = place_of(i)
            j = a * FF_GROUPS + n
            dg = nt(dm[...], block_of(wa_buf.at[slot]))
            d = (dg * slope_buf[slot].astype(F32)).astype(BF16)
            du[j] = d
            pl.when(a == 1)(lambda: give_du(j, n).start())
            dbi_ref[l, a, n] = jnp.sum(d.astype(F32), axis=0, keepdims=True)
            acc[...] += nn(d, block_of(wb_buf.at[slot]))
            pl.when(lax.rem(i, 4) == 3)(lambda: reduction.tick(clock + 2 + lax.div(i, 4)))

        stream(2 * FF_GROUPS, ff_feeds, ff_body)

        def out_feeds(i, slot):
            return (feed(2, slot, weight(i, first + OUT_GROUP), wa_buf.at[slot]),)

        begin(out_feeds)
        r_load.wait()

        def first_norm(at):
            dy = acc[at, :]
            dr, part = norm_back(dy, r_buf[at, :], vec_ref[l, 1:2, :])
            dr1[at, :] = dr
            da[at, :] = dr.astype(BF16)
            add_small(l, 3, part)
            add_small(l, 4, dy)
            add_small(l, 5, dr)

        row_tiles(rows, first_norm)
        if l > 0:
            load(0, saved[l - 1][6], r_buf).start()
        da_copy = exchange(1, da, da_sib)
        da_copy.start()

        def out_body(i, slot):
            dctx[:, pl.ds(pl.multiple_of(i * 512, 512), 512)] = nt(da[...], block_of(wa_buf.at[slot])).astype(BF16)

        stream(2, out_feeds, out_body)

        pairs = width // 128

        def pair_feeds(p, slot):
            far = lax.rem(p + pairs // 2, pairs)
            return (
                feed(5, slot, columns(qkv_ref.at[0], p, 128), pair_buf.at[slot, 0, pl.ds(0, rows)]),
                feed(6, slot, columns(qkv_ref.at[1], p, 128), pair_buf.at[slot, 1, pl.ds(0, rows)]),
                feed(7, slot, columns(sib_ref.at[0], far, 128), pair_buf.at[slot, 1, pl.ds(rows, rows)]),
                feed(8, slot, columns(qkv_ref.at[2], p, 128), pair_buf.at[slot, 2, pl.ds(0, rows)]),
                feed(9, slot, columns(sib_ref.at[1], far, 128), pair_buf.at[slot, 2, pl.ds(rows, rows)]),
                feed(10, slot, columns(ctx_ref, p, 128), pair_buf.at[slot, 3, pl.ds(0, rows)]),
                feed(11, slot, lse_ref.at[p], lse_buf.at[slot]),
            )

        begin(pair_feeds)
        right_load.wait()
        right_sib_load.wait()

        def in_body(n, _):
            give_du(FF_GROUPS + n, n).wait()
            unit(du[n], du_sib[n], right_buf[...], right_sib_buf[...], lax.rem(n, 2), base + FF_GROUPS + n, n == 0)
            pl.when(lax.rem(n, 2) == 1)(lambda: reduction.tick(clock + 4 + lax.div(n, 2)))
            return 0

        lax.fori_loop(0, FF_GROUPS, in_body, 0)

        right_load = load(1, xb_ref, right_buf)
        right_load.start()
        right_sib_load = load(2, xb_sib_ref, right_sib_buf)
        right_sib_load.start()
        left_load = load(3, columns(ctx_ref, 0, 512), left_buf.at[0])
        left_load.start()
        left_sib_load = load(4, ctx_sib_ref, left_sib_buf.at[0])
        left_sib_load.start()
        da_copy.wait()
        left_load.wait()
        left_sib_load.wait()
        unit(left_buf[0], left_sib_buf[0], da[...], da_sib[...], 0, base + 2 * FF_GROUPS)
        unit_store(0, base + 2 * FF_GROUPS).wait()

        def dx_feeds(i, slot):
            return (feed(3, slot, weight(lax.rem(i, 2), first + lax.rem(lax.div(i, 2) + 2, 3)), wa_buf.at[slot]),)

        begin(dx_feeds)

        def give_pair(p):
            far = lax.rem(p + pairs // 2, pairs)
            at = pl.ds(pl.multiple_of(far * 128, 128), 128)
            return pltpu.make_async_remote_copy(
                src_ref=kv_out.at[:, :, at], dst_ref=kv_far.at[:, :, at], send_sem=pair_send.at[p], recv_sem=pair_recv.at[far],
                device_id=partners[FLIP_C], device_id_type=MESH,
            )

        def pair_body(p, slot):
            far = lax.rem(p + pairs // 2, pairs)
            here = pl.ds(pl.multiple_of(p * 128, 128), 128)
            mask = spread_mask(mask_ref[p], key_ref[...])
            dq, dk, dv = attend_back_pair(
                pair_buf[slot, 0, 0:rows], pair_buf[slot, 1], pair_buf[slot, 2], hot_buf[...], mask,
                pair_buf[slot, 3, 0:rows], lse_buf[slot], dctx[:, here],
            )
            dqkv[0, :, here] = dq.astype(BF16)
            dqkv[1, :, here] = dk[:rows].astype(BF16)
            dqkv[2, :, here] = dv[:rows].astype(BF16)
            there = pl.ds(pl.multiple_of(far * 128, 128), 128)
            kv_out[0, :, there] = dk[rows:].astype(BF16)
            kv_out[1, :, there] = dv[rows:].astype(BF16)
            give_pair(p).start()
            pl.when(lax.rem(p, 3) == 1)(lambda: reduction.tick(clock + 6 + lax.div(p, 3)))

        stream(pairs, pair_feeds, pair_body)

        def settle_pair(p, _):
            give_pair(p).wait()
            return 0

        lax.fori_loop(0, pairs, settle_pair, 0)
        for n in range(2):
            add_rows(dqkv.at[1 + n], kv_far.at[n], rows)
        d_copy = exchange(3, dqkv.at[:, :, pl.ds(512, 512)], d_sib)
        d_copy.start()
        right_load.wait()
        right_sib_load.wait()
        d_copy.wait()

        def qkv_body(n, _):
            unit(
                dqkv[n, :, 0:512], d_sib[n], right_buf[...], right_sib_buf[...],
                lax.rem(n + 1, 2), base + 2 * FF_GROUPS + 1 + n, n == 0,
            )
            pl.when(n == 1)(lambda: reduction.tick(clock + 9))
            return 0

        lax.fori_loop(0, 3, qkv_body, 0)

        def start_dx(at):
            acc[at, :] = dr1[at, :]

        row_tiles(rows, start_dx)

        def dx_body(i, slot):
            a, n = lax.rem(i, 2), lax.div(i, 2)
            d = dqkv[n, :, pl.ds(pl.multiple_of(a * 512, 512), 512)]
            qkv_sums_ref[l, n, a] = jnp.sum(d.astype(F32), axis=0, keepdims=True)
            acc[...] += nn(d, block_of(wa_buf.at[slot]))
            pl.when(i == 3)(lambda: reduction.tick(clock + 10))

        stream(6, dx_feeds, dx_body)
        done = clock + 11

    def narrow(at):
        da[at, :] = acc[at, :].astype(BF16)

    row_tiles(rows, narrow)
    unit_store(1, total - 1).wait()
    ending.tick(0)
    dp, y = lax.axis_index("dp"), lax.axis_index("tensor")
    core = dp % 2
    turned = unit_order(y, ((dp // 2) % 2, (dp // 4) % 2, (dp // 8) % 2))

    def in_order(pair):
        rows_ab = lax.dot_general(
            jnp.concatenate(pair, axis=0), turned, (((1,), (0,)), ((), ())),
            precision=lax.Precision.HIGHEST, preferred_element_type=F32,
        )
        near = jnp.where(core == 0, rows_ab[0:1], rows_ab[1:2])
        far = jnp.where(core == 0, rows_ab[1:2], rows_ab[0:1])
        return [
            jnp.concatenate([near[:, h * 256 : (h + 1) * 256], far[:, h * 256 : (h + 1) * 256]], axis=1)
            for h in range(2)
        ]

    for l in range(layers):
        for n, source in enumerate((5, 2, 3, 0, 4, 1)):
            row = n * layers + l if n < 2 else 2 * layers + (n // 2 - 1) * 2 * layers + 2 * l + n % 2
            packed[row : row + 1, :] = small_ref[l, source : source + 1, :]
        for n, t in enumerate((0, 2)):
            for h, part in enumerate(in_order([qkv_sums_ref[l, t, a] for a in range(2)])):
                packed[6 * layers + h * layers + l : 6 * layers + h * layers + l + 1, n * 512 : (n + 1) * 512] = part
        for n in range(FF_GROUPS):
            for h, part in enumerate(in_order([dbi_ref[l, a, n] for a in range(2)])):
                row = 8 * layers + h * 2 * layers + 2 * l + n // 2
                packed[row : row + 1, (n % 2) * 512 : (n % 2 + 1) * 512] = part

    for n, bit in enumerate((FLIP_C, FLIP_Y, FLIP_X, FLIP_Z0, FLIP_Z1)):
        cross = pltpu.make_async_remote_copy(
            src_ref=packed, dst_ref=far_buf.at[n], send_sem=far_send.at[n], recv_sem=far_recv.at[n],
            device_id=partners[bit], device_id_type=MESH,
        )
        cross.start()
        reduction.tick(done + n)
        ending.tick(1 + n)
        cross.wait()
        packed[...] += far_buf[n]

    swap(0, da, dx_out, True)
    swap(1, x_ref, x_out, True)

    def rest(n, _):
        reduction.tick(done + n)
        ending.tick(1 + n)
        return 0

    lax.fori_loop(5, PARTED * PARTS + LAST_TICK - 1, rest, 0)
    swap(0, da, dx_out, False)
    swap(1, x_ref, x_out, False)


def backward(upstream, stream_low, weights, hot, mask, mask_rows, vectors, saved):
    rows, width = upstream.shape
    layers = len(saved)
    total = layers * GROUPS
    anywhere = pl.BlockSpec(memory_space=pl.ANY)
    in_vmem = pl.BlockSpec(memory_space=pltpu.VMEM)
    low = lambda *shape: pltpu.VMEM(shape, BF16)
    dma = lambda *shape: pltpu.SemaphoreType.DMA(shape)
    ends = PARTED * PARTS
    return pl.pallas_call(
        functools.partial(backward_kernel, layers),
        out_shape=(
            jax.ShapeDtypeStruct((total, 16, 32, width), BF16),
            jax.ShapeDtypeStruct((total, 16, 32, width), BF16),
            jax.ShapeDtypeStruct((rows, width), BF16),
            jax.ShapeDtypeStruct((rows, width), BF16),
            jax.ShapeDtypeStruct((12 * layers, width), F32),
        ),
        in_specs=[anywhere] * 3 + [in_vmem] * 4 + [anywhere] * (PER_LAYER * layers),
        out_specs=(anywhere, anywhere, anywhere, anywhere, in_vmem),
        scratch_shapes=[
            pltpu.VMEM((rows, width), F32),
            pltpu.VMEM((rows, width), F32),
            low(rows, width),
            low(rows, width),
            low(rows, width),
            low(rows, width),
            low(2 * FF_GROUPS, rows, 512),
            low(FF_GROUPS, rows, 512),
            low(rows, width),
            low(3, rows, width),
            low(3, rows, 512),
            low(2, rows, width),
            low(2, rows, width),
            low(2, 2, 256, width),
            low(2, 2, 256, width),
            pltpu.VMEM((rows, width), F32),
            low(2, rows, 512),
            low(2, rows, 512),
            low(2, rows, 512),
            low(rows, width),
            low(rows, width),
            low(2, 4, 2 * rows, 128),
            pltpu.VMEM((2, 2, rows), F32),
            low(2, 16, 32, width),
            low(SLOTS, 8, 32, width),
            low(SLOTS, 4, 32, width),
            low(SLOTS, 2, 32, width),
            low(SLOTS, 1, 32, width),
            low(SLOTS, 8, 32, width),
            low(2, 8, 32, width),
            dma(12, 2),
            dma(5),
            dma(1),
            dma(2),
            dma(6),
            dma(6),
            dma(FF_GROUPS),
            dma(FF_GROUPS),
            dma(width // 128),
            dma(width // 128),
            dma(7, SLOTS),
            dma(7, SLOTS),
            dma(total),
            dma(total),
            dma(2),
            dma(SLOTS),
            pltpu.SemaphoreType.REGULAR((4,)),
            pltpu.SemaphoreType.REGULAR((3,)),
            pltpu.VMEM((layers, 2, FF_GROUPS, 1, 512), F32),
            pltpu.VMEM((layers, 3, 2, 1, 512), F32),
            pltpu.VMEM((layers, 8, width), F32),
            pltpu.VMEM((5, 12 * layers, width), F32),
            dma(5),
            dma(5),
            low(ends, 8, 32 // PARTS, width),
            low(ends, 4, 32 // PARTS, width),
            low(ends, 2, 32 // PARTS, width),
            low(ends, 1, 32 // PARTS, width),
            low(ends, 8, 32 // PARTS, width),
            low(2, 8, 32 // PARTS, width),
            dma(7, ends),
            dma(7, ends),
            dma(ends),
            dma(ends),
            dma(2),
            dma(ends),
        ],
        compiler_params=pltpu.CompilerParams(
            collective_id=1, has_side_effects=True, vmem_limit_bytes=60 << 20
        ),
        cost_estimate=pl.CostEstimate(flops=60 << 30, bytes_accessed=300 << 20, transcendentals=1 << 24),
        name="backward",
    )(upstream, stream_low, weights, hot, mask, mask_rows, vectors, *[ref for one in saved for ref in one])


def flip_order(values, axis, bits):
    for i, bit in enumerate(bits):
        values = jnp.where(bit == 0, values, jnp.flip(values, axis + i))
    return values


def sequence_shards(
    block_input, segment_ids, random_blocks, w_qkv, b_qv, w_out, b_out, w_in, b_in, w_down, b_down,
    ln_gain, ln_bias, cotangent,
):
    y = lax.axis_index("tensor")
    dp = lax.axis_index("dp")
    core, x_bit, z0, z1 = dp % 2, (dp // 2) % 2, (dp // 4) % 2, dp // 8
    code = core * 8 + x_bit * 4 + z0 * 2 + z1
    code_arg = code.reshape(1).astype(jnp.int32)
    device_bits = (core, x_bit, z0, z1)

    rows, _, width = block_input.shape
    layers = w_qkv.shape[0]
    blocks = random_blocks.shape[2]
    own_blocks = blocks // 2
    heads = random_blocks.shape[1] * 2

    chosen = random_blocks[0]
    near = jnp.concatenate([chosen.reshape(-1), segment_ids[0]])
    sibling = flip(near, FLIP_C)
    across, diagonal = flip(chosen.reshape(-1), FLIP_Y), flip(chosen.reshape(-1), SWAP)
    mine = jnp.concatenate([near[: chosen.size], across, near[chosen.size :]])
    other = jnp.concatenate([sibling[: chosen.size], diagonal, sibling[chosen.size :]])
    packed = jnp.where(core == y, mine, other)
    chosen = packed[: 2 * chosen.size].reshape(2, heads // 2, blocks, -1)
    segments = packed[2 * random_blocks.size :]
    chosen = flip_order(chosen.reshape(2, 2, 2, 2, blocks, -1), 1, device_bits[:3])
    chosen = chosen.transpose(1, 0, 2, 3, 4, 5).reshape(heads, blocks, -1)
    segments = segments.reshape(2, rows)
    segments = jnp.where(core == 0, segments, segments[::-1]).reshape(-1)
    query_block = core * own_blocks + jnp.arange(own_blocks)
    key_block = jnp.arange(blocks) ^ (core * own_blocks)
    allowed = (
        (jnp.abs(query_block[:, None] - key_block[None, :]) <= 1)
        | (key_block[None, :] == 0)
        | (key_block[None, :] == blocks - 1)
        | (query_block[:, None] == 0)
        | (query_block[:, None] == blocks - 1)
    )
    chosen = lax.dynamic_slice_in_dim(chosen, core * own_blocks, own_blocks, axis=1)
    allowed = allowed[None] | jnp.any(chosen[:, :, None, :] == key_block[None, None, :, None], axis=3)
    block_rows = rows // own_blocks
    documents = jnp.arange(HEAD_DIM - own_blocks)
    mask = jnp.pad(
        jnp.where(allowed, 0.0, BIG).astype(F32).transpose(0, 2, 1), ((0, 0), (0, 0), (0, HEAD_DIM - own_blocks))
    )
    mask = mask.reshape(heads // 2, 2, blocks, HEAD_DIM).transpose(0, 2, 1, 3).reshape(heads // 2, blocks, 2 * HEAD_DIM)
    document_part = jnp.where(
        (segments[:, None] == documents[None, :]) | (documents[None, :] > 7), 0.0, BIG
    ).astype(F32)
    mask_rows = jnp.pad(document_part, ((0, 0), (own_blocks, 0)))
    mask_rows = jnp.concatenate([mask_rows, mask_rows], axis=1)
    block_rows = rows // own_blocks
    hot = jnp.concatenate(
        [
            jnp.repeat(jnp.eye(own_blocks, dtype=BF16), block_rows, axis=0),
            (segments[:rows, None] == documents[None, :]).astype(BF16),
        ],
        axis=1,
    )
    hot = jnp.concatenate([hot, hot], axis=1)

    bias_pack = jnp.concatenate(
        [
            flip_order(b_qv.reshape(layers * 2, 2, 2, 2, 2, -1), 1, device_bits).reshape(-1),
            flip_order(b_in.reshape(layers * FF_GROUPS, 2, 2, 2, 2, -1), 1, device_bits).reshape(-1),
        ]
    )
    bias_far = flip(bias_pack, FLIP_Y)
    n_qv = b_qv.size

    def local_bias(near, far, count):
        near, far = near.reshape(count, 2, 1, 256), far.reshape(count, 2, 1, 256)
        return jnp.concatenate([near, far], axis=2).reshape(count, 2, 512)

    bias_qv = local_bias(bias_pack[:n_qv], bias_far[:n_qv], layers * 2).reshape(layers, 2, 2, 1, 512)
    bias_qkv = jnp.stack([bias_qv[:, 0], jnp.zeros_like(bias_qv[:, 0]), bias_qv[:, 1]], axis=1)
    bias_in = local_bias(bias_pack[n_qv:], bias_far[n_qv:], layers * FF_GROUPS)
    bias_in = bias_in.reshape(layers, FF_GROUPS, 2, 1, 512).swapaxes(1, 2)

    vectors = [
        jnp.stack(
            [
                b_out[l], ln_gain[l, 0], ln_bias[l, 0], b_down[l], ln_gain[l, 1], ln_bias[l, 1],
                b_out[l], b_out[l],
            ]
        )
        for l in range(layers)
    ]
    vectors = jnp.stack(vectors)
    weights, upstream_low, stream_low, saved = forward(
        block_input, cotangent, w_qkv, w_out, w_in, w_down, hot, mask, mask_rows, bias_qkv, bias_in, vectors
    )
    _, grads, dx_low, x_low, packed = backward(
        upstream_low, stream_low, weights, hot, mask, mask_rows, vectors, saved
    )
    grads = grads.reshape(layers * GROUPS, 512, width)
    block_output, input_grad = widen_rows(x_low, dx_low)

    def placing(shape, block, index, turned, count, start):
        return place(
            grads, shape, block, index, turned, count, lambda l, i: (layers - 1 - l) * GROUPS + start + i, code_arg
        )

    g_b_out, g_b_down, g_gain, g_shift, g_b_qv, g_b_in = hand_out(packed, y.reshape(1).astype(jnp.int32), layers)
    g_down = placing(w_down.shape, (1, 512, width), lambda l, i: (l, i, 0), False, FF_GROUPS, 0)
    g_in = placing(w_in.shape, (1, width, 512), lambda l, i: (l, 0, i), True, FF_GROUPS, FF_GROUPS)
    g_qkv = placing(w_qkv.shape, (1, 1, width, 512), lambda l, i: (l, i, 0, 0), True, 3, 2 * FF_GROUPS + 1)
    g_out = placing(w_out.shape, (1, 512, width), lambda l, i: (l, 0, 0), False, 1, 2 * FF_GROUPS)
    return (
        block_output,
        input_grad,
        g_qkv,
        g_b_qv,
        g_out,
        g_b_out,
        g_in,
        g_b_in,
        g_down,
        g_b_down,
        g_gain,
        g_shift,
    )


def as_sent(array):

    def short(part):
        return part.astype(jnp.bfloat16) if part.dtype == jnp.float32 else part

    return jax.tree.map(short, array)


def norm_rows(values, gain_row, shift_row):
    row_mean = jnp.mean(values, axis=-1, keepdims=True)
    centred = values - row_mean
    variance = jnp.mean(centred * centred, axis=-1, keepdims=True)
    return centred * lax.rsqrt(variance + 1e-06) * gain_row + shift_row


def gelu_exact(values):
    return jax.nn.gelu(values, approximate=False)


def block_mask(chosen_blocks, segment_rows):
    nblocks = chosen_blocks.shape[2]
    block_index = jnp.arange(nblocks)
    near_blocks = jnp.abs(block_index[:, None] - block_index[None, :]) <= 1
    edge_blocks = (
        (block_index[None, :] == 0)
        | (block_index[None, :] == nblocks - 1)
        | (block_index[:, None] == 0)
        | (block_index[:, None] == nblocks - 1)
    )
    picked_blocks = jnp.any(chosen_blocks[..., None] == block_index, axis=3)
    allowed = near_blocks | edge_blocks | picked_blocks
    block_rows = segment_rows.shape[1] // nblocks
    allowed = jnp.repeat(jnp.repeat(allowed, block_rows, axis=2), block_rows, axis=3)
    same_doc = segment_rows[:, :, None] == segment_rows[:, None, :]
    return allowed & same_doc[:, None]


def masked_scores(queries, key_rows, allowed, score_scale):
    scores = (
        jnp.einsum("qshd,kshd->shqk", queries, key_rows, preferred_element_type=jnp.float32)
        * score_scale
    )
    return jnp.where(allowed, scores, -1e30)


def shards(
    block_input,
    segment_ids,
    random_blocks,
    w_qkv,
    b_qv,
    w_out,
    b_out,
    w_in,
    b_in,
    w_down,
    b_down,
    ln_gain,
    ln_bias,
    cotangent,
):
    score_scale = HEAD_DIM ** (-0.5)
    shard_rows, seq_count, model_width = block_input.shape
    layers = w_qkv.shape[0]
    local_width = w_qkv.shape[3]
    local_heads = local_width // HEAD_DIM
    allowed = block_mask(random_blocks, segment_ids)
    saved_acts = []
    stream = block_input
    for layer_index in range(layers):
        w_proj = w_qkv[layer_index].astype(jnp.bfloat16)
        w_mix = w_out[layer_index].astype(jnp.bfloat16)
        rows_low = stream.astype(jnp.bfloat16)
        full_rows = lax.all_gather(rows_low, "tensor", axis=0, tiled=True)
        length = full_rows.shape[0]
        projected = jnp.einsum(
            "lsd,tdc->tlsc", full_rows, w_proj, preferred_element_type=jnp.float32
        )
        qkv_bias = jnp.stack(
            [b_qv[layer_index, 0], jnp.zeros_like(b_qv[layer_index, 0]), b_qv[layer_index, 1]]
        )
        qkv_low = (projected + qkv_bias[:, None, None, :]).astype(jnp.bfloat16)
        head_view = qkv_low.reshape(3, length, seq_count, local_heads, HEAD_DIM)
        scores = masked_scores(head_view[0], head_view[1], allowed, score_scale)
        row_top = jnp.max(scores, axis=-1, keepdims=True)
        log_total = row_top + jnp.log(jnp.sum(jnp.exp(scores - row_top), axis=-1, keepdims=True))
        probs_low = jnp.exp(scores - log_total).astype(jnp.bfloat16)
        context = jnp.einsum(
            "shqk,kshd->qshd", probs_low, head_view[2], preferred_element_type=jnp.float32
        )
        context = context.reshape(length, seq_count, local_width).astype(jnp.bfloat16)
        mixed = lax.psum_scatter(
            jnp.einsum("lsc,cd->lsd", context, w_mix, preferred_element_type=jnp.float32).astype(
                jnp.bfloat16
            ),
            "tensor",
            scatter_dimension=0,
            tiled=True,
        ).astype(jnp.float32)
        first_sum = stream + mixed + b_out[layer_index]
        hidden_rows = norm_rows(first_sum, ln_gain[layer_index, 0], ln_bias[layer_index, 0])
        hidden_low = hidden_rows.astype(jnp.bfloat16)
        up_weight = w_in[layer_index].astype(jnp.bfloat16)
        backward_weight = w_down[layer_index].astype(jnp.bfloat16)
        hidden_full = lax.all_gather(hidden_low, "tensor", axis=0, tiled=True)
        preactivation = (
            jnp.einsum("twn,nj->twj", hidden_full, up_weight, preferred_element_type=jnp.float32)
            + b_in[layer_index]
        )
        activation_reduced = gelu_exact(preactivation).astype(jnp.bfloat16)
        grown = lax.psum_scatter(
            jnp.einsum(
                "unj,jp->unp",
                activation_reduced,
                backward_weight,
                preferred_element_type=jnp.float32,
            ).astype(jnp.bfloat16),
            "tensor",
            scatter_dimension=0,
            tiled=True,
        ).astype(jnp.float32)
        second_sum = hidden_rows + grown + b_down[layer_index]
        stream = norm_rows(second_sum, ln_gain[layer_index, 1], ln_bias[layer_index, 1])
        keep_rows, keep_hidden = (full_rows, hidden_full)
        saved_acts.append(
            (
                keep_rows,
                head_view,
                log_total,
                context,
                first_sum,
                keep_hidden,
                preactivation,
                activation_reduced,
                second_sum,
                up_weight,
                backward_weight,
            )
        )
    upstream = cotangent
    grads_by_layer = [None] * layers
    for layer_index in reversed(range(layers)):
        (
            keep_rows,
            head_view,
            log_total,
            context,
            first_sum,
            keep_hidden,
            preactivation,
            activation_reduced,
            second_sum,
            up_weight,
            backward_weight,
        ) = saved_acts[layer_index]
        full_rows, hidden_full = (keep_rows, keep_hidden)
        length = full_rows.shape[0]
        w_proj = w_qkv[layer_index].astype(jnp.bfloat16)
        w_mix = w_out[layer_index].astype(jnp.bfloat16)
        _, pull_second = jax.vjp(
            norm_rows, second_sum, ln_gain[layer_index, 1], ln_bias[layer_index, 1]
        )
        d_second, d_gain_two, d_shift_two = pull_second(upstream)
        _, pull_gelu = jax.vjp(gelu_exact, preactivation)
        widened_full = lax.all_gather(d_second.astype(jnp.bfloat16), "tensor", axis=0, tiled=True)
        down_gradient = jnp.einsum(
            "uxc,uxw->cw", activation_reduced, widened_full, preferred_element_type=jnp.float32
        )
        activation_gradient = jnp.einsum(
            "mra,xa->mrx", widened_full, backward_weight, preferred_element_type=jnp.float32
        )
        preactivation_gradient_reduced = pull_gelu(activation_gradient)[0].astype(jnp.bfloat16)
        up_gradient = jnp.einsum(
            "kmx,kmt->xt",
            hidden_full,
            preactivation_gradient_reduced,
            preferred_element_type=jnp.float32,
        )
        g_up_bias = jnp.sum(preactivation_gradient_reduced.astype(jnp.float32), axis=(0, 1))
        d_hidden = d_second + lax.psum_scatter(
            jnp.einsum(
                "hmp,tp->hmt",
                preactivation_gradient_reduced,
                up_weight,
                preferred_element_type=jnp.float32,
            ).astype(jnp.bfloat16),
            "tensor",
            scatter_dimension=0,
            tiled=True,
        ).astype(jnp.float32)
        _, pull_first = jax.vjp(
            norm_rows, first_sum, ln_gain[layer_index, 0], ln_bias[layer_index, 0]
        )
        d_first, d_gain_one, d_shift_one = pull_first(d_hidden)
        full_mixed = lax.all_gather(d_first.astype(jnp.bfloat16), "tensor", axis=0, tiled=True)
        g_out = jnp.einsum("lsc,lsd->cd", context, full_mixed, preferred_element_type=jnp.float32)
        d_context = jnp.einsum(
            "lsd,cd->lsc", full_mixed, w_mix, preferred_element_type=jnp.float32
        ).astype(jnp.bfloat16)
        d_context = d_context.reshape(length, seq_count, local_heads, HEAD_DIM)
        queries, key_rows, value_rows = (head_view[0], head_view[1], head_view[2])
        scores = masked_scores(queries, key_rows, allowed, score_scale)
        attn_probs = jnp.exp(scores - log_total)
        probs_low = attn_probs.astype(jnp.bfloat16)
        d_probs = jnp.einsum(
            "qshd,kshd->shqk", d_context, value_rows, preferred_element_type=jnp.float32
        )
        d_scores = attn_probs * (d_probs - jnp.sum(d_probs * attn_probs, axis=-1, keepdims=True))
        d_scores = d_scores.astype(jnp.bfloat16)
        d_query = (
            jnp.einsum("shqk,kshd->qshd", d_scores, key_rows, preferred_element_type=jnp.float32)
            * score_scale
        )
        d_key = (
            jnp.einsum("shqk,qshd->kshd", d_scores, queries, preferred_element_type=jnp.float32)
            * score_scale
        )
        d_value = jnp.einsum(
            "shqk,qshd->kshd", probs_low, d_context, preferred_element_type=jnp.float32
        )
        d_qkv = (
            jnp.stack([d_query, d_key, d_value])
            .reshape(3, length, seq_count, local_width)
            .astype(jnp.bfloat16)
        )
        g_proj = jnp.einsum("lsd,tlsc->tdc", full_rows, d_qkv, preferred_element_type=jnp.float32)
        qkv_sums = jnp.sum(d_qkv.astype(jnp.float32), axis=(1, 2))
        g_bias = jnp.stack([qkv_sums[0], qkv_sums[2]])
        upstream = d_first + lax.psum_scatter(
            jnp.einsum("tlsc,tdc->lsd", d_qkv, w_proj, preferred_element_type=jnp.float32).astype(
                jnp.bfloat16
            ),
            "tensor",
            scatter_dimension=0,
            tiled=True,
        ).astype(jnp.float32)
        weight_grads = (g_proj, g_bias, g_out, up_gradient, g_up_bias, down_gradient)
        small_grads = (
            jnp.sum(d_first, axis=(0, 1)),
            jnp.sum(d_second, axis=(0, 1)),
            jnp.stack([d_gain_one, d_gain_two]),
            jnp.stack([d_shift_one, d_shift_two]),
        )
        grads_by_layer[layer_index] = (weight_grads, small_grads)
    weight_stack = tuple(
        (
            jnp.stack([grads_by_layer[layer_index][0][member] for layer_index in range(layers)])
            for member in range(6)
        )
    )
    small_stack = tuple(
        (
            jnp.stack([grads_by_layer[layer_index][1][member] for layer_index in range(layers)])
            for member in range(4)
        )
    )
    weight_stack = jax.tree.map(
        lambda part: part.astype(jnp.float32), lax.psum(as_sent(weight_stack), "dp")
    )
    small_stack = lax.psum(small_stack, ("dp", "tensor"))
    return (
        stream,
        upstream,
        weight_stack[0],
        weight_stack[1],
        weight_stack[2],
        small_stack[0],
        weight_stack[3],
        weight_stack[4],
        weight_stack[5],
        small_stack[1],
        small_stack[2],
        small_stack[3],
    )


def solution(mesh):
    by_sequence = mesh.shape["tensor"] == 2 and mesh.shape["dp"] == 16
    return jax.shard_map(
        sequence_shards if by_sequence else shards,
        mesh=mesh,
        in_specs=(
            P("tensor", "dp", None),
            P("dp", None),
            P("dp", "tensor", None, None),
            P(None, None, None, "tensor"),
            P(None, None, "tensor"),
            P(None, "tensor", None),
            P(),
            P(None, None, "tensor"),
            P(None, "tensor"),
            P(None, "tensor", None),
            P(),
            P(),
            P(),
            P("tensor", "dp", None),
        ),
        out_specs=(
            P("tensor", "dp", None),
            P("tensor", "dp", None),
            P(None, None, None, "tensor"),
            P(None, None, "tensor"),
            P(None, "tensor", None),
            P(),
            P(None, None, "tensor"),
            P(None, "tensor"),
            P(None, "tensor", None),
            P(),
            P(),
            P(),
        ),
        check_vma=False,
    )
```

```python
import functools

import jax
import jax.numpy as jnp
from jax import lax
from jax.experimental import pallas as pl
from jax.experimental.pallas import tpu as pltpu
from jax.sharding import PartitionSpec as P

HEAD_DIM = 64
BIG = -1e30
BF16 = jnp.bfloat16
F32 = jnp.float32
MESH = pl.DeviceIdType.MESH
VMEM_LIMIT = 56 << 20

FLIP_Y, FLIP_C, FLIP_X, FLIP_Z0, FLIP_Z1 = 1, 2, 4, 8, 16
SWAP = FLIP_Y + FLIP_C
DEVICES = 32

GROUPS = 12
OUT_GROUP = 3
FF_GROUPS = 4


def in_group(s):
    return 4 + 2 * s


def down_group(s):
    return 5 + 2 * s


def flip(values, bit):
    pairs = [(i, i ^ bit) for i in range(DEVICES)]
    return jax.tree.map(lambda v: lax.ppermute(v, ("dp", "tensor"), pairs), values)


def nt(a, b):
    return lax.dot_general(a, b, (((1,), (1,)), ((), ())), preferred_element_type=F32)


def nn(a, b):
    return lax.dot_general(a, b, (((1,), (0,)), ((), ())), preferred_element_type=F32)


def tn(a, b):
    return lax.dot_general(a, b, (((0,), (0,)), ((), ())), preferred_element_type=F32)


def block_of(ref):
    width = ref.shape[-1]
    return ref[...].reshape(-1, width)


def place_kernel(turned, rows_too, code_ref, g_ref, *refs):
    refs = list(refs)
    sources = [refs.pop(0) for _ in range(rows_too)]
    o_ref = refs.pop(0)
    targets = [refs.pop(0) for _ in range(rows_too)]
    code = code_ref[0]
    step = pl.program_id(0) * pl.num_programs(1) + pl.program_id(1)
    if rows_too:
        wide, sem = refs[-2:]
        copies = [
            pltpu.make_async_copy(wide.at[n], target.at[:, 0], sem.at[n]) for n, target in enumerate(targets)
        ]

        @pl.when(step == 0)
        def _():
            for n, source in enumerate(sources):
                wide[n] = source[...].astype(F32)
                copies[n].start()

    for j in range(16):
        start = pl.multiple_of((j ^ code) * 32, 32)
        block = g_ref[0, pl.ds(start, 32), :].astype(F32)
        if turned:
            refs[0][j * 32 : (j + 1) * 32, :] = block
        else:
            o_ref[0, j * 32 : (j + 1) * 32, :] = block
    if turned:
        o_ref[...] = refs[0][...].T.reshape(o_ref.shape)
    if rows_too:

        @pl.when(step == pl.num_programs(0) * pl.num_programs(1) - 1)
        def _():
            for copy in copies:
                copy.wait()


def place(sums, shape, block, index, turned, count, group, code, rows_too=()):
    width = sums.shape[-1]
    anywhere = pl.BlockSpec(memory_space=pl.ANY)
    scratch = [pltpu.VMEM((512, width), F32)] if turned else []
    if rows_too:
        scratch += [
            pltpu.VMEM((len(rows_too),) + rows_too[0].shape, F32),
            pltpu.SemaphoreType.DMA((len(rows_too),)),
        ]
    return pl.pallas_call(
        functools.partial(place_kernel, turned, len(rows_too)),
        out_shape=[jax.ShapeDtypeStruct(shape, F32)]
        + [jax.ShapeDtypeStruct((r.shape[0], 1, r.shape[1]), F32) for r in rows_too],
        grid_spec=pltpu.PrefetchScalarGridSpec(
            num_scalar_prefetch=1,
            grid=(shape[0], count),
            in_specs=[pl.BlockSpec((1, 512, width), lambda l, i, code: (group(l, i), 0, 0))]
            + [pl.BlockSpec(r.shape, lambda l, i, code: (0, 0)) for r in rows_too],
            out_specs=[pl.BlockSpec(block, lambda l, i, code: index(l, i))] + [anywhere for _ in rows_too],
            scratch_shapes=scratch,
        ),
        compiler_params=pltpu.CompilerParams(vmem_limit_bytes=VMEM_LIMIT),
        cost_estimate=pl.CostEstimate(
            flops=0, bytes_accessed=shape[0] * count * 512 * width * 6, transcendentals=0
        ),
        name="place",
    )(code, sums, *rows_too)


def hand_out_kernel(layers, y_ref, packed, out, down, gain, shift, qv, hidden):
    y = y_ref[0]
    width = packed.shape[1]
    out[...] = packed[0:layers, :]
    down[...] = packed[layers : 2 * layers, :]
    for l in range(layers):
        for n in range(2):
            row = 2 * layers + 2 * l + n
            gain[l, n : n + 1, :] = packed[row : row + 1, :]
            row += 2 * layers
            shift[l, n : n + 1, :] = packed[row : row + 1, :]
            at = 8 * layers + 2 * l + n
            hidden[l : l + 1, n * width : (n + 1) * width] = jnp.where(
                y == 0, packed[at : at + 1, :], packed[at + 2 * layers : at + 2 * layers + 1, :]
            )
            half = slice(n * width // 2, (n + 1) * width // 2)
            at = 6 * layers + l
            qv[l, n : n + 1, :] = jnp.where(
                y == 0, packed[at : at + 1, half], packed[at + layers : at + layers + 1, half]
            )


def hand_out(packed, y, layers):
    width = packed.shape[1]
    full = lambda *shape: jax.ShapeDtypeStruct(shape, F32)
    in_vmem = pl.BlockSpec(memory_space=pltpu.VMEM)
    return pl.pallas_call(
        functools.partial(hand_out_kernel, layers),
        out_shape=(
            full(layers, width),
            full(layers, width),
            full(layers, 2, width),
            full(layers, 2, width),
            full(layers, 2, width // 2),
            full(layers, 2 * width),
        ),
        in_specs=[pl.BlockSpec(memory_space=pltpu.SMEM), in_vmem],
        out_specs=(in_vmem,) * 6,
        name="hand_out",
    )(y, packed)


def partner(bits):
    dp, y = lax.axis_index("dp"), lax.axis_index("tensor")
    other = dp
    for step in (1, 2, 4, 8):
        if bits & (2 * step):
            other = other + step * (1 - 2 * ((dp // step) % 2))
    return (other, 1 - y if bits & FLIP_Y else y)


def all_partners(bits):
    return {bit: partner(bit) for bit in bits}


def greet(partners):
    barrier = pltpu.get_barrier_semaphore()
    for other in partners.values():
        pl.semaphore_signal(barrier, inc=1, device_id=other, device_id_type=MESH)
    pl.semaphore_wait(barrier, len(partners))


def add_into(into, other, count):
    def step(i, _):
        into[i] = (into[i].astype(F32) + other[i].astype(F32)).astype(BF16)
        return 0

    lax.fori_loop(0, count, step, 0)


def add_rows(into, other, rows):
    def step(i, _):
        at = pl.ds(pl.multiple_of(i * 32, 32), 32)
        into[at, :] = (into[at, :].astype(F32) + other[at, :].astype(F32)).astype(BF16)
        return 0

    lax.fori_loop(0, rows // 32, step, 0)


def add_into(into, other, count):
    def step(i, _):
        into[i] = (into[i].astype(F32) + other[i].astype(F32)).astype(BF16)
        return 0

    lax.fori_loop(0, count, step, 0)


SLOTS = 6
PARTED = 2
PARTS = 2
LAST_TICK = 8


class Reduction:
    def __init__(self, grads, sums, first, groups, parts, partners, bufs, sems):
        self.grads, self.sums, self.first, self.parts, self.partners = grads, sums, first, parts, partners
        self.count = groups * parts
        self.y_buf, self.x_buf, self.z0_buf, self.z1_buf, self.all_buf, self.keep_buf = bufs
        self.slots = self.y_buf.shape[0]
        self.send_sem, self.recv_sem, self.core_send, self.core_recv, self.keep_sem, self.out_sem = sems[:6]
        self.in_free, self.out_free = sems[6:] if len(sems) > 6 else (None, None)

    def blocks(self, ref, i, at):
        if self.parts == 1:
            return ref.at[self.first + i, pl.ds(at, 8)]
        size = 32 // self.parts
        part = pl.ds(pl.multiple_of(lax.rem(i, self.parts) * size, size), size)
        return ref.at[self.first + lax.div(i, self.parts), pl.ds(at, 8), part]

    def copy(self, step, i):
        slot = lax.rem(i, self.slots)
        ys, al = self.y_buf.at[slot], self.all_buf.at[slot]
        bit, source, target = (
            (FLIP_Y, self.blocks(self.grads, i, 8), ys),
            (FLIP_X, ys.at[pl.ds(4, 4)], self.x_buf.at[slot]),
            (FLIP_Z0, ys.at[pl.ds(2, 2)], self.z0_buf.at[slot]),
            (FLIP_Z1, ys.at[pl.ds(1, 1)], self.z1_buf.at[slot]),
            (FLIP_Z1, al.at[pl.ds(0, 1)], al.at[pl.ds(1, 1)]),
            (FLIP_Z0, al.at[pl.ds(0, 2)], al.at[pl.ds(2, 2)]),
            (FLIP_X, al.at[pl.ds(0, 4)], al.at[pl.ds(4, 4)]),
            (FLIP_C, al, self.blocks(self.sums, i, 8)),
        )[step]
        return pltpu.make_async_remote_copy(
            src_ref=source,
            dst_ref=target,
            send_sem=self.send_sem.at[step, slot] if step < 7 else self.core_send.at[i],
            recv_sem=self.recv_sem.at[step, slot] if step < 7 else self.core_recv.at[i],
            device_id=self.partners[bit],
            device_id_type=MESH,
        )

    def keep(self, i):
        slot = lax.rem(i, 2)
        return pltpu.make_async_copy(
            self.blocks(self.grads, i, 0), self.keep_buf.at[slot], self.keep_sem.at[slot]
        )

    def out(self, i):
        slot = lax.rem(i, self.slots)
        return pltpu.make_async_copy(
            self.all_buf.at[slot], self.blocks(self.sums, i, 0), self.out_sem.at[slot]
        )

    def take(self, sems, n, i):
        if sems is not None:
            pl.when(i >= self.slots)(lambda: pl.semaphore_wait(sems.at[n], 1))

    def give(self, sems, n, bit, i):
        if sems is not None:
            pl.when(i + self.slots < self.count)(
                lambda: pl.semaphore_signal(
                    sems.at[n], inc=1, device_id=self.partners[bit], device_id_type=MESH
                )
            )

    def tick(self, t):
        def at(offset, body):
            i = t - offset
            pl.when((i >= 0) & (i < self.count))(lambda: body(i, lax.rem(i, self.slots)))

        def set_out(i, slot):
            self.take(self.in_free, 0, i)
            self.copy(0, i).start()
            self.keep(i).start()

        def finish(i, slot):
            self.copy(7, i).wait()
            self.out(i).wait()
            for n, bit in enumerate((FLIP_X, FLIP_Z0, FLIP_Z1)):
                self.give(self.out_free, n, bit, i)

        def to_core(i, slot):
            self.copy(6, i).wait()
            self.copy(7, i).start()
            self.out(i).start()

        def back_x(i, slot):
            self.copy(5, i).wait()
            self.take(self.out_free, 0, i)
            self.copy(6, i).start()

        def back_z0(i, slot):
            self.copy(4, i).wait()
            self.take(self.out_free, 1, i)
            self.copy(5, i).start()

        def back_z1(i, slot):
            self.copy(3, i).wait()
            add_into(self.y_buf.at[slot], self.z1_buf.at[slot], 1)
            self.all_buf[slot, 0] = self.y_buf[slot, 0]
            for n, bit in enumerate((FLIP_Y, FLIP_X, FLIP_Z0, FLIP_Z1)):
                self.give(self.in_free, n, bit, i)
            self.take(self.out_free, 2, i)
            self.copy(4, i).start()

        def on_z1(i, slot):
            self.copy(2, i).wait()
            add_into(self.y_buf.at[slot], self.z0_buf.at[slot], 2)
            self.take(self.in_free, 3, i)
            self.copy(3, i).start()

        def on_z0(i, slot):
            self.copy(1, i).wait()
            add_into(self.y_buf.at[slot], self.x_buf.at[slot], 4)
            self.take(self.in_free, 2, i)
            self.copy(2, i).start()

        def on_x(i, slot):
            self.copy(0, i).wait()
            self.keep(i).wait()
            add_into(self.y_buf.at[slot], self.keep_buf.at[lax.rem(i, 2)], 8)
            self.take(self.in_free, 1, i)
            self.copy(1, i).start()

        at(0, set_out)
        at(8, finish)
        at(7, to_core)
        at(6, back_x)
        at(5, back_z0)
        at(4, back_z1)
        at(3, on_z1)
        at(2, on_z0)
        at(1, on_x)


def unit_order(y, core_free_bits):
    taken = lax.broadcasted_iota(jnp.int32, (512, 512), 0)
    column = lax.broadcasted_iota(jnp.int32, (512, 512), 1)
    where = lax.rem(column, 32)
    for own, weight in zip((y,) + core_free_bits, (256, 128, 64, 32)):
        bit = lax.rem(lax.div(column, weight), 2)
        where = where + weight * (bit + own - 2 * own * bit)
    return (taken == where).astype(F32)


def begin(feeds):
    for copy in feeds(0, 0):
        copy.start()


def stream(count, feeds, body):
    def step(i, _):
        slot = lax.rem(i, 2)

        @pl.when(i + 1 < count)
        def _():
            for copy in feeds(i + 1, 1 - slot):
                copy.start()

        for copy in feeds(i, slot):
            copy.wait()
        body(i, slot)
        return 0

    lax.fori_loop(0, count, step, 0)


def norm(r, gain, shift):
    centred = r - jnp.mean(r, axis=-1, keepdims=True)
    rstd = lax.rsqrt(jnp.mean(centred * centred, axis=-1, keepdims=True) + 1e-06)
    return centred * rstd * gain + shift


def norm_back(dy, r, gain):
    centred = r - jnp.mean(r, axis=-1, keepdims=True)
    rstd = lax.rsqrt(jnp.mean(centred * centred, axis=-1, keepdims=True) + 1e-06)
    unit = centred * rstd
    dunit = dy * gain
    dr = rstd * (
        dunit
        - jnp.mean(dunit, axis=-1, keepdims=True)
        - unit * jnp.mean(dunit * unit, axis=-1, keepdims=True)
    )
    return dr, dy * unit


def gelu_and_slope(u):
    cdf = 0.5 * (1.0 + lax.erf(u * (0.5**0.5)))
    pdf = jnp.exp(-0.5 * u * u) * 0.3989422804014327
    return u * cdf, cdf + u * pdf


TILE = 64


def row_tiles(rows, body):
    def step(i, _):
        body(pl.ds(pl.multiple_of(i * TILE, TILE), TILE))
        return 0

    lax.fori_loop(0, rows // TILE, step, 0)


def pair_lanes(values, e):
    lane = lax.broadcasted_iota(jnp.int32, values.shape, 1)
    return jnp.where(lane // HEAD_DIM == e, values, jnp.zeros_like(values))


def spread_mask(block_part, document_part):
    blocks, lanes = block_part.shape
    each = document_part.shape[0] // blocks
    part = jnp.broadcast_to(block_part[:, None, :], (blocks, each, lanes)).reshape(blocks * each, lanes)
    return (part + document_part).astype(BF16)


def both_heads(values):
    return jnp.concatenate([pair_lanes(values, 0), pair_lanes(values, 1)], axis=0)


def attend_pair(query, keys, values, hot, mask):
    scale = HEAD_DIM**-0.5
    rows = query.shape[0]
    query = query * jnp.asarray(scale, BF16)
    right = jnp.concatenate([both_heads(query), both_heads(hot)], axis=1)
    s = nt(jnp.concatenate([keys, mask], axis=1), right)
    top = jnp.max(s, axis=0, keepdims=True)
    p = jnp.exp(s - top)
    total = jnp.sum(p, axis=0, keepdims=True)
    c = nn(values.T, p.astype(BF16)) * (1.0 / total)
    context = jnp.concatenate([c[:HEAD_DIM, :rows], c[HEAD_DIM:, rows:]], axis=0).T
    lse = top + jnp.log(total)
    return context, [lse[:, :rows], lse[:, rows:]]


def attend_back_pair(query, keys, values, hot, mask, ctx, lse, dctx):
    scale = HEAD_DIM**-0.5
    rows = query.shape[0]
    query = query * jnp.asarray(scale, BF16)
    keys_t = keys.T
    delta_t = (dctx.astype(F32) * ctx.astype(F32)).T
    left = jnp.concatenate([keys, mask], axis=1)
    tile = rows // 2
    dk, dv, dq = 0.0, 0.0, []
    for part in range(2):
        at = slice(part * tile, (part + 1) * tile)
        heads = []
        for e in range(2):
            lanes = slice(e * HEAD_DIM, (e + 1) * HEAD_DIM)
            query_e = pair_lanes(query[at], e)
            dctx_e = pair_lanes(dctx[at], e)
            right = jnp.concatenate([query_e, pair_lanes(hot[at], e)], axis=1)
            p = jnp.exp(nt(left, right) - lse[e : e + 1, at])
            dp = nt(values, dctx_e)
            delta = jnp.sum(delta_t[lanes, at], axis=0, keepdims=True)
            ds = (p * (dp - delta)).astype(BF16)
            dk = dk + nn(ds, query_e)
            dv = dv + nn(p.astype(BF16), dctx_e)
            heads.append(nn(keys_t[lanes, :], ds) * scale)
        dq.append(jnp.concatenate(heads, axis=0).T)
    return jnp.concatenate(dq, axis=0), dk, dv


class Spread:
    def __init__(self, weights, pairs, partners, send_sem, recv_sem):
        self.weights, self.pairs, self.partners = weights, pairs, partners
        self.send_sem, self.recv_sem = send_sem, recv_sem

    def copy(self, step, t):
        w = self.weights
        even, odd = 2 * t, 2 * t + 1
        bit, source, target = (
            (FLIP_Y, w.at[0, even, 0, pl.ds(0, 64)], w.at[0, even, 1, pl.ds(0, 64)]),
            (FLIP_Y, w.at[0, odd, 0, pl.ds(0, 64)], w.at[0, odd, 1, pl.ds(0, 64)]),
            (FLIP_X, w.at[0, even, 1, pl.ds(0, 64)], w.at[0, even, 1, pl.ds(128, 64)]),
            (FLIP_Z0, w.at[0, odd, 1, pl.ds(0, 64)], w.at[0, odd, 1, pl.ds(64, 64)]),
            (FLIP_Z0, w.at[0, even, 1, pl.ds(0, 64)], w.at[0, even, 1, pl.ds(64, 64)]),
            (FLIP_Z0, w.at[0, even, 1, pl.ds(128, 64)], w.at[0, even, 1, pl.ds(192, 64)]),
            (FLIP_X, w.at[0, odd, 1, pl.ds(0, 128)], w.at[0, odd, 1, pl.ds(128, 128)]),
            (FLIP_C, w.at[0, even, 1], w.at[1, even, 1]),
            (FLIP_C, w.at[0, odd, 1], w.at[1, odd, 1]),
        )[step]
        return pltpu.make_async_remote_copy(
            src_ref=source,
            dst_ref=target,
            send_sem=self.send_sem.at[step, t],
            recv_sem=self.recv_sem.at[step, t],
            device_id=self.partners[bit],
            device_id_type=MESH,
        )

    def tick(self, t):
        def at(offset, waits, starts):
            i = t - offset

            @pl.when((i >= 0) & (i < self.pairs))
            def _():
                for step in waits:
                    self.copy(step, i).wait()
                for step in starts:
                    self.copy(step, i).start()

        at(0, (), (0, 1))
        at(5, (7, 8), ())
        at(1, (0, 1), (2, 3))
        at(2, (2, 3), (4, 5, 6))
        at(4, (4, 5, 6), (7, 8))


PER_LAYER = 14
DEPTH = 3


def forward_kernel(layers, *refs):
    refs = list(refs)
    x_ref, up_ref, wq_ref, wo_ref, wi_ref, wd_ref = refs[:6]
    hot_buf, mask_ref, key_ref, bq_ref, bi_ref, vec_ref = refs[6:12]
    w_ref, up_out, x_out = refs[12:15]
    saved = [refs[15 + PER_LAYER * l : 15 + PER_LAYER * (l + 1)] for l in range(layers)]
    (
        x, acc, r_buf, low, xb, qkv, kv_sib, ctx, lse, hl, g_all, slope_all,
        col_buf, row_buf, turn_buf, made_buf, wa_buf, wb_buf,
        feed_sem, load_sem, col_sem, row_sem, made_sem, store_sem, block_sem,
        core_send, core_recv, kv_send, kv_recv, g_send, g_recv, spread_send, spread_recv,
    ) = refs[15 + PER_LAYER * layers :]
    rows, width = acc.shape
    dp, y = lax.axis_index("dp"), lax.axis_index("tensor")
    core = dp % 2
    stays = core == y
    partners = all_partners((FLIP_Y, FLIP_X, FLIP_Z0, FLIP_C, SWAP))
    spread = Spread(w_ref, layers * GROUPS // 2, partners, spread_send, spread_recv)
    greet(partners)

    def feed(n, slot, source, target):
        return pltpu.make_async_copy(source, target, feed_sem.at[n, slot])

    def load(n, source, target):
        return pltpu.make_async_copy(source, target, load_sem.at[n])

    def store(n, source, target):
        return pltpu.make_async_copy(source, target, store_sem.at[n])

    def exchange(n, source, target, bits=FLIP_C):
        return pltpu.make_async_remote_copy(
            src_ref=source, dst_ref=target, send_sem=core_send.at[n], recv_sem=core_recv.at[n],
            device_id=partners[bits], device_id_type=MESH,
        )

    def columns(ref, i, size):
        return ref.at[:, pl.ds(pl.multiple_of(i * size, size), size)]

    def swap(n, source, target, begin):
        here = store(n, source, target)
        there = exchange(n, source, target, SWAP)

        @pl.when(stays)
        def _():
            here.start() if begin else here.wait()

        @pl.when(jnp.logical_not(stays))
        def _():
            there.start() if begin else there.wait()

    items = []
    for l in range(layers):
        items += [(True, wq_ref.at[l, (t + 1) % 3], l * GROUPS + t) for t in range(3)]
        items += [(False, wo_ref.at[l], l * GROUPS + OUT_GROUP)]
        for n in range(FF_GROUPS):
            items += [(True, wi_ref.at[l, :, pl.ds(n * 512, 512)], l * GROUPS + in_group(n))]
            items += [(False, wd_ref.at[l, pl.ds(n * 512, 512)], l * GROUPS + down_group(n))]
    fetches, counts, ahead = [], [0, 0], [[], []]
    for m, (turned, source, group) in enumerate(items):
        slot = counts[turned] % DEPTH
        buf, sem = (col_buf, col_sem) if turned else (row_buf, row_sem)
        fetches.append((pltpu.make_async_copy(source, buf.at[slot], sem.at[slot]), slot))
        ahead[turned].append(m)
        counts[turned] += 1
    bits = [(dp // step) % 2 for step in (1, 2, 4, 8)]
    made = {}

    def convert(m):
        turned, _, group = items[m]
        copy, slot = fetches[m]
        copy.wait()
        if turned:

            def turn(i, _):
                strip = col_buf[slot, :, pl.ds(pl.multiple_of(i * 128, 128), 128)]
                turn_buf[pl.ds(pl.multiple_of(i * 128, 128), 128), :] = strip.astype(BF16).T
                return 0

            lax.fori_loop(0, 4, turn, 0)
        if m >= 2:
            made[m - 2].wait()

        def block(j, _):
            where = 0
            for bit, weight in zip(bits, (8, 4, 2, 1)):
                own = (j // weight) % 2
                where = where + weight * (own + bit - 2 * own * bit)
            at = pl.ds(pl.multiple_of(where * 32, 32), 32)
            rows_32 = turn_buf[at, :] if turned else row_buf[slot, at, :]
            made_buf[m % 2, pl.ds(pl.multiple_of(j * 32, 32), 32), :] = rows_32.astype(BF16)
            return 0

        lax.fori_loop(0, 16, block, 0)
        later = [n for n in ahead[turned] if n > m]
        if len(later) >= DEPTH:
            fetches[later[DEPTH - 1]][0].start()
        parts = [
            pltpu.make_async_copy(
                made_buf.at[m % 2, pl.ds(a * 256, 256)], w_ref.at[a, group, 0], made_sem.at[m % 2, a]
            )
            for a in range(2)
        ]

        class Both:
            def wait(self):
                for part in parts:
                    part.wait()

        for part in parts:
            part.start()
        made[m] = Both()

    load_x = load(0, x_ref.at[:, 0], x)
    load_x.start()
    for kind in range(2):
        for m in ahead[kind][:DEPTH]:
            fetches[m][0].start()
    load_x.wait()

    def narrow_x(at):
        low[at, :] = x[at, :].astype(BF16)

    row_tiles(rows, narrow_x)
    swap(0, low, xb, True)
    for m in range(len(items)):
        convert(m)
        if m % 4 == 3:
            spread.tick(m // 4)
    for m in range(len(items) - 2, len(items)):
        made[m].wait()
    swap(0, low, xb, False)
    load_up = load(1, up_ref.at[:, 0], row_buf.at[0])
    load_up.start()

    def widen(at):
        x[at, :] = xb[at, :].astype(F32)

    row_tiles(rows, widen)

    pairs = width // 128
    for l in range(layers):
        (
            qkv_out, sib_out, ctx_out, ctx_sib_out, lse_out, r1_out, r2_out, hl_out, hl_sib_out,
            g_out, g_sib_out, slope_out, xb_out, xb_sib_out,
        ) = saved[l]
        first = l * GROUPS
        clock = 6 + 6 * l
        xb_store = store(0, xb, xb_out)
        xb_store.start()
        xb_copy = exchange(2 + 3 * l, xb, xb_sib_out)
        xb_copy.start()

        def give_kv(n, a):
            at = pl.ds(pl.multiple_of(a * 512, 512), 512)
            return pltpu.make_async_remote_copy(
                src_ref=qkv.at[1 + n, :, at], dst_ref=kv_sib.at[n, :, at],
                send_sem=kv_send.at[n, a], recv_sem=kv_recv.at[n, a],
                device_id=partners[FLIP_C], device_id_type=MESH,
            )

        def which(i):
            n = lax.div(i, 2)
            return lax.rem(n + 1, 3), n, lax.rem(i, 2)

        def qkv_feeds(i, slot):
            _, n, a = which(i)
            return (feed(0, slot, w_ref.at[a, first + n], wa_buf.at[slot]),)

        def qkv_body(i, slot):
            t, _, a = which(i)
            at = pl.ds(pl.multiple_of(a * 512, 512), 512)
            qkv[t, :, at] = (nt(xb[...], block_of(wa_buf.at[slot])) + bq_ref[l, t, a]).astype(BF16)
            pl.when(t > 0)(lambda: give_kv(t - 1, a).start())
            pl.when(i == 2)(lambda: spread.tick(clock))

        if l == 0:
            begin(qkv_feeds)
        stream(6, qkv_feeds, qkv_body)
        qkv_store = store(1, qkv, qkv_out)
        qkv_store.start()
        for n in range(2):
            for a in range(2):
                give_kv(n, a).wait()
        sib_store = store(2, kv_sib, sib_out)
        sib_store.start()

        feed(2, 0, w_ref.at[0, first + OUT_GROUP], wb_buf.at[0]).start()

        def pair_body(p, _):
            far = lax.rem(p + pairs // 2, pairs)
            here = pl.ds(pl.multiple_of(p * 128, 128), 128)
            there = pl.ds(pl.multiple_of(far * 128, 128), 128)
            mask = spread_mask(mask_ref[p], key_ref[...])
            keys = jnp.concatenate([qkv[1, :, here], kv_sib[0, :, there]], axis=0)
            values = jnp.concatenate([qkv[2, :, here], kv_sib[1, :, there]], axis=0)
            context, parts = attend_pair(qkv[0, :, here], keys, values, hot_buf[...], mask)
            ctx[:, here] = context.astype(BF16)
            for e in range(2):
                lse[p, e : e + 1, :] = parts[e]
            pl.when(lax.rem(p, 5) == 2)(lambda: spread.tick(clock + 1 + lax.div(p, 5)))
            return 0

        lax.fori_loop(0, pairs, pair_body, 0)
        ctx_store = store(3, ctx, ctx_out)
        ctx_store.start()
        lse_store = store(4, lse, lse_out)
        lse_store.start()
        ctx_copy = exchange(3 + 3 * l, ctx.at[:, pl.ds(512, 512)], ctx_sib_out)
        ctx_copy.start()

        def place_of(i):
            return 1 - lax.rem(i, 2), lax.div(i, 2)

        def ff_feeds(i, slot):
            a, n = place_of(i)
            return (
                feed(0, slot, w_ref.at[a, first + in_group(n)], wa_buf.at[slot]),
                feed(2, slot, w_ref.at[a, first + down_group(n)], wb_buf.at[slot]),
            )

        ff_feeds(0, 0)[0].start()

        def out_feeds(i, slot):
            return (feed(2, slot, w_ref.at[i, first + OUT_GROUP], wb_buf.at[slot]),)

        def out_body(i, slot):
            part = nn(ctx[:, pl.ds(pl.multiple_of(i * 512, 512), 512)], block_of(wb_buf.at[slot]))

            @pl.when(i == 0)
            def _():
                acc[...] = part

            @pl.when(i == 1)
            def _():
                acc[...] += part

        stream(2, out_feeds, out_body)
        ff_feeds(0, 0)[1].start()
        sib_store.wait()

        def first_norm(at):
            r1 = x[at, :] + acc[at, :] + vec_ref[l, 0:1, :]
            r_buf[at, :] = r1
            h = norm(r1, vec_ref[l, 1:2, :], vec_ref[l, 2:3, :])
            hl[at, :] = h.astype(BF16)
            acc[at, :] = h + vec_ref[l, 3:4, :]

        row_tiles(rows, first_norm)
        r1_store = store(5, r_buf, r1_out)
        r1_store.start()
        hl_store = store(6, hl, hl_out)
        hl_store.start()
        hl_copy = exchange(4 + 3 * l, hl, hl_sib_out)
        hl_copy.start()

        def g_store(j):
            return pltpu.make_async_copy(g_all.at[j], columns(g_out, j, 512), block_sem.at[0, j])

        def slope_store(j):
            return pltpu.make_async_copy(slope_all.at[j], columns(slope_out, j, 512), block_sem.at[1, j])

        def g_copy(n):
            return pltpu.make_async_remote_copy(
                src_ref=g_all.at[FF_GROUPS + n], dst_ref=columns(g_sib_out, n, 512),
                send_sem=g_send.at[l, n], recv_sem=g_recv.at[l, n],
                device_id=partners[FLIP_C], device_id_type=MESH,
            )

        def ff_body(i, slot):
            a, n = place_of(i)
            j = a * FF_GROUPS + n
            u = nt(hl[...], block_of(wa_buf.at[slot])) + bi_ref[l, a, n]
            g, slope = gelu_and_slope(u)
            g = g.astype(BF16)
            g_all[j] = g
            slope_all[j] = slope.astype(BF16)
            g_store(j).start()
            slope_store(j).start()
            pl.when(a == 1)(lambda: g_copy(n).start())
            acc[...] += nn(g, block_of(wb_buf.at[slot]))
            pl.when(lax.rem(i, 3) == 1)(lambda: spread.tick(clock + 3 + lax.div(i, 3)))

        stream(2 * FF_GROUPS, ff_feeds, ff_body)
        r1_store.wait()
        xb_store.wait()
        xb_copy.wait()
        if l + 1 < layers:
            feed(0, 0, w_ref.at[0, first + GROUPS], wa_buf.at[0]).start()
        if l == 0:
            load_up.wait()

            def narrow_up(at):
                low[at, :] = row_buf[0, at, :].astype(BF16)

            row_tiles(rows, narrow_up)
            swap(9, low, up_out, True)

        def second_norm(at):
            r2 = acc[at, :]
            r_buf[at, :] = r2
            x2 = norm(r2, vec_ref[l, 4:5, :], vec_ref[l, 5:6, :])
            x[at, :] = x2
            xb[at, :] = x2.astype(BF16)

        row_tiles(rows, second_norm)
        r2_store = store(5, r_buf, r2_out)
        r2_store.start()
        if l == layers - 1:
            x_store = store(10, xb, x_out)
            x_store.start()

        def settle(j, _):
            g_store(j).wait()
            slope_store(j).wait()
            return 0

        lax.fori_loop(0, 2 * FF_GROUPS, settle, 0)

        def settle_sent(n, _):
            g_copy(n).wait()
            return 0

        lax.fori_loop(0, FF_GROUPS, settle_sent, 0)
        for copy in (qkv_store, ctx_store, lse_store, ctx_copy, hl_store, hl_copy, r2_store):
            copy.wait()
    x_store.wait()
    swap(9, low, up_out, False)


def forward(block_input, cotangent, w_qkv, w_out, w_in, w_down, hot, mask, mask_rows, bias_qkv, bias_in, vectors):
    rows, _, width = block_input.shape
    layers = w_qkv.shape[0]
    total = layers * GROUPS
    anywhere = pl.BlockSpec(memory_space=pl.ANY)
    in_vmem = pl.BlockSpec(memory_space=pltpu.VMEM)
    low = lambda *shape: pltpu.VMEM(shape, BF16)
    full = lambda *shape: pltpu.VMEM(shape, F32)
    dma = lambda *shape: pltpu.SemaphoreType.DMA(shape)
    low_out = lambda *shape: jax.ShapeDtypeStruct(shape, BF16)
    full_out = lambda *shape: jax.ShapeDtypeStruct(shape, F32)
    layer_out = (
        low_out(3, rows, width),
        low_out(2, rows, width),
        low_out(rows, width),
        low_out(rows, width // 2),
        full_out(width // 128, 2, rows),
        full_out(rows, width),
        full_out(rows, width),
        low_out(rows, width),
        low_out(rows, width),
        low_out(rows, 4 * width),
        low_out(rows, 2 * width),
        low_out(rows, 4 * width),
        low_out(rows, width),
        low_out(rows, width),
    )
    outs = pl.pallas_call(
        functools.partial(forward_kernel, layers),
        out_shape=(low_out(2, total, 2, 256, width), low_out(rows, width), low_out(rows, width)) + layer_out * layers,
        in_specs=[anywhere] * 6 + [in_vmem] * 6,
        out_specs=(anywhere,) * (3 + PER_LAYER * layers),
        scratch_shapes=[
            full(rows, width),
            full(rows, width),
            full(rows, width),
            low(rows, width),
            low(rows, width),
            low(3, rows, width),
            low(2, rows, width),
            low(rows, width),
            full(width // 128, 2, rows),
            low(rows, width),
            low(2 * FF_GROUPS, rows, 512),
            low(2 * FF_GROUPS, rows, 512),
            full(DEPTH, width, 512),
            full(DEPTH, 512, width),
            low(512, width),
            low(2, 512, width),
            low(2, 2, 256, width),
            low(2, 2, 256, width),
            dma(3, 2),
            dma(3),
            dma(DEPTH),
            dma(DEPTH),
            dma(2, 2),
            dma(11),
            dma(2, 2 * FF_GROUPS),
            dma(11),
            dma(11),
            dma(2, 2),
            dma(2, 2),
            dma(layers, FF_GROUPS),
            dma(layers, FF_GROUPS),
            dma(9, total // 2),
            dma(9, total // 2),
        ],
        compiler_params=pltpu.CompilerParams(collective_id=0, has_side_effects=True, vmem_limit_bytes=60 << 20),
        cost_estimate=pl.CostEstimate(flops=30 << 30, bytes_accessed=300 << 20, transcendentals=1 << 24),
        name="forward",
    )(block_input, cotangent, w_qkv, w_out, w_in, w_down, hot, mask, mask_rows, bias_qkv, bias_in, vectors)
    saved = [outs[3 + PER_LAYER * l : 3 + PER_LAYER * (l + 1)] for l in range(layers)]
    return outs[0], outs[1], outs[2], saved


def backward_kernel(layers, *refs):
    refs = list(refs)
    up_ref, x_ref, w_ref, hot_buf, mask_ref, key_ref, vec_ref = refs[:7]
    saved = [refs[7 + PER_LAYER * l : 7 + PER_LAYER * (l + 1)] for l in range(layers)]
    at_ref = 7 + PER_LAYER * layers
    grads, sums, dx_out, x_out, packed = refs[at_ref : at_ref + 5]
    (
        acc, dr1, dm, dm_sib, da, da_sib, du, du_sib, dctx, dqkv, d_sib, kv_out, kv_far,
        wa_buf, wb_buf, r_buf, slope_buf, left_buf, left_sib_buf, right_buf, right_sib_buf,
        pair_buf, lse_buf, unit_buf,
        y_buf, x_buf, z0_buf, z1_buf, all_buf, keep_buf,
        feed_sem, load_sem, store_sem, swap_sem, core_send, core_recv, du_send, du_recv, pair_send, pair_recv,
        send_sem, recv_sem, sum_send, sum_recv, keep_sem, out_sem, in_free, out_free,
        dbi_ref, qkv_sums_ref, small_ref, far_buf, far_send, far_recv,
    ) = refs[at_ref + 5 : -12]
    part_bufs, part_sems = refs[-12:-6], refs[-6:]
    rows, width = acc.shape
    total = layers * GROUPS
    partners = all_partners((FLIP_Y, FLIP_X, FLIP_Z0, FLIP_Z1, FLIP_C, SWAP))
    whole = total - PARTED
    reduction = Reduction(
        grads, sums, 0, whole, 1, partners,
        (y_buf, x_buf, z0_buf, z1_buf, all_buf, keep_buf),
        (send_sem, recv_sem, sum_send, sum_recv, keep_sem, out_sem, in_free, out_free),
    )
    ending = Reduction(grads, sums, whole, PARTED, PARTS, partners, part_bufs, part_sems)
    greet(partners)

    def feed(n, slot, source, target):
        return pltpu.make_async_copy(source, target, feed_sem.at[n, slot])

    def load(n, source, target):
        return pltpu.make_async_copy(source, target, load_sem.at[n])

    def exchange(n, source, target):
        return pltpu.make_async_remote_copy(
            src_ref=source, dst_ref=target, send_sem=core_send.at[n], recv_sem=core_recv.at[n],
            device_id=partners[FLIP_C], device_id_type=MESH,
        )

    def give_du(j, n):
        return pltpu.make_async_remote_copy(
            src_ref=du.at[j], dst_ref=du_sib.at[n], send_sem=du_send.at[n], recv_sem=du_recv.at[n],
            device_id=partners[FLIP_C], device_id_type=MESH,
        )

    def weight(a, group):
        return w_ref.at[a, group]

    def columns(ref, i, size):
        return ref.at[:, pl.ds(pl.multiple_of(i * size, size), size)]

    def unit_store(slot, index):
        return pltpu.make_async_copy(unit_buf.at[slot], grads.at[index], store_sem.at[0])

    def unit(left, left_sib, right, right_sib, slot, index, fresh=False):
        made = (tn(left, right) + tn(left_sib, right_sib)).astype(BF16)
        unit_buf[slot] = made.reshape(unit_buf.shape[1:])
        if fresh is not False:
            pl.when(jnp.logical_not(fresh))(lambda: unit_store(slot, index).wait())
        else:
            unit_store(slot, index).wait()
        unit_store(slot, index).start()

    def add_small(l, row, value):
        small_ref[l, row : row + 1, :] += jnp.sum(value, axis=0, keepdims=True)

    stays = lax.axis_index("dp") % 2 == lax.axis_index("tensor")

    def swap(n, source, target, begin):
        here = pltpu.make_async_copy(source, target, swap_sem.at[n])
        there = pltpu.make_async_remote_copy(
            src_ref=source, dst_ref=target, send_sem=core_send.at[4 + n], recv_sem=core_recv.at[4 + n],
            device_id=partners[SWAP], device_id_type=MESH,
        )

        @pl.when(stays)
        def _():
            here.start() if begin else here.wait()

        @pl.when(jnp.logical_not(stays))
        def _():
            there.start() if begin else there.wait()

    swap(1, x_ref, x_out, True)
    load(0, saved[-1][6], r_buf).start()
    start_up = load(1, up_ref, da)
    start_up.start()
    start_up.wait()
    small_ref[...] = jnp.zeros_like(small_ref)

    def widen(at):
        acc[at, :] = da[at, :].astype(F32)

    row_tiles(rows, widen)
    done = 0
    for l in reversed(range(layers)):
        qkv_ref, sib_ref, ctx_ref, ctx_sib_ref, lse_ref, r1_ref, r2_ref, hl_ref, hl_sib_ref, g_ref, g_sib_ref, slope_ref, xb_ref, xb_sib_ref = saved[l]
        first = l * GROUPS
        base = (layers - 1 - l) * GROUPS
        clock = 11 * (layers - 1 - l)

        def down_feeds(i, slot):
            return (
                feed(0, slot, columns(g_ref, i, 512), left_buf.at[slot]),
                feed(1, slot, columns(g_sib_ref, i, 512), left_sib_buf.at[slot]),
            )

        begin(down_feeds)
        load(0, r2_ref, r_buf).wait()

        def second(at):
            dy = acc[at, :]
            dr, part = norm_back(dy, r_buf[at, :], vec_ref[l, 4:5, :])
            acc[at, :] = dr
            dm[at, :] = dr.astype(BF16)
            add_small(l, 0, part)
            add_small(l, 1, dy)
            add_small(l, 2, dr)

        row_tiles(rows, second)
        dm_copy = exchange(0, dm, dm_sib)
        dm_copy.start()
        r_load = load(0, r1_ref, r_buf)
        r_load.start()
        right_load = load(1, hl_ref, right_buf)
        right_load.start()
        right_sib_load = load(2, hl_sib_ref, right_sib_buf)
        right_sib_load.start()
        dm_copy.wait()

        def down_body(i, slot):
            fresh = (i == 0) if l == layers - 1 else False
            unit(left_buf[slot], left_sib_buf[slot], dm[...], dm_sib[...], lax.rem(i, 2), base + i, fresh)
            pl.when(lax.rem(i, 2) == 1)(lambda: reduction.tick(clock + lax.div(i, 2)))

        def place_of(i):
            a = 1 - lax.div(i, FF_GROUPS)
            return a, lax.rem(i, FF_GROUPS)

        def ff_feeds(i, slot):
            a, n = place_of(i)
            j = a * FF_GROUPS + n
            return (
                feed(2, slot, weight(a, first + down_group(n)), wa_buf.at[slot]),
                feed(3, slot, weight(a, first + in_group(n)), wb_buf.at[slot]),
                feed(4, slot, columns(slope_ref, j, 512), slope_buf.at[slot]),
            )

        begin(ff_feeds)
        stream(FF_GROUPS, down_feeds, down_body)
        unit_store(1, base + FF_GROUPS - 1).wait()

        def ff_body(i, slot):
            a, n = place_of(i)
            j = a * FF_GROUPS + n
            dg = nt(dm[...], block_of(wa_buf.at[slot]))
            d = (dg * slope_buf[slot].astype(F32)).astype(BF16)
            du[j] = d
            pl.when(a == 1)(lambda: give_du(j, n).start())
            dbi_ref[l, a, n] = jnp.sum(d.astype(F32), axis=0, keepdims=True)
            acc[...] += nn(d, block_of(wb_buf.at[slot]))
            pl.when(lax.rem(i, 4) == 3)(lambda: reduction.tick(clock + 2 + lax.div(i, 4)))

        stream(2 * FF_GROUPS, ff_feeds, ff_body)

        def out_feeds(i, slot):
            return (feed(2, slot, weight(i, first + OUT_GROUP), wa_buf.at[slot]),)

        begin(out_feeds)
        r_load.wait()

        def first_norm(at):
            dy = acc[at, :]
            dr, part = norm_back(dy, r_buf[at, :], vec_ref[l, 1:2, :])
            dr1[at, :] = dr
            da[at, :] = dr.astype(BF16)
            add_small(l, 3, part)
            add_small(l, 4, dy)
            add_small(l, 5, dr)

        row_tiles(rows, first_norm)
        if l > 0:
            load(0, saved[l - 1][6], r_buf).start()
        da_copy = exchange(1, da, da_sib)
        da_copy.start()

        def out_body(i, slot):
            dctx[:, pl.ds(pl.multiple_of(i * 512, 512), 512)] = nt(da[...], block_of(wa_buf.at[slot])).astype(BF16)

        stream(2, out_feeds, out_body)

        pairs = width // 128

        def pair_feeds(p, slot):
            far = lax.rem(p + pairs // 2, pairs)
            return (
                feed(5, slot, columns(qkv_ref.at[0], p, 128), pair_buf.at[slot, 0, pl.ds(0, rows)]),
                feed(6, slot, columns(qkv_ref.at[1], p, 128), pair_buf.at[slot, 1, pl.ds(0, rows)]),
                feed(7, slot, columns(sib_ref.at[0], far, 128), pair_buf.at[slot, 1, pl.ds(rows, rows)]),
                feed(8, slot, columns(qkv_ref.at[2], p, 128), pair_buf.at[slot, 2, pl.ds(0, rows)]),
                feed(9, slot, columns(sib_ref.at[1], far, 128), pair_buf.at[slot, 2, pl.ds(rows, rows)]),
                feed(10, slot, columns(ctx_ref, p, 128), pair_buf.at[slot, 3, pl.ds(0, rows)]),
                feed(11, slot, lse_ref.at[p], lse_buf.at[slot]),
            )

        begin(pair_feeds)
        right_load.wait()
        right_sib_load.wait()

        def in_body(n, _):
            give_du(FF_GROUPS + n, n).wait()
            unit(du[n], du_sib[n], right_buf[...], right_sib_buf[...], lax.rem(n, 2), base + FF_GROUPS + n, n == 0)
            pl.when(lax.rem(n, 2) == 1)(lambda: reduction.tick(clock + 4 + lax.div(n, 2)))
            return 0

        lax.fori_loop(0, FF_GROUPS, in_body, 0)

        right_load = load(1, xb_ref, right_buf)
        right_load.start()
        right_sib_load = load(2, xb_sib_ref, right_sib_buf)
        right_sib_load.start()
        left_load = load(3, columns(ctx_ref, 0, 512), left_buf.at[0])
        left_load.start()
        left_sib_load = load(4, ctx_sib_ref, left_sib_buf.at[0])
        left_sib_load.start()
        da_copy.wait()
        left_load.wait()
        left_sib_load.wait()
        unit(left_buf[0], left_sib_buf[0], da[...], da_sib[...], 0, base + 2 * FF_GROUPS)
        unit_store(0, base + 2 * FF_GROUPS).wait()

        def dx_feeds(i, slot):
            return (feed(3, slot, weight(lax.rem(i, 2), first + lax.rem(lax.div(i, 2) + 2, 3)), wa_buf.at[slot]),)

        begin(dx_feeds)

        def give_pair(p):
            far = lax.rem(p + pairs // 2, pairs)
            at = pl.ds(pl.multiple_of(far * 128, 128), 128)
            return pltpu.make_async_remote_copy(
                src_ref=kv_out.at[:, :, at], dst_ref=kv_far.at[:, :, at], send_sem=pair_send.at[p], recv_sem=pair_recv.at[far],
                device_id=partners[FLIP_C], device_id_type=MESH,
            )

        def pair_body(p, slot):
            far = lax.rem(p + pairs // 2, pairs)
            here = pl.ds(pl.multiple_of(p * 128, 128), 128)
            mask = spread_mask(mask_ref[p], key_ref[...])
            dq, dk, dv = attend_back_pair(
                pair_buf[slot, 0, 0:rows], pair_buf[slot, 1], pair_buf[slot, 2], hot_buf[...], mask,
                pair_buf[slot, 3, 0:rows], lse_buf[slot], dctx[:, here],
            )
            dqkv[0, :, here] = dq.astype(BF16)
            dqkv[1, :, here] = dk[:rows].astype(BF16)
            dqkv[2, :, here] = dv[:rows].astype(BF16)
            there = pl.ds(pl.multiple_of(far * 128, 128), 128)
            kv_out[0, :, there] = dk[rows:].astype(BF16)
            kv_out[1, :, there] = dv[rows:].astype(BF16)
            give_pair(p).start()
            pl.when(lax.rem(p, 3) == 1)(lambda: reduction.tick(clock + 6 + lax.div(p, 3)))

        stream(pairs, pair_feeds, pair_body)

        def settle_pair(p, _):
            give_pair(p).wait()
            return 0

        lax.fori_loop(0, pairs, settle_pair, 0)
        for n in range(2):
            add_rows(dqkv.at[1 + n], kv_far.at[n], rows)
        d_copy = exchange(3, dqkv.at[:, :, pl.ds(512, 512)], d_sib)
        d_copy.start()
        right_load.wait()
        right_sib_load.wait()
        d_copy.wait()

        def qkv_body(n, _):
            unit(
                dqkv[n, :, 0:512], d_sib[n], right_buf[...], right_sib_buf[...],
                lax.rem(n + 1, 2), base + 2 * FF_GROUPS + 1 + n, n == 0,
            )
            pl.when(n == 1)(lambda: reduction.tick(clock + 9))
            return 0

        lax.fori_loop(0, 3, qkv_body, 0)

        def start_dx(at):
            acc[at, :] = dr1[at, :]

        row_tiles(rows, start_dx)

        def dx_body(i, slot):
            a, n = lax.rem(i, 2), lax.div(i, 2)
            d = dqkv[n, :, pl.ds(pl.multiple_of(a * 512, 512), 512)]
            qkv_sums_ref[l, n, a] = jnp.sum(d.astype(F32), axis=0, keepdims=True)
            acc[...] += nn(d, block_of(wa_buf.at[slot]))
            pl.when(i == 3)(lambda: reduction.tick(clock + 10))

        stream(6, dx_feeds, dx_body)
        done = clock + 11

    def narrow(at):
        da[at, :] = acc[at, :].astype(BF16)

    row_tiles(rows, narrow)
    unit_store(1, total - 1).wait()
    ending.tick(0)
    dp, y = lax.axis_index("dp"), lax.axis_index("tensor")
    core = dp % 2
    turned = unit_order(y, ((dp // 2) % 2, (dp // 4) % 2, (dp // 8) % 2))

    def in_order(pair):
        rows_ab = lax.dot_general(
            jnp.concatenate(pair, axis=0), turned, (((1,), (0,)), ((), ())),
            precision=lax.Precision.HIGHEST, preferred_element_type=F32,
        )
        near = jnp.where(core == 0, rows_ab[0:1], rows_ab[1:2])
        far = jnp.where(core == 0, rows_ab[1:2], rows_ab[0:1])
        return [
            jnp.concatenate([near[:, h * 256 : (h + 1) * 256], far[:, h * 256 : (h + 1) * 256]], axis=1)
            for h in range(2)
        ]

    for l in range(layers):
        for n, source in enumerate((5, 2, 3, 0, 4, 1)):
            row = n * layers + l if n < 2 else 2 * layers + (n // 2 - 1) * 2 * layers + 2 * l + n % 2
            packed[row : row + 1, :] = small_ref[l, source : source + 1, :]
        for n, t in enumerate((0, 2)):
            for h, part in enumerate(in_order([qkv_sums_ref[l, t, a] for a in range(2)])):
                packed[6 * layers + h * layers + l : 6 * layers + h * layers + l + 1, n * 512 : (n + 1) * 512] = part
        for n in range(FF_GROUPS):
            for h, part in enumerate(in_order([dbi_ref[l, a, n] for a in range(2)])):
                row = 8 * layers + h * 2 * layers + 2 * l + n // 2
                packed[row : row + 1, (n % 2) * 512 : (n % 2 + 1) * 512] = part

    for n, bit in enumerate((FLIP_C, FLIP_Y, FLIP_X, FLIP_Z0, FLIP_Z1)):
        cross = pltpu.make_async_remote_copy(
            src_ref=packed, dst_ref=far_buf.at[n], send_sem=far_send.at[n], recv_sem=far_recv.at[n],
            device_id=partners[bit], device_id_type=MESH,
        )
        cross.start()
        reduction.tick(done + n)
        ending.tick(1 + n)
        cross.wait()
        packed[...] += far_buf[n]

    swap(0, da, dx_out, True)

    def rest(n, _):
        reduction.tick(done + n)
        ending.tick(1 + n)
        return 0

    lax.fori_loop(5, PARTED * PARTS + LAST_TICK - 1, rest, 0)
    swap(0, da, dx_out, False)
    swap(1, x_ref, x_out, False)


def backward(upstream, stream_low, weights, hot, mask, mask_rows, vectors, saved):
    rows, width = upstream.shape
    layers = len(saved)
    total = layers * GROUPS
    anywhere = pl.BlockSpec(memory_space=pl.ANY)
    in_vmem = pl.BlockSpec(memory_space=pltpu.VMEM)
    low = lambda *shape: pltpu.VMEM(shape, BF16)
    dma = lambda *shape: pltpu.SemaphoreType.DMA(shape)
    ends = PARTED * PARTS
    return pl.pallas_call(
        functools.partial(backward_kernel, layers),
        out_shape=(
            jax.ShapeDtypeStruct((total, 16, 32, width), BF16),
            jax.ShapeDtypeStruct((total, 16, 32, width), BF16),
            jax.ShapeDtypeStruct((rows, width), BF16),
            jax.ShapeDtypeStruct((rows, width), BF16),
            jax.ShapeDtypeStruct((12 * layers, width), F32),
        ),
        in_specs=[anywhere] * 3 + [in_vmem] * 4 + [anywhere] * (PER_LAYER * layers),
        out_specs=(anywhere, anywhere, anywhere, anywhere, in_vmem),
        scratch_shapes=[
            pltpu.VMEM((rows, width), F32),
            pltpu.VMEM((rows, width), F32),
            low(rows, width),
            low(rows, width),
            low(rows, width),
            low(rows, width),
            low(2 * FF_GROUPS, rows, 512),
            low(FF_GROUPS, rows, 512),
            low(rows, width),
            low(3, rows, width),
            low(3, rows, 512),
            low(2, rows, width),
            low(2, rows, width),
            low(2, 2, 256, width),
            low(2, 2, 256, width),
            pltpu.VMEM((rows, width), F32),
            low(2, rows, 512),
            low(2, rows, 512),
            low(2, rows, 512),
            low(rows, width),
            low(rows, width),
            low(2, 4, 2 * rows, 128),
            pltpu.VMEM((2, 2, rows), F32),
            low(2, 16, 32, width),
            low(SLOTS, 8, 32, width),
            low(SLOTS, 4, 32, width),
            low(SLOTS, 2, 32, width),
            low(SLOTS, 1, 32, width),
            low(SLOTS, 8, 32, width),
            low(2, 8, 32, width),
            dma(12, 2),
            dma(5),
            dma(1),
            dma(2),
            dma(6),
            dma(6),
            dma(FF_GROUPS),
            dma(FF_GROUPS),
            dma(width // 128),
            dma(width // 128),
            dma(7, SLOTS),
            dma(7, SLOTS),
            dma(total),
            dma(total),
            dma(2),
            dma(SLOTS),
            pltpu.SemaphoreType.REGULAR((4,)),
            pltpu.SemaphoreType.REGULAR((3,)),
            pltpu.VMEM((layers, 2, FF_GROUPS, 1, 512), F32),
            pltpu.VMEM((layers, 3, 2, 1, 512), F32),
            pltpu.VMEM((layers, 8, width), F32),
            pltpu.VMEM((5, 12 * layers, width), F32),
            dma(5),
            dma(5),
            low(ends, 8, 32 // PARTS, width),
            low(ends, 4, 32 // PARTS, width),
            low(ends, 2, 32 // PARTS, width),
            low(ends, 1, 32 // PARTS, width),
            low(ends, 8, 32 // PARTS, width),
            low(2, 8, 32 // PARTS, width),
            dma(7, ends),
            dma(7, ends),
            dma(ends),
            dma(ends),
            dma(2),
            dma(ends),
        ],
        compiler_params=pltpu.CompilerParams(
            collective_id=1, has_side_effects=True, vmem_limit_bytes=60 << 20
        ),
        cost_estimate=pl.CostEstimate(flops=60 << 30, bytes_accessed=300 << 20, transcendentals=1 << 24),
        name="backward",
    )(upstream, stream_low, weights, hot, mask, mask_rows, vectors, *[ref for one in saved for ref in one])


def flip_order(values, axis, bits):
    for i, bit in enumerate(bits):
        values = jnp.where(bit == 0, values, jnp.flip(values, axis + i))
    return values


def sequence_shards(
    block_input, segment_ids, random_blocks, w_qkv, b_qv, w_out, b_out, w_in, b_in, w_down, b_down,
    ln_gain, ln_bias, cotangent,
):
    y = lax.axis_index("tensor")
    dp = lax.axis_index("dp")
    core, x_bit, z0, z1 = dp % 2, (dp // 2) % 2, (dp // 4) % 2, dp // 8
    code = core * 8 + x_bit * 4 + z0 * 2 + z1
    code_arg = code.reshape(1).astype(jnp.int32)
    device_bits = (core, x_bit, z0, z1)

    rows, _, width = block_input.shape
    layers = w_qkv.shape[0]
    blocks = random_blocks.shape[2]
    own_blocks = blocks // 2
    heads = random_blocks.shape[1] * 2

    chosen = random_blocks[0]
    near = jnp.concatenate([chosen.reshape(-1), segment_ids[0]])
    sibling = flip(near, FLIP_C)
    across, diagonal = flip(chosen.reshape(-1), FLIP_Y), flip(chosen.reshape(-1), SWAP)
    mine = jnp.concatenate([near[: chosen.size], across, near[chosen.size :]])
    other = jnp.concatenate([sibling[: chosen.size], diagonal, sibling[chosen.size :]])
    packed = jnp.where(core == y, mine, other)
    chosen = packed[: 2 * chosen.size].reshape(2, heads // 2, blocks, -1)
    segments = packed[2 * random_blocks.size :]
    chosen = flip_order(chosen.reshape(2, 2, 2, 2, blocks, -1), 1, device_bits[:3])
    chosen = chosen.transpose(1, 0, 2, 3, 4, 5).reshape(heads, blocks, -1)
    segments = segments.reshape(2, rows)
    segments = jnp.where(core == 0, segments, segments[::-1]).reshape(-1)
    query_block = core * own_blocks + jnp.arange(own_blocks)
    key_block = jnp.arange(blocks) ^ (core * own_blocks)
    allowed = (
        (jnp.abs(query_block[:, None] - key_block[None, :]) <= 1)
        | (key_block[None, :] == 0)
        | (key_block[None, :] == blocks - 1)
        | (query_block[:, None] == 0)
        | (query_block[:, None] == blocks - 1)
    )
    chosen = lax.dynamic_slice_in_dim(chosen, core * own_blocks, own_blocks, axis=1)
    allowed = allowed[None] | jnp.any(chosen[:, :, None, :] == key_block[None, None, :, None], axis=3)
    block_rows = rows // own_blocks
    documents = jnp.arange(HEAD_DIM - own_blocks)
    mask = jnp.pad(
        jnp.where(allowed, 0.0, BIG).astype(F32).transpose(0, 2, 1), ((0, 0), (0, 0), (0, HEAD_DIM - own_blocks))
    )
    mask = mask.reshape(heads // 2, 2, blocks, HEAD_DIM).transpose(0, 2, 1, 3).reshape(heads // 2, blocks, 2 * HEAD_DIM)
    document_part = jnp.where(
        (segments[:, None] == documents[None, :]) | (documents[None, :] > 7), 0.0, BIG
    ).astype(F32)
    mask_rows = jnp.pad(document_part, ((0, 0), (own_blocks, 0)))
    mask_rows = jnp.concatenate([mask_rows, mask_rows], axis=1)
    block_rows = rows // own_blocks
    hot = jnp.concatenate(
        [
            jnp.repeat(jnp.eye(own_blocks, dtype=BF16), block_rows, axis=0),
            (segments[:rows, None] == documents[None, :]).astype(BF16),
        ],
        axis=1,
    )
    hot = jnp.concatenate([hot, hot], axis=1)

    bias_pack = jnp.concatenate(
        [
            flip_order(b_qv.reshape(layers * 2, 2, 2, 2, 2, -1), 1, device_bits).reshape(-1),
            flip_order(b_in.reshape(layers * FF_GROUPS, 2, 2, 2, 2, -1), 1, device_bits).reshape(-1),
        ]
    )
    bias_far = flip(bias_pack, FLIP_Y)
    n_qv = b_qv.size

    def local_bias(near, far, count):
        near, far = near.reshape(count, 2, 1, 256), far.reshape(count, 2, 1, 256)
        return jnp.concatenate([near, far], axis=2).reshape(count, 2, 512)

    bias_qv = local_bias(bias_pack[:n_qv], bias_far[:n_qv], layers * 2).reshape(layers, 2, 2, 1, 512)
    bias_qkv = jnp.stack([bias_qv[:, 0], jnp.zeros_like(bias_qv[:, 0]), bias_qv[:, 1]], axis=1)
    bias_in = local_bias(bias_pack[n_qv:], bias_far[n_qv:], layers * FF_GROUPS)
    bias_in = bias_in.reshape(layers, FF_GROUPS, 2, 1, 512).swapaxes(1, 2)

    vectors = [
        jnp.stack(
            [
                b_out[l], ln_gain[l, 0], ln_bias[l, 0], b_down[l], ln_gain[l, 1], ln_bias[l, 1],
                b_out[l], b_out[l],
            ]
        )
        for l in range(layers)
    ]
    vectors = jnp.stack(vectors)
    weights, upstream_low, stream_low, saved = forward(
        block_input, cotangent, w_qkv, w_out, w_in, w_down, hot, mask, mask_rows, bias_qkv, bias_in, vectors
    )
    _, grads, dx_low, x_low, packed = backward(
        upstream_low, stream_low, weights, hot, mask, mask_rows, vectors, saved
    )
    grads = grads.reshape(layers * GROUPS, 512, width)

    def placing(shape, block, index, turned, count, start, rows_too=()):
        return place(
            grads, shape, block, index, turned, count, lambda l, i: (layers - 1 - l) * GROUPS + start + i, code_arg,
            rows_too,
        )

    g_b_out, g_b_down, g_gain, g_shift, g_b_qv, g_b_in = hand_out(packed, y.reshape(1).astype(jnp.int32), layers)
    g_down, block_output, input_grad = placing(
        w_down.shape, (1, 512, width), lambda l, i: (l, i, 0), False, FF_GROUPS, 0, (x_low, dx_low)
    )
    (g_in,) = placing(w_in.shape, (1, width, 512), lambda l, i: (l, 0, i), True, FF_GROUPS, FF_GROUPS)
    (g_qkv,) = placing(w_qkv.shape, (1, 1, width, 512), lambda l, i: (l, i, 0, 0), True, 3, 2 * FF_GROUPS + 1)
    (g_out,) = placing(w_out.shape, (1, 512, width), lambda l, i: (l, 0, 0), False, 1, 2 * FF_GROUPS)
    return (
        block_output,
        input_grad,
        g_qkv,
        g_b_qv,
        g_out,
        g_b_out,
        g_in,
        g_b_in,
        g_down,
        g_b_down,
        g_gain,
        g_shift,
    )


def as_sent(array):

    def short(part):
        return part.astype(jnp.bfloat16) if part.dtype == jnp.float32 else part

    return jax.tree.map(short, array)


def norm_rows(values, gain_row, shift_row):
    row_mean = jnp.mean(values, axis=-1, keepdims=True)
    centred = values - row_mean
    variance = jnp.mean(centred * centred, axis=-1, keepdims=True)
    return centred * lax.rsqrt(variance + 1e-06) * gain_row + shift_row


def gelu_exact(values):
    return jax.nn.gelu(values, approximate=False)


def block_mask(chosen_blocks, segment_rows):
    nblocks = chosen_blocks.shape[2]
    block_index = jnp.arange(nblocks)
    near_blocks = jnp.abs(block_index[:, None] - block_index[None, :]) <= 1
    edge_blocks = (
        (block_index[None, :] == 0)
        | (block_index[None, :] == nblocks - 1)
        | (block_index[:, None] == 0)
        | (block_index[:, None] == nblocks - 1)
    )
    picked_blocks = jnp.any(chosen_blocks[..., None] == block_index, axis=3)
    allowed = near_blocks | edge_blocks | picked_blocks
    block_rows = segment_rows.shape[1] // nblocks
    allowed = jnp.repeat(jnp.repeat(allowed, block_rows, axis=2), block_rows, axis=3)
    same_doc = segment_rows[:, :, None] == segment_rows[:, None, :]
    return allowed & same_doc[:, None]


def masked_scores(queries, key_rows, allowed, score_scale):
    scores = (
        jnp.einsum("qshd,kshd->shqk", queries, key_rows, preferred_element_type=jnp.float32)
        * score_scale
    )
    return jnp.where(allowed, scores, -1e30)


def shards(
    block_input,
    segment_ids,
    random_blocks,
    w_qkv,
    b_qv,
    w_out,
    b_out,
    w_in,
    b_in,
    w_down,
    b_down,
    ln_gain,
    ln_bias,
    cotangent,
):
    score_scale = HEAD_DIM ** (-0.5)
    shard_rows, seq_count, model_width = block_input.shape
    layers = w_qkv.shape[0]
    local_width = w_qkv.shape[3]
    local_heads = local_width // HEAD_DIM
    allowed = block_mask(random_blocks, segment_ids)
    saved_acts = []
    stream = block_input
    for layer_index in range(layers):
        w_proj = w_qkv[layer_index].astype(jnp.bfloat16)
        w_mix = w_out[layer_index].astype(jnp.bfloat16)
        rows_low = stream.astype(jnp.bfloat16)
        full_rows = lax.all_gather(rows_low, "tensor", axis=0, tiled=True)
        length = full_rows.shape[0]
        projected = jnp.einsum(
            "lsd,tdc->tlsc", full_rows, w_proj, preferred_element_type=jnp.float32
        )
        qkv_bias = jnp.stack(
            [b_qv[layer_index, 0], jnp.zeros_like(b_qv[layer_index, 0]), b_qv[layer_index, 1]]
        )
        qkv_low = (projected + qkv_bias[:, None, None, :]).astype(jnp.bfloat16)
        head_view = qkv_low.reshape(3, length, seq_count, local_heads, HEAD_DIM)
        scores = masked_scores(head_view[0], head_view[1], allowed, score_scale)
        row_top = jnp.max(scores, axis=-1, keepdims=True)
        log_total = row_top + jnp.log(jnp.sum(jnp.exp(scores - row_top), axis=-1, keepdims=True))
        probs_low = jnp.exp(scores - log_total).astype(jnp.bfloat16)
        context = jnp.einsum(
            "shqk,kshd->qshd", probs_low, head_view[2], preferred_element_type=jnp.float32
        )
        context = context.reshape(length, seq_count, local_width).astype(jnp.bfloat16)
        mixed = lax.psum_scatter(
            jnp.einsum("lsc,cd->lsd", context, w_mix, preferred_element_type=jnp.float32).astype(
                jnp.bfloat16
            ),
            "tensor",
            scatter_dimension=0,
            tiled=True,
        ).astype(jnp.float32)
        first_sum = stream + mixed + b_out[layer_index]
        hidden_rows = norm_rows(first_sum, ln_gain[layer_index, 0], ln_bias[layer_index, 0])
        hidden_low = hidden_rows.astype(jnp.bfloat16)
        up_weight = w_in[layer_index].astype(jnp.bfloat16)
        backward_weight = w_down[layer_index].astype(jnp.bfloat16)
        hidden_full = lax.all_gather(hidden_low, "tensor", axis=0, tiled=True)
        preactivation = (
            jnp.einsum("twn,nj->twj", hidden_full, up_weight, preferred_element_type=jnp.float32)
            + b_in[layer_index]
        )
        activation_reduced = gelu_exact(preactivation).astype(jnp.bfloat16)
        grown = lax.psum_scatter(
            jnp.einsum(
                "unj,jp->unp",
                activation_reduced,
                backward_weight,
                preferred_element_type=jnp.float32,
            ).astype(jnp.bfloat16),
            "tensor",
            scatter_dimension=0,
            tiled=True,
        ).astype(jnp.float32)
        second_sum = hidden_rows + grown + b_down[layer_index]
        stream = norm_rows(second_sum, ln_gain[layer_index, 1], ln_bias[layer_index, 1])
        keep_rows, keep_hidden = (full_rows, hidden_full)
        saved_acts.append(
            (
                keep_rows,
                head_view,
                log_total,
                context,
                first_sum,
                keep_hidden,
                preactivation,
                activation_reduced,
                second_sum,
                up_weight,
                backward_weight,
            )
        )
    upstream = cotangent
    grads_by_layer = [None] * layers
    for layer_index in reversed(range(layers)):
        (
            keep_rows,
            head_view,
            log_total,
            context,
            first_sum,
            keep_hidden,
            preactivation,
            activation_reduced,
            second_sum,
            up_weight,
            backward_weight,
        ) = saved_acts[layer_index]
        full_rows, hidden_full = (keep_rows, keep_hidden)
        length = full_rows.shape[0]
        w_proj = w_qkv[layer_index].astype(jnp.bfloat16)
        w_mix = w_out[layer_index].astype(jnp.bfloat16)
        _, pull_second = jax.vjp(
            norm_rows, second_sum, ln_gain[layer_index, 1], ln_bias[layer_index, 1]
        )
        d_second, d_gain_two, d_shift_two = pull_second(upstream)
        _, pull_gelu = jax.vjp(gelu_exact, preactivation)
        widened_full = lax.all_gather(d_second.astype(jnp.bfloat16), "tensor", axis=0, tiled=True)
        down_gradient = jnp.einsum(
            "uxc,uxw->cw", activation_reduced, widened_full, preferred_element_type=jnp.float32
        )
        activation_gradient = jnp.einsum(
            "mra,xa->mrx", widened_full, backward_weight, preferred_element_type=jnp.float32
        )
        preactivation_gradient_reduced = pull_gelu(activation_gradient)[0].astype(jnp.bfloat16)
        up_gradient = jnp.einsum(
            "kmx,kmt->xt",
            hidden_full,
            preactivation_gradient_reduced,
            preferred_element_type=jnp.float32,
        )
        g_up_bias = jnp.sum(preactivation_gradient_reduced.astype(jnp.float32), axis=(0, 1))
        d_hidden = d_second + lax.psum_scatter(
            jnp.einsum(
                "hmp,tp->hmt",
                preactivation_gradient_reduced,
                up_weight,
                preferred_element_type=jnp.float32,
            ).astype(jnp.bfloat16),
            "tensor",
            scatter_dimension=0,
            tiled=True,
        ).astype(jnp.float32)
        _, pull_first = jax.vjp(
            norm_rows, first_sum, ln_gain[layer_index, 0], ln_bias[layer_index, 0]
        )
        d_first, d_gain_one, d_shift_one = pull_first(d_hidden)
        full_mixed = lax.all_gather(d_first.astype(jnp.bfloat16), "tensor", axis=0, tiled=True)
        g_out = jnp.einsum("lsc,lsd->cd", context, full_mixed, preferred_element_type=jnp.float32)
        d_context = jnp.einsum(
            "lsd,cd->lsc", full_mixed, w_mix, preferred_element_type=jnp.float32
        ).astype(jnp.bfloat16)
        d_context = d_context.reshape(length, seq_count, local_heads, HEAD_DIM)
        queries, key_rows, value_rows = (head_view[0], head_view[1], head_view[2])
        scores = masked_scores(queries, key_rows, allowed, score_scale)
        attn_probs = jnp.exp(scores - log_total)
        probs_low = attn_probs.astype(jnp.bfloat16)
        d_probs = jnp.einsum(
            "qshd,kshd->shqk", d_context, value_rows, preferred_element_type=jnp.float32
        )
        d_scores = attn_probs * (d_probs - jnp.sum(d_probs * attn_probs, axis=-1, keepdims=True))
        d_scores = d_scores.astype(jnp.bfloat16)
        d_query = (
            jnp.einsum("shqk,kshd->qshd", d_scores, key_rows, preferred_element_type=jnp.float32)
            * score_scale
        )
        d_key = (
            jnp.einsum("shqk,qshd->kshd", d_scores, queries, preferred_element_type=jnp.float32)
            * score_scale
        )
        d_value = jnp.einsum(
            "shqk,qshd->kshd", probs_low, d_context, preferred_element_type=jnp.float32
        )
        d_qkv = (
            jnp.stack([d_query, d_key, d_value])
            .reshape(3, length, seq_count, local_width)
            .astype(jnp.bfloat16)
        )
        g_proj = jnp.einsum("lsd,tlsc->tdc", full_rows, d_qkv, preferred_element_type=jnp.float32)
        qkv_sums = jnp.sum(d_qkv.astype(jnp.float32), axis=(1, 2))
        g_bias = jnp.stack([qkv_sums[0], qkv_sums[2]])
        upstream = d_first + lax.psum_scatter(
            jnp.einsum("tlsc,tdc->lsd", d_qkv, w_proj, preferred_element_type=jnp.float32).astype(
                jnp.bfloat16
            ),
            "tensor",
            scatter_dimension=0,
            tiled=True,
        ).astype(jnp.float32)
        weight_grads = (g_proj, g_bias, g_out, up_gradient, g_up_bias, down_gradient)
        small_grads = (
            jnp.sum(d_first, axis=(0, 1)),
            jnp.sum(d_second, axis=(0, 1)),
            jnp.stack([d_gain_one, d_gain_two]),
            jnp.stack([d_shift_one, d_shift_two]),
        )
        grads_by_layer[layer_index] = (weight_grads, small_grads)
    weight_stack = tuple(
        (
            jnp.stack([grads_by_layer[layer_index][0][member] for layer_index in range(layers)])
            for member in range(6)
        )
    )
    small_stack = tuple(
        (
            jnp.stack([grads_by_layer[layer_index][1][member] for layer_index in range(layers)])
            for member in range(4)
        )
    )
    weight_stack = jax.tree.map(
        lambda part: part.astype(jnp.float32), lax.psum(as_sent(weight_stack), "dp")
    )
    small_stack = lax.psum(small_stack, ("dp", "tensor"))
    return (
        stream,
        upstream,
        weight_stack[0],
        weight_stack[1],
        weight_stack[2],
        small_stack[0],
        weight_stack[3],
        weight_stack[4],
        weight_stack[5],
        small_stack[1],
        small_stack[2],
        small_stack[3],
    )


def solution(mesh):
    by_sequence = mesh.shape["tensor"] == 2 and mesh.shape["dp"] == 16
    return jax.shard_map(
        sequence_shards if by_sequence else shards,
        mesh=mesh,
        in_specs=(
            P("tensor", "dp", None),
            P("dp", None),
            P("dp", "tensor", None, None),
            P(None, None, None, "tensor"),
            P(None, None, "tensor"),
            P(None, "tensor", None),
            P(),
            P(None, None, "tensor"),
            P(None, "tensor"),
            P(None, "tensor", None),
            P(),
            P(),
            P(),
            P("tensor", "dp", None),
        ),
        out_specs=(
            P("tensor", "dp", None),
            P("tensor", "dp", None),
            P(None, None, None, "tensor"),
            P(None, None, "tensor"),
            P(None, "tensor", None),
            P(),
            P(None, None, "tensor"),
            P(None, "tensor"),
            P(None, "tensor", None),
            P(),
            P(),
            P(),
        ),
        check_vma=False,
    )
```

```python
import functools

import jax
import jax.numpy as jnp
from jax import lax
from jax.experimental import pallas as pl
from jax.experimental.pallas import tpu as pltpu
from jax.sharding import PartitionSpec as P

HEAD_DIM = 64
BIG = -1e30
BF16 = jnp.bfloat16
F32 = jnp.float32
MESH = pl.DeviceIdType.MESH
VMEM_LIMIT = 56 << 20

FLIP_Y, FLIP_C, FLIP_X, FLIP_Z0, FLIP_Z1 = 1, 2, 4, 8, 16
SWAP = FLIP_Y + FLIP_C
DEVICES = 32

GROUPS = 12
OUT_GROUP = 3
FF_GROUPS = 4


def in_group(s):
    return 4 + 2 * s


def down_group(s):
    return 5 + 2 * s


def flip(values, bit):
    pairs = [(i, i ^ bit) for i in range(DEVICES)]
    return jax.tree.map(lambda v: lax.ppermute(v, ("dp", "tensor"), pairs), values)


def nt(a, b):
    return lax.dot_general(a, b, (((1,), (1,)), ((), ())), preferred_element_type=F32)


def nn(a, b):
    return lax.dot_general(a, b, (((1,), (0,)), ((), ())), preferred_element_type=F32)


def tn(a, b):
    return lax.dot_general(a, b, (((0,), (0,)), ((), ())), preferred_element_type=F32)


def block_of(ref):
    width = ref.shape[-1]
    return ref[...].reshape(-1, width)


def place_kernel(turned, rows_too, code_ref, g_ref, *refs):
    refs = list(refs)
    sources = [refs.pop(0) for _ in range(rows_too)]
    o_ref = refs.pop(0)
    targets = [refs.pop(0) for _ in range(rows_too)]
    code = code_ref[0]
    step = pl.program_id(0) * pl.num_programs(1) + pl.program_id(1)
    if rows_too:
        wide, sem = refs[-2:]
        copies = [
            pltpu.make_async_copy(wide.at[n], target.at[:, 0], sem.at[n]) for n, target in enumerate(targets)
        ]

        @pl.when(step == 0)
        def _():
            for n, source in enumerate(sources):
                wide[n] = source[...].astype(F32)
                copies[n].start()

    for j in range(16):
        start = pl.multiple_of((j ^ code) * 32, 32)
        block = g_ref[0, pl.ds(start, 32), :].astype(F32)
        if turned:
            refs[0][j * 32 : (j + 1) * 32, :] = block
        else:
            o_ref[0, j * 32 : (j + 1) * 32, :] = block
    if turned:
        o_ref[...] = refs[0][...].T.reshape(o_ref.shape)
    if rows_too:

        @pl.when(step == pl.num_programs(0) * pl.num_programs(1) - 1)
        def _():
            for copy in copies:
                copy.wait()


def place(sums, shape, block, index, turned, count, group, code, rows_too=()):
    width = sums.shape[-1]
    anywhere = pl.BlockSpec(memory_space=pl.ANY)
    scratch = [pltpu.VMEM((512, width), F32)] if turned else []
    if rows_too:
        scratch += [
            pltpu.VMEM((len(rows_too),) + rows_too[0].shape, F32),
            pltpu.SemaphoreType.DMA((len(rows_too),)),
        ]
    return pl.pallas_call(
        functools.partial(place_kernel, turned, len(rows_too)),
        out_shape=[jax.ShapeDtypeStruct(shape, F32)]
        + [jax.ShapeDtypeStruct((r.shape[0], 1, r.shape[1]), F32) for r in rows_too],
        grid_spec=pltpu.PrefetchScalarGridSpec(
            num_scalar_prefetch=1,
            grid=(shape[0], count),
            in_specs=[pl.BlockSpec((1, 512, width), lambda l, i, code: (group(l, i), 0, 0))]
            + [pl.BlockSpec(r.shape, lambda l, i, code: (0, 0)) for r in rows_too],
            out_specs=[pl.BlockSpec(block, lambda l, i, code: index(l, i))] + [anywhere for _ in rows_too],
            scratch_shapes=scratch,
        ),
        compiler_params=pltpu.CompilerParams(vmem_limit_bytes=VMEM_LIMIT),
        cost_estimate=pl.CostEstimate(
            flops=0, bytes_accessed=shape[0] * count * 512 * width * 6, transcendentals=0
        ),
        name="place",
    )(code, sums, *rows_too)


def hand_out_kernel(layers, y_ref, packed, out, down, gain, shift, qv, hidden):
    y = y_ref[0]
    width = packed.shape[1]
    out[...] = packed[0:layers, :]
    down[...] = packed[layers : 2 * layers, :]
    for l in range(layers):
        for n in range(2):
            row = 2 * layers + 2 * l + n
            gain[l, n : n + 1, :] = packed[row : row + 1, :]
            row += 2 * layers
            shift[l, n : n + 1, :] = packed[row : row + 1, :]
            at = 8 * layers + 2 * l + n
            hidden[l : l + 1, n * width : (n + 1) * width] = jnp.where(
                y == 0, packed[at : at + 1, :], packed[at + 2 * layers : at + 2 * layers + 1, :]
            )
            half = slice(n * width // 2, (n + 1) * width // 2)
            at = 6 * layers + l
            qv[l, n : n + 1, :] = jnp.where(
                y == 0, packed[at : at + 1, half], packed[at + layers : at + layers + 1, half]
            )


def hand_out(packed, y, layers):
    width = packed.shape[1]
    full = lambda *shape: jax.ShapeDtypeStruct(shape, F32)
    in_vmem = pl.BlockSpec(memory_space=pltpu.VMEM)
    return pl.pallas_call(
        functools.partial(hand_out_kernel, layers),
        out_shape=(
            full(layers, width),
            full(layers, width),
            full(layers, 2, width),
            full(layers, 2, width),
            full(layers, 2, width // 2),
            full(layers, 2 * width),
        ),
        in_specs=[pl.BlockSpec(memory_space=pltpu.SMEM), in_vmem],
        out_specs=(in_vmem,) * 6,
        name="hand_out",
    )(y, packed)


def partner(bits):
    dp, y = lax.axis_index("dp"), lax.axis_index("tensor")
    other = dp
    for step in (1, 2, 4, 8):
        if bits & (2 * step):
            other = other + step * (1 - 2 * ((dp // step) % 2))
    return (other, 1 - y if bits & FLIP_Y else y)


def all_partners(bits):
    return {bit: partner(bit) for bit in bits}


def greet(partners):
    barrier = pltpu.get_barrier_semaphore()
    for other in partners.values():
        pl.semaphore_signal(barrier, inc=1, device_id=other, device_id_type=MESH)
    pl.semaphore_wait(barrier, len(partners))


def add_into(into, other, count):
    def step(i, _):
        into[i] = (into[i].astype(F32) + other[i].astype(F32)).astype(BF16)
        return 0

    lax.fori_loop(0, count, step, 0)


def add_rows(into, other, rows):
    def step(i, _):
        at = pl.ds(pl.multiple_of(i * 32, 32), 32)
        into[at, :] = (into[at, :].astype(F32) + other[at, :].astype(F32)).astype(BF16)
        return 0

    lax.fori_loop(0, rows // 32, step, 0)


def add_into(into, other, count):
    def step(i, _):
        into[i] = (into[i].astype(F32) + other[i].astype(F32)).astype(BF16)
        return 0

    lax.fori_loop(0, count, step, 0)


SLOTS = 6
PARTED = 2
PARTS = 2
LAST_TICK = 8


class Reduction:
    def __init__(self, grads, sums, first, groups, parts, partners, bufs, sems):
        self.grads, self.sums, self.first, self.parts, self.partners = grads, sums, first, parts, partners
        self.count = groups * parts
        self.y_buf, self.x_buf, self.z0_buf, self.z1_buf, self.all_buf, self.keep_buf = bufs
        self.slots = self.y_buf.shape[0]
        self.send_sem, self.recv_sem, self.core_send, self.core_recv, self.keep_sem, self.out_sem = sems[:6]
        self.in_free, self.out_free = sems[6:] if len(sems) > 6 else (None, None)

    def blocks(self, ref, i, at):
        if self.parts == 1:
            return ref.at[self.first + i, pl.ds(at, 8)]
        size = 32 // self.parts
        part = pl.ds(pl.multiple_of(lax.rem(i, self.parts) * size, size), size)
        return ref.at[self.first + lax.div(i, self.parts), pl.ds(at, 8), part]

    def copy(self, step, i):
        slot = lax.rem(i, self.slots)
        ys, al = self.y_buf.at[slot], self.all_buf.at[slot]
        bit, source, target = (
            (FLIP_Y, self.blocks(self.grads, i, 8), ys),
            (FLIP_X, ys.at[pl.ds(4, 4)], self.x_buf.at[slot]),
            (FLIP_Z0, ys.at[pl.ds(2, 2)], self.z0_buf.at[slot]),
            (FLIP_Z1, ys.at[pl.ds(1, 1)], self.z1_buf.at[slot]),
            (FLIP_Z1, al.at[pl.ds(0, 1)], al.at[pl.ds(1, 1)]),
            (FLIP_Z0, al.at[pl.ds(0, 2)], al.at[pl.ds(2, 2)]),
            (FLIP_X, al.at[pl.ds(0, 4)], al.at[pl.ds(4, 4)]),
            (FLIP_C, al, self.blocks(self.sums, i, 8)),
        )[step]
        return pltpu.make_async_remote_copy(
            src_ref=source,
            dst_ref=target,
            send_sem=self.send_sem.at[step, slot] if step < 7 else self.core_send.at[i],
            recv_sem=self.recv_sem.at[step, slot] if step < 7 else self.core_recv.at[i],
            device_id=self.partners[bit],
            device_id_type=MESH,
        )

    def keep(self, i):
        slot = lax.rem(i, 2)
        return pltpu.make_async_copy(
            self.blocks(self.grads, i, 0), self.keep_buf.at[slot], self.keep_sem.at[slot]
        )

    def out(self, i):
        slot = lax.rem(i, self.slots)
        return pltpu.make_async_copy(
            self.all_buf.at[slot], self.blocks(self.sums, i, 0), self.out_sem.at[slot]
        )

    def take(self, sems, n, i):
        if sems is not None:
            pl.when(i >= self.slots)(lambda: pl.semaphore_wait(sems.at[n], 1))

    def give(self, sems, n, bit, i):
        if sems is not None:
            pl.when(i + self.slots < self.count)(
                lambda: pl.semaphore_signal(
                    sems.at[n], inc=1, device_id=self.partners[bit], device_id_type=MESH
                )
            )

    def tick(self, t):
        def at(offset, body):
            i = t - offset
            pl.when((i >= 0) & (i < self.count))(lambda: body(i, lax.rem(i, self.slots)))

        def set_out(i, slot):
            self.take(self.in_free, 0, i)
            self.copy(0, i).start()
            self.keep(i).start()

        def finish(i, slot):
            self.copy(7, i).wait()
            self.out(i).wait()
            for n, bit in enumerate((FLIP_X, FLIP_Z0, FLIP_Z1)):
                self.give(self.out_free, n, bit, i)

        def to_core(i, slot):
            self.copy(6, i).wait()
            self.copy(7, i).start()
            self.out(i).start()

        def back_x(i, slot):
            self.copy(5, i).wait()
            self.take(self.out_free, 0, i)
            self.copy(6, i).start()

        def back_z0(i, slot):
            self.copy(4, i).wait()
            self.take(self.out_free, 1, i)
            self.copy(5, i).start()

        def back_z1(i, slot):
            self.copy(3, i).wait()
            add_into(self.y_buf.at[slot], self.z1_buf.at[slot], 1)
            self.all_buf[slot, 0] = self.y_buf[slot, 0]
            for n, bit in enumerate((FLIP_Y, FLIP_X, FLIP_Z0, FLIP_Z1)):
                self.give(self.in_free, n, bit, i)
            self.take(self.out_free, 2, i)
            self.copy(4, i).start()

        def on_z1(i, slot):
            self.copy(2, i).wait()
            add_into(self.y_buf.at[slot], self.z0_buf.at[slot], 2)
            self.take(self.in_free, 3, i)
            self.copy(3, i).start()

        def on_z0(i, slot):
            self.copy(1, i).wait()
            add_into(self.y_buf.at[slot], self.x_buf.at[slot], 4)
            self.take(self.in_free, 2, i)
            self.copy(2, i).start()

        def on_x(i, slot):
            self.copy(0, i).wait()
            self.keep(i).wait()
            add_into(self.y_buf.at[slot], self.keep_buf.at[lax.rem(i, 2)], 8)
            self.take(self.in_free, 1, i)
            self.copy(1, i).start()

        at(0, set_out)
        at(8, finish)
        at(7, to_core)
        at(6, back_x)
        at(5, back_z0)
        at(4, back_z1)
        at(3, on_z1)
        at(2, on_z0)
        at(1, on_x)


def unit_order(y, core_free_bits):
    taken = lax.broadcasted_iota(jnp.int32, (512, 512), 0)
    column = lax.broadcasted_iota(jnp.int32, (512, 512), 1)
    where = lax.rem(column, 32)
    for own, weight in zip((y,) + core_free_bits, (256, 128, 64, 32)):
        bit = lax.rem(lax.div(column, weight), 2)
        where = where + weight * (bit + own - 2 * own * bit)
    return (taken == where).astype(F32)


def begin(feeds):
    for copy in feeds(0, 0):
        copy.start()


def stream(count, feeds, body):
    def step(i, _):
        slot = lax.rem(i, 2)

        @pl.when(i + 1 < count)
        def _():
            for copy in feeds(i + 1, 1 - slot):
                copy.start()

        for copy in feeds(i, slot):
            copy.wait()
        body(i, slot)
        return 0

    lax.fori_loop(0, count, step, 0)


def norm(r, gain, shift):
    centred = r - jnp.mean(r, axis=-1, keepdims=True)
    rstd = lax.rsqrt(jnp.mean(centred * centred, axis=-1, keepdims=True) + 1e-06)
    return centred * rstd * gain + shift


def norm_back(dy, r, gain):
    centred = r - jnp.mean(r, axis=-1, keepdims=True)
    rstd = lax.rsqrt(jnp.mean(centred * centred, axis=-1, keepdims=True) + 1e-06)
    unit = centred * rstd
    dunit = dy * gain
    dr = rstd * (
        dunit
        - jnp.mean(dunit, axis=-1, keepdims=True)
        - unit * jnp.mean(dunit * unit, axis=-1, keepdims=True)
    )
    return dr, dy * unit


def gelu_and_slope(u):
    cdf = 0.5 * (1.0 + lax.erf(u * (0.5**0.5)))
    pdf = jnp.exp(-0.5 * u * u) * 0.3989422804014327
    return u * cdf, cdf + u * pdf


TILE = 128


def row_tiles(rows, body):
    def step(i, _):
        body(pl.ds(pl.multiple_of(i * TILE, TILE), TILE))
        return 0

    lax.fori_loop(0, rows // TILE, step, 0)


def pair_lanes(values, e):
    lane = lax.broadcasted_iota(jnp.int32, values.shape, 1)
    return jnp.where(lane // HEAD_DIM == e, values, jnp.zeros_like(values))


def spread_mask(block_part, document_part):
    blocks, lanes = block_part.shape
    each = document_part.shape[0] // blocks
    part = jnp.broadcast_to(block_part[:, None, :], (blocks, each, lanes)).reshape(blocks * each, lanes)
    return (part + document_part).astype(BF16)


def both_heads(values):
    return jnp.concatenate([pair_lanes(values, 0), pair_lanes(values, 1)], axis=0)


def attend_pair(query, keys, values, hot, mask):
    scale = HEAD_DIM**-0.5
    rows = query.shape[0]
    query = query * jnp.asarray(scale, BF16)
    right = jnp.concatenate([both_heads(query), both_heads(hot)], axis=1)
    s = nt(jnp.concatenate([keys, mask], axis=1), right)
    top = jnp.max(s, axis=0, keepdims=True)
    p = jnp.exp(s - top)
    total = jnp.sum(p, axis=0, keepdims=True)
    c = nn(values.T, p.astype(BF16)) * (1.0 / total)
    context = jnp.concatenate([c[:HEAD_DIM, :rows], c[HEAD_DIM:, rows:]], axis=0).T
    lse = top + jnp.log(total)
    return context, [lse[:, :rows], lse[:, rows:]]


def attend_back_pair(query, keys, values, hot, mask, ctx, lse, dctx):
    scale = HEAD_DIM**-0.5
    rows = query.shape[0]
    query = query * jnp.asarray(scale, BF16)
    keys_t = keys.T
    delta_t = (dctx.astype(F32) * ctx.astype(F32)).T
    left = jnp.concatenate([keys, mask], axis=1)
    tile = rows // 2
    dk, dv, dq = 0.0, 0.0, []
    for part in range(2):
        at = slice(part * tile, (part + 1) * tile)
        heads = []
        for e in range(2):
            lanes = slice(e * HEAD_DIM, (e + 1) * HEAD_DIM)
            query_e = pair_lanes(query[at], e)
            dctx_e = pair_lanes(dctx[at], e)
            right = jnp.concatenate([query_e, pair_lanes(hot[at], e)], axis=1)
            p = jnp.exp(nt(left, right) - lse[e : e + 1, at])
            dp = nt(values, dctx_e)
            delta = jnp.sum(delta_t[lanes, at], axis=0, keepdims=True)
            ds = (p * (dp - delta)).astype(BF16)
            dk = dk + nn(ds, query_e)
            dv = dv + nn(p.astype(BF16), dctx_e)
            heads.append(nn(keys_t[lanes, :], ds) * scale)
        dq.append(jnp.concatenate(heads, axis=0).T)
    return jnp.concatenate(dq, axis=0), dk, dv


class Spread:
    def __init__(self, weights, pairs, partners, send_sem, recv_sem):
        self.weights, self.pairs, self.partners = weights, pairs, partners
        self.send_sem, self.recv_sem = send_sem, recv_sem

    def copy(self, step, t):
        w = self.weights
        even, odd = 2 * t, 2 * t + 1
        bit, source, target = (
            (FLIP_Y, w.at[0, even, 0, pl.ds(0, 64)], w.at[0, even, 1, pl.ds(0, 64)]),
            (FLIP_Y, w.at[0, odd, 0, pl.ds(0, 64)], w.at[0, odd, 1, pl.ds(0, 64)]),
            (FLIP_X, w.at[0, even, 1, pl.ds(0, 64)], w.at[0, even, 1, pl.ds(128, 64)]),
            (FLIP_Z0, w.at[0, odd, 1, pl.ds(0, 64)], w.at[0, odd, 1, pl.ds(64, 64)]),
            (FLIP_Z0, w.at[0, even, 1, pl.ds(0, 64)], w.at[0, even, 1, pl.ds(64, 64)]),
            (FLIP_Z0, w.at[0, even, 1, pl.ds(128, 64)], w.at[0, even, 1, pl.ds(192, 64)]),
            (FLIP_X, w.at[0, odd, 1, pl.ds(0, 128)], w.at[0, odd, 1, pl.ds(128, 128)]),
            (FLIP_C, w.at[0, even, 1], w.at[1, even, 1]),
            (FLIP_C, w.at[0, odd, 1], w.at[1, odd, 1]),
        )[step]
        return pltpu.make_async_remote_copy(
            src_ref=source,
            dst_ref=target,
            send_sem=self.send_sem.at[step, t],
            recv_sem=self.recv_sem.at[step, t],
            device_id=self.partners[bit],
            device_id_type=MESH,
        )

    def tick(self, t):
        def at(offset, waits, starts):
            i = t - offset

            @pl.when((i >= 0) & (i < self.pairs))
            def _():
                for step in waits:
                    self.copy(step, i).wait()
                for step in starts:
                    self.copy(step, i).start()

        at(0, (), (0, 1))
        at(5, (7, 8), ())
        at(1, (0, 1), (2, 3))
        at(2, (2, 3), (4, 5, 6))
        at(4, (4, 5, 6), (7, 8))


PER_LAYER = 14
DEPTH = 3


def forward_kernel(layers, *refs):
    refs = list(refs)
    x_ref, up_ref, wq_ref, wo_ref, wi_ref, wd_ref = refs[:6]
    hot_buf, mask_ref, key_ref, bq_ref, bi_ref, vec_ref = refs[6:12]
    w_ref, up_out, x_out = refs[12:15]
    saved = [refs[15 + PER_LAYER * l : 15 + PER_LAYER * (l + 1)] for l in range(layers)]
    (
        x, acc, r_buf, low, xb, qkv, kv_sib, ctx, lse, hl, g_all, slope_all,
        col_buf, row_buf, turn_buf, made_buf, wa_buf, wb_buf,
        feed_sem, load_sem, col_sem, row_sem, made_sem, store_sem, block_sem,
        core_send, core_recv, kv_send, kv_recv, g_send, g_recv, spread_send, spread_recv,
    ) = refs[15 + PER_LAYER * layers :]
    rows, width = acc.shape
    dp, y = lax.axis_index("dp"), lax.axis_index("tensor")
    core = dp % 2
    stays = core == y
    partners = all_partners((FLIP_Y, FLIP_X, FLIP_Z0, FLIP_C, SWAP))
    spread = Spread(w_ref, layers * GROUPS // 2, partners, spread_send, spread_recv)
    greet(partners)

    def feed(n, slot, source, target):
        return pltpu.make_async_copy(source, target, feed_sem.at[n, slot])

    def load(n, source, target):
        return pltpu.make_async_copy(source, target, load_sem.at[n])

    def store(n, source, target):
        return pltpu.make_async_copy(source, target, store_sem.at[n])

    def exchange(n, source, target, bits=FLIP_C):
        return pltpu.make_async_remote_copy(
            src_ref=source, dst_ref=target, send_sem=core_send.at[n], recv_sem=core_recv.at[n],
            device_id=partners[bits], device_id_type=MESH,
        )

    def columns(ref, i, size):
        return ref.at[:, pl.ds(pl.multiple_of(i * size, size), size)]

    def swap(n, source, target, begin):
        here = store(n, source, target)
        there = exchange(n, source, target, SWAP)

        @pl.when(stays)
        def _():
            here.start() if begin else here.wait()

        @pl.when(jnp.logical_not(stays))
        def _():
            there.start() if begin else there.wait()

    items = []
    for l in range(layers):
        items += [(True, wq_ref.at[l, (t + 1) % 3], l * GROUPS + t) for t in range(3)]
        items += [(False, wo_ref.at[l], l * GROUPS + OUT_GROUP)]
        for n in range(FF_GROUPS):
            items += [(True, wi_ref.at[l, :, pl.ds(n * 512, 512)], l * GROUPS + in_group(n))]
            items += [(False, wd_ref.at[l, pl.ds(n * 512, 512)], l * GROUPS + down_group(n))]
    fetches, counts, ahead = [], [0, 0], [[], []]
    for m, (turned, source, group) in enumerate(items):
        slot = counts[turned] % DEPTH
        buf, sem = (col_buf, col_sem) if turned else (row_buf, row_sem)
        fetches.append((pltpu.make_async_copy(source, buf.at[slot], sem.at[slot]), slot))
        ahead[turned].append(m)
        counts[turned] += 1
    bits = [(dp // step) % 2 for step in (1, 2, 4, 8)]
    made = {}

    def convert(m):
        turned, _, group = items[m]
        copy, slot = fetches[m]
        copy.wait()
        if turned:

            def turn(i, _):
                strip = col_buf[slot, :, pl.ds(pl.multiple_of(i * 128, 128), 128)]
                turn_buf[pl.ds(pl.multiple_of(i * 128, 128), 128), :] = strip.astype(BF16).T
                return 0

            lax.fori_loop(0, 4, turn, 0)
        if m >= 2:
            made[m - 2].wait()

        def block(j, _):
            where = 0
            for bit, weight in zip(bits, (8, 4, 2, 1)):
                own = (j // weight) % 2
                where = where + weight * (own + bit - 2 * own * bit)
            at = pl.ds(pl.multiple_of(where * 32, 32), 32)
            rows_32 = turn_buf[at, :] if turned else row_buf[slot, at, :]
            made_buf[m % 2, pl.ds(pl.multiple_of(j * 32, 32), 32), :] = rows_32.astype(BF16)
            return 0

        lax.fori_loop(0, 16, block, 0)
        later = [n for n in ahead[turned] if n > m]
        if len(later) >= DEPTH:
            fetches[later[DEPTH - 1]][0].start()
        parts = [
            pltpu.make_async_copy(
                made_buf.at[m % 2, pl.ds(a * 256, 256)], w_ref.at[a, group, 0], made_sem.at[m % 2, a]
            )
            for a in range(2)
        ]

        class Both:
            def wait(self):
                for part in parts:
                    part.wait()

        for part in parts:
            part.start()
        made[m] = Both()

    load_x = load(0, x_ref.at[:, 0], x)
    load_x.start()
    for kind in range(2):
        for m in ahead[kind][:DEPTH]:
            fetches[m][0].start()
    load_x.wait()

    def narrow_x(at):
        low[at, :] = x[at, :].astype(BF16)

    row_tiles(rows, narrow_x)
    swap(0, low, xb, True)
    for m in range(len(items)):
        convert(m)
        if m % 4 == 3:
            spread.tick(m // 4)
    for m in range(len(items) - 2, len(items)):
        made[m].wait()
    swap(0, low, xb, False)
    load_up = load(1, up_ref.at[:, 0], row_buf.at[0])
    load_up.start()

    def widen(at):
        x[at, :] = xb[at, :].astype(F32)

    row_tiles(rows, widen)

    pairs = width // 128
    for l in range(layers):
        (
            qkv_out, sib_out, ctx_out, ctx_sib_out, lse_out, r1_out, r2_out, hl_out, hl_sib_out,
            g_out, g_sib_out, slope_out, xb_out, xb_sib_out,
        ) = saved[l]
        first = l * GROUPS
        clock = 6 + 6 * l
        xb_store = store(0, xb, xb_out)
        xb_store.start()
        xb_copy = exchange(2 + 3 * l, xb, xb_sib_out)
        xb_copy.start()

        def give_kv(n, a):
            at = pl.ds(pl.multiple_of(a * 512, 512), 512)
            return pltpu.make_async_remote_copy(
                src_ref=qkv.at[1 + n, :, at], dst_ref=kv_sib.at[n, :, at],
                send_sem=kv_send.at[n, a], recv_sem=kv_recv.at[n, a],
                device_id=partners[FLIP_C], device_id_type=MESH,
            )

        def which(i):
            n = lax.div(i, 2)
            return lax.rem(n + 1, 3), n, lax.rem(i, 2)

        def qkv_feeds(i, slot):
            _, n, a = which(i)
            return (feed(0, slot, w_ref.at[a, first + n], wa_buf.at[slot]),)

        def qkv_body(i, slot):
            t, _, a = which(i)
            at = pl.ds(pl.multiple_of(a * 512, 512), 512)
            qkv[t, :, at] = (nt(xb[...], block_of(wa_buf.at[slot])) + bq_ref[l, t, a]).astype(BF16)
            pl.when(t > 0)(lambda: give_kv(t - 1, a).start())
            pl.when(i == 2)(lambda: spread.tick(clock))

        if l == 0:
            begin(qkv_feeds)
        stream(6, qkv_feeds, qkv_body)
        qkv_store = store(1, qkv, qkv_out)
        qkv_store.start()
        for n in range(2):
            for a in range(2):
                give_kv(n, a).wait()
        sib_store = store(2, kv_sib, sib_out)
        sib_store.start()

        feed(2, 0, w_ref.at[0, first + OUT_GROUP], wb_buf.at[0]).start()

        def pair_body(p, _):
            far = lax.rem(p + pairs // 2, pairs)
            here = pl.ds(pl.multiple_of(p * 128, 128), 128)
            there = pl.ds(pl.multiple_of(far * 128, 128), 128)
            mask = spread_mask(mask_ref[p], key_ref[...])
            keys = jnp.concatenate([qkv[1, :, here], kv_sib[0, :, there]], axis=0)
            values = jnp.concatenate([qkv[2, :, here], kv_sib[1, :, there]], axis=0)
            context, parts = attend_pair(qkv[0, :, here], keys, values, hot_buf[...], mask)
            ctx[:, here] = context.astype(BF16)
            for e in range(2):
                lse[p, e : e + 1, :] = parts[e]
            pl.when(lax.rem(p, 5) == 2)(lambda: spread.tick(clock + 1 + lax.div(p, 5)))
            return 0

        lax.fori_loop(0, pairs, pair_body, 0)
        ctx_store = store(3, ctx, ctx_out)
        ctx_store.start()
        lse_store = store(4, lse, lse_out)
        lse_store.start()
        ctx_copy = exchange(3 + 3 * l, ctx.at[:, pl.ds(512, 512)], ctx_sib_out)
        ctx_copy.start()

        def place_of(i):
            return 1 - lax.rem(i, 2), lax.div(i, 2)

        def ff_feeds(i, slot):
            a, n = place_of(i)
            return (
                feed(0, slot, w_ref.at[a, first + in_group(n)], wa_buf.at[slot]),
                feed(2, slot, w_ref.at[a, first + down_group(n)], wb_buf.at[slot]),
            )

        ff_feeds(0, 0)[0].start()

        def out_feeds(i, slot):
            return (feed(2, slot, w_ref.at[i, first + OUT_GROUP], wb_buf.at[slot]),)

        def out_body(i, slot):
            part = nn(ctx[:, pl.ds(pl.multiple_of(i * 512, 512), 512)], block_of(wb_buf.at[slot]))

            @pl.when(i == 0)
            def _():
                acc[...] = part

            @pl.when(i == 1)
            def _():
                acc[...] += part

        stream(2, out_feeds, out_body)
        ff_feeds(0, 0)[1].start()
        sib_store.wait()

        def first_norm(at):
            r1 = x[at, :] + acc[at, :] + vec_ref[l, 0:1, :]
            r_buf[at, :] = r1
            h = norm(r1, vec_ref[l, 1:2, :], vec_ref[l, 2:3, :])
            hl[at, :] = h.astype(BF16)
            acc[at, :] = h + vec_ref[l, 3:4, :]

        row_tiles(rows, first_norm)
        r1_store = store(5, r_buf, r1_out)
        r1_store.start()
        hl_store = store(6, hl, hl_out)
        hl_store.start()
        hl_copy = exchange(4 + 3 * l, hl, hl_sib_out)
        hl_copy.start()

        def g_store(j):
            return pltpu.make_async_copy(g_all.at[j], columns(g_out, j, 512), block_sem.at[0, j])

        def slope_store(j):
            return pltpu.make_async_copy(slope_all.at[j], columns(slope_out, j, 512), block_sem.at[1, j])

        def g_copy(n):
            return pltpu.make_async_remote_copy(
                src_ref=g_all.at[FF_GROUPS + n], dst_ref=columns(g_sib_out, n, 512),
                send_sem=g_send.at[l, n], recv_sem=g_recv.at[l, n],
                device_id=partners[FLIP_C], device_id_type=MESH,
            )

        def ff_body(i, slot):
            a, n = place_of(i)
            j = a * FF_GROUPS + n
            u = nt(hl[...], block_of(wa_buf.at[slot])) + bi_ref[l, a, n]
            g, slope = gelu_and_slope(u)
            g = g.astype(BF16)
            g_all[j] = g
            slope_all[j] = slope.astype(BF16)
            g_store(j).start()
            slope_store(j).start()
            pl.when(a == 1)(lambda: g_copy(n).start())
            acc[...] += nn(g, block_of(wb_buf.at[slot]))
            pl.when(lax.rem(i, 3) == 1)(lambda: spread.tick(clock + 3 + lax.div(i, 3)))

        stream(2 * FF_GROUPS, ff_feeds, ff_body)
        r1_store.wait()
        xb_store.wait()
        xb_copy.wait()
        if l + 1 < layers:
            feed(0, 0, w_ref.at[0, first + GROUPS], wa_buf.at[0]).start()
        if l == 0:
            load_up.wait()

            def narrow_up(at):
                low[at, :] = row_buf[0, at, :].astype(BF16)

            row_tiles(rows, narrow_up)
            swap(9, low, up_out, True)

        def second_norm(at):
            r2 = acc[at, :]
            r_buf[at, :] = r2
            x2 = norm(r2, vec_ref[l, 4:5, :], vec_ref[l, 5:6, :])
            x[at, :] = x2
            xb[at, :] = x2.astype(BF16)

        row_tiles(rows, second_norm)
        r2_store = store(5, r_buf, r2_out)
        r2_store.start()
        if l == layers - 1:
            x_store = store(10, xb, x_out)
            x_store.start()

        def settle(j, _):
            g_store(j).wait()
            slope_store(j).wait()
            return 0

        lax.fori_loop(0, 2 * FF_GROUPS, settle, 0)

        def settle_sent(n, _):
            g_copy(n).wait()
            return 0

        lax.fori_loop(0, FF_GROUPS, settle_sent, 0)
        for copy in (qkv_store, ctx_store, lse_store, ctx_copy, hl_store, hl_copy, r2_store):
            copy.wait()
    x_store.wait()
    swap(9, low, up_out, False)


def forward(block_input, cotangent, w_qkv, w_out, w_in, w_down, hot, mask, mask_rows, bias_qkv, bias_in, vectors):
    rows, _, width = block_input.shape
    layers = w_qkv.shape[0]
    total = layers * GROUPS
    anywhere = pl.BlockSpec(memory_space=pl.ANY)
    in_vmem = pl.BlockSpec(memory_space=pltpu.VMEM)
    low = lambda *shape: pltpu.VMEM(shape, BF16)
    full = lambda *shape: pltpu.VMEM(shape, F32)
    dma = lambda *shape: pltpu.SemaphoreType.DMA(shape)
    low_out = lambda *shape: jax.ShapeDtypeStruct(shape, BF16)
    full_out = lambda *shape: jax.ShapeDtypeStruct(shape, F32)
    layer_out = (
        low_out(3, rows, width),
        low_out(2, rows, width),
        low_out(rows, width),
        low_out(rows, width // 2),
        full_out(width // 128, 2, rows),
        full_out(rows, width),
        full_out(rows, width),
        low_out(rows, width),
        low_out(rows, width),
        low_out(rows, 4 * width),
        low_out(rows, 2 * width),
        low_out(rows, 4 * width),
        low_out(rows, width),
        low_out(rows, width),
    )
    outs = pl.pallas_call(
        functools.partial(forward_kernel, layers),
        out_shape=(low_out(2, total, 2, 256, width), low_out(rows, width), low_out(rows, width)) + layer_out * layers,
        in_specs=[anywhere] * 6 + [in_vmem] * 6,
        out_specs=(anywhere,) * (3 + PER_LAYER * layers),
        scratch_shapes=[
            full(rows, width),
            full(rows, width),
            full(rows, width),
            low(rows, width),
            low(rows, width),
            low(3, rows, width),
            low(2, rows, width),
            low(rows, width),
            full(width // 128, 2, rows),
            low(rows, width),
            low(2 * FF_GROUPS, rows, 512),
            low(2 * FF_GROUPS, rows, 512),
            full(DEPTH, width, 512),
            full(DEPTH, 512, width),
            low(512, width),
            low(2, 512, width),
            low(2, 2, 256, width),
            low(2, 2, 256, width),
            dma(3, 2),
            dma(3),
            dma(DEPTH),
            dma(DEPTH),
            dma(2, 2),
            dma(11),
            dma(2, 2 * FF_GROUPS),
            dma(11),
            dma(11),
            dma(2, 2),
            dma(2, 2),
            dma(layers, FF_GROUPS),
            dma(layers, FF_GROUPS),
            dma(9, total // 2),
            dma(9, total // 2),
        ],
        compiler_params=pltpu.CompilerParams(collective_id=0, has_side_effects=True, vmem_limit_bytes=60 << 20),
        cost_estimate=pl.CostEstimate(flops=30 << 30, bytes_accessed=300 << 20, transcendentals=1 << 24),
        name="forward",
    )(block_input, cotangent, w_qkv, w_out, w_in, w_down, hot, mask, mask_rows, bias_qkv, bias_in, vectors)
    saved = [outs[3 + PER_LAYER * l : 3 + PER_LAYER * (l + 1)] for l in range(layers)]
    return outs[0], outs[1], outs[2], saved


def backward_kernel(layers, *refs):
    refs = list(refs)
    up_ref, x_ref, w_ref, hot_buf, mask_ref, key_ref, vec_ref = refs[:7]
    saved = [refs[7 + PER_LAYER * l : 7 + PER_LAYER * (l + 1)] for l in range(layers)]
    at_ref = 7 + PER_LAYER * layers
    grads, sums, dx_out, x_out, packed = refs[at_ref : at_ref + 5]
    (
        acc, dr1, dm, dm_sib, da, da_sib, du, du_sib, dctx, dqkv, d_sib, kv_out, kv_far,
        wa_buf, wb_buf, r_buf, slope_buf, left_buf, left_sib_buf, right_buf, right_sib_buf,
        pair_buf, lse_buf, unit_buf,
        y_buf, x_buf, z0_buf, z1_buf, all_buf, keep_buf,
        feed_sem, load_sem, store_sem, swap_sem, core_send, core_recv, du_send, du_recv, pair_send, pair_recv,
        send_sem, recv_sem, sum_send, sum_recv, keep_sem, out_sem, in_free, out_free,
        dbi_ref, qkv_sums_ref, small_ref, far_buf, far_send, far_recv,
    ) = refs[at_ref + 5 : -12]
    part_bufs, part_sems = refs[-12:-6], refs[-6:]
    rows, width = acc.shape
    total = layers * GROUPS
    partners = all_partners((FLIP_Y, FLIP_X, FLIP_Z0, FLIP_Z1, FLIP_C, SWAP))
    whole = total - PARTED
    reduction = Reduction(
        grads, sums, 0, whole, 1, partners,
        (y_buf, x_buf, z0_buf, z1_buf, all_buf, keep_buf),
        (send_sem, recv_sem, sum_send, sum_recv, keep_sem, out_sem, in_free, out_free),
    )
    ending = Reduction(grads, sums, whole, PARTED, PARTS, partners, part_bufs, part_sems)
    greet(partners)

    def feed(n, slot, source, target):
        return pltpu.make_async_copy(source, target, feed_sem.at[n, slot])

    def load(n, source, target):
        return pltpu.make_async_copy(source, target, load_sem.at[n])

    def exchange(n, source, target):
        return pltpu.make_async_remote_copy(
            src_ref=source, dst_ref=target, send_sem=core_send.at[n], recv_sem=core_recv.at[n],
            device_id=partners[FLIP_C], device_id_type=MESH,
        )

    def give_du(j, n):
        return pltpu.make_async_remote_copy(
            src_ref=du.at[j], dst_ref=du_sib.at[n], send_sem=du_send.at[n], recv_sem=du_recv.at[n],
            device_id=partners[FLIP_C], device_id_type=MESH,
        )

    def weight(a, group):
        return w_ref.at[a, group]

    def columns(ref, i, size):
        return ref.at[:, pl.ds(pl.multiple_of(i * size, size), size)]

    def unit_store(slot, index):
        return pltpu.make_async_copy(unit_buf.at[slot], grads.at[index], store_sem.at[0])

    def unit(left, left_sib, right, right_sib, slot, index, fresh=False):
        made = (tn(left, right) + tn(left_sib, right_sib)).astype(BF16)
        unit_buf[slot] = made.reshape(unit_buf.shape[1:])
        if fresh is not False:
            pl.when(jnp.logical_not(fresh))(lambda: unit_store(slot, index).wait())
        else:
            unit_store(slot, index).wait()
        unit_store(slot, index).start()

    def add_small(l, row, value):
        small_ref[l, row : row + 1, :] += jnp.sum(value, axis=0, keepdims=True)

    stays = lax.axis_index("dp") % 2 == lax.axis_index("tensor")

    def swap(n, source, target, begin):
        here = pltpu.make_async_copy(source, target, swap_sem.at[n])
        there = pltpu.make_async_remote_copy(
            src_ref=source, dst_ref=target, send_sem=core_send.at[4 + n], recv_sem=core_recv.at[4 + n],
            device_id=partners[SWAP], device_id_type=MESH,
        )

        @pl.when(stays)
        def _():
            here.start() if begin else here.wait()

        @pl.when(jnp.logical_not(stays))
        def _():
            there.start() if begin else there.wait()

    swap(1, x_ref, x_out, True)
    load(0, saved[-1][6], r_buf).start()
    start_up = load(1, up_ref, da)
    start_up.start()
    start_up.wait()
    small_ref[...] = jnp.zeros_like(small_ref)

    def widen(at):
        acc[at, :] = da[at, :].astype(F32)

    row_tiles(rows, widen)
    done = 0
    for l in reversed(range(layers)):
        qkv_ref, sib_ref, ctx_ref, ctx_sib_ref, lse_ref, r1_ref, r2_ref, hl_ref, hl_sib_ref, g_ref, g_sib_ref, slope_ref, xb_ref, xb_sib_ref = saved[l]
        first = l * GROUPS
        base = (layers - 1 - l) * GROUPS
        clock = 11 * (layers - 1 - l)

        def down_feeds(i, slot):
            return (
                feed(0, slot, columns(g_ref, i, 512), left_buf.at[slot]),
                feed(1, slot, columns(g_sib_ref, i, 512), left_sib_buf.at[slot]),
            )

        begin(down_feeds)
        load(0, r2_ref, r_buf).wait()

        def second(at):
            dy = acc[at, :]
            dr, part = norm_back(dy, r_buf[at, :], vec_ref[l, 4:5, :])
            acc[at, :] = dr
            dm[at, :] = dr.astype(BF16)
            add_small(l, 0, part)
            add_small(l, 1, dy)
            add_small(l, 2, dr)

        row_tiles(rows, second)
        dm_copy = exchange(0, dm, dm_sib)
        dm_copy.start()
        r_load = load(0, r1_ref, r_buf)
        r_load.start()
        right_load = load(1, hl_ref, right_buf)
        right_load.start()
        right_sib_load = load(2, hl_sib_ref, right_sib_buf)
        right_sib_load.start()
        dm_copy.wait()

        def down_body(i, slot):
            fresh = (i == 0) if l == layers - 1 else False
            unit(left_buf[slot], left_sib_buf[slot], dm[...], dm_sib[...], lax.rem(i, 2), base + i, fresh)
            pl.when(lax.rem(i, 2) == 1)(lambda: reduction.tick(clock + lax.div(i, 2)))

        def place_of(i):
            a = 1 - lax.div(i, FF_GROUPS)
            return a, lax.rem(i, FF_GROUPS)

        def ff_feeds(i, slot):
            a, n = place_of(i)
            j = a * FF_GROUPS + n
            return (
                feed(2, slot, weight(a, first + down_group(n)), wa_buf.at[slot]),
                feed(3, slot, weight(a, first + in_group(n)), wb_buf.at[slot]),
                feed(4, slot, columns(slope_ref, j, 512), slope_buf.at[slot]),
            )

        begin(ff_feeds)
        stream(FF_GROUPS, down_feeds, down_body)
        unit_store(1, base + FF_GROUPS - 1).wait()

        def ff_body(i, slot):
            a, n = place_of(i)
            j = a * FF_GROUPS + n
            dg = nt(dm[...], block_of(wa_buf.at[slot]))
            d = (dg * slope_buf[slot].astype(F32)).astype(BF16)
            du[j] = d
            pl.when(a == 1)(lambda: give_du(j, n).start())
            dbi_ref[l, a, n] = jnp.sum(d.astype(F32), axis=0, keepdims=True)
            acc[...] += nn(d, block_of(wb_buf.at[slot]))
            pl.when(lax.rem(i, 4) == 3)(lambda: reduction.tick(clock + 2 + lax.div(i, 4)))

        stream(2 * FF_GROUPS, ff_feeds, ff_body)

        def out_feeds(i, slot):
            return (feed(2, slot, weight(i, first + OUT_GROUP), wa_buf.at[slot]),)

        begin(out_feeds)
        r_load.wait()

        def first_norm(at):
            dy = acc[at, :]
            dr, part = norm_back(dy, r_buf[at, :], vec_ref[l, 1:2, :])
            dr1[at, :] = dr
            da[at, :] = dr.astype(BF16)
            add_small(l, 3, part)
            add_small(l, 4, dy)
            add_small(l, 5, dr)

        row_tiles(rows, first_norm)
        if l > 0:
            load(0, saved[l - 1][6], r_buf).start()
        da_copy = exchange(1, da, da_sib)
        da_copy.start()

        def out_body(i, slot):
            dctx[:, pl.ds(pl.multiple_of(i * 512, 512), 512)] = nt(da[...], block_of(wa_buf.at[slot])).astype(BF16)

        stream(2, out_feeds, out_body)

        pairs = width // 128

        def pair_feeds(p, slot):
            far = lax.rem(p + pairs // 2, pairs)
            return (
                feed(5, slot, columns(qkv_ref.at[0], p, 128), pair_buf.at[slot, 0, pl.ds(0, rows)]),
                feed(6, slot, columns(qkv_ref.at[1], p, 128), pair_buf.at[slot, 1, pl.ds(0, rows)]),
                feed(7, slot, columns(sib_ref.at[0], far, 128), pair_buf.at[slot, 1, pl.ds(rows, rows)]),
                feed(8, slot, columns(qkv_ref.at[2], p, 128), pair_buf.at[slot, 2, pl.ds(0, rows)]),
                feed(9, slot, columns(sib_ref.at[1], far, 128), pair_buf.at[slot, 2, pl.ds(rows, rows)]),
                feed(10, slot, columns(ctx_ref, p, 128), pair_buf.at[slot, 3, pl.ds(0, rows)]),
                feed(11, slot, lse_ref.at[p], lse_buf.at[slot]),
            )

        begin(pair_feeds)
        right_load.wait()
        right_sib_load.wait()

        def in_body(n, _):
            give_du(FF_GROUPS + n, n).wait()
            unit(du[n], du_sib[n], right_buf[...], right_sib_buf[...], lax.rem(n, 2), base + FF_GROUPS + n, n == 0)
            pl.when(lax.rem(n, 2) == 1)(lambda: reduction.tick(clock + 4 + lax.div(n, 2)))
            return 0

        lax.fori_loop(0, FF_GROUPS, in_body, 0)

        right_load = load(1, xb_ref, right_buf)
        right_load.start()
        right_sib_load = load(2, xb_sib_ref, right_sib_buf)
        right_sib_load.start()
        left_load = load(3, columns(ctx_ref, 0, 512), left_buf.at[0])
        left_load.start()
        left_sib_load = load(4, ctx_sib_ref, left_sib_buf.at[0])
        left_sib_load.start()
        da_copy.wait()
        left_load.wait()
        left_sib_load.wait()
        unit(left_buf[0], left_sib_buf[0], da[...], da_sib[...], 0, base + 2 * FF_GROUPS)
        unit_store(0, base + 2 * FF_GROUPS).wait()

        def dx_feeds(i, slot):
            return (feed(3, slot, weight(lax.rem(i, 2), first + lax.rem(lax.div(i, 2) + 2, 3)), wa_buf.at[slot]),)

        begin(dx_feeds)

        def give_pair(p):
            far = lax.rem(p + pairs // 2, pairs)
            at = pl.ds(pl.multiple_of(far * 128, 128), 128)
            return pltpu.make_async_remote_copy(
                src_ref=kv_out.at[:, :, at], dst_ref=kv_far.at[:, :, at], send_sem=pair_send.at[p], recv_sem=pair_recv.at[far],
                device_id=partners[FLIP_C], device_id_type=MESH,
            )

        def pair_body(p, slot):
            far = lax.rem(p + pairs // 2, pairs)
            here = pl.ds(pl.multiple_of(p * 128, 128), 128)
            mask = spread_mask(mask_ref[p], key_ref[...])
            dq, dk, dv = attend_back_pair(
                pair_buf[slot, 0, 0:rows], pair_buf[slot, 1], pair_buf[slot, 2], hot_buf[...], mask,
                pair_buf[slot, 3, 0:rows], lse_buf[slot], dctx[:, here],
            )
            dqkv[0, :, here] = dq.astype(BF16)
            dqkv[1, :, here] = dk[:rows].astype(BF16)
            dqkv[2, :, here] = dv[:rows].astype(BF16)
            there = pl.ds(pl.multiple_of(far * 128, 128), 128)
            kv_out[0, :, there] = dk[rows:].astype(BF16)
            kv_out[1, :, there] = dv[rows:].astype(BF16)
            give_pair(p).start()
            pl.when(lax.rem(p, 3) == 1)(lambda: reduction.tick(clock + 6 + lax.div(p, 3)))

        stream(pairs, pair_feeds, pair_body)

        def settle_pair(p, _):
            give_pair(p).wait()
            return 0

        lax.fori_loop(0, pairs, settle_pair, 0)
        for n in range(2):
            add_rows(dqkv.at[1 + n], kv_far.at[n], rows)
        d_copy = exchange(3, dqkv.at[:, :, pl.ds(512, 512)], d_sib)
        d_copy.start()
        right_load.wait()
        right_sib_load.wait()
        d_copy.wait()

        def qkv_body(n, _):
            unit(
                dqkv[n, :, 0:512], d_sib[n], right_buf[...], right_sib_buf[...],
                lax.rem(n + 1, 2), base + 2 * FF_GROUPS + 1 + n, n == 0,
            )
            pl.when(n == 1)(lambda: reduction.tick(clock + 9))
            return 0

        lax.fori_loop(0, 3, qkv_body, 0)

        def start_dx(at):
            acc[at, :] = dr1[at, :]

        row_tiles(rows, start_dx)

        def dx_body(i, slot):
            a, n = lax.rem(i, 2), lax.div(i, 2)
            d = dqkv[n, :, pl.ds(pl.multiple_of(a * 512, 512), 512)]
            qkv_sums_ref[l, n, a] = jnp.sum(d.astype(F32), axis=0, keepdims=True)
            acc[...] += nn(d, block_of(wa_buf.at[slot]))
            pl.when(i == 3)(lambda: reduction.tick(clock + 10))

        stream(6, dx_feeds, dx_body)
        done = clock + 11

    def narrow(at):
        da[at, :] = acc[at, :].astype(BF16)

    row_tiles(rows, narrow)
    unit_store(1, total - 1).wait()
    ending.tick(0)
    dp, y = lax.axis_index("dp"), lax.axis_index("tensor")
    core = dp % 2
    turned = unit_order(y, ((dp // 2) % 2, (dp // 4) % 2, (dp // 8) % 2))

    def in_order(pair):
        rows_ab = lax.dot_general(
            jnp.concatenate(pair, axis=0), turned, (((1,), (0,)), ((), ())),
            precision=lax.Precision.HIGHEST, preferred_element_type=F32,
        )
        near = jnp.where(core == 0, rows_ab[0:1], rows_ab[1:2])
        far = jnp.where(core == 0, rows_ab[1:2], rows_ab[0:1])
        return [
            jnp.concatenate([near[:, h * 256 : (h + 1) * 256], far[:, h * 256 : (h + 1) * 256]], axis=1)
            for h in range(2)
        ]

    for l in range(layers):
        for n, source in enumerate((5, 2, 3, 0, 4, 1)):
            row = n * layers + l if n < 2 else 2 * layers + (n // 2 - 1) * 2 * layers + 2 * l + n % 2
            packed[row : row + 1, :] = small_ref[l, source : source + 1, :]
        for n, t in enumerate((0, 2)):
            for h, part in enumerate(in_order([qkv_sums_ref[l, t, a] for a in range(2)])):
                packed[6 * layers + h * layers + l : 6 * layers + h * layers + l + 1, n * 512 : (n + 1) * 512] = part
        for n in range(FF_GROUPS):
            for h, part in enumerate(in_order([dbi_ref[l, a, n] for a in range(2)])):
                row = 8 * layers + h * 2 * layers + 2 * l + n // 2
                packed[row : row + 1, (n % 2) * 512 : (n % 2 + 1) * 512] = part

    for n, bit in enumerate((FLIP_C, FLIP_Y, FLIP_X, FLIP_Z0, FLIP_Z1)):
        cross = pltpu.make_async_remote_copy(
            src_ref=packed, dst_ref=far_buf.at[n], send_sem=far_send.at[n], recv_sem=far_recv.at[n],
            device_id=partners[bit], device_id_type=MESH,
        )
        cross.start()
        reduction.tick(done + n)
        ending.tick(1 + n)
        cross.wait()
        packed[...] += far_buf[n]

    swap(0, da, dx_out, True)

    def rest(n, _):
        reduction.tick(done + n)
        ending.tick(1 + n)
        return 0

    lax.fori_loop(5, PARTED * PARTS + LAST_TICK - 1, rest, 0)
    swap(0, da, dx_out, False)
    swap(1, x_ref, x_out, False)


def backward(upstream, stream_low, weights, hot, mask, mask_rows, vectors, saved):
    rows, width = upstream.shape
    layers = len(saved)
    total = layers * GROUPS
    anywhere = pl.BlockSpec(memory_space=pl.ANY)
    in_vmem = pl.BlockSpec(memory_space=pltpu.VMEM)
    low = lambda *shape: pltpu.VMEM(shape, BF16)
    dma = lambda *shape: pltpu.SemaphoreType.DMA(shape)
    ends = PARTED * PARTS
    return pl.pallas_call(
        functools.partial(backward_kernel, layers),
        out_shape=(
            jax.ShapeDtypeStruct((total, 16, 32, width), BF16),
            jax.ShapeDtypeStruct((total, 16, 32, width), BF16),
            jax.ShapeDtypeStruct((rows, width), BF16),
            jax.ShapeDtypeStruct((rows, width), BF16),
            jax.ShapeDtypeStruct((12 * layers, width), F32),
        ),
        in_specs=[anywhere] * 3 + [in_vmem] * 4 + [anywhere] * (PER_LAYER * layers),
        out_specs=(anywhere, anywhere, anywhere, anywhere, in_vmem),
        scratch_shapes=[
            pltpu.VMEM((rows, width), F32),
            pltpu.VMEM((rows, width), F32),
            low(rows, width),
            low(rows, width),
            low(rows, width),
            low(rows, width),
            low(2 * FF_GROUPS, rows, 512),
            low(FF_GROUPS, rows, 512),
            low(rows, width),
            low(3, rows, width),
            low(3, rows, 512),
            low(2, rows, width),
            low(2, rows, width),
            low(2, 2, 256, width),
            low(2, 2, 256, width),
            pltpu.VMEM((rows, width), F32),
            low(2, rows, 512),
            low(2, rows, 512),
            low(2, rows, 512),
            low(rows, width),
            low(rows, width),
            low(2, 4, 2 * rows, 128),
            pltpu.VMEM((2, 2, rows), F32),
            low(2, 16, 32, width),
            low(SLOTS, 8, 32, width),
            low(SLOTS, 4, 32, width),
            low(SLOTS, 2, 32, width),
            low(SLOTS, 1, 32, width),
            low(SLOTS, 8, 32, width),
            low(2, 8, 32, width),
            dma(12, 2),
            dma(5),
            dma(1),
            dma(2),
            dma(6),
            dma(6),
            dma(FF_GROUPS),
            dma(FF_GROUPS),
            dma(width // 128),
            dma(width // 128),
            dma(7, SLOTS),
            dma(7, SLOTS),
            dma(total),
            dma(total),
            dma(2),
            dma(SLOTS),
            pltpu.SemaphoreType.REGULAR((4,)),
            pltpu.SemaphoreType.REGULAR((3,)),
            pltpu.VMEM((layers, 2, FF_GROUPS, 1, 512), F32),
            pltpu.VMEM((layers, 3, 2, 1, 512), F32),
            pltpu.VMEM((layers, 8, width), F32),
            pltpu.VMEM((5, 12 * layers, width), F32),
            dma(5),
            dma(5),
            low(ends, 8, 32 // PARTS, width),
            low(ends, 4, 32 // PARTS, width),
            low(ends, 2, 32 // PARTS, width),
            low(ends, 1, 32 // PARTS, width),
            low(ends, 8, 32 // PARTS, width),
            low(2, 8, 32 // PARTS, width),
            dma(7, ends),
            dma(7, ends),
            dma(ends),
            dma(ends),
            dma(2),
            dma(ends),
        ],
        compiler_params=pltpu.CompilerParams(
            collective_id=1, has_side_effects=True, vmem_limit_bytes=60 << 20
        ),
        cost_estimate=pl.CostEstimate(flops=60 << 30, bytes_accessed=300 << 20, transcendentals=1 << 24),
        name="backward",
    )(upstream, stream_low, weights, hot, mask, mask_rows, vectors, *[ref for one in saved for ref in one])


def flip_order(values, axis, bits):
    for i, bit in enumerate(bits):
        values = jnp.where(bit == 0, values, jnp.flip(values, axis + i))
    return values


def sequence_shards(
    block_input, segment_ids, random_blocks, w_qkv, b_qv, w_out, b_out, w_in, b_in, w_down, b_down,
    ln_gain, ln_bias, cotangent,
):
    y = lax.axis_index("tensor")
    dp = lax.axis_index("dp")
    core, x_bit, z0, z1 = dp % 2, (dp // 2) % 2, (dp // 4) % 2, dp // 8
    code = core * 8 + x_bit * 4 + z0 * 2 + z1
    code_arg = code.reshape(1).astype(jnp.int32)
    device_bits = (core, x_bit, z0, z1)

    rows, _, width = block_input.shape
    layers = w_qkv.shape[0]
    blocks = random_blocks.shape[2]
    own_blocks = blocks // 2
    heads = random_blocks.shape[1] * 2

    chosen = random_blocks[0]
    near = jnp.concatenate([chosen.reshape(-1), segment_ids[0]])
    sibling = flip(near, FLIP_C)
    across, diagonal = flip(chosen.reshape(-1), FLIP_Y), flip(chosen.reshape(-1), SWAP)
    mine = jnp.concatenate([near[: chosen.size], across, near[chosen.size :]])
    other = jnp.concatenate([sibling[: chosen.size], diagonal, sibling[chosen.size :]])
    packed = jnp.where(core == y, mine, other)
    chosen = packed[: 2 * chosen.size].reshape(2, heads // 2, blocks, -1)
    segments = packed[2 * random_blocks.size :]
    chosen = flip_order(chosen.reshape(2, 2, 2, 2, blocks, -1), 1, device_bits[:3])
    chosen = chosen.transpose(1, 0, 2, 3, 4, 5).reshape(heads, blocks, -1)
    segments = segments.reshape(2, rows)
    segments = jnp.where(core == 0, segments, segments[::-1]).reshape(-1)
    query_block = core * own_blocks + jnp.arange(own_blocks)
    key_block = jnp.arange(blocks) ^ (core * own_blocks)
    allowed = (
        (jnp.abs(query_block[:, None] - key_block[None, :]) <= 1)
        | (key_block[None, :] == 0)
        | (key_block[None, :] == blocks - 1)
        | (query_block[:, None] == 0)
        | (query_block[:, None] == blocks - 1)
    )
    chosen = lax.dynamic_slice_in_dim(chosen, core * own_blocks, own_blocks, axis=1)
    allowed = allowed[None] | jnp.any(chosen[:, :, None, :] == key_block[None, None, :, None], axis=3)
    block_rows = rows // own_blocks
    documents = jnp.arange(HEAD_DIM - own_blocks)
    mask = jnp.pad(
        jnp.where(allowed, 0.0, BIG).astype(F32).transpose(0, 2, 1), ((0, 0), (0, 0), (0, HEAD_DIM - own_blocks))
    )
    mask = mask.reshape(heads // 2, 2, blocks, HEAD_DIM).transpose(0, 2, 1, 3).reshape(heads // 2, blocks, 2 * HEAD_DIM)
    document_part = jnp.where(
        (segments[:, None] == documents[None, :]) | (documents[None, :] > 7), 0.0, BIG
    ).astype(F32)
    mask_rows = jnp.pad(document_part, ((0, 0), (own_blocks, 0)))
    mask_rows = jnp.concatenate([mask_rows, mask_rows], axis=1)
    block_rows = rows // own_blocks
    hot = jnp.concatenate(
        [
            jnp.repeat(jnp.eye(own_blocks, dtype=BF16), block_rows, axis=0),
            (segments[:rows, None] == documents[None, :]).astype(BF16),
        ],
        axis=1,
    )
    hot = jnp.concatenate([hot, hot], axis=1)

    bias_pack = jnp.concatenate(
        [
            flip_order(b_qv.reshape(layers * 2, 2, 2, 2, 2, -1), 1, device_bits).reshape(-1),
            flip_order(b_in.reshape(layers * FF_GROUPS, 2, 2, 2, 2, -1), 1, device_bits).reshape(-1),
        ]
    )
    bias_far = flip(bias_pack, FLIP_Y)
    n_qv = b_qv.size

    def local_bias(near, far, count):
        near, far = near.reshape(count, 2, 1, 256), far.reshape(count, 2, 1, 256)
        return jnp.concatenate([near, far], axis=2).reshape(count, 2, 512)

    bias_qv = local_bias(bias_pack[:n_qv], bias_far[:n_qv], layers * 2).reshape(layers, 2, 2, 1, 512)
    bias_qkv = jnp.stack([bias_qv[:, 0], jnp.zeros_like(bias_qv[:, 0]), bias_qv[:, 1]], axis=1)
    bias_in = local_bias(bias_pack[n_qv:], bias_far[n_qv:], layers * FF_GROUPS)
    bias_in = bias_in.reshape(layers, FF_GROUPS, 2, 1, 512).swapaxes(1, 2)

    vectors = [
        jnp.stack(
            [
                b_out[l], ln_gain[l, 0], ln_bias[l, 0], b_down[l], ln_gain[l, 1], ln_bias[l, 1],
                b_out[l], b_out[l],
            ]
        )
        for l in range(layers)
    ]
    vectors = jnp.stack(vectors)
    weights, upstream_low, stream_low, saved = forward(
        block_input, cotangent, w_qkv, w_out, w_in, w_down, hot, mask, mask_rows, bias_qkv, bias_in, vectors
    )
    _, grads, dx_low, x_low, packed = backward(
        upstream_low, stream_low, weights, hot, mask, mask_rows, vectors, saved
    )
    grads = grads.reshape(layers * GROUPS, 512, width)

    def placing(shape, block, index, turned, count, start, rows_too=()):
        return place(
            grads, shape, block, index, turned, count, lambda l, i: (layers - 1 - l) * GROUPS + start + i, code_arg,
            rows_too,
        )

    g_b_out, g_b_down, g_gain, g_shift, g_b_qv, g_b_in = hand_out(packed, y.reshape(1).astype(jnp.int32), layers)
    g_down, block_output, input_grad = placing(
        w_down.shape, (1, 512, width), lambda l, i: (l, i, 0), False, FF_GROUPS, 0, (x_low, dx_low)
    )
    (g_in,) = placing(w_in.shape, (1, width, 512), lambda l, i: (l, 0, i), True, FF_GROUPS, FF_GROUPS)
    (g_qkv,) = placing(w_qkv.shape, (1, 1, width, 512), lambda l, i: (l, i, 0, 0), True, 3, 2 * FF_GROUPS + 1)
    (g_out,) = placing(w_out.shape, (1, 512, width), lambda l, i: (l, 0, 0), False, 1, 2 * FF_GROUPS)
    return (
        block_output,
        input_grad,
        g_qkv,
        g_b_qv,
        g_out,
        g_b_out,
        g_in,
        g_b_in,
        g_down,
        g_b_down,
        g_gain,
        g_shift,
    )


def as_sent(array):

    def short(part):
        return part.astype(jnp.bfloat16) if part.dtype == jnp.float32 else part

    return jax.tree.map(short, array)


def norm_rows(values, gain_row, shift_row):
    row_mean = jnp.mean(values, axis=-1, keepdims=True)
    centred = values - row_mean
    variance = jnp.mean(centred * centred, axis=-1, keepdims=True)
    return centred * lax.rsqrt(variance + 1e-06) * gain_row + shift_row


def gelu_exact(values):
    return jax.nn.gelu(values, approximate=False)


def block_mask(chosen_blocks, segment_rows):
    nblocks = chosen_blocks.shape[2]
    block_index = jnp.arange(nblocks)
    near_blocks = jnp.abs(block_index[:, None] - block_index[None, :]) <= 1
    edge_blocks = (
        (block_index[None, :] == 0)
        | (block_index[None, :] == nblocks - 1)
        | (block_index[:, None] == 0)
        | (block_index[:, None] == nblocks - 1)
    )
    picked_blocks = jnp.any(chosen_blocks[..., None] == block_index, axis=3)
    allowed = near_blocks | edge_blocks | picked_blocks
    block_rows = segment_rows.shape[1] // nblocks
    allowed = jnp.repeat(jnp.repeat(allowed, block_rows, axis=2), block_rows, axis=3)
    same_doc = segment_rows[:, :, None] == segment_rows[:, None, :]
    return allowed & same_doc[:, None]


def masked_scores(queries, key_rows, allowed, score_scale):
    scores = (
        jnp.einsum("qshd,kshd->shqk", queries, key_rows, preferred_element_type=jnp.float32)
        * score_scale
    )
    return jnp.where(allowed, scores, -1e30)


def shards(
    block_input,
    segment_ids,
    random_blocks,
    w_qkv,
    b_qv,
    w_out,
    b_out,
    w_in,
    b_in,
    w_down,
    b_down,
    ln_gain,
    ln_bias,
    cotangent,
):
    score_scale = HEAD_DIM ** (-0.5)
    shard_rows, seq_count, model_width = block_input.shape
    layers = w_qkv.shape[0]
    local_width = w_qkv.shape[3]
    local_heads = local_width // HEAD_DIM
    allowed = block_mask(random_blocks, segment_ids)
    saved_acts = []
    stream = block_input
    for layer_index in range(layers):
        w_proj = w_qkv[layer_index].astype(jnp.bfloat16)
        w_mix = w_out[layer_index].astype(jnp.bfloat16)
        rows_low = stream.astype(jnp.bfloat16)
        full_rows = lax.all_gather(rows_low, "tensor", axis=0, tiled=True)
        length = full_rows.shape[0]
        projected = jnp.einsum(
            "lsd,tdc->tlsc", full_rows, w_proj, preferred_element_type=jnp.float32
        )
        qkv_bias = jnp.stack(
            [b_qv[layer_index, 0], jnp.zeros_like(b_qv[layer_index, 0]), b_qv[layer_index, 1]]
        )
        qkv_low = (projected + qkv_bias[:, None, None, :]).astype(jnp.bfloat16)
        head_view = qkv_low.reshape(3, length, seq_count, local_heads, HEAD_DIM)
        scores = masked_scores(head_view[0], head_view[1], allowed, score_scale)
        row_top = jnp.max(scores, axis=-1, keepdims=True)
        log_total = row_top + jnp.log(jnp.sum(jnp.exp(scores - row_top), axis=-1, keepdims=True))
        probs_low = jnp.exp(scores - log_total).astype(jnp.bfloat16)
        context = jnp.einsum(
            "shqk,kshd->qshd", probs_low, head_view[2], preferred_element_type=jnp.float32
        )
        context = context.reshape(length, seq_count, local_width).astype(jnp.bfloat16)
        mixed = lax.psum_scatter(
            jnp.einsum("lsc,cd->lsd", context, w_mix, preferred_element_type=jnp.float32).astype(
                jnp.bfloat16
            ),
            "tensor",
            scatter_dimension=0,
            tiled=True,
        ).astype(jnp.float32)
        first_sum = stream + mixed + b_out[layer_index]
        hidden_rows = norm_rows(first_sum, ln_gain[layer_index, 0], ln_bias[layer_index, 0])
        hidden_low = hidden_rows.astype(jnp.bfloat16)
        up_weight = w_in[layer_index].astype(jnp.bfloat16)
        backward_weight = w_down[layer_index].astype(jnp.bfloat16)
        hidden_full = lax.all_gather(hidden_low, "tensor", axis=0, tiled=True)
        preactivation = (
            jnp.einsum("twn,nj->twj", hidden_full, up_weight, preferred_element_type=jnp.float32)
            + b_in[layer_index]
        )
        activation_reduced = gelu_exact(preactivation).astype(jnp.bfloat16)
        grown = lax.psum_scatter(
            jnp.einsum(
                "unj,jp->unp",
                activation_reduced,
                backward_weight,
                preferred_element_type=jnp.float32,
            ).astype(jnp.bfloat16),
            "tensor",
            scatter_dimension=0,
            tiled=True,
        ).astype(jnp.float32)
        second_sum = hidden_rows + grown + b_down[layer_index]
        stream = norm_rows(second_sum, ln_gain[layer_index, 1], ln_bias[layer_index, 1])
        keep_rows, keep_hidden = (full_rows, hidden_full)
        saved_acts.append(
            (
                keep_rows,
                head_view,
                log_total,
                context,
                first_sum,
                keep_hidden,
                preactivation,
                activation_reduced,
                second_sum,
                up_weight,
                backward_weight,
            )
        )
    upstream = cotangent
    grads_by_layer = [None] * layers
    for layer_index in reversed(range(layers)):
        (
            keep_rows,
            head_view,
            log_total,
            context,
            first_sum,
            keep_hidden,
            preactivation,
            activation_reduced,
            second_sum,
            up_weight,
            backward_weight,
        ) = saved_acts[layer_index]
        full_rows, hidden_full = (keep_rows, keep_hidden)
        length = full_rows.shape[0]
        w_proj = w_qkv[layer_index].astype(jnp.bfloat16)
        w_mix = w_out[layer_index].astype(jnp.bfloat16)
        _, pull_second = jax.vjp(
            norm_rows, second_sum, ln_gain[layer_index, 1], ln_bias[layer_index, 1]
        )
        d_second, d_gain_two, d_shift_two = pull_second(upstream)
        _, pull_gelu = jax.vjp(gelu_exact, preactivation)
        widened_full = lax.all_gather(d_second.astype(jnp.bfloat16), "tensor", axis=0, tiled=True)
        down_gradient = jnp.einsum(
            "uxc,uxw->cw", activation_reduced, widened_full, preferred_element_type=jnp.float32
        )
        activation_gradient = jnp.einsum(
            "mra,xa->mrx", widened_full, backward_weight, preferred_element_type=jnp.float32
        )
        preactivation_gradient_reduced = pull_gelu(activation_gradient)[0].astype(jnp.bfloat16)
        up_gradient = jnp.einsum(
            "kmx,kmt->xt",
            hidden_full,
            preactivation_gradient_reduced,
            preferred_element_type=jnp.float32,
        )
        g_up_bias = jnp.sum(preactivation_gradient_reduced.astype(jnp.float32), axis=(0, 1))
        d_hidden = d_second + lax.psum_scatter(
            jnp.einsum(
                "hmp,tp->hmt",
                preactivation_gradient_reduced,
                up_weight,
                preferred_element_type=jnp.float32,
            ).astype(jnp.bfloat16),
            "tensor",
            scatter_dimension=0,
            tiled=True,
        ).astype(jnp.float32)
        _, pull_first = jax.vjp(
            norm_rows, first_sum, ln_gain[layer_index, 0], ln_bias[layer_index, 0]
        )
        d_first, d_gain_one, d_shift_one = pull_first(d_hidden)
        full_mixed = lax.all_gather(d_first.astype(jnp.bfloat16), "tensor", axis=0, tiled=True)
        g_out = jnp.einsum("lsc,lsd->cd", context, full_mixed, preferred_element_type=jnp.float32)
        d_context = jnp.einsum(
            "lsd,cd->lsc", full_mixed, w_mix, preferred_element_type=jnp.float32
        ).astype(jnp.bfloat16)
        d_context = d_context.reshape(length, seq_count, local_heads, HEAD_DIM)
        queries, key_rows, value_rows = (head_view[0], head_view[1], head_view[2])
        scores = masked_scores(queries, key_rows, allowed, score_scale)
        attn_probs = jnp.exp(scores - log_total)
        probs_low = attn_probs.astype(jnp.bfloat16)
        d_probs = jnp.einsum(
            "qshd,kshd->shqk", d_context, value_rows, preferred_element_type=jnp.float32
        )
        d_scores = attn_probs * (d_probs - jnp.sum(d_probs * attn_probs, axis=-1, keepdims=True))
        d_scores = d_scores.astype(jnp.bfloat16)
        d_query = (
            jnp.einsum("shqk,kshd->qshd", d_scores, key_rows, preferred_element_type=jnp.float32)
            * score_scale
        )
        d_key = (
            jnp.einsum("shqk,qshd->kshd", d_scores, queries, preferred_element_type=jnp.float32)
            * score_scale
        )
        d_value = jnp.einsum(
            "shqk,qshd->kshd", probs_low, d_context, preferred_element_type=jnp.float32
        )
        d_qkv = (
            jnp.stack([d_query, d_key, d_value])
            .reshape(3, length, seq_count, local_width)
            .astype(jnp.bfloat16)
        )
        g_proj = jnp.einsum("lsd,tlsc->tdc", full_rows, d_qkv, preferred_element_type=jnp.float32)
        qkv_sums = jnp.sum(d_qkv.astype(jnp.float32), axis=(1, 2))
        g_bias = jnp.stack([qkv_sums[0], qkv_sums[2]])
        upstream = d_first + lax.psum_scatter(
            jnp.einsum("tlsc,tdc->lsd", d_qkv, w_proj, preferred_element_type=jnp.float32).astype(
                jnp.bfloat16
            ),
            "tensor",
            scatter_dimension=0,
            tiled=True,
        ).astype(jnp.float32)
        weight_grads = (g_proj, g_bias, g_out, up_gradient, g_up_bias, down_gradient)
        small_grads = (
            jnp.sum(d_first, axis=(0, 1)),
            jnp.sum(d_second, axis=(0, 1)),
            jnp.stack([d_gain_one, d_gain_two]),
            jnp.stack([d_shift_one, d_shift_two]),
        )
        grads_by_layer[layer_index] = (weight_grads, small_grads)
    weight_stack = tuple(
        (
            jnp.stack([grads_by_layer[layer_index][0][member] for layer_index in range(layers)])
            for member in range(6)
        )
    )
    small_stack = tuple(
        (
            jnp.stack([grads_by_layer[layer_index][1][member] for layer_index in range(layers)])
            for member in range(4)
        )
    )
    weight_stack = jax.tree.map(
        lambda part: part.astype(jnp.float32), lax.psum(as_sent(weight_stack), "dp")
    )
    small_stack = lax.psum(small_stack, ("dp", "tensor"))
    return (
        stream,
        upstream,
        weight_stack[0],
        weight_stack[1],
        weight_stack[2],
        small_stack[0],
        weight_stack[3],
        weight_stack[4],
        weight_stack[5],
        small_stack[1],
        small_stack[2],
        small_stack[3],
    )


def solution(mesh):
    by_sequence = mesh.shape["tensor"] == 2 and mesh.shape["dp"] == 16
    return jax.shard_map(
        sequence_shards if by_sequence else shards,
        mesh=mesh,
        in_specs=(
            P("tensor", "dp", None),
            P("dp", None),
            P("dp", "tensor", None, None),
            P(None, None, None, "tensor"),
            P(None, None, "tensor"),
            P(None, "tensor", None),
            P(),
            P(None, None, "tensor"),
            P(None, "tensor"),
            P(None, "tensor", None),
            P(),
            P(),
            P(),
            P("tensor", "dp", None),
        ),
        out_specs=(
            P("tensor", "dp", None),
            P("tensor", "dp", None),
            P(None, None, None, "tensor"),
            P(None, None, "tensor"),
            P(None, "tensor", None),
            P(),
            P(None, None, "tensor"),
            P(None, "tensor"),
            P(None, "tensor", None),
            P(),
            P(),
            P(),
        ),
        check_vma=False,
    )
```
